32 devices in a mesh: head: 2 (over x), seq: 16 (over z, y, core).
Axes of the slice: x: 2, y: 2, z: 4, core: 2. Of those that a mesh axis runs over, the one named last changes fastest.
Arguments:
- layer_input: bfloat16 [16, 1024, 1024], P('seq', 'head'), may hold values from -6 to 6
- segment_ids: int32 [16384], replicated, may hold values from 0 to 31, never falling along the last dimension, each value on 1 to 4096 neighbouring positions
- norm1_gain: bfloat16 [1024], P(('head', 'seq')), may hold values from 0.5 to 1.5
- w_query: bfloat16 [1024, 256], P(('head', 'seq')), may hold values from -0.1875 to 0.1875
- w_key: bfloat16 [1024, 256], P(('head', 'seq')), may hold values from -0.1875 to 0.1875
- w_value: bfloat16 [1024, 1024], P(('head', 'seq')), may hold values from -0.1875 to 0.1875
- w_out: bfloat16 [1024, 1024], P(('head', 'seq')), may hold values from -1.5 to 1.5
- norm2_gain: bfloat16 [1024], P(('head', 'seq')), may hold values from 0.5 to 1.5
- w_gate: bfloat16 [1024, 2752], P('seq', 'head'), may hold values from -0.1875 to 0.1875
- w_up: bfloat16 [1024, 2752], P('seq', 'head'), may hold values from -0.1875 to 0.1875
- w_down: bfloat16 [2752, 1024], P('head', 'seq'), may hold values from -0.109375 to 0.109375
- output_grad: bfloat16 [16, 1024, 1024], P('seq', 'head'), may hold values from -6 to 6
Outputs:
- layer_output: bfloat16 [16, 1024, 1024], P('seq', 'head')
- input_grad: float32 [16, 1024, 1024], P('seq', 'head')
- d_norm1_gain: float32 [1024], P(('head', 'seq'))
- d_w_query: float32 [1024, 256], P(('head', 'seq'))
- d_w_key: float32 [1024, 256], P(('head', 'seq'))
- d_w_value: float32 [1024, 1024], P(('head', 'seq'))
- d_w_out: float32 [1024, 1024], P(('head', 'seq'))
- d_norm2_gain: float32 [1024], P(('head', 'seq'))
- d_w_gate: float32 [1024, 2752], P('seq', 'head')
- d_w_up: float32 [1024, 2752], P('seq', 'head')
- d_w_down: float32 [2752, 1024], P('head', 'seq')
The draws below stay inside these ranges and needn't reach their ends.
Inputs may be any that keep to these rules, and one draw needn't show every extreme that they name: `segment_ids`: document numbers never fall along the stream; each document has 1 to 4096 tokens and one has exactly 4096.
All inputs are finite; a program needn't handle non-finite values.
Results may differ from the reference program's by a relative error of at most 0.013.
Values may be sent and summed in bfloat16 or wider, within the bound.
A program may use at most 320 MiB of HBM per device.

```python
import math
import jax
import jax.numpy as jnp
import numpy as np
from jax import lax

D = 1024
HEADS = 16
QD = 16
VD = 64
FF = 2752
DOC_MAX = 4096
QK = 256
HV = 1024
SEG_TOK = 1024
BLOCKS = 16
STREAM = 16384
DOCS = 32


def level_of(rng, extent, shards, low, top_value):
    factor_of, own = 1.0, jax.random.fold_in(rng, 6)
    for dim, shards_of in shards:
        draws = jnp.exp(jax.random.uniform(jax.random.fold_in(own, dim), (shards_of,), jnp.float32, low / len(shards), top_value / len(shards)))
        factor_of = factor_of * jnp.repeat(draws, extent[dim] // shards_of).reshape([-1 if axis == dim else 1 for axis in range(len(extent))])
    return factor_of


def profile(amount, total, limit, skew):
    loads = [(1 << 20) // math.isqrt(grade ** skew) + 1 for grade in range(2, amount + 1)]
    surplus, holding = total - limit - (amount - 1), [1] * (amount - 1)
    while surplus > 0:
        free = [i for i in range(amount - 1) if holding[i] < limit]
        pool, left = sum([loads[i] for i in free]), surplus
        for i in free:
            extra = min(limit - holding[i], max(1, left * loads[i] // pool), surplus)
            holding[i] = holding[i] + extra
            surplus = surplus - extra
    return np.array([limit] + holding)


def uneven(own_key, amount, total, bound, lean):
    if amount == 2:
        one = jax.random.randint(own_key, (), max(1, total - bound), min(bound, total - 1) + 1)
        return jnp.stack([one, total - one])
    lengths = jnp.asarray(profile(amount, total, bound, lean), jnp.int32)
    twos = (amount - 1) // 2
    source_of, taker = lengths[1:1 + 2 * twos:2], lengths[2:2 + 2 * twos:2]
    margin = jnp.minimum(source_of - 1, bound - taker)
    moved = jax.random.randint(jax.random.fold_in(own_key, 1), (twos,), 0, 1 << 20) % (margin + 1)
    lengths = lengths.at[1:1 + 2 * twos:2].set(source_of - moved).at[2:2 + 2 * twos:2].set(taker + moved)
    return lengths[jax.random.permutation(jax.random.fold_in(own_key, 2), amount)]


def noise(stream_key, shape, width, reach, cuts=(), held_as=jnp.bfloat16):
    loudness = level_of(stream_key, shape, cuts, -0.22, 0.18) if cuts else 1.0
    values = jax.random.normal(stream_key, shape, jnp.float32) * width * loudness
    return jnp.minimum(jnp.maximum(values, -reach), reach).astype(held_as)


def setup_inputs(seed: int = 0) -> dict:
    keys = jax.random.split(jax.random.key(seed), 13)
    layer_input = noise(keys[0], (BLOCKS, SEG_TOK, D), 1.0, 6.0, ((0, 16), (1, 2)))
    segment_ids = jnp.searchsorted(jnp.cumsum(uneven(keys[1], DOCS, STREAM, DOC_MAX, 2)), jnp.arange(STREAM), side="right").astype(jnp.int32)
    norm1_gain = jnp.clip(1.0 + 0.1 * jax.random.normal(keys[2], (D,), jnp.float32), 0.5, 1.5).astype(jnp.bfloat16)
    w_query = noise(keys[3], (D, QK), D ** -0.5, 0.1875, ((0, 32),))
    w_key = noise(keys[4], (D, QK), D ** -0.5, 0.1875, ((0, 32),))
    w_value = noise(keys[5], (D, HV), D ** -0.5, 0.1875, ((0, 32),))
    w_out = noise(keys[6], (HV, D), (HV // 64) ** -0.5, 1.5, ((0, 32),))
    norm2_gain = jnp.clip(1.0 + 0.1 * jax.random.normal(keys[7], (D,), jnp.float32), 0.5, 1.5).astype(jnp.bfloat16)
    w_gate = noise(keys[8], (D, FF), D ** -0.5, 0.1875, ((0, 16), (1, 2)))
    w_up = noise(keys[9], (D, FF), D ** -0.5, 0.1875, ((0, 16), (1, 2)))
    w_down = noise(keys[10], (FF, D), FF ** -0.5, 0.109375, ((0, 2), (1, 16)))
    output_grad = noise(keys[11], (BLOCKS, SEG_TOK, D), 1.0, 6.0, ((0, 16), (1, 2)))
    return {"layer_input": layer_input, "segment_ids": segment_ids, "norm1_gain": norm1_gain, "w_query": w_query, "w_key": w_key, "w_value": w_value, "w_out": w_out, "norm2_gain": norm2_gain, "w_gate": w_gate, "w_up": w_up, "w_down": w_down, "output_grad": output_grad}


@jax.custom_vjp
def low(v):
    return lax.optimization_barrier(v.astype(jnp.bfloat16)).astype(jnp.float32)

@jax.custom_vjp
def low_back(v):
    return v

def low_keep(v):
    return (low(v), None)

def low_pass(kept, grad):
    return (grad,)

def back_keep(v):
    return (v, None)

def back_low(kept, grad):
    return (low(grad),)
low.defvjp(low_keep, low_pass)
low_back.defvjp(back_keep, back_low)
EPSILON = 1e-05
HIGHEST = lax.Precision.HIGHEST

def matmul(left, right):
    return jnp.dot(left, right, precision=HIGHEST, preferred_element_type=jnp.float32)

def rms_scale(values, gain):
    return values * lax.rsqrt(lax.optimization_barrier(jnp.mean(values * values, axis=-1, keepdims=True)) + EPSILON) * gain

def attention(query, key, value, segment_ids):
    window = DOC_MAX + SEG_TOK
    scale = QD ** (-0.5)

    def block(index):
        query_start = (index * SEG_TOK).astype(jnp.int32)
        key_start = jnp.maximum(query_start - DOC_MAX, 0).astype(jnp.int32)
        query_heads = lax.dynamic_slice_in_dim(query, query_start, SEG_TOK, 0).reshape(SEG_TOK, HEADS, QD)
        key_heads = lax.dynamic_slice_in_dim(key, key_start, window, 0).reshape(window, HEADS, QD)
        value_heads = lax.dynamic_slice_in_dim(value, key_start, window, 0).reshape(window, HEADS, VD)
        query_ids = lax.dynamic_slice_in_dim(segment_ids, query_start, SEG_TOK, 0)
        key_ids = lax.dynamic_slice_in_dim(segment_ids, key_start, window, 0)
        query_pos = query_start + jnp.arange(SEG_TOK, dtype=jnp.int32)
        key_pos = key_start + jnp.arange(window, dtype=jnp.int32)
        visible = (query_ids[:, None] == key_ids[None, :]) & (key_pos[None, :] <= query_pos[:, None])
        scores = low_back(jnp.einsum('qhd,khd->hqk', query_heads, key_heads, precision=HIGHEST) * scale)
        weights = jnp.where(visible[None], 1.0 + scores + 0.5 * scores * scores, 0.0)
        denominator = lax.optimization_barrier(jnp.sum(weights, axis=2))
        numerator = low_back(jnp.einsum('hqk,khd->qhd', low(weights), value_heads, precision=HIGHEST))
        outcome = low_back(low(numerator / denominator.T[:, :, None]))
        return outcome.reshape(SEG_TOK, HEADS * VD)
    blocks = lax.map(jax.checkpoint(block), jnp.arange(BLOCKS, dtype=jnp.int32))
    return blocks.reshape(STREAM, HEADS * VD)

def forward(inputs, gain_one, w_query, w_key, w_value, w_out, gain_two, w_gate, w_up, w_down, segment_ids):
    normed_one = low(rms_scale(inputs, gain_one))
    query = low_back(low(matmul(normed_one, w_query)))
    key = low_back(low(matmul(normed_one, w_key)))
    value = low_back(low(matmul(normed_one, w_value)))
    attended = attention(query, key, value, segment_ids)
    residual = inputs + low_back(matmul(attended, w_out))
    normed_two = low(rms_scale(residual, gain_two))
    gate = low_back(matmul(normed_two, w_gate))
    up_proj = low_back(matmul(normed_two, w_up))
    hidden = low(jax.nn.silu(gate) * up_proj)
    return residual + low_back(matmul(hidden, w_down))

def reference(layer_input, segment_ids, norm1_gain, w_query, w_key, w_value, w_out, norm2_gain, w_gate, w_up, w_down, output_grad):
    inputs = layer_input.astype(jnp.float32).reshape(STREAM, D)
    weight_list = [norm1_gain, w_query, w_key, w_value, w_out, norm2_gain, w_gate, w_up, w_down]
    weight_list = [item.astype(jnp.float32) for item in weight_list]

    def apply(inputs, g_one, w_q, w_k, w_v, w_o, g_two, w_g, w_u, w_d):
        return forward(inputs, g_one, w_q, w_k, w_v, w_o, g_two, w_g, w_u, w_d, segment_ids)
    outcome, pull = jax.vjp(apply, inputs, *weight_list)
    gradients = pull(output_grad.astype(jnp.float32).reshape(STREAM, D))
    return (outcome.astype(jnp.bfloat16).reshape(BLOCKS, SEG_TOK, D), gradients[0].reshape(BLOCKS, SEG_TOK, D), gradients[1], gradients[2], gradients[3], gradients[4], gradients[5], gradients[6], gradients[7], gradients[8], gradients[9])
```

```python
import functools

import jax
import jax.numpy as jnp
import numpy as np
from jax import lax
from jax.experimental import pallas as pl
from jax.experimental.pallas import tpu as pltpu
from jax.sharding import PartitionSpec as P

HEADS = 16
QD = 16
VD = 64
DOC_MAX = 4096
EPSILON = 1e-05
PAIRS = HEADS // 2
WIDE = 2 * VD
FEATS = 160
TILE = 256

BF = jnp.bfloat16
F32 = jnp.float32


def flip_seq(value, code):
    n = lax.axis_size("seq")
    return lax.ppermute(value, "seq", [(i, i ^ code) for i in range(n)])


def flip_head(value):
    n = lax.axis_size("head")
    return lax.ppermute(value, "head", [(i, i ^ 1) for i in range(n)])


def shift_seq(value, distance):
    n = lax.axis_size("seq")
    return lax.ppermute(
        value, "seq", [(i, i + distance) for i in range(n) if 0 <= i + distance < n]
    )


def layout():
    chips = lax.axis_size("seq") // 2
    near = 2 if chips <= 8 else 8
    far = chips // near
    return far, near


def place_kernel(groups, count, *refs):
    pieces, out, sem = refs[:count], refs[count], refs[count + 1]
    me = lax.axis_index("seq")
    head = lax.axis_index("head")
    n = lax.axis_size("seq")
    copies = []
    for piece, blocks in zip(pieces, groups):
        for index, (rel_head, rel_seq) in blocks:
            place = me ^ rel_seq
            if rel_head is not None:
                place = place + (head ^ rel_head) * n
            copies.append(
                pltpu.make_async_copy(piece.at[index], out.at[place], sem.at[len(copies)])
            )
    for copy in copies:
        copy.start()
    for copy in copies:
        copy.wait()


def place(pieces, groups, blocks):
    rows, cols = pieces[0].shape[-2:]
    total = sum(len(g) for g in groups)
    out = pl.pallas_call(
        functools.partial(place_kernel, groups, len(pieces)),
        out_shape=jax.ShapeDtypeStruct((blocks, rows, cols), pieces[0].dtype),
        in_specs=[pl.BlockSpec(memory_space=pl.ANY)] * len(pieces),
        out_specs=pl.BlockSpec(memory_space=pltpu.VMEM),
        scratch_shapes=[pltpu.SemaphoreType.DMA((total,))],
        compiler_params=pltpu.CompilerParams(vmem_limit_bytes=16 << 20),
        cost_estimate=pl.CostEstimate(
            flops=0, bytes_accessed=4 * blocks * rows * cols, transcendentals=0
        ),
        name="place",
    )(*pieces)
    return out.reshape(blocks * rows, cols)


def gather(shard, head_first):
    far, near = layout()
    far_codes = [2 * near * r for r in range(far)]
    near_codes = [2 * r for r in range(near)]
    if head_first:
        shard = jnp.stack([shard, flip_head(shard)])
    column = jnp.stack([shard] + [flip_seq(shard, code) for code in far_codes[1:]])
    held = [(column, 0, 0)]
    held += [(flip_seq(column, code), 0, code) for code in near_codes[1:]]
    if not head_first:
        held += [(flip_head(buf), 1, code) for buf, _, code in held]
    held += [(flip_seq(buf, 1), rel, code + 1) for buf, rel, code in held]
    result = []
    for buf, rel, code in held:
        if head_first:
            blocks = [((r, g), (g, code + far_codes[r])) for r in range(far) for g in range(2)]
        else:
            blocks = [((r,), (rel, code + far_codes[r])) for r in range(far)]
        result.append((buf, blocks))
    return result


def gather_rows(shard):
    got = gather(shard, False)
    return place([b for b, _ in got], [g for _, g in got], 2 * lax.axis_size("seq"))


def gather_halves(shard, head_first):
    got = gather(shard, head_first)
    halves = []
    for rel in range(2):
        pieces, groups = [], []
        for buf, blocks in got:
            mine = [(i, (None, code)) for i, (r, code) in blocks if r == rel]
            if mine:
                pieces.append(buf)
                groups.append(mine)
        halves.append(place(pieces, groups, lax.axis_size("seq")))
    return halves


def add_low(*terms):
    total = terms[0].astype(F32)
    for term in terms[1:]:
        total = total + term.astype(F32)
    return total.astype(BF)


def pick(value, index, axis):
    return lax.dynamic_index_in_dim(value, index, axis, keepdims=False)


def scatter(grads, head_first):
    far, near = layout()
    seq = lax.axis_index("seq")
    far_at, near_at = seq // (2 * near), (seq // 2) % near
    both = [
        add_low(grads[rel][0], flip_seq(grads[rel][1], 1)) for rel in range(2)
    ]
    rows = both[0].shape[0] // (far * near)
    cols = both[0].shape[1]
    if head_first:
        whole = add_low(both[0], flip_head(both[1])).reshape(far, near, rows, cols)
    else:
        whole = jnp.stack(both).reshape(2, far, near, rows, cols).transpose(1, 2, 0, 3, 4)
    parts = [pick(whole, near_at, 1)]
    parts += [flip_seq(pick(whole, near_at ^ r, 1), 2 * r) for r in range(1, near)]
    column = add_low(*parts)
    parts = [pick(column, far_at, 0)]
    parts += [flip_seq(pick(column, far_at ^ r, 0), 2 * near * r) for r in range(1, far)]
    if head_first:
        return sum(part.astype(F32) for part in parts)
    both = add_low(*parts)
    return both[0].astype(F32) + flip_head(both[1]).astype(F32)


def sum_everywhere(value):
    value = value + flip_head(value)
    code = 1
    while code < lax.axis_size("seq"):
        value = value + flip_seq(value, code)
        code *= 2
    return value


def feature_table():
    first, second, one, two, scale = [], [], [], [], []
    for a in range(QD):
        for b in range(a, QD):
            first.append(a)
            second.append(b)
            one.append(0.0)
            two.append(0.0)
            scale.append((1.0 if a == b else 2.0) / (2.0 * QD))
    for a in range(QD):
        first.append(a)
        second.append(-1000)
        one.append(0.0)
        two.append(1.0)
        scale.append(QD**-0.5)
    first.append(-1000)
    second.append(-1000)
    one.append(1.0)
    two.append(1.0)
    scale.append(1.0)
    pad = FEATS - len(first)
    table = np.zeros((8, FEATS), np.float32)
    table[0] = np.array(first + [-1000] * pad)
    table[1] = np.array(second + [-1000] * pad)
    table[2] = np.array(one + [0.0] * pad)
    table[3] = np.array(two + [0.0] * pad)
    table[4] = np.array(scale + [0.0] * pad)
    return table


def mm(a, b, dims):
    return lax.dot_general(a, b, ((dims[0], dims[1]), ((), ())), preferred_element_type=F32)


NN = ((1,), (0,))
NT = ((1,), (1,))
TN = ((0,), (0,))


def selectors(table, head):
    lanes = HEADS * QD
    row = (lax.broadcasted_iota(jnp.int32, (lanes, FEATS), 0) - head * QD).astype(F32)
    one = (row == table[0:1, :]).astype(F32).astype(BF)
    two = (row == table[1:2, :]).astype(F32).astype(BF)
    return one, two


def factors(values, table, sel):
    return (
        mm(values, sel[0], NN) + table[2:3, :],
        mm(values, sel[1], NN) + table[3:4, :],
    )


def half_mask(rows, part):
    lane = lax.broadcasted_iota(jnp.int32, (rows, WIDE), 1)
    return (lane >= VD) if part else (lane < VD)


def head_mask(rows, head):
    lane = lax.broadcasted_iota(jnp.int32, (rows, HEADS * QD), 1)
    return (lane >= head * QD) & (lane < (head + 1) * QD)


def keep(mask, value):
    return jnp.where(mask, value.astype(F32), 0.0).astype(BF)


def state_kernel(table_ref, keys_ref, values_ref, last_ref, wide_ref, thin_ref):
    pair = pl.program_id(0)
    table = table_ref[...]
    keys = keys_ref[...]
    rows = keys.shape[0]
    last = last_ref[...]
    total = None
    for part in range(2):
        sel = selectors(table, 2 * pair + part)
        one, two = factors(keys, table, sel)
        phi = one * two * last
        value = keep(half_mask(rows, part), values_ref[...])
        new = mm(phi.astype(BF), value, TN)
        total = new if total is None else total + new
        thin_ref[0, part : part + 1, :] = jnp.sum(phi, axis=0, keepdims=True)
    thin_ref[0, 2:, :] = jnp.zeros((6, FEATS), F32)
    wide_ref[0] = total.astype(BF)


def visible_tile(mask_ref, row_ids_ref, col_ids_ref, rows):
    for i in range(rows // TILE):
        for j in range(i + 1):
            same = (
                row_ids_ref[i * TILE : (i + 1) * TILE, :]
                == col_ids_ref[:, j * TILE : (j + 1) * TILE]
            )
            if i == j:
                same = same & (
                    lax.broadcasted_iota(jnp.int32, (TILE, TILE), 1)
                    <= lax.broadcasted_iota(jnp.int32, (TILE, TILE), 0)
                )
            mask_ref[i * TILE : (i + 1) * TILE, j * TILE : (j + 1) * TILE] = same.astype(F32)


def local_kernel(
    query_ref, keys_ref, values_ref, row_ids_ref, col_ids_ref, num_ref, den_ref, mask_ref
):
    pair = pl.program_id(0)
    rows = query_ref.shape[0]

    @pl.when(pair == 0)
    def _():
        visible_tile(mask_ref, row_ids_ref, col_ids_ref, rows)

    for i in range(rows // TILE):
        here = slice(i * TILE, (i + 1) * TILE)
        num = jnp.zeros((TILE, WIDE), F32)
        dens = []
        for part in range(2):
            head = 2 * pair + part
            query = keep(head_mask(TILE, head), query_ref[here, :] * (QD**-0.5))
            den = jnp.zeros((TILE, 1), F32)
            for j in range(i + 1):
                there = slice(j * TILE, (j + 1) * TILE)
                s = mm(query, keys_ref[there, :], NT)
                w = (1.0 + s + 0.5 * s * s) * mask_ref[here, there]
                den = den + jnp.sum(w, axis=1, keepdims=True)
                num = num + mm(
                    w.astype(BF), keep(half_mask(TILE, part), values_ref[there, :]), NN
                )
            dens.append(den)
        num_ref[here, :] = num
        den_ref[here, :] = jnp.where(half_mask(TILE, 0), dens[0], dens[1])


def finish_kernel(
    table_ref, query_ref, num_ref, den_ref, first_ref, wide_ref, thin_ref, out_ref, rden_ref
):
    pair = pl.program_id(0)
    table = table_ref[...]
    query = query_ref[...]
    rows = query.shape[0]
    first = first_ref[...]
    num, den = num_ref[...], den_ref[...]
    for part in range(2):
        sel = selectors(table, 2 * pair + part)
        one, two = factors(query, table, sel)
        phi = one * two * (table[4:5, :] * first)
        mask = half_mask(rows, part)
        extra = mm(phi.astype(BF), wide_ref[0], NN)
        num = num + jnp.where(mask, extra, 0.0)
        more = jnp.sum(phi * thin_ref[0, part : part + 1, :], axis=1, keepdims=True)
        den = den + jnp.where(mask, more, 0.0)
    rden = 1.0 / den
    rden_ref[...] = rden
    out_ref[...] = (num * rden).astype(BF)


def prepare(grad_ref, out_ref, rden_ref):
    rows = grad_ref.shape[0]
    grad = grad_ref[...].astype(F32)
    rden = rden_ref[...]
    dnum = (grad * rden).astype(BF)
    prod = grad * out_ref[...].astype(F32) * rden
    deltas = [
        jnp.sum(jnp.where(half_mask(rows, part), prod, 0.0), axis=1, keepdims=True)
        for part in range(2)
    ]
    return dnum, deltas


def grad_state_kernel(
    table_ref, query_ref, grad_ref, out_ref, rden_ref, first_ref, wide_ref, thin_ref
):
    pair = pl.program_id(0)
    table = table_ref[...]
    query = query_ref[...]
    rows = query.shape[0]
    dnum, deltas = prepare(grad_ref, out_ref, rden_ref)
    total = None
    for part in range(2):
        sel = selectors(table, 2 * pair + part)
        one, two = factors(query, table, sel)
        phi = one * two * (table[4:5, :] * first_ref[...])
        new = mm(phi.astype(BF), keep(half_mask(rows, part), dnum), TN)
        total = new if total is None else total + new
        thin_ref[0, part : part + 1, :] = -jnp.sum(phi * deltas[part], axis=0, keepdims=True)
    thin_ref[0, 2:, :] = jnp.zeros((6, FEATS), F32)
    wide_ref[0] = total.astype(BF)


def local_grad_kernel(
    table_ref,
    query_ref,
    keys_ref,
    values_ref,
    grad_ref,
    out_ref,
    rden_ref,
    row_ids_ref,
    col_ids_ref,
    first_ref,
    wide_ref,
    thin_ref,
    dq_ref,
    dk_ref,
    dv_ref,
    mask_ref,
    dq_acc,
    dk_acc,
):
    pair = pl.program_id(0)
    table = table_ref[...]
    query = query_ref[...]
    keys = keys_ref[...]
    rows = query.shape[0]
    tiles = rows // TILE
    scale = QD**-0.5

    @pl.when(pair == 0)
    def _():
        visible_tile(mask_ref, row_ids_ref, col_ids_ref, rows)
        dq_acc[...] = jnp.zeros_like(dq_acc)
        dk_acc[...] = jnp.zeros_like(dk_acc)

    dnum, deltas = prepare(grad_ref, out_ref, rden_ref)
    dv = [jnp.zeros((TILE, WIDE), F32) for _ in range(tiles)]
    for part in range(2):
        head = 2 * pair + part
        at_head = head_mask(rows, head)
        q_head = keep(at_head, query * scale)
        k_head = keep(at_head, keys * scale)
        d_head = keep(half_mask(rows, part), dnum)
        for i in range(tiles):
            here = slice(i * TILE, (i + 1) * TILE)
            dq = dq_acc[here, :]
            for j in range(i + 1):
                there = slice(j * TILE, (j + 1) * TILE)
                s = mm(q_head[here], keys[there], NT)
                mask = mask_ref[here, there]
                w = ((1.0 + s + 0.5 * s * s) * mask).astype(BF)
                dp = mm(d_head[here], values_ref[there, :], NT)
                ds = ((dp - deltas[part][here]) * ((1.0 + s) * mask)).astype(BF)
                dq = dq + mm(ds, k_head[there], NN)
                dk_acc[there, :] += mm(ds, q_head[here], TN)
                dv[j] = dv[j] + mm(w, d_head[here], TN)
            dq_acc[here, :] = dq
        sel = selectors(table, head)
        one, two = factors(query, table, sel)
        dphi = mm(d_head, wide_ref[0], NT) - deltas[part] * thin_ref[0, part : part + 1, :]
        dphi = dphi * (table[4:5, :] * first_ref[...])
        dq_acc[...] += mm((dphi * two).astype(BF), sel[0], NT) + mm(
            (dphi * one).astype(BF), sel[1], NT
        )
    for j in range(tiles):
        dv_ref[j * TILE : (j + 1) * TILE, :] = dv[j]

    @pl.when(pair == PAIRS - 1)
    def _():
        dq_ref[...] = dq_acc[...].astype(BF)
        dk_ref[...] = dk_acc[...]


def finish_grad_kernel(
    table_ref, keys_ref, values_ref, dk_in_ref, dv_in_ref, last_ref, wide_ref, thin_ref,
    dk_ref, dv_ref, dk_acc,
):
    pair = pl.program_id(0)
    table = table_ref[...]
    keys = keys_ref[...]
    rows = keys.shape[0]
    last = last_ref[...]

    @pl.when(pair == 0)
    def _():
        dk_acc[...] = dk_in_ref[...]

    dv = dv_in_ref[...]
    for part in range(2):
        sel = selectors(table, 2 * pair + part)
        one, two = factors(keys, table, sel)
        mask = half_mask(rows, part)
        phi = one * two * last
        dv = dv + jnp.where(mask, mm(phi.astype(BF), wide_ref[0], NN), 0.0)
        dphi = mm(keep(mask, values_ref[...]), wide_ref[0], NT) + thin_ref[0, part : part + 1, :]
        dphi = dphi * last
        dk_acc[...] += mm((dphi * two).astype(BF), sel[0], NT) + mm(
            (dphi * one).astype(BF), sel[1], NT
        )
    dv_ref[...] = dv.astype(BF)

    @pl.when(pair == PAIRS - 1)
    def _():
        dk_ref[...] = dk_acc[...].astype(BF)


def full_spec(shape):
    return pl.BlockSpec(shape, lambda p: (0,) * len(shape))


def pair_spec(rows):
    return pl.BlockSpec((rows, WIDE), lambda p: (0, p))


def state_specs():
    return [
        pl.BlockSpec((1, FEATS, WIDE), lambda p: (p, 0, 0)),
        pl.BlockSpec((1, 8, FEATS), lambda p: (p, 0, 0)),
    ]


STATE_SHAPES = (
    jax.ShapeDtypeStruct((PAIRS, FEATS, WIDE), BF),
    jax.ShapeDtypeStruct((PAIRS, 8, FEATS), F32),
)


def run(kernel, in_specs, out_specs, out_shape, args, scratch=(), flops=0):
    moved = sum(a.size * a.dtype.itemsize for a in args)
    return pl.pallas_call(
        kernel,
        grid=(PAIRS,),
        in_specs=in_specs,
        out_specs=out_specs,
        out_shape=out_shape,
        scratch_shapes=scratch,
        compiler_params=pltpu.CompilerParams(vmem_limit_bytes=48 << 20),
        cost_estimate=pl.CostEstimate(flops=flops, bytes_accessed=moved, transcendentals=0),
        name=kernel.__name__,
    )(*args)


def exchange(wide, thin, ids, rows, forward):
    head, seq = lax.axis_index("head"), lax.axis_index("seq")
    n = lax.axis_size("seq")
    segments = 2 * n
    firsts = ids.reshape(segments, rows)[:, 0]
    lasts = ids.reshape(segments, rows)[:, rows - 1]
    step = 1 if forward else -1
    near_end, far_end = (lasts, firsts) if forward else (firsts, lasts)

    def end_of(which, segment):
        return which[jnp.clip(segment, 0, segments - 1)]

    seg = 2 * seq + head
    takes = end_of(far_end, seg)
    core = seq % 2
    late_head = head if forward else 1 - head
    late_core = core if forward else 1 - core

    def gate(flag):
        return jnp.where(flag, 1.0, 0.0).astype(F32)

    def wider(state):
        return [part.astype(F32) for part in state]

    def narrow(state):
        return [state[0].astype(BF), state[1]]

    def merge(own, other, late, other_takes, joined):
        gained = [part * (gate(other_takes) * late) for part in other]
        own_factor = jnp.where(late == 1, 1.0, gate(joined))
        other_factor = jnp.where(late == 1, gate(joined), 1.0)
        joint = [a * own_factor + b * other_factor for a, b in zip(own, other)]
        return gained, joint

    own = [wide, thin]
    other = [flip_head(part) for part in own]
    first_of, second_of = 2 * seq, 2 * seq + 1
    if not forward:
        first_of, second_of = second_of, first_of
    total, joint = merge(
        wider(own),
        wider(other),
        late_head,
        end_of(near_end, seg - step) == takes,
        end_of(near_end, first_of) == end_of(near_end, second_of),
    )
    joint = narrow(joint)
    other = [flip_seq(part, 1) for part in joint]
    base = 4 * (seq // 2)
    early_end, late_end = (base + 1, base + 3) if forward else (base + 2, base)
    gained, joint = merge(
        wider(joint),
        wider(other),
        late_core,
        end_of(near_end, early_end) == takes,
        end_of(near_end, early_end) == end_of(near_end, late_end),
    )
    total = [a + b for a, b in zip(total, gained)]
    joint = narrow(joint)
    half = PAIRS // 2
    mine = [lax.dynamic_slice_in_dim(part, core * half, half, 0) for part in joint]
    hops = -(-DOC_MAX // (4 * rows))
    far = None
    for hop in range(1, hops + 1):
        got = wider([shift_seq(part, 2 * hop * step) for part in mine])
        nearer, farther = late_end - 4 * step, late_end - 4 * step * hop
        joined = gate(end_of(near_end, nearer) == end_of(near_end, farther))
        got = [part * joined for part in got]
        far = got if far is None else [a + b for a, b in zip(far, got)]
    far = narrow(far)
    other = [flip_seq(part, 1) for part in far]
    comes = (seq // 2 >= 1) if forward else (seq // 2 < n // 2 - 1)
    use = gate(comes & (end_of(near_end, late_end - 4 * step) == takes))
    result = []
    for a, b, so_far in zip(far, other, total):
        low = jnp.where(core == 0, a, b).astype(F32)
        high = jnp.where(core == 0, b, a).astype(F32)
        result.append(so_far + use * jnp.concatenate([low, high], axis=0))
    return narrow(result)


def rms_scale(values, gain):
    return values * lax.rsqrt(jnp.mean(values * values, axis=-1, keepdims=True) + EPSILON) * gain


def swish_mix(gate, up_proj):
    return jax.nn.silu(gate) * up_proj


def dot_nn(a, b):
    return jnp.dot(a, b, preferred_element_type=F32)


def dot_nt(a, b):
    return lax.dot_general(a, b, (((1,), (1,)), ((), ())), preferred_element_type=F32)


def dot_tn(a, b):
    return lax.dot_general(a, b, (((0,), (0,)), ((), ())), preferred_element_type=F32)


def row_grads(left, right, by_head):
    head, core = lax.axis_index("head"), lax.axis_index("seq") % 2
    tokens = left.shape[0]
    chips = lax.axis_size("seq") // 2
    heads = 2 if by_head else 1
    rows = left.shape[1] // (heads * chips * 2)
    split = left.reshape(tokens, heads, chips, 2, rows)
    out = []
    for rel in range(heads):
        plane = pick(split, head ^ rel, 1) if by_head else split[:, 0]
        out.append([pick(plane, core ^ r, 2).reshape(tokens, chips * rows) for r in range(2)])
    if by_head:
        return [[dot_tn(part, right).astype(BF) for part in parts] for parts in out]
    return [[dot_tn(part, r).astype(BF) for part in out[0]] for r in right]


def body(
    layer_input,
    segment_ids,
    norm1_gain,
    w_query,
    w_key,
    w_value,
    w_out,
    norm2_gain,
    w_gate,
    w_up,
    w_down,
    output_grad,
):
    rows = layer_input.shape[1]
    head, seq = lax.axis_index("head"), lax.axis_index("seq")
    n_seq = lax.axis_size("seq")
    qk = HEADS * QD
    inputs = layer_input[0].astype(F32)
    width = inputs.shape[1]

    slot = head * n_seq + seq
    small = norm1_gain.shape[0]
    gains = jnp.zeros((2, width // small, small), F32)
    gains = lax.dynamic_update_slice(
        gains, jnp.stack([norm1_gain, norm2_gain]).astype(F32)[:, None, :], (0, slot, 0)
    ).reshape(2, width)
    gains = sum_everywhere(gains)
    gain_first, gain_second = gains[0], gains[1]

    qkv_full = gather_rows(jnp.concatenate([w_query, w_key, w_value], axis=1))
    out_full = gather_rows(w_out)
    gate_w = gather_halves(w_gate, False)
    up_w = gather_halves(w_up, False)
    down_w = gather_halves(w_down.T, True)

    segment = 2 * seq + head
    ids = lax.dynamic_slice_in_dim(segment_ids, segment * rows, rows)
    row_ids, col_ids = ids[:, None], ids[None, :]
    first = (row_ids == ids[0]).astype(F32)
    last = (row_ids == ids[rows - 1]).astype(F32)
    table = jnp.asarray(feature_table())

    normed_one = rms_scale(inputs, gain_first).astype(BF)
    qkv = dot_nn(normed_one, qkv_full).astype(BF)
    query, keys, values = qkv[:, :qk], qkv[:, qk : 2 * qk], qkv[:, 2 * qk :]
    vcols = HEADS * VD
    t_spec, q_spec = full_spec((8, FEATS)), full_spec((rows, qk))
    one_spec, row_spec = full_spec((rows, 1)), full_spec((1, rows))
    p_spec = pair_spec(rows)
    f32_like = jax.ShapeDtypeStruct((rows, vcols), F32)
    bf_like = jax.ShapeDtypeStruct((rows, vcols), BF)
    state = run(
        state_kernel,
        [t_spec, q_spec, p_spec, one_spec],
        state_specs(),
        STATE_SHAPES,
        (table, keys, values, last),
        flops=8 * rows * qk * FEATS * HEADS,
    )
    num, den = run(
        local_kernel,
        [q_spec, q_spec, p_spec, one_spec, row_spec],
        [p_spec, p_spec],
        [f32_like, f32_like],
        (query, keys, values, row_ids, col_ids),
        [pltpu.VMEM((rows, rows), F32)],
        flops=8 * rows * rows * qk * HEADS,
    )
    before = exchange(*state, segment_ids, rows, True)
    attended, rden = run(
        finish_kernel,
        [t_spec, q_spec, p_spec, p_spec, one_spec] + state_specs(),
        [p_spec, p_spec],
        [bf_like, f32_like],
        (table, query, num, den, first, *before),
        flops=8 * rows * qk * FEATS * HEADS,
    )
    residual = inputs + dot_nn(attended, out_full)
    normed_two = rms_scale(residual, gain_second).astype(BF)

    grad_output = output_grad[0]
    outcome = residual
    grad_normed_two = None
    hiddens, grad_gates, grad_ups = [], [], []
    for w_g, w_u, w_d in zip(gate_w, up_w, down_w):
        gate = dot_nn(normed_two, w_g)
        up_proj = dot_nn(normed_two, w_u)
        grad_hidden = dot_nn(grad_output, w_d)
        hidden, mix_pull = jax.vjp(swish_mix, gate, up_proj)
        grad_gate, grad_up = mix_pull(grad_hidden)
        hiddens.append(hidden.astype(BF))
        grad_gates.append(grad_gate.astype(BF))
        grad_ups.append(grad_up.astype(BF))
        outcome = outcome + dot_nt(hiddens[-1], w_d)
        more = dot_nt(grad_gates[-1], w_g) + dot_nt(grad_ups[-1], w_u)
        grad_normed_two = more if grad_normed_two is None else grad_normed_two + more
    outcome = outcome.astype(BF)
    d_gate = scatter(row_grads(normed_two, grad_gates, False), True)
    d_up = scatter(row_grads(normed_two, grad_ups, False), True)
    d_down = scatter(row_grads(grad_output, hiddens, False), False).T

    _, norm_pull = jax.vjp(rms_scale, residual, gain_second)
    grad_resid_two, grad_gain_two = norm_pull(grad_normed_two)
    grad_middle = grad_output.astype(F32) + grad_resid_two
    grad_middle_low = grad_middle.astype(BF)
    d_out = scatter(row_grads(attended, grad_middle_low, True), True)
    grad_attended = dot_nt(grad_middle_low, out_full).astype(BF)

    grad_state = run(
        grad_state_kernel,
        [t_spec, q_spec, p_spec, p_spec, p_spec, one_spec],
        state_specs(),
        STATE_SHAPES,
        (table, query, grad_attended, attended, rden, first),
        flops=8 * rows * qk * FEATS * HEADS,
    )
    qk_f32 = jax.ShapeDtypeStruct((rows, qk), F32)
    qk_bf = jax.ShapeDtypeStruct((rows, qk), BF)
    grad_query, grad_key, grad_value = run(
        local_grad_kernel,
        [t_spec, q_spec, q_spec, p_spec, p_spec, p_spec, p_spec, one_spec, row_spec, one_spec]
        + state_specs(),
        [q_spec, q_spec, p_spec],
        [qk_bf, qk_f32, f32_like],
        (table, query, keys, values, grad_attended, attended, rden, row_ids, col_ids, first)
        + tuple(before),
        [pltpu.VMEM((rows, rows), F32), pltpu.VMEM((rows, qk), F32), pltpu.VMEM((rows, qk), F32)],
        flops=20 * rows * rows * qk * HEADS,
    )
    after = exchange(*grad_state, segment_ids, rows, False)
    grad_key, grad_value = run(
        finish_grad_kernel,
        [t_spec, q_spec, p_spec, q_spec, p_spec, one_spec] + state_specs(),
        [q_spec, p_spec],
        [qk_bf, bf_like],
        (table, keys, values, grad_key, grad_value, last, *after),
        [pltpu.VMEM((rows, qk), F32)],
        flops=16 * rows * qk * FEATS * HEADS,
    )
    grad_qkv = jnp.concatenate([grad_query, grad_key, grad_value], axis=1)
    d_qkv = scatter(row_grads(normed_one, grad_qkv, True), True)
    grad_normed_one = dot_nt(grad_qkv, qkv_full)
    _, first_pull = jax.vjp(rms_scale, inputs, gain_first)
    grad_inputs, grad_gain_one = first_pull(grad_normed_one)
    grad_layer = grad_middle + grad_inputs
    grad_gains = sum_everywhere(jnp.stack([grad_gain_one, grad_gain_two]))
    grad_gains = lax.dynamic_slice_in_dim(
        grad_gains.reshape(2, width // small, small), slot, 1, 1
    )[:, 0]
    return (
        outcome[None],
        grad_layer[None],
        grad_gains[0],
        d_qkv[:, :qk],
        d_qkv[:, qk : 2 * qk],
        d_qkv[:, 2 * qk :],
        d_out,
        grad_gains[1],
        d_gate,
        d_up,
        d_down,
    )


def solution(mesh):
    split = P(("head", "seq"))
    rows = P(("head", "seq"), None)
    block = P("seq", "head", None)
    wide, tall = P("seq", "head"), P("head", "seq")
    in_specs = (block, P(), split, rows, rows, rows, rows, split, wide, wide, tall, block)
    out_specs = (block, block, split, rows, rows, rows, rows, split, wide, wide, tall)
    return jax.shard_map(body, mesh=mesh, in_specs=in_specs, out_specs=out_specs, check_vma=False)
```

```python
import functools

import jax
import jax.numpy as jnp
import numpy as np
from jax import lax
from jax.experimental import pallas as pl
from jax.experimental.pallas import tpu as pltpu
from jax.sharding import PartitionSpec as P

HEADS = 16
QD = 16
VD = 64
DOC_MAX = 4096
EPSILON = 1e-05
PAIRS = HEADS // 2
WIDE = 2 * VD
FEATS = 160
TILE = 256

BF = jnp.bfloat16
F32 = jnp.float32


def flip_seq(value, code):
    n = lax.axis_size("seq")
    return lax.ppermute(value, "seq", [(i, i ^ code) for i in range(n)])


def flip_head(value):
    n = lax.axis_size("head")
    return lax.ppermute(value, "head", [(i, i ^ 1) for i in range(n)])


def shift_seq(value, distance):
    n = lax.axis_size("seq")
    return lax.ppermute(
        value, "seq", [(i, i + distance) for i in range(n) if 0 <= i + distance < n]
    )


def layout():
    chips = lax.axis_size("seq") // 2
    near = 2 if chips <= 8 else 8
    far = chips // near
    return far, near


def place_kernel(groups, count, *refs):
    pieces, out, sem = refs[:count], refs[count], refs[count + 1]
    me = lax.axis_index("seq")
    head = lax.axis_index("head")
    n = lax.axis_size("seq")
    copies = []
    for piece, blocks in zip(pieces, groups):
        for index, (rel_head, rel_seq) in blocks:
            place = me ^ rel_seq
            if rel_head is not None:
                place = place + (head ^ rel_head) * n
            copies.append(
                pltpu.make_async_copy(piece.at[index], out.at[place], sem.at[len(copies)])
            )
    for copy in copies:
        copy.start()
    for copy in copies:
        copy.wait()


def place(pieces, groups, blocks):
    rows, cols = pieces[0].shape[-2:]
    total = sum(len(g) for g in groups)
    out = pl.pallas_call(
        functools.partial(place_kernel, groups, len(pieces)),
        out_shape=jax.ShapeDtypeStruct((blocks, rows, cols), pieces[0].dtype),
        in_specs=[pl.BlockSpec(memory_space=pl.ANY)] * len(pieces),
        out_specs=pl.BlockSpec(memory_space=pltpu.VMEM),
        scratch_shapes=[pltpu.SemaphoreType.DMA((total,))],
        compiler_params=pltpu.CompilerParams(vmem_limit_bytes=16 << 20),
        cost_estimate=pl.CostEstimate(
            flops=0, bytes_accessed=4 * blocks * rows * cols, transcendentals=0
        ),
        name="place",
    )(*pieces)
    return out.reshape(blocks * rows, cols)


def gather(shard, head_first):
    far, near = layout()
    far_codes = [2 * near * r for r in range(far)]
    near_codes = [2 * r for r in range(near)]
    if head_first:
        shard = jnp.stack([shard, flip_head(shard)])
    column = jnp.stack([shard] + [flip_seq(shard, code) for code in far_codes[1:]])
    held = [(column, 0, 0)]
    held += [(flip_seq(column, code), 0, code) for code in near_codes[1:]]
    if not head_first:
        held += [(flip_head(buf), 1, code) for buf, _, code in held]
    held += [(flip_seq(buf, 1), rel, code + 1) for buf, rel, code in held]
    result = []
    for buf, rel, code in held:
        if head_first:
            blocks = [((r, g), (g, code + far_codes[r])) for r in range(far) for g in range(2)]
        else:
            blocks = [((r,), (rel, code + far_codes[r])) for r in range(far)]
        result.append((buf, blocks))
    return result


def gather_rows(shard):
    got = gather(shard, False)
    return place([b for b, _ in got], [g for _, g in got], 2 * lax.axis_size("seq"))


def gather_halves(shard, head_first):
    got = gather(shard, head_first)
    halves = []
    for rel in range(2):
        pieces, groups = [], []
        for buf, blocks in got:
            mine = [(i, (None, code)) for i, (r, code) in blocks if r == rel]
            if mine:
                pieces.append(buf)
                groups.append(mine)
        halves.append(place(pieces, groups, lax.axis_size("seq")))
    return halves


def add_low(*terms):
    total = terms[0].astype(F32)
    for term in terms[1:]:
        total = total + term.astype(F32)
    return total.astype(BF)


def pick(value, index, axis):
    return lax.dynamic_index_in_dim(value, index, axis, keepdims=False)


def scatter(grads, head_first):
    far, near = layout()
    seq = lax.axis_index("seq")
    far_at, near_at = seq // (2 * near), (seq // 2) % near
    both = [
        add_low(grads[rel][0], flip_seq(grads[rel][1], 1)) for rel in range(2)
    ]
    rows = both[0].shape[0] // (far * near)
    cols = both[0].shape[1]
    if head_first:
        whole = add_low(both[0], flip_head(both[1])).reshape(far, near, rows, cols)
    else:
        whole = jnp.stack(both).reshape(2, far, near, rows, cols).transpose(1, 2, 0, 3, 4)
    parts = [pick(whole, near_at, 1)]
    parts += [flip_seq(pick(whole, near_at ^ r, 1), 2 * r) for r in range(1, near)]
    column = add_low(*parts)
    parts = [pick(column, far_at, 0)]
    parts += [flip_seq(pick(column, far_at ^ r, 0), 2 * near * r) for r in range(1, far)]
    if head_first:
        return sum(part.astype(F32) for part in parts)
    both = add_low(*parts)
    return both[0].astype(F32) + flip_head(both[1]).astype(F32)


def sum_everywhere(value):
    value = value + flip_head(value)
    code = 1
    while code < lax.axis_size("seq"):
        value = value + flip_seq(value, code)
        code *= 2
    return value


def feature_table():
    first, second, one, two, scale = [], [], [], [], []
    for a in range(QD):
        for b in range(a, QD):
            first.append(a)
            second.append(b)
            one.append(0.0)
            two.append(0.0)
            scale.append((1.0 if a == b else 2.0) / (2.0 * QD))
    for a in range(QD):
        first.append(a)
        second.append(-1000)
        one.append(0.0)
        two.append(1.0)
        scale.append(QD**-0.5)
    first.append(-1000)
    second.append(-1000)
    one.append(1.0)
    two.append(1.0)
    scale.append(1.0)
    pad = FEATS - len(first)
    table = np.zeros((8, FEATS), np.float32)
    table[0] = np.array(first + [-1000] * pad)
    table[1] = np.array(second + [-1000] * pad)
    table[2] = np.array(one + [0.0] * pad)
    table[3] = np.array(two + [0.0] * pad)
    table[4] = np.array(scale + [0.0] * pad)
    return table


def mm(a, b, dims):
    return lax.dot_general(a, b, ((dims[0], dims[1]), ((), ())), preferred_element_type=F32)


NN = ((1,), (0,))
NT = ((1,), (1,))
TN = ((0,), (0,))


def selectors(table, head):
    lanes = HEADS * QD
    row = (lax.broadcasted_iota(jnp.int32, (lanes, FEATS), 0) - head * QD).astype(F32)
    one = (row == table[0:1, :]).astype(F32).astype(BF)
    two = (row == table[1:2, :]).astype(F32).astype(BF)
    return one, two


def factors(values, table, sel):
    return (
        mm(values, sel[0], NN) + table[2:3, :],
        mm(values, sel[1], NN) + table[3:4, :],
    )


def half_mask(rows, part):
    lane = lax.broadcasted_iota(jnp.int32, (rows, WIDE), 1)
    return (lane >= VD) if part else (lane < VD)


def head_mask(rows, head):
    lane = lax.broadcasted_iota(jnp.int32, (rows, HEADS * QD), 1)
    return (lane >= head * QD) & (lane < (head + 1) * QD)


def keep(mask, value):
    return jnp.where(mask, value.astype(F32), 0.0).astype(BF)


def state_kernel(table_ref, keys_ref, values_ref, last_ref, wide_ref, thin_ref):
    pair = pl.program_id(0)
    table = table_ref[...]
    keys = keys_ref[...]
    rows = keys.shape[0]
    last = last_ref[...]
    total = None
    for part in range(2):
        sel = selectors(table, 2 * pair + part)
        one, two = factors(keys, table, sel)
        phi = one * two * last
        value = keep(half_mask(rows, part), values_ref[...])
        new = mm(phi.astype(BF), value, TN)
        total = new if total is None else total + new
        thin_ref[0, part : part + 1, :] = jnp.sum(phi, axis=0, keepdims=True)
    thin_ref[0, 2:, :] = jnp.zeros((6, FEATS), F32)
    wide_ref[0] = total.astype(BF)


def visible_tile(mask_ref, row_ids_ref, col_ids_ref, rows):
    for i in range(rows // TILE):
        for j in range(i + 1):
            same = (
                row_ids_ref[i * TILE : (i + 1) * TILE, :]
                == col_ids_ref[:, j * TILE : (j + 1) * TILE]
            )
            if i == j:
                same = same & (
                    lax.broadcasted_iota(jnp.int32, (TILE, TILE), 1)
                    <= lax.broadcasted_iota(jnp.int32, (TILE, TILE), 0)
                )
            mask_ref[i * TILE : (i + 1) * TILE, j * TILE : (j + 1) * TILE] = same.astype(F32)


def local_kernel(
    query_ref, keys_ref, values_ref, row_ids_ref, col_ids_ref, num_ref, den_ref, mask_ref
):
    pair = pl.program_id(0)
    rows = query_ref.shape[0]

    @pl.when(pair == 0)
    def _():
        visible_tile(mask_ref, row_ids_ref, col_ids_ref, rows)

    for i in range(rows // TILE):
        here = slice(i * TILE, (i + 1) * TILE)
        num = jnp.zeros((TILE, WIDE), F32)
        dens = []
        for part in range(2):
            head = 2 * pair + part
            query = keep(head_mask(TILE, head), query_ref[here, :] * (QD**-0.5))
            den = jnp.zeros((TILE, 1), F32)
            for j in range(i + 1):
                there = slice(j * TILE, (j + 1) * TILE)
                s = mm(query, keys_ref[there, :], NT)
                w = (1.0 + s + 0.5 * s * s) * mask_ref[here, there]
                den = den + jnp.sum(w, axis=1, keepdims=True)
                num = num + mm(
                    w.astype(BF), keep(half_mask(TILE, part), values_ref[there, :]), NN
                )
            dens.append(den)
        num_ref[here, :] = num
        den_ref[here, :] = jnp.where(half_mask(TILE, 0), dens[0], dens[1])


def finish_kernel(
    table_ref, query_ref, num_ref, den_ref, first_ref, wide_ref, thin_ref, out_ref, rden_ref
):
    pair = pl.program_id(0)
    table = table_ref[...]
    query = query_ref[...]
    rows = query.shape[0]
    first = first_ref[...]
    num, den = num_ref[...], den_ref[...]
    for part in range(2):
        sel = selectors(table, 2 * pair + part)
        one, two = factors(query, table, sel)
        phi = one * two * (table[4:5, :] * first)
        mask = half_mask(rows, part)
        extra = mm(phi.astype(BF), wide_ref[0], NN)
        num = num + jnp.where(mask, extra, 0.0)
        more = jnp.sum(phi * thin_ref[0, part : part + 1, :], axis=1, keepdims=True)
        den = den + jnp.where(mask, more, 0.0)
    rden = 1.0 / den
    rden_ref[...] = rden
    out_ref[...] = (num * rden).astype(BF)


def prepare(grad_ref, out_ref, rden_ref):
    rows = grad_ref.shape[0]
    grad = grad_ref[...].astype(F32)
    rden = rden_ref[...]
    dnum = (grad * rden).astype(BF)
    prod = grad * out_ref[...].astype(F32) * rden
    deltas = [
        jnp.sum(jnp.where(half_mask(rows, part), prod, 0.0), axis=1, keepdims=True)
        for part in range(2)
    ]
    return dnum, deltas


def grad_state_kernel(
    table_ref, query_ref, grad_ref, out_ref, rden_ref, first_ref, wide_ref, thin_ref
):
    pair = pl.program_id(0)
    table = table_ref[...]
    query = query_ref[...]
    rows = query.shape[0]
    dnum, deltas = prepare(grad_ref, out_ref, rden_ref)
    total = None
    for part in range(2):
        sel = selectors(table, 2 * pair + part)
        one, two = factors(query, table, sel)
        phi = one * two * (table[4:5, :] * first_ref[...])
        new = mm(phi.astype(BF), keep(half_mask(rows, part), dnum), TN)
        total = new if total is None else total + new
        thin_ref[0, part : part + 1, :] = -jnp.sum(phi * deltas[part], axis=0, keepdims=True)
    thin_ref[0, 2:, :] = jnp.zeros((6, FEATS), F32)
    wide_ref[0] = total.astype(BF)


def local_grad_kernel(
    table_ref,
    query_ref,
    keys_ref,
    values_ref,
    grad_ref,
    out_ref,
    rden_ref,
    row_ids_ref,
    col_ids_ref,
    first_ref,
    wide_ref,
    thin_ref,
    dq_ref,
    dk_ref,
    dv_ref,
    mask_ref,
    dq_acc,
    dk_acc,
):
    pair = pl.program_id(0)
    table = table_ref[...]
    query = query_ref[...]
    keys = keys_ref[...]
    rows = query.shape[0]
    tiles = rows // TILE
    scale = QD**-0.5

    @pl.when(pair == 0)
    def _():
        visible_tile(mask_ref, row_ids_ref, col_ids_ref, rows)
        dq_acc[...] = jnp.zeros_like(dq_acc)
        dk_acc[...] = jnp.zeros_like(dk_acc)

    dnum, deltas = prepare(grad_ref, out_ref, rden_ref)
    dv = [jnp.zeros((TILE, WIDE), F32) for _ in range(tiles)]
    for part in range(2):
        head = 2 * pair + part
        at_head = head_mask(rows, head)
        q_head = keep(at_head, query * scale)
        k_head = keep(at_head, keys * scale)
        d_head = keep(half_mask(rows, part), dnum)
        for i in range(tiles):
            here = slice(i * TILE, (i + 1) * TILE)
            dq = dq_acc[here, :]
            for j in range(i + 1):
                there = slice(j * TILE, (j + 1) * TILE)
                s = mm(q_head[here], keys[there], NT)
                mask = mask_ref[here, there]
                w = ((1.0 + s + 0.5 * s * s) * mask).astype(BF)
                dp = mm(d_head[here], values_ref[there, :], NT)
                ds = ((dp - deltas[part][here]) * ((1.0 + s) * mask)).astype(BF)
                dq = dq + mm(ds, k_head[there], NN)
                dk_acc[there, :] += mm(ds, q_head[here], TN)
                dv[j] = dv[j] + mm(w, d_head[here], TN)
            dq_acc[here, :] = dq
        sel = selectors(table, head)
        one, two = factors(query, table, sel)
        dphi = mm(d_head, wide_ref[0], NT) - deltas[part] * thin_ref[0, part : part + 1, :]
        dphi = dphi * (table[4:5, :] * first_ref[...])
        dq_acc[...] += mm((dphi * two).astype(BF), sel[0], NT) + mm(
            (dphi * one).astype(BF), sel[1], NT
        )
    for j in range(tiles):
        dv_ref[j * TILE : (j + 1) * TILE, :] = dv[j]

    @pl.when(pair == PAIRS - 1)
    def _():
        dq_ref[...] = dq_acc[...].astype(BF)
        dk_ref[...] = dk_acc[...]


def finish_grad_kernel(
    table_ref, keys_ref, values_ref, dk_in_ref, dv_in_ref, last_ref, wide_ref, thin_ref,
    dk_ref, dv_ref, dk_acc,
):
    pair = pl.program_id(0)
    table = table_ref[...]
    keys = keys_ref[...]
    rows = keys.shape[0]
    last = last_ref[...]

    @pl.when(pair == 0)
    def _():
        dk_acc[...] = dk_in_ref[...]

    dv = dv_in_ref[...]
    for part in range(2):
        sel = selectors(table, 2 * pair + part)
        one, two = factors(keys, table, sel)
        mask = half_mask(rows, part)
        phi = one * two * last
        dv = dv + jnp.where(mask, mm(phi.astype(BF), wide_ref[0], NN), 0.0)
        dphi = mm(keep(mask, values_ref[...]), wide_ref[0], NT) + thin_ref[0, part : part + 1, :]
        dphi = dphi * last
        dk_acc[...] += mm((dphi * two).astype(BF), sel[0], NT) + mm(
            (dphi * one).astype(BF), sel[1], NT
        )
    dv_ref[...] = dv.astype(BF)

    @pl.when(pair == PAIRS - 1)
    def _():
        dk_ref[...] = dk_acc[...].astype(BF)


def full_spec(shape):
    return pl.BlockSpec(shape, lambda p: (0,) * len(shape))


def pair_spec(rows):
    return pl.BlockSpec((rows, WIDE), lambda p: (0, p))


def state_specs():
    return [
        pl.BlockSpec((1, FEATS, WIDE), lambda p: (p, 0, 0)),
        pl.BlockSpec((1, 8, FEATS), lambda p: (p, 0, 0)),
    ]


STATE_SHAPES = (
    jax.ShapeDtypeStruct((PAIRS, FEATS, WIDE), BF),
    jax.ShapeDtypeStruct((PAIRS, 8, FEATS), F32),
)


def run(kernel, in_specs, out_specs, out_shape, args, scratch=(), flops=0):
    moved = sum(a.size * a.dtype.itemsize for a in args)
    return pl.pallas_call(
        kernel,
        grid=(PAIRS,),
        in_specs=in_specs,
        out_specs=out_specs,
        out_shape=out_shape,
        scratch_shapes=scratch,
        compiler_params=pltpu.CompilerParams(vmem_limit_bytes=48 << 20),
        cost_estimate=pl.CostEstimate(flops=flops, bytes_accessed=moved, transcendentals=0),
        name=kernel.__name__,
    )(*args)


def exchange(wide, thin, ids, rows, forward):
    head, seq = lax.axis_index("head"), lax.axis_index("seq")
    n = lax.axis_size("seq")
    segments = 2 * n
    firsts = ids.reshape(segments, rows)[:, 0]
    lasts = ids.reshape(segments, rows)[:, rows - 1]
    step = 1 if forward else -1
    near_end, far_end = (lasts, firsts) if forward else (firsts, lasts)

    def end_of(which, segment):
        return which[jnp.clip(segment, 0, segments - 1)]

    seg = 2 * seq + head
    takes = end_of(far_end, seg)
    core = seq % 2
    late_head = head if forward else 1 - head
    late_core = core if forward else 1 - core

    def gate(flag):
        return jnp.where(flag, 1.0, 0.0).astype(F32)

    def wider(state):
        return [part.astype(F32) for part in state]

    def narrow(state):
        return [state[0].astype(BF), state[1]]

    def merge(own, other, late, other_takes, joined):
        gained = [part * (gate(other_takes) * late) for part in other]
        own_factor = jnp.where(late == 1, 1.0, gate(joined))
        other_factor = jnp.where(late == 1, gate(joined), 1.0)
        joint = [a * own_factor + b * other_factor for a, b in zip(own, other)]
        return gained, joint

    own = [wide, thin]
    other = [flip_head(part) for part in own]
    first_of, second_of = 2 * seq, 2 * seq + 1
    if not forward:
        first_of, second_of = second_of, first_of
    total, joint = merge(
        wider(own),
        wider(other),
        late_head,
        end_of(near_end, seg - step) == takes,
        end_of(near_end, first_of) == end_of(near_end, second_of),
    )
    joint = narrow(joint)
    other = [flip_seq(part, 1) for part in joint]
    base = 4 * (seq // 2)
    early_end, late_end = (base + 1, base + 3) if forward else (base + 2, base)
    gained, joint = merge(
        wider(joint),
        wider(other),
        late_core,
        end_of(near_end, early_end) == takes,
        end_of(near_end, early_end) == end_of(near_end, late_end),
    )
    total = [a + b for a, b in zip(total, gained)]
    joint = narrow(joint)
    half = PAIRS // 2
    mine = [lax.dynamic_slice_in_dim(part, core * half, half, 0) for part in joint]
    hops = -(-DOC_MAX // (4 * rows))
    far = None
    for hop in range(1, hops + 1):
        got = wider([shift_seq(part, 2 * hop * step) for part in mine])
        nearer, farther = late_end - 4 * step, late_end - 4 * step * hop
        joined = gate(end_of(near_end, nearer) == end_of(near_end, farther))
        got = [part * joined for part in got]
        far = got if far is None else [a + b for a, b in zip(far, got)]
    far = narrow(far)
    other = [flip_seq(part, 1) for part in far]
    comes = (seq // 2 >= 1) if forward else (seq // 2 < n // 2 - 1)
    use = gate(comes & (end_of(near_end, late_end - 4 * step) == takes))
    result = []
    for a, b, so_far in zip(far, other, total):
        low = jnp.where(core == 0, a, b).astype(F32)
        high = jnp.where(core == 0, b, a).astype(F32)
        result.append(so_far + use * jnp.concatenate([low, high], axis=0))
    return narrow(result)


MESH = pl.DeviceIdType.MESH
GAIN_COLS = 128


class Links:
    def __init__(self):
        self.head, self.seq = lax.axis_index("head"), lax.axis_index("seq")
        self.n = lax.axis_size("seq")
        self.z, self.y, self.c = self.seq // 4, (self.seq // 2) % 2, self.seq % 2
        self.core = self.at(self.head, self.seq ^ 1)
        self.x = self.at(1 - self.head, self.seq)
        self.near = self.at(self.head, self.seq ^ 2)
        self.far = [self.at(self.head, self.seq ^ (4 * r)) for r in range(4)]

    def at(self, head, seq):
        return {"head": head, "seq": seq}

    def shifted(self, distance):
        return self.at(self.head, lax.rem(self.seq + distance + self.n, self.n))

    def greet(self):
        barrier = pltpu.get_barrier_semaphore()
        partners = [self.core, self.x, self.near] + self.far[1:]
        partners += [self.shifted(d) for d in (2, 4, -2, -4)]
        for partner in partners:
            pl.semaphore_signal(barrier, inc=1, device_id=partner, device_id_type=MESH)
        pl.semaphore_wait(barrier, len(partners))


class Copies:
    def __init__(self, send, recv, local):
        self.send, self.recv, self.local = send, recv, local
        self.used, self.used_local = 0, 0
        self.started, self.started_local = [], []

    def remote(self, src, dst, partner):
        i = self.used
        self.used += 1
        return pltpu.make_async_remote_copy(
            src_ref=src,
            dst_ref=dst,
            send_sem=self.send.at[i],
            recv_sem=self.recv.at[i],
            device_id=partner,
            device_id_type=MESH,
        )

    def go(self, *copies):
        for copy in copies:
            copy.start()
            self.started.append(copy)

    def keep(self, src, dst):
        copy = pltpu.make_async_copy(src, dst, self.local.at[self.used_local])
        self.used_local += 1
        copy.start()
        self.started_local.append(copy)
        return copy

    def drain(self):
        for copy in self.started:
            copy.wait_send()
        for copy in self.started_local:
            copy.wait()


def arrived(*copies):
    for copy in copies:
        copy.wait_recv()


class WideGather:
    def __init__(self, copies, links, shard, own, other, other_there):
        n, y, c = links, links.y, links.c
        self.copies = copies
        self.place = own.at[n.z, y, c]
        self.shard = shard
        self.far = [copies.remote(shard, self.place, n.far[r]) for r in range(1, 4)]
        mine, theirs = own.at[:, y, c], own.at[:, 1 - y, c]
        self.near = copies.remote(mine, mine, n.near)
        self.cross = [
            copies.remote(mine, other_there.at[:, y, c], n.x),
            copies.remote(theirs, other_there.at[:, 1 - y, c], n.x),
        ]
        self.core = [
            copies.remote(part, part, n.core)
            for part in (mine, theirs, other.at[:, y, c], other.at[:, 1 - y, c])
        ]

    def begin(self):
        self.copies.go(*self.far)
        self.own = self.copies.keep(self.shard, self.place)

    def one(self):
        arrived(*self.far)
        self.own.wait()
        self.copies.started_local.remove(self.own)
        self.copies.go(self.near, self.cross[0], self.core[0])

    def two(self):
        arrived(self.near)
        self.copies.go(self.cross[1], self.core[1])

    def three(self):
        arrived(self.cross[0])
        self.copies.go(self.core[2])

    def four(self):
        arrived(self.cross[1])
        self.copies.go(self.core[3])

    def end(self):
        arrived(*self.core)


class TallGather:
    def __init__(self, copies, links, shard, own, other):
        n, y, c = links, links.y, links.c
        self.copies = copies
        self.shard, self.place = shard, own.at[n.z, y, c]
        received = other.at[n.z, y, c]
        self.cross = copies.remote(shard, received, n.x)
        self.far_own = [copies.remote(shard, self.place, n.far[r]) for r in range(1, 4)]
        self.far_other = [copies.remote(received, received, n.far[r]) for r in range(1, 4)]
        mine = [own.at[:, y, c], other.at[:, y, c]]
        theirs = [own.at[:, 1 - y, c], other.at[:, 1 - y, c]]
        self.near = [copies.remote(part, part, n.near) for part in mine]
        self.core = [copies.remote(part, part, n.core) for part in mine + theirs]

    def begin(self):
        self.copies.go(self.cross)
        self.own = self.copies.keep(self.shard, self.place)

    def zero(self):
        self.copies.go(*self.far_own)
        arrived(self.cross)
        self.copies.go(*self.far_other)

    def one(self):
        arrived(*self.far_own)
        self.own.wait()
        self.copies.started_local.remove(self.own)
        self.copies.go(self.near[0], self.core[0])

    def two(self):
        arrived(*self.far_other)
        self.copies.go(self.near[1], self.core[1])

    def three(self):
        arrived(self.near[0])
        self.copies.go(self.core[2])

    def four(self):
        arrived(self.near[1])
        self.copies.go(self.core[3])

    def end(self):
        arrived(*self.core)


class Exchange:
    def __init__(self, copies, links, gates, first, bufs, forward):
        n = links
        self.copies, self.gates, self.first, self.bufs = copies, gates, first, bufs
        half = PAIRS // 2
        step = 2 if forward else -2
        own, a, j, b, j2, r1, r2, far = bufs

        def both(src, dst, partner):
            return [copies.remote(s, d, partner) for s, d in zip(src, dst)]

        def halves(state):
            return [
                state[0].at[pl.ds(n.c * half, half)],
                state[1].at[pl.ds(n.c * half, half)],
            ]

        self.rounds = [
            both(own, a, n.x),
            both(j, b, n.core),
            both(halves(j2), r1, n.shifted(step)) + both(halves(j2), r2, n.shifted(2 * step)),
            both(halves(far), halves(far), n.core),
        ]
        self.halves = halves
        self.total = None

    def gate(self, i):
        return self.gates[self.first + i]

    def begin(self):
        self.copies.go(*self.rounds[0])

    def one(self):
        own, a, j, b, j2, r1, r2, far = self.bufs
        arrived(*self.rounds[0])
        for s, d, t in zip(own, a, j):
            t[...] = (
                s[...].astype(F32) * self.gate(1) + d[...].astype(F32) * self.gate(2)
            ).astype(t.dtype)
        self.copies.go(*self.rounds[1])

    def two(self):
        own, a, j, b, j2, r1, r2, far = self.bufs
        arrived(*self.rounds[1])
        for s, d, t in zip(j, b, j2):
            t[...] = (
                s[...].astype(F32) * self.gate(4) + d[...].astype(F32) * self.gate(5)
            ).astype(t.dtype)
        self.copies.go(*self.rounds[2])

    def three(self):
        own, a, j, b, j2, r1, r2, far = self.bufs
        arrived(*self.rounds[2])
        for s, d, t in zip(r1, r2, self.halves(far)):
            t[...] = (s[...].astype(F32) + d[...].astype(F32) * self.gate(6)).astype(t.dtype)
        self.copies.go(*self.rounds[3])

    def four(self, out):
        own, a, j, b, j2, r1, r2, far = self.bufs
        arrived(*self.rounds[3])
        for s, d, f, t in zip(a, b, far, out):
            t[...] = (
                s[...].astype(F32) * self.gate(0)
                + d[...].astype(F32) * self.gate(3)
                + f[...].astype(F32) * self.gate(7)
            ).astype(t.dtype)


def exchange_shapes():
    shapes = []
    for name in range(8):
        pairs = PAIRS // 2 if name in (5, 6) else PAIRS
        shapes += [pltpu.VMEM((pairs, FEATS, WIDE), BF), pltpu.VMEM((pairs, 8, FEATS), F32)]
    return shapes


def exchange_gates(ids, rows, forward):
    head, seq = lax.axis_index("head"), lax.axis_index("seq")
    n = lax.axis_size("seq")
    segments = 2 * n
    ends = ids.reshape(segments, rows)
    firsts, lasts = ends[:, 0], ends[:, rows - 1]
    step = 1 if forward else -1
    near_end, far_end = (lasts, firsts) if forward else (firsts, lasts)
    seg = 2 * seq + head
    base = 4 * (seq // 2)
    core = seq % 2
    late_head = (head == 1) if forward else (head == 0)
    late_core = (core == 1) if forward else (core == 0)
    pair_early, pair_late = (2 * seq, 2 * seq + 1) if forward else (2 * seq + 1, 2 * seq)
    early_end, late_end = (base + 1, base + 3) if forward else (base + 2, base)
    chip = seq // 2
    near_ok = (chip >= 1) if forward else (chip < n // 2 - 1)
    far_ok = (chip >= 2) if forward else (chip < n // 2 - 2)
    where = jnp.stack(
        [seg - step, pair_early, pair_late, early_end, late_end, late_end - 4 * step,
         late_end - 8 * step]
    )
    docs = near_end[jnp.clip(where, 0, segments - 1)]
    takes = far_end[seg]
    joined = docs[1] == docs[2]
    joined2 = docs[3] == docs[4]
    flags = [
        late_head & (docs[0] == takes),
        late_head | joined,
        (~late_head) | joined,
        late_core & (docs[3] == takes),
        late_core | joined2,
        (~late_core) | joined2,
        far_ok & (docs[5] == docs[6]),
        near_ok & (docs[5] == takes),
    ]
    return jnp.stack(flags).astype(F32)


def pair_lanes(pair, start=0):
    return pl.ds(pl.multiple_of(start + pair * WIDE, WIDE), WIDE)


def state_pair(pair, table, keys, value, last, wide_ref, thin_ref):
    rows = keys.shape[0]
    total = None
    for part in range(2):
        sel = selectors(table, 2 * pair + part)
        one, two = factors(keys, table, sel)
        phi = one * two * last
        new = mm(phi.astype(BF), keep(half_mask(rows, part), value), TN)
        total = new if total is None else total + new
        thin_ref[pair, part : part + 1, :] = jnp.sum(phi, axis=0, keepdims=True)
    thin_ref[pair, 2:, :] = jnp.zeros((6, FEATS), F32)
    wide_ref[pair] = total.astype(BF)


def local_pair(pair, qkv, num_ref, den_ref, mask_ref):
    rows = qkv.shape[0]
    qk = HEADS * QD
    for i in range(rows // TILE):
        here = slice(i * TILE, (i + 1) * TILE)
        num = jnp.zeros((TILE, WIDE), F32)
        dens = []
        for part in range(2):
            head = 2 * pair + part
            query = keep(head_mask(TILE, head), qkv[here, :qk] * (QD**-0.5))
            den = jnp.zeros((TILE, 1), F32)
            for j in range(i + 1):
                there = slice(j * TILE, (j + 1) * TILE)
                s = mm(query, qkv[there, qk : 2 * qk], NT)
                w = (1.0 + s + 0.5 * s * s) * mask_ref[here, there]
                den = den + jnp.sum(w, axis=1, keepdims=True)
                value = qkv[there, pair_lanes(pair, 2 * qk)]
                num = num + mm(w.astype(BF), keep(half_mask(TILE, part), value), NN)
            dens.append(den)
        num_ref[here, pair_lanes(pair)] = num
        den_ref[here, pair_lanes(pair)] = jnp.where(half_mask(TILE, 0), dens[0], dens[1])


def finish_pair(pair, table, query, first, num_ref, den_ref, wide_ref, thin_ref, out_ref):
    rows = query.shape[0]
    lanes = pair_lanes(pair)
    num, den = num_ref[:, lanes], den_ref[:, lanes]
    for part in range(2):
        sel = selectors(table, 2 * pair + part)
        one, two = factors(query, table, sel)
        phi = one * two * (table[4:5, :] * first)
        mask = half_mask(rows, part)
        num = num + jnp.where(mask, mm(phi.astype(BF), wide_ref[pair], NN), 0.0)
        more = jnp.sum(phi * thin_ref[pair, part : part + 1, :], axis=1, keepdims=True)
        den = den + jnp.where(mask, more, 0.0)
    rden = 1.0 / den
    den_ref[:, lanes] = rden
    out_ref[:, lanes] = (num * rden).astype(BF)


def each_pair(low, high, step):
    def one(pair, carry):
        step(pair)
        return carry

    lax.fori_loop(low, high, one, 0)


WIDE_COPIES, TALL_COPIES, EXCHANGE_COPIES = 10, 15, 10
FWD_COPIES = 5 * WIDE_COPIES + TALL_COPIES + EXCHANGE_COPIES
FWD_LOCALS = 20


def forward_kernel(
    x_ref, qs_ref, os_ref, gs_ref, us_ref, ds_ref, row_ids_ref, col_ids_ref, first_ref, last_ref,
    table_ref, gates_ref,
    g_own, g_other, u_own, u_other, d_own, d_other, wq_out, wo_out, qkv_out, att_out, rden_out,
    res_out, n2_out, wide_out, thin_out, gain_out,
    wq, wo, normed, qkv, num, den, mask, att, res, n2, wide, thin, gain, *rest,
):
    bufs, (send, recv, local) = rest[:16], rest[16:]
    states = [(bufs[2 * i], bufs[2 * i + 1]) for i in range(8)]
    n = Links()
    copies = Copies(send, recv, local)
    rows, width = x_ref.shape
    qk, hv = HEADS * QD, HEADS * VD
    cut = 7 * 128
    full = wq.shape[-1]

    def side(ref, head, lo=None, hi=None):
        return ref.at[head] if lo is None else ref.at[head, :, :, :, :, pl.ds(lo, hi - lo)]

    q_parts = []
    for lo, hi in ((0, cut), (cut, full)):
        shard = qs_ref.at[:, pl.ds(lo, hi - lo)]
        own, other = side(wq, n.head, lo, hi), side(wq, 1 - n.head, lo, hi)
        q_parts.append(WideGather(copies, n, shard, own, other, own))
    own, other = side(wo, n.head), side(wo, 1 - n.head)
    outs = WideGather(copies, n, os_ref, own, other, own)
    gates = WideGather(copies, n, gs_ref, g_own, g_other, g_other)
    ups = WideGather(copies, n, us_ref, u_own, u_other, u_other)
    downs = TallGather(copies, n, ds_ref, d_own, d_other)
    swap = Exchange(copies, n, gates_ref, 0, states, True)

    n.greet()
    for part in q_parts:
        part.begin()
    outs.begin()
    gates.begin()
    ups.begin()
    downs.begin()

    table = table_ref[...]
    x = x_ref[...].astype(F32)
    scaled = x * lax.rsqrt(jnp.mean(x * x, axis=-1, keepdims=True) + EPSILON)
    visible_tile(mask, row_ids_ref, col_ids_ref, rows)
    for part in q_parts:
        part.one()
    outs.one()
    for part in q_parts:
        part.two()
        part.three()
    outs.two()
    outs.three()
    for part in q_parts:
        part.four()
    downs.zero()
    for part in q_parts:
        part.end()
    outs.four()
    gates.one()

    pick_gain = (
        lax.broadcasted_iota(jnp.int32, (8, GAIN_COLS), 0)
        == lax.broadcasted_iota(jnp.int32, (8, GAIN_COLS), 1)
    ).astype(F32).astype(BF)
    gain[...] = mm(pick_gain, wq[..., full - GAIN_COLS :].reshape(width, GAIN_COLS), NT)
    normed[...] = (scaled * gain[0:1, :]).astype(BF)
    h1 = normed[...]
    for lo in range(0, 2 * qk + hv, 256):
        weight = wq[..., lo : lo + 256].reshape(width, 256)
        qkv[:, lo : lo + 256] = mm(h1, weight, NN).astype(BF)
    copies.keep(qkv, qkv_out)
    copies.keep(wq, wq_out)
    copies.keep(gain, gain_out)

    def do_state(pair):
        state_pair(
            pair, table, qkv[:, qk : 2 * qk], qkv[:, pair_lanes(pair, 2 * qk)], last_ref[...],
            states[0][0], states[0][1],
        )

    def do_local(pair):
        local_pair(pair, qkv, num, den, mask)

    each_pair(0, PAIRS, do_state)
    swap.begin()
    outs.end()
    copies.keep(wo, wo_out)
    each_pair(0, 3, do_local)
    swap.one()
    gates.two()
    ups.one()
    each_pair(3, 5, do_local)
    swap.two()
    downs.one()
    gates.three()
    each_pair(5, PAIRS, do_local)
    swap.three()
    ups.two()
    downs.two()
    swap.four((wide, thin))
    copies.keep(wide, wide_out)
    copies.keep(thin, thin_out)

    def do_finish(pair):
        finish_pair(
            pair, table, qkv[:, :qk], first_ref[...], num, den, wide, thin, att
        )

    each_pair(0, PAIRS, do_finish)
    gates.four()
    downs.three()
    copies.keep(att, att_out)
    copies.keep(den, rden_out)
    o = att[...]
    for lo in range(0, width, 256):
        weight = wo[..., lo : lo + 256].reshape(hv, 256)
        res[:, lo : lo + 256] = x_ref[:, lo : lo + 256].astype(F32) + mm(o, weight, NN)
    copies.keep(res, res_out)
    y1 = res[...]
    n2[...] = (
        y1 * lax.rsqrt(jnp.mean(y1 * y1, axis=-1, keepdims=True) + EPSILON) * gain[1:2, :]
    ).astype(BF)
    copies.keep(n2, n2_out)
    downs.four()
    ups.three()
    gates.end()
    downs.end()
    ups.four()
    ups.end()
    copies.drain()


def forward(x, q_shard, o_shard, ffn, row_ids, col_ids, first, last, table, gates):
    rows, width = x.shape
    qk, hv = HEADS * QD, HEADS * VD
    full = q_shard.shape[-1]
    small, fine, ff = q_shard.shape[0], ffn[0].shape[0], ffn[0].shape[1]
    half = jax.ShapeDtypeStruct((4, 2, 2, fine, ff), BF)
    wq_shape, wo_shape = (2, 4, 2, 2, small, full), (2, 4, 2, 2, small, width)

    def like(shape, dtype):
        return jax.ShapeDtypeStruct(shape, dtype)

    out_shape = [half] * 6 + [
        like(wq_shape, BF), like(wo_shape, BF), like((rows, 2 * qk + hv), BF),
        like((rows, hv), BF), like((rows, hv), F32), like((rows, width), F32),
        like((rows, width), BF), STATE_SHAPES[0], STATE_SHAPES[1], like((8, width), F32),
    ]
    scratch = [
        pltpu.VMEM(wq_shape, BF), pltpu.VMEM(wo_shape, BF), pltpu.VMEM((rows, width), BF),
        pltpu.VMEM((rows, 2 * qk + hv), BF), pltpu.VMEM((rows, hv), F32),
        pltpu.VMEM((rows, hv), F32), pltpu.VMEM((rows, rows), F32), pltpu.VMEM((rows, hv), BF),
        pltpu.VMEM((rows, width), F32), pltpu.VMEM((rows, width), BF),
        pltpu.VMEM((PAIRS, FEATS, WIDE), BF), pltpu.VMEM((PAIRS, 8, FEATS), F32),
        pltpu.VMEM((8, width), F32),
    ] + exchange_shapes() + [
        pltpu.SemaphoreType.DMA((FWD_COPIES,)), pltpu.SemaphoreType.DMA((FWD_COPIES,)),
        pltpu.SemaphoreType.DMA((FWD_LOCALS,)),
    ]
    vmem = pl.BlockSpec(memory_space=pltpu.VMEM)
    return pl.pallas_call(
        forward_kernel,
        out_shape=out_shape,
        in_specs=[vmem] * 11 + [pl.BlockSpec(memory_space=pltpu.SMEM)],
        out_specs=[pl.BlockSpec(memory_space=pl.ANY)] * len(out_shape),
        scratch_shapes=scratch,
        compiler_params=pltpu.CompilerParams(
            collective_id=1, has_side_effects=True, vmem_limit_bytes=56 << 20
        ),
        cost_estimate=pl.CostEstimate(flops=8 << 30, bytes_accessed=64 << 20, transcendentals=0),
        name="forward",
    )(x, q_shard, o_shard, *ffn, row_ids, col_ids, first, last, table, gates)


def rms_scale(values, gain):
    return values * lax.rsqrt(jnp.mean(values * values, axis=-1, keepdims=True) + EPSILON) * gain


def swish_mix(gate, up_proj):
    return jax.nn.silu(gate) * up_proj


def dot_nn(a, b):
    return jnp.dot(a, b, preferred_element_type=F32)


def dot_nt(a, b):
    return lax.dot_general(a, b, (((1,), (1,)), ((), ())), preferred_element_type=F32)


def dot_tn(a, b):
    return lax.dot_general(a, b, (((0,), (0,)), ((), ())), preferred_element_type=F32)


def row_grads(left, right, by_head):
    head, core = lax.axis_index("head"), lax.axis_index("seq") % 2
    tokens = left.shape[0]
    chips = lax.axis_size("seq") // 2
    heads = 2 if by_head else 1
    rows = left.shape[1] // (heads * chips * 2)
    split = left.reshape(tokens, heads, chips, 2, rows)
    out = []
    for rel in range(heads):
        plane = pick(split, head ^ rel, 1) if by_head else split[:, 0]
        out.append([pick(plane, core ^ r, 2).reshape(tokens, chips * rows) for r in range(2)])
    if by_head:
        return [[dot_tn(part, right).astype(BF) for part in parts] for parts in out]
    return [[dot_tn(part, r).astype(BF) for part in out[0]] for r in right]


def plain_forward(
    inputs, segment_ids, norm1_gain, w_query, w_key, w_value, w_out, norm2_gain, w_gate, w_up,
    w_down, row_ids, col_ids, first, last, table,
):
    head, seq = lax.axis_index("head"), lax.axis_index("seq")
    n_seq = lax.axis_size("seq")
    rows, width = inputs.shape
    qk = HEADS * QD
    slot = head * n_seq + seq
    small = norm1_gain.shape[0]
    gains = jnp.zeros((2, width // small, small), F32)
    gains = lax.dynamic_update_slice(
        gains, jnp.stack([norm1_gain, norm2_gain]).astype(F32)[:, None, :], (0, slot, 0)
    ).reshape(2, width)
    gains = sum_everywhere(gains)
    gain_first, gain_second = gains[0], gains[1]

    qkv_full = gather_rows(jnp.concatenate([w_query, w_key, w_value], axis=1))
    out_full = gather_rows(w_out)
    gate_w = gather_halves(w_gate, False)
    up_w = gather_halves(w_up, False)
    down_w = gather_halves(w_down.T, True)

    normed_one = rms_scale(inputs, gain_first).astype(BF)
    qkv = dot_nn(normed_one, qkv_full).astype(BF)
    query, keys, values = qkv[:, :qk], qkv[:, qk : 2 * qk], qkv[:, 2 * qk :]
    vcols = HEADS * VD
    t_spec, q_spec = full_spec((8, FEATS)), full_spec((rows, qk))
    one_spec, row_spec = full_spec((rows, 1)), full_spec((1, rows))
    p_spec = pair_spec(rows)
    f32_like = jax.ShapeDtypeStruct((rows, vcols), F32)
    bf_like = jax.ShapeDtypeStruct((rows, vcols), BF)
    state = run(
        state_kernel,
        [t_spec, q_spec, p_spec, one_spec],
        state_specs(),
        STATE_SHAPES,
        (table, keys, values, last),
        flops=8 * rows * qk * FEATS * HEADS,
    )
    num, den = run(
        local_kernel,
        [q_spec, q_spec, p_spec, one_spec, row_spec],
        [p_spec, p_spec],
        [f32_like, f32_like],
        (query, keys, values, row_ids, col_ids),
        [pltpu.VMEM((rows, rows), F32)],
        flops=8 * rows * rows * qk * HEADS,
    )
    before = exchange(*state, segment_ids, rows, True)
    attended, rden = run(
        finish_kernel,
        [t_spec, q_spec, p_spec, p_spec, one_spec] + state_specs(),
        [p_spec, p_spec],
        [bf_like, f32_like],
        (table, query, num, den, first, *before),
        flops=8 * rows * qk * FEATS * HEADS,
    )
    residual = inputs + dot_nn(attended, out_full)
    normed_two = rms_scale(residual, gain_second).astype(BF)

    return (
        gate_w, up_w, down_w, qkv_full, out_full, gain_first, gain_second, normed_one,
        query, keys, values, attended, rden, residual, normed_two, before,
    )


def body(
    layer_input,
    segment_ids,
    norm1_gain,
    w_query,
    w_key,
    w_value,
    w_out,
    norm2_gain,
    w_gate,
    w_up,
    w_down,
    output_grad,
):
    rows = layer_input.shape[1]
    head, seq = lax.axis_index("head"), lax.axis_index("seq")
    n_seq = lax.axis_size("seq")
    qk = HEADS * QD
    inputs = layer_input[0].astype(F32)
    width = inputs.shape[1]

    segment = 2 * seq + head
    ids = lax.dynamic_slice_in_dim(segment_ids, segment * rows, rows)
    row_ids, col_ids = ids[:, None], ids[None, :]
    first = (row_ids == ids[0]).astype(F32)
    last = (row_ids == ids[rows - 1]).astype(F32)
    table = jnp.asarray(feature_table())
    vcols = HEADS * VD
    t_spec, q_spec = full_spec((8, FEATS)), full_spec((rows, qk))
    one_spec, row_spec = full_spec((rows, 1)), full_spec((1, rows))
    p_spec = pair_spec(rows)
    f32_like = jax.ShapeDtypeStruct((rows, vcols), F32)
    bf_like = jax.ShapeDtypeStruct((rows, vcols), BF)
    slot = head * n_seq + seq
    small = norm1_gain.shape[0]

    if n_seq == 16:
        gain_cols = jnp.stack([norm1_gain, norm2_gain], axis=1)
        gain_cols = jnp.pad(gain_cols, ((0, 0), (0, GAIN_COLS - 2)))
        (
            g_own, g_other, u_own, u_other, d_own, d_other, wq, wo, qkv, attended, rden,
            residual, normed_two, wide, thin, gains,
        ) = forward(
            layer_input[0],
            jnp.concatenate([w_query, w_key, w_value, gain_cols], axis=1),
            w_out,
            [w_gate, w_up, w_down.T],
            row_ids, col_ids, first, last, table, exchange_gates(segment_ids, rows, True),
        )

        def flat(weight):
            return weight.reshape(-1, weight.shape[-1])

        gate_w, up_w, down_w = (
            [flat(g_own), flat(g_other)], [flat(u_own), flat(u_other)], [flat(d_own), flat(d_other)],
        )
        qkv_full, out_full = flat(wq)[:, : 2 * qk + vcols], flat(wo)
        gain_first, gain_second = gains[0], gains[1]
        normed_one = rms_scale(inputs, gain_first).astype(BF)
        query, keys, values = qkv[:, :qk], qkv[:, qk : 2 * qk], qkv[:, 2 * qk :]
        before = (wide, thin)
    else:
        (
            gate_w, up_w, down_w, qkv_full, out_full, gain_first, gain_second, normed_one,
            query, keys, values, attended, rden, residual, normed_two, before,
        ) = plain_forward(
            inputs, segment_ids, norm1_gain, w_query, w_key, w_value, w_out, norm2_gain, w_gate,
            w_up, w_down, row_ids, col_ids, first, last, table,
        )

    grad_output = output_grad[0]
    outcome = residual
    grad_normed_two = None
    hiddens, grad_gates, grad_ups = [], [], []
    for w_g, w_u, w_d in zip(gate_w, up_w, down_w):
        gate = dot_nn(normed_two, w_g)
        up_proj = dot_nn(normed_two, w_u)
        grad_hidden = dot_nn(grad_output, w_d)
        hidden, mix_pull = jax.vjp(swish_mix, gate, up_proj)
        grad_gate, grad_up = mix_pull(grad_hidden)
        hiddens.append(hidden.astype(BF))
        grad_gates.append(grad_gate.astype(BF))
        grad_ups.append(grad_up.astype(BF))
        outcome = outcome + dot_nt(hiddens[-1], w_d)
        more = dot_nt(grad_gates[-1], w_g) + dot_nt(grad_ups[-1], w_u)
        grad_normed_two = more if grad_normed_two is None else grad_normed_two + more
    outcome = outcome.astype(BF)
    d_gate = scatter(row_grads(normed_two, grad_gates, False), True)
    d_up = scatter(row_grads(normed_two, grad_ups, False), True)
    d_down = scatter(row_grads(grad_output, hiddens, False), False).T

    _, norm_pull = jax.vjp(rms_scale, residual, gain_second)
    grad_resid_two, grad_gain_two = norm_pull(grad_normed_two)
    grad_middle = grad_output.astype(F32) + grad_resid_two
    grad_middle_low = grad_middle.astype(BF)
    d_out = scatter(row_grads(attended, grad_middle_low, True), True)
    grad_attended = dot_nt(grad_middle_low, out_full).astype(BF)

    grad_state = run(
        grad_state_kernel,
        [t_spec, q_spec, p_spec, p_spec, p_spec, one_spec],
        state_specs(),
        STATE_SHAPES,
        (table, query, grad_attended, attended, rden, first),
        flops=8 * rows * qk * FEATS * HEADS,
    )
    qk_f32 = jax.ShapeDtypeStruct((rows, qk), F32)
    qk_bf = jax.ShapeDtypeStruct((rows, qk), BF)
    grad_query, grad_key, grad_value = run(
        local_grad_kernel,
        [t_spec, q_spec, q_spec, p_spec, p_spec, p_spec, p_spec, one_spec, row_spec, one_spec]
        + state_specs(),
        [q_spec, q_spec, p_spec],
        [qk_bf, qk_f32, f32_like],
        (table, query, keys, values, grad_attended, attended, rden, row_ids, col_ids, first)
        + tuple(before),
        [pltpu.VMEM((rows, rows), F32), pltpu.VMEM((rows, qk), F32), pltpu.VMEM((rows, qk), F32)],
        flops=20 * rows * rows * qk * HEADS,
    )
    after = exchange(*grad_state, segment_ids, rows, False)
    grad_key, grad_value = run(
        finish_grad_kernel,
        [t_spec, q_spec, p_spec, q_spec, p_spec, one_spec] + state_specs(),
        [q_spec, p_spec],
        [qk_bf, bf_like],
        (table, keys, values, grad_key, grad_value, last, *after),
        [pltpu.VMEM((rows, qk), F32)],
        flops=16 * rows * qk * FEATS * HEADS,
    )
    grad_qkv = jnp.concatenate([grad_query, grad_key, grad_value], axis=1)
    d_qkv = scatter(row_grads(normed_one, grad_qkv, True), True)
    grad_normed_one = dot_nt(grad_qkv, qkv_full)
    _, first_pull = jax.vjp(rms_scale, inputs, gain_first)
    grad_inputs, grad_gain_one = first_pull(grad_normed_one)
    grad_layer = grad_middle + grad_inputs
    grad_gains = sum_everywhere(jnp.stack([grad_gain_one, grad_gain_two]))
    grad_gains = lax.dynamic_slice_in_dim(
        grad_gains.reshape(2, width // small, small), slot, 1, 1
    )[:, 0]
    return (
        outcome[None],
        grad_layer[None],
        grad_gains[0],
        d_qkv[:, :qk],
        d_qkv[:, qk : 2 * qk],
        d_qkv[:, 2 * qk :],
        d_out,
        grad_gains[1],
        d_gate,
        d_up,
        d_down,
    )


def solution(mesh):
    split = P(("head", "seq"))
    rows = P(("head", "seq"), None)
    block = P("seq", "head", None)
    wide, tall = P("seq", "head"), P("head", "seq")
    in_specs = (block, P(), split, rows, rows, rows, rows, split, wide, wide, tall, block)
    out_specs = (block, block, split, rows, rows, rows, rows, split, wide, wide, tall)
    return jax.shard_map(body, mesh=mesh, in_specs=in_specs, out_specs=out_specs, check_vma=False)
```

```python
import functools

import jax
import jax.numpy as jnp
import numpy as np
from jax import lax
from jax.experimental import pallas as pl
from jax.experimental.pallas import tpu as pltpu
from jax.sharding import PartitionSpec as P

HEADS = 16
QD = 16
VD = 64
DOC_MAX = 4096
EPSILON = 1e-05
PAIRS = HEADS // 2
WIDE = 2 * VD
FEATS = 160
TILE = 256

BF = jnp.bfloat16
F32 = jnp.float32


def flip_seq(value, code):
    n = lax.axis_size("seq")
    return lax.ppermute(value, "seq", [(i, i ^ code) for i in range(n)])


def flip_head(value):
    n = lax.axis_size("head")
    return lax.ppermute(value, "head", [(i, i ^ 1) for i in range(n)])


def shift_seq(value, distance):
    n = lax.axis_size("seq")
    return lax.ppermute(
        value, "seq", [(i, i + distance) for i in range(n) if 0 <= i + distance < n]
    )


def layout():
    chips = lax.axis_size("seq") // 2
    near = 2 if chips <= 8 else 8
    far = chips // near
    return far, near


def place_kernel(groups, count, *refs):
    pieces, out, sem = refs[:count], refs[count], refs[count + 1]
    me = lax.axis_index("seq")
    head = lax.axis_index("head")
    n = lax.axis_size("seq")
    copies = []
    for piece, blocks in zip(pieces, groups):
        for index, (rel_head, rel_seq) in blocks:
            place = me ^ rel_seq
            if rel_head is not None:
                place = place + (head ^ rel_head) * n
            copies.append(
                pltpu.make_async_copy(piece.at[index], out.at[place], sem.at[len(copies)])
            )
    for copy in copies:
        copy.start()
    for copy in copies:
        copy.wait()


def place(pieces, groups, blocks):
    rows, cols = pieces[0].shape[-2:]
    total = sum(len(g) for g in groups)
    out = pl.pallas_call(
        functools.partial(place_kernel, groups, len(pieces)),
        out_shape=jax.ShapeDtypeStruct((blocks, rows, cols), pieces[0].dtype),
        in_specs=[pl.BlockSpec(memory_space=pl.ANY)] * len(pieces),
        out_specs=pl.BlockSpec(memory_space=pltpu.VMEM),
        scratch_shapes=[pltpu.SemaphoreType.DMA((total,))],
        compiler_params=pltpu.CompilerParams(vmem_limit_bytes=16 << 20),
        cost_estimate=pl.CostEstimate(
            flops=0, bytes_accessed=4 * blocks * rows * cols, transcendentals=0
        ),
        name="place",
    )(*pieces)
    return out.reshape(blocks * rows, cols)


def gather(shard, head_first):
    far, near = layout()
    far_codes = [2 * near * r for r in range(far)]
    near_codes = [2 * r for r in range(near)]
    if head_first:
        shard = jnp.stack([shard, flip_head(shard)])
    column = jnp.stack([shard] + [flip_seq(shard, code) for code in far_codes[1:]])
    held = [(column, 0, 0)]
    held += [(flip_seq(column, code), 0, code) for code in near_codes[1:]]
    if not head_first:
        held += [(flip_head(buf), 1, code) for buf, _, code in held]
    held += [(flip_seq(buf, 1), rel, code + 1) for buf, rel, code in held]
    result = []
    for buf, rel, code in held:
        if head_first:
            blocks = [((r, g), (g, code + far_codes[r])) for r in range(far) for g in range(2)]
        else:
            blocks = [((r,), (rel, code + far_codes[r])) for r in range(far)]
        result.append((buf, blocks))
    return result


def gather_rows(shard):
    got = gather(shard, False)
    return place([b for b, _ in got], [g for _, g in got], 2 * lax.axis_size("seq"))


def gather_halves(shard, head_first):
    got = gather(shard, head_first)
    halves = []
    for rel in range(2):
        pieces, groups = [], []
        for buf, blocks in got:
            mine = [(i, (None, code)) for i, (r, code) in blocks if r == rel]
            if mine:
                pieces.append(buf)
                groups.append(mine)
        halves.append(place(pieces, groups, lax.axis_size("seq")))
    return halves


def add_low(*terms):
    total = terms[0].astype(F32)
    for term in terms[1:]:
        total = total + term.astype(F32)
    return total.astype(BF)


def pick(value, index, axis):
    return lax.dynamic_index_in_dim(value, index, axis, keepdims=False)


def scatter(grads, head_first):
    far, near = layout()
    seq = lax.axis_index("seq")
    far_at, near_at = seq // (2 * near), (seq // 2) % near
    both = [
        add_low(grads[rel][0], flip_seq(grads[rel][1], 1)) for rel in range(2)
    ]
    rows = both[0].shape[0] // (far * near)
    cols = both[0].shape[1]
    if head_first:
        whole = add_low(both[0], flip_head(both[1])).reshape(far, near, rows, cols)
    else:
        whole = jnp.stack(both).reshape(2, far, near, rows, cols).transpose(1, 2, 0, 3, 4)
    parts = [pick(whole, near_at, 1)]
    parts += [flip_seq(pick(whole, near_at ^ r, 1), 2 * r) for r in range(1, near)]
    column = add_low(*parts)
    parts = [pick(column, far_at, 0)]
    parts += [flip_seq(pick(column, far_at ^ r, 0), 2 * near * r) for r in range(1, far)]
    if head_first:
        return sum(part.astype(F32) for part in parts)
    both = add_low(*parts)
    return both[0].astype(F32) + flip_head(both[1]).astype(F32)


def sum_everywhere(value):
    value = value + flip_head(value)
    code = 1
    while code < lax.axis_size("seq"):
        value = value + flip_seq(value, code)
        code *= 2
    return value


def feature_table():
    first, second, one, two, scale = [], [], [], [], []
    for a in range(QD):
        for b in range(a, QD):
            first.append(a)
            second.append(b)
            one.append(0.0)
            two.append(0.0)
            scale.append((1.0 if a == b else 2.0) / (2.0 * QD))
    for a in range(QD):
        first.append(a)
        second.append(-1000)
        one.append(0.0)
        two.append(1.0)
        scale.append(QD**-0.5)
    first.append(-1000)
    second.append(-1000)
    one.append(1.0)
    two.append(1.0)
    scale.append(1.0)
    pad = FEATS - len(first)
    table = np.zeros((8, FEATS), np.float32)
    table[0] = np.array(first + [-1000] * pad)
    table[1] = np.array(second + [-1000] * pad)
    table[2] = np.array(one + [0.0] * pad)
    table[3] = np.array(two + [0.0] * pad)
    table[4] = np.array(scale + [0.0] * pad)
    return table


def mm(a, b, dims):
    return lax.dot_general(a, b, ((dims[0], dims[1]), ((), ())), preferred_element_type=F32)


NN = ((1,), (0,))
NT = ((1,), (1,))
TN = ((0,), (0,))


def selectors(table, head):
    lanes = HEADS * QD
    row = (lax.broadcasted_iota(jnp.int32, (lanes, FEATS), 0) - head * QD).astype(F32)
    one = (row == table[0:1, :]).astype(F32).astype(BF)
    two = (row == table[1:2, :]).astype(F32).astype(BF)
    return one, two


def factors(values, table, sel):
    return (
        mm(values, sel[0], NN) + table[2:3, :],
        mm(values, sel[1], NN) + table[3:4, :],
    )


def half_mask(rows, part):
    lane = lax.broadcasted_iota(jnp.int32, (rows, WIDE), 1)
    return (lane >= VD) if part else (lane < VD)


def head_mask(rows, head):
    lane = lax.broadcasted_iota(jnp.int32, (rows, HEADS * QD), 1)
    return (lane >= head * QD) & (lane < (head + 1) * QD)


def keep(mask, value):
    return jnp.where(mask, value.astype(F32), 0.0).astype(BF)


def state_kernel(table_ref, keys_ref, values_ref, last_ref, wide_ref, thin_ref):
    pair = pl.program_id(0)
    table = table_ref[...]
    keys = keys_ref[...]
    rows = keys.shape[0]
    last = last_ref[...]
    total = None
    for part in range(2):
        sel = selectors(table, 2 * pair + part)
        one, two = factors(keys, table, sel)
        phi = one * two * last
        value = keep(half_mask(rows, part), values_ref[...])
        new = mm(phi.astype(BF), value, TN)
        total = new if total is None else total + new
        thin_ref[0, part : part + 1, :] = jnp.sum(phi, axis=0, keepdims=True)
    thin_ref[0, 2:, :] = jnp.zeros((6, FEATS), F32)
    wide_ref[0] = total.astype(BF)


def visible_tile(mask_ref, row_ids_ref, col_ids_ref, rows):
    for i in range(rows // TILE):
        for j in range(i + 1):
            same = (
                row_ids_ref[i * TILE : (i + 1) * TILE, :]
                == col_ids_ref[:, j * TILE : (j + 1) * TILE]
            )
            if i == j:
                same = same & (
                    lax.broadcasted_iota(jnp.int32, (TILE, TILE), 1)
                    <= lax.broadcasted_iota(jnp.int32, (TILE, TILE), 0)
                )
            mask_ref[i * TILE : (i + 1) * TILE, j * TILE : (j + 1) * TILE] = same.astype(F32)


def local_kernel(
    query_ref, keys_ref, values_ref, row_ids_ref, col_ids_ref, num_ref, den_ref, mask_ref
):
    pair = pl.program_id(0)
    rows = query_ref.shape[0]

    @pl.when(pair == 0)
    def _():
        visible_tile(mask_ref, row_ids_ref, col_ids_ref, rows)

    for i in range(rows // TILE):
        here = slice(i * TILE, (i + 1) * TILE)
        num = jnp.zeros((TILE, WIDE), F32)
        dens = []
        for part in range(2):
            head = 2 * pair + part
            query = keep(head_mask(TILE, head), query_ref[here, :] * (QD**-0.5))
            den = jnp.zeros((TILE, 1), F32)
            for j in range(i + 1):
                there = slice(j * TILE, (j + 1) * TILE)
                s = mm(query, keys_ref[there, :], NT)
                w = (1.0 + s + 0.5 * s * s) * mask_ref[here, there]
                den = den + jnp.sum(w, axis=1, keepdims=True)
                num = num + mm(
                    w.astype(BF), keep(half_mask(TILE, part), values_ref[there, :]), NN
                )
            dens.append(den)
        num_ref[here, :] = num
        den_ref[here, :] = jnp.where(half_mask(TILE, 0), dens[0], dens[1])


def finish_kernel(
    table_ref, query_ref, num_ref, den_ref, first_ref, wide_ref, thin_ref, out_ref, rden_ref
):
    pair = pl.program_id(0)
    table = table_ref[...]
    query = query_ref[...]
    rows = query.shape[0]
    first = first_ref[...]
    num, den = num_ref[...], den_ref[...]
    for part in range(2):
        sel = selectors(table, 2 * pair + part)
        one, two = factors(query, table, sel)
        phi = one * two * (table[4:5, :] * first)
        mask = half_mask(rows, part)
        extra = mm(phi.astype(BF), wide_ref[0], NN)
        num = num + jnp.where(mask, extra, 0.0)
        more = jnp.sum(phi * thin_ref[0, part : part + 1, :], axis=1, keepdims=True)
        den = den + jnp.where(mask, more, 0.0)
    rden = 1.0 / den
    rden_ref[...] = rden
    out_ref[...] = (num * rden).astype(BF)


def prepare(grad_ref, out_ref, rden_ref):
    rows = grad_ref.shape[0]
    grad = grad_ref[...].astype(F32)
    rden = rden_ref[...]
    dnum = (grad * rden).astype(BF)
    prod = grad * out_ref[...].astype(F32) * rden
    deltas = [
        jnp.sum(jnp.where(half_mask(rows, part), prod, 0.0), axis=1, keepdims=True)
        for part in range(2)
    ]
    return dnum, deltas


def grad_state_kernel(
    table_ref, query_ref, grad_ref, out_ref, rden_ref, first_ref, wide_ref, thin_ref
):
    pair = pl.program_id(0)
    table = table_ref[...]
    query = query_ref[...]
    rows = query.shape[0]
    dnum, deltas = prepare(grad_ref, out_ref, rden_ref)
    total = None
    for part in range(2):
        sel = selectors(table, 2 * pair + part)
        one, two = factors(query, table, sel)
        phi = one * two * (table[4:5, :] * first_ref[...])
        new = mm(phi.astype(BF), keep(half_mask(rows, part), dnum), TN)
        total = new if total is None else total + new
        thin_ref[0, part : part + 1, :] = -jnp.sum(phi * deltas[part], axis=0, keepdims=True)
    thin_ref[0, 2:, :] = jnp.zeros((6, FEATS), F32)
    wide_ref[0] = total.astype(BF)


def local_grad_kernel(
    table_ref,
    query_ref,
    keys_ref,
    values_ref,
    grad_ref,
    out_ref,
    rden_ref,
    row_ids_ref,
    col_ids_ref,
    first_ref,
    wide_ref,
    thin_ref,
    dq_ref,
    dk_ref,
    dv_ref,
    mask_ref,
    dq_acc,
    dk_acc,
):
    pair = pl.program_id(0)
    table = table_ref[...]
    query = query_ref[...]
    keys = keys_ref[...]
    rows = query.shape[0]
    tiles = rows // TILE
    scale = QD**-0.5

    @pl.when(pair == 0)
    def _():
        visible_tile(mask_ref, row_ids_ref, col_ids_ref, rows)
        dq_acc[...] = jnp.zeros_like(dq_acc)
        dk_acc[...] = jnp.zeros_like(dk_acc)

    dnum, deltas = prepare(grad_ref, out_ref, rden_ref)
    dv = [jnp.zeros((TILE, WIDE), F32) for _ in range(tiles)]
    for part in range(2):
        head = 2 * pair + part
        at_head = head_mask(rows, head)
        q_head = keep(at_head, query * scale)
        k_head = keep(at_head, keys * scale)
        d_head = keep(half_mask(rows, part), dnum)
        for i in range(tiles):
            here = slice(i * TILE, (i + 1) * TILE)
            dq = dq_acc[here, :]
            for j in range(i + 1):
                there = slice(j * TILE, (j + 1) * TILE)
                s = mm(q_head[here], keys[there], NT)
                mask = mask_ref[here, there]
                w = ((1.0 + s + 0.5 * s * s) * mask).astype(BF)
                dp = mm(d_head[here], values_ref[there, :], NT)
                ds = ((dp - deltas[part][here]) * ((1.0 + s) * mask)).astype(BF)
                dq = dq + mm(ds, k_head[there], NN)
                dk_acc[there, :] += mm(ds, q_head[here], TN)
                dv[j] = dv[j] + mm(w, d_head[here], TN)
            dq_acc[here, :] = dq
        sel = selectors(table, head)
        one, two = factors(query, table, sel)
        dphi = mm(d_head, wide_ref[0], NT) - deltas[part] * thin_ref[0, part : part + 1, :]
        dphi = dphi * (table[4:5, :] * first_ref[...])
        dq_acc[...] += mm((dphi * two).astype(BF), sel[0], NT) + mm(
            (dphi * one).astype(BF), sel[1], NT
        )
    for j in range(tiles):
        dv_ref[j * TILE : (j + 1) * TILE, :] = dv[j]

    @pl.when(pair == PAIRS - 1)
    def _():
        dq_ref[...] = dq_acc[...].astype(BF)
        dk_ref[...] = dk_acc[...]


def finish_grad_kernel(
    table_ref, keys_ref, values_ref, dk_in_ref, dv_in_ref, last_ref, wide_ref, thin_ref,
    dk_ref, dv_ref, dk_acc,
):
    pair = pl.program_id(0)
    table = table_ref[...]
    keys = keys_ref[...]
    rows = keys.shape[0]
    last = last_ref[...]

    @pl.when(pair == 0)
    def _():
        dk_acc[...] = dk_in_ref[...]

    dv = dv_in_ref[...]
    for part in range(2):
        sel = selectors(table, 2 * pair + part)
        one, two = factors(keys, table, sel)
        mask = half_mask(rows, part)
        phi = one * two * last
        dv = dv + jnp.where(mask, mm(phi.astype(BF), wide_ref[0], NN), 0.0)
        dphi = mm(keep(mask, values_ref[...]), wide_ref[0], NT) + thin_ref[0, part : part + 1, :]
        dphi = dphi * last
        dk_acc[...] += mm((dphi * two).astype(BF), sel[0], NT) + mm(
            (dphi * one).astype(BF), sel[1], NT
        )
    dv_ref[...] = dv.astype(BF)

    @pl.when(pair == PAIRS - 1)
    def _():
        dk_ref[...] = dk_acc[...].astype(BF)


def full_spec(shape):
    return pl.BlockSpec(shape, lambda p: (0,) * len(shape))


def pair_spec(rows):
    return pl.BlockSpec((rows, WIDE), lambda p: (0, p))


def state_specs():
    return [
        pl.BlockSpec((1, FEATS, WIDE), lambda p: (p, 0, 0)),
        pl.BlockSpec((1, 8, FEATS), lambda p: (p, 0, 0)),
    ]


STATE_SHAPES = (
    jax.ShapeDtypeStruct((PAIRS, FEATS, WIDE), BF),
    jax.ShapeDtypeStruct((PAIRS, 8, FEATS), F32),
)


def run(kernel, in_specs, out_specs, out_shape, args, scratch=(), flops=0):
    moved = sum(a.size * a.dtype.itemsize for a in args)
    return pl.pallas_call(
        kernel,
        grid=(PAIRS,),
        in_specs=in_specs,
        out_specs=out_specs,
        out_shape=out_shape,
        scratch_shapes=scratch,
        compiler_params=pltpu.CompilerParams(vmem_limit_bytes=48 << 20),
        cost_estimate=pl.CostEstimate(flops=flops, bytes_accessed=moved, transcendentals=0),
        name=kernel.__name__,
    )(*args)


def exchange(wide, thin, ids, rows, forward):
    head, seq = lax.axis_index("head"), lax.axis_index("seq")
    n = lax.axis_size("seq")
    segments = 2 * n
    firsts = ids.reshape(segments, rows)[:, 0]
    lasts = ids.reshape(segments, rows)[:, rows - 1]
    step = 1 if forward else -1
    near_end, far_end = (lasts, firsts) if forward else (firsts, lasts)

    def end_of(which, segment):
        return which[jnp.clip(segment, 0, segments - 1)]

    seg = 2 * seq + head
    takes = end_of(far_end, seg)
    core = seq % 2
    late_head = head if forward else 1 - head
    late_core = core if forward else 1 - core

    def gate(flag):
        return jnp.where(flag, 1.0, 0.0).astype(F32)

    def wider(state):
        return [part.astype(F32) for part in state]

    def narrow(state):
        return [state[0].astype(BF), state[1]]

    def merge(own, other, late, other_takes, joined):
        gained = [part * (gate(other_takes) * late) for part in other]
        own_factor = jnp.where(late == 1, 1.0, gate(joined))
        other_factor = jnp.where(late == 1, gate(joined), 1.0)
        joint = [a * own_factor + b * other_factor for a, b in zip(own, other)]
        return gained, joint

    own = [wide, thin]
    other = [flip_head(part) for part in own]
    first_of, second_of = 2 * seq, 2 * seq + 1
    if not forward:
        first_of, second_of = second_of, first_of
    total, joint = merge(
        wider(own),
        wider(other),
        late_head,
        end_of(near_end, seg - step) == takes,
        end_of(near_end, first_of) == end_of(near_end, second_of),
    )
    joint = narrow(joint)
    other = [flip_seq(part, 1) for part in joint]
    base = 4 * (seq // 2)
    early_end, late_end = (base + 1, base + 3) if forward else (base + 2, base)
    gained, joint = merge(
        wider(joint),
        wider(other),
        late_core,
        end_of(near_end, early_end) == takes,
        end_of(near_end, early_end) == end_of(near_end, late_end),
    )
    total = [a + b for a, b in zip(total, gained)]
    joint = narrow(joint)
    half = PAIRS // 2
    mine = [lax.dynamic_slice_in_dim(part, core * half, half, 0) for part in joint]
    hops = -(-DOC_MAX // (4 * rows))
    far = None
    for hop in range(1, hops + 1):
        got = wider([shift_seq(part, 2 * hop * step) for part in mine])
        nearer, farther = late_end - 4 * step, late_end - 4 * step * hop
        joined = gate(end_of(near_end, nearer) == end_of(near_end, farther))
        got = [part * joined for part in got]
        far = got if far is None else [a + b for a, b in zip(far, got)]
    far = narrow(far)
    other = [flip_seq(part, 1) for part in far]
    comes = (seq // 2 >= 1) if forward else (seq // 2 < n // 2 - 1)
    use = gate(comes & (end_of(near_end, late_end - 4 * step) == takes))
    result = []
    for a, b, so_far in zip(far, other, total):
        low = jnp.where(core == 0, a, b).astype(F32)
        high = jnp.where(core == 0, b, a).astype(F32)
        result.append(so_far + use * jnp.concatenate([low, high], axis=0))
    return narrow(result)


MESH = pl.DeviceIdType.MESH
GAIN_COLS = 128


class Links:
    def __init__(self):
        self.head, self.seq = lax.axis_index("head"), lax.axis_index("seq")
        self.n = lax.axis_size("seq")
        self.z, self.y, self.c = self.seq // 4, (self.seq // 2) % 2, self.seq % 2
        self.core = self.at(self.head, self.seq ^ 1)
        self.x = self.at(1 - self.head, self.seq)
        self.near = self.at(self.head, self.seq ^ 2)
        self.far = [self.at(self.head, self.seq ^ (4 * r)) for r in range(4)]

    def at(self, head, seq):
        return {"head": head, "seq": seq}

    def shifted(self, distance):
        return self.at(self.head, lax.rem(self.seq + distance + self.n, self.n))

    def greet(self):
        barrier = pltpu.get_barrier_semaphore()
        partners = [self.core, self.x, self.near] + self.far[1:]
        partners += [self.shifted(d) for d in (2, 4, -2, -4)]
        for partner in partners:
            pl.semaphore_signal(barrier, inc=1, device_id=partner, device_id_type=MESH)
        pl.semaphore_wait(barrier, len(partners))


class Copies:
    def __init__(self, send, recv, local):
        self.send, self.recv, self.local = send, recv, local
        self.used, self.used_local = 0, 0
        self.started, self.started_local = [], []

    def remote(self, src, dst, partner):
        i = self.used
        self.used += 1
        return pltpu.make_async_remote_copy(
            src_ref=src,
            dst_ref=dst,
            send_sem=self.send.at[i],
            recv_sem=self.recv.at[i],
            device_id=partner,
            device_id_type=MESH,
        )

    def go(self, *copies):
        for copy in copies:
            copy.start()
            self.started.append(copy)

    def keep(self, src, dst):
        copy = pltpu.make_async_copy(src, dst, self.local.at[self.used_local])
        self.used_local += 1
        copy.start()
        self.started_local.append(copy)
        return copy

    def finish(self, copy):
        copy.wait()
        self.started_local = [other for other in self.started_local if other is not copy]

    def drain(self):
        for copy in self.started:
            copy.wait_send()
        for copy in self.started_local:
            copy.wait()


def arrived(*copies):
    for copy in copies:
        copy.wait_recv()


class WideGather:
    def __init__(self, copies, links, shard, own, other, other_there):
        n, y, c = links, links.y, links.c
        self.copies = copies
        self.place = own.at[n.z, y, c]
        self.shard = shard
        self.far = [copies.remote(shard, self.place, n.far[r]) for r in range(1, 4)]
        mine, theirs = own.at[:, y, c], own.at[:, 1 - y, c]
        self.near = copies.remote(mine, mine, n.near)
        self.cross = [
            copies.remote(mine, other_there.at[:, y, c], n.x),
            copies.remote(theirs, other_there.at[:, 1 - y, c], n.x),
        ]
        self.core = [
            copies.remote(part, part, n.core)
            for part in (mine, theirs, other.at[:, y, c], other.at[:, 1 - y, c])
        ]

    def begin(self):
        self.copies.go(*self.far)
        self.own = self.copies.keep(self.shard, self.place)

    def one(self):
        arrived(*self.far)
        self.copies.finish(self.own)
        self.copies.go(self.near, self.cross[0], self.core[0])

    def two(self):
        arrived(self.near)
        self.copies.go(self.cross[1], self.core[1])

    def three(self):
        arrived(self.cross[0])
        self.copies.go(self.core[2])

    def four(self):
        arrived(self.cross[1])
        self.copies.go(self.core[3])

    def end(self):
        arrived(*self.core)


class TallGather:
    def __init__(self, copies, links, shard, own, other):
        n, y, c = links, links.y, links.c
        self.copies = copies
        self.shard, self.place = shard, own.at[n.z, y, c]
        received = other.at[n.z, y, c]
        self.cross = copies.remote(shard, received, n.x)
        self.far_own = [copies.remote(shard, self.place, n.far[r]) for r in range(1, 4)]
        self.far_other = [copies.remote(received, received, n.far[r]) for r in range(1, 4)]
        mine = [own.at[:, y, c], other.at[:, y, c]]
        theirs = [own.at[:, 1 - y, c], other.at[:, 1 - y, c]]
        self.near = [copies.remote(part, part, n.near) for part in mine]
        self.core = [copies.remote(part, part, n.core) for part in mine + theirs]

    def begin(self):
        self.copies.go(self.cross)
        self.own = self.copies.keep(self.shard, self.place)

    def zero(self):
        self.copies.go(*self.far_own)
        arrived(self.cross)
        self.copies.go(*self.far_other)

    def one(self):
        arrived(*self.far_own)
        self.copies.finish(self.own)
        self.copies.go(self.near[0], self.core[0])

    def two(self):
        arrived(*self.far_other)
        self.copies.go(self.near[1], self.core[1])

    def three(self):
        arrived(self.near[0])
        self.copies.go(self.core[2])

    def four(self):
        arrived(self.near[1])
        self.copies.go(self.core[3])

    def end(self):
        arrived(*self.core)


class Exchange:
    def __init__(self, copies, links, gates, first, bufs, forward):
        n = links
        self.copies, self.gates, self.first, self.bufs = copies, gates, first, bufs
        half = PAIRS // 2
        step = 2 if forward else -2
        own, a, j, b, j2, r1, r2, far = bufs

        def both(src, dst, partner):
            return [copies.remote(s, d, partner) for s, d in zip(src, dst)]

        def halves(state):
            return [
                state[0].at[pl.ds(n.c * half, half)],
                state[1].at[pl.ds(n.c * half, half)],
            ]

        self.rounds = [
            both(own, a, n.x),
            both(j, b, n.core),
            both(halves(j2), r1, n.shifted(step)) + both(halves(j2), r2, n.shifted(2 * step)),
            both(halves(far), halves(far), n.core),
        ]
        self.halves = halves
        self.total = None

    def gate(self, i):
        return self.gates[self.first + i]

    def begin(self):
        self.copies.go(*self.rounds[0])

    def one(self):
        own, a, j, b, j2, r1, r2, far = self.bufs
        arrived(*self.rounds[0])
        for s, d, t in zip(own, a, j):
            t[...] = (
                s[...].astype(F32) * self.gate(1) + d[...].astype(F32) * self.gate(2)
            ).astype(t.dtype)
        self.copies.go(*self.rounds[1])

    def two(self):
        own, a, j, b, j2, r1, r2, far = self.bufs
        arrived(*self.rounds[1])
        for s, d, t in zip(j, b, j2):
            t[...] = (
                s[...].astype(F32) * self.gate(4) + d[...].astype(F32) * self.gate(5)
            ).astype(t.dtype)
        self.copies.go(*self.rounds[2])

    def three(self):
        own, a, j, b, j2, r1, r2, far = self.bufs
        arrived(*self.rounds[2])
        for s, d, t in zip(r1, r2, self.halves(far)):
            t[...] = (s[...].astype(F32) + d[...].astype(F32) * self.gate(6)).astype(t.dtype)
        self.copies.go(*self.rounds[3])

    def four(self, out):
        own, a, j, b, j2, r1, r2, far = self.bufs
        arrived(*self.rounds[3])
        for s, d, f, t in zip(a, b, far, out):
            t[...] = (
                s[...].astype(F32) * self.gate(0)
                + d[...].astype(F32) * self.gate(3)
                + f[...].astype(F32) * self.gate(7)
            ).astype(t.dtype)


def exchange_shapes():
    shapes = []
    for name in range(8):
        pairs = PAIRS // 2 if name in (5, 6) else PAIRS
        shapes += [pltpu.VMEM((pairs, FEATS, WIDE), BF), pltpu.VMEM((pairs, 8, FEATS), F32)]
    return shapes


def exchange_gates(ids, rows, forward):
    head, seq = lax.axis_index("head"), lax.axis_index("seq")
    n = lax.axis_size("seq")
    segments = 2 * n
    ends = ids.reshape(segments, rows)
    firsts, lasts = ends[:, 0], ends[:, rows - 1]
    step = 1 if forward else -1
    near_end, far_end = (lasts, firsts) if forward else (firsts, lasts)
    seg = 2 * seq + head
    base = 4 * (seq // 2)
    core = seq % 2
    late_head = (head == 1) if forward else (head == 0)
    late_core = (core == 1) if forward else (core == 0)
    pair_early, pair_late = (2 * seq, 2 * seq + 1) if forward else (2 * seq + 1, 2 * seq)
    early_end, late_end = (base + 1, base + 3) if forward else (base + 2, base)
    chip = seq // 2
    near_ok = (chip >= 1) if forward else (chip < n // 2 - 1)
    far_ok = (chip >= 2) if forward else (chip < n // 2 - 2)
    where = jnp.stack(
        [seg - step, pair_early, pair_late, early_end, late_end, late_end - 4 * step,
         late_end - 8 * step]
    )
    docs = near_end[jnp.clip(where, 0, segments - 1)]
    takes = far_end[seg]
    joined = docs[1] == docs[2]
    joined2 = docs[3] == docs[4]
    flags = [
        late_head & (docs[0] == takes),
        late_head | joined,
        (~late_head) | joined,
        late_core & (docs[3] == takes),
        late_core | joined2,
        (~late_core) | joined2,
        far_ok & (docs[5] == docs[6]),
        near_ok & (docs[5] == takes),
    ]
    return jnp.stack(flags).astype(F32)


def pair_lanes(pair, start=0):
    return pl.ds(pl.multiple_of(start + pair * WIDE, WIDE), WIDE)


def state_pair(pair, table, keys, value, last, wide_ref, thin_ref):
    rows = keys.shape[0]
    total = None
    for part in range(2):
        sel = selectors(table, 2 * pair + part)
        one, two = factors(keys, table, sel)
        phi = one * two * last
        new = mm(phi.astype(BF), keep(half_mask(rows, part), value), TN)
        total = new if total is None else total + new
        thin_ref[pair, part : part + 1, :] = jnp.sum(phi, axis=0, keepdims=True)
    thin_ref[pair, 2:, :] = jnp.zeros((6, FEATS), F32)
    wide_ref[pair] = total.astype(BF)


def local_pair(pair, qkv, num_ref, den_ref, mask_ref):
    rows = qkv.shape[0]
    qk = HEADS * QD
    for i in range(rows // TILE):
        here = slice(i * TILE, (i + 1) * TILE)
        num = jnp.zeros((TILE, WIDE), F32)
        dens = []
        for part in range(2):
            head = 2 * pair + part
            query = keep(head_mask(TILE, head), qkv[here, :qk] * (QD**-0.5))
            den = jnp.zeros((TILE, 1), F32)
            for j in range(i + 1):
                there = slice(j * TILE, (j + 1) * TILE)
                s = mm(query, qkv[there, qk : 2 * qk], NT)
                w = (1.0 + s + 0.5 * s * s) * mask_ref[here, there]
                den = den + jnp.sum(w, axis=1, keepdims=True)
                value = qkv[there, pair_lanes(pair, 2 * qk)]
                num = num + mm(w.astype(BF), keep(half_mask(TILE, part), value), NN)
            dens.append(den)
        num_ref[here, pair_lanes(pair)] = num
        den_ref[here, pair_lanes(pair)] = jnp.where(half_mask(TILE, 0), dens[0], dens[1])


def finish_pair(pair, table, query, first, num_ref, den_ref, wide_ref, thin_ref, out_ref):
    rows = query.shape[0]
    lanes = pair_lanes(pair)
    num, den = num_ref[:, lanes], den_ref[:, lanes]
    for part in range(2):
        sel = selectors(table, 2 * pair + part)
        one, two = factors(query, table, sel)
        phi = one * two * (table[4:5, :] * first)
        mask = half_mask(rows, part)
        num = num + jnp.where(mask, mm(phi.astype(BF), wide_ref[pair], NN), 0.0)
        more = jnp.sum(phi * thin_ref[pair, part : part + 1, :], axis=1, keepdims=True)
        den = den + jnp.where(mask, more, 0.0)
    rden = 1.0 / den
    den_ref[:, lanes] = rden
    out_ref[:, lanes] = (num * rden).astype(BF)


def each_pair(low, high, step):
    def one(pair, carry):
        step(pair)
        return carry

    lax.fori_loop(low, high, one, 0)


WIDE_COPIES, TALL_COPIES, EXCHANGE_COPIES = 10, 15, 10
FWD_COPIES = 5 * WIDE_COPIES + TALL_COPIES + EXCHANGE_COPIES
FWD_LOCALS = 20


def forward_kernel(
    x_ref, qs_ref, os_ref, gs_ref, us_ref, ds_ref, row_ids_ref, col_ids_ref, first_ref, last_ref,
    table_ref, gates_ref,
    g_own, g_other, u_own, u_other, d_own, d_other, wq_out, wo_out, qkv_out, att_out, rden_out,
    res_out, n2_out, wide_out, thin_out, gain_out,
    wq, wo, normed, qkv, num, den, mask, att, res, n2, wide, thin, gain, *rest,
):
    bufs, (send, recv, local) = rest[:16], rest[16:]
    states = [(bufs[2 * i], bufs[2 * i + 1]) for i in range(8)]
    n = Links()
    copies = Copies(send, recv, local)
    rows, width = x_ref.shape
    qk, hv = HEADS * QD, HEADS * VD
    cut = 7 * 128
    full = wq.shape[-1]

    def side(ref, head, lo=None, hi=None):
        return ref.at[head] if lo is None else ref.at[head, :, :, :, :, pl.ds(lo, hi - lo)]

    q_parts = []
    for lo, hi in ((0, cut), (cut, full)):
        shard = qs_ref.at[:, pl.ds(lo, hi - lo)]
        own, other = side(wq, n.head, lo, hi), side(wq, 1 - n.head, lo, hi)
        q_parts.append(WideGather(copies, n, shard, own, other, own))
    own, other = side(wo, n.head), side(wo, 1 - n.head)
    outs = WideGather(copies, n, os_ref, own, other, own)
    gates = WideGather(copies, n, gs_ref, g_own, g_other, g_other)
    ups = WideGather(copies, n, us_ref, u_own, u_other, u_other)
    downs = TallGather(copies, n, ds_ref, d_own, d_other)
    swap = Exchange(copies, n, gates_ref, 0, states, True)

    n.greet()
    for part in q_parts:
        part.begin()
    outs.begin()
    gates.begin()
    ups.begin()
    downs.begin()

    table = table_ref[...]
    x = x_ref[...].astype(F32)
    scaled = x * lax.rsqrt(jnp.mean(x * x, axis=-1, keepdims=True) + EPSILON)
    visible_tile(mask, row_ids_ref, col_ids_ref, rows)
    for part in q_parts:
        part.one()
    outs.one()
    for part in q_parts:
        part.two()
        part.three()
    outs.two()
    outs.three()
    for part in q_parts:
        part.four()
    downs.zero()
    for part in q_parts:
        part.end()
    outs.four()
    gates.one()

    pick_gain = (
        lax.broadcasted_iota(jnp.int32, (8, GAIN_COLS), 0)
        == lax.broadcasted_iota(jnp.int32, (8, GAIN_COLS), 1)
    ).astype(F32).astype(BF)
    gain[...] = mm(pick_gain, wq[..., full - GAIN_COLS :].reshape(width, GAIN_COLS), NT)
    normed[...] = (scaled * gain[0:1, :]).astype(BF)
    h1 = normed[...]
    for lo in range(0, 2 * qk + hv, 256):
        weight = wq[..., lo : lo + 256].reshape(width, 256)
        qkv[:, lo : lo + 256] = mm(h1, weight, NN).astype(BF)
    copies.keep(qkv, qkv_out)
    copies.keep(wq, wq_out)
    copies.keep(gain, gain_out)

    def do_state(pair):
        state_pair(
            pair, table, qkv[:, qk : 2 * qk], qkv[:, pair_lanes(pair, 2 * qk)], last_ref[...],
            states[0][0], states[0][1],
        )

    def do_local(pair):
        local_pair(pair, qkv, num, den, mask)

    each_pair(0, PAIRS, do_state)
    swap.begin()
    outs.end()
    copies.keep(wo, wo_out)
    each_pair(0, 3, do_local)
    swap.one()
    gates.two()
    ups.one()
    each_pair(3, 5, do_local)
    swap.two()
    downs.one()
    gates.three()
    each_pair(5, PAIRS, do_local)
    swap.three()
    ups.two()
    downs.two()
    swap.four((wide, thin))
    copies.keep(wide, wide_out)
    copies.keep(thin, thin_out)

    def do_finish(pair):
        finish_pair(
            pair, table, qkv[:, :qk], first_ref[...], num, den, wide, thin, att
        )

    each_pair(0, PAIRS, do_finish)
    gates.four()
    downs.three()
    copies.keep(att, att_out)
    copies.keep(den, rden_out)
    o = att[...]
    for lo in range(0, width, 256):
        weight = wo[..., lo : lo + 256].reshape(hv, 256)
        res[:, lo : lo + 256] = x_ref[:, lo : lo + 256].astype(F32) + mm(o, weight, NN)
    copies.keep(res, res_out)
    y1 = res[...]
    n2[...] = (
        y1 * lax.rsqrt(jnp.mean(y1 * y1, axis=-1, keepdims=True) + EPSILON) * gain[1:2, :]
    ).astype(BF)
    copies.keep(n2, n2_out)
    downs.four()
    ups.three()
    gates.end()
    downs.end()
    ups.four()
    ups.end()
    copies.drain()


def forward(x, q_shard, o_shard, ffn, row_ids, col_ids, first, last, table, gates):
    rows, width = x.shape
    qk, hv = HEADS * QD, HEADS * VD
    full = q_shard.shape[-1]
    small, fine, ff = q_shard.shape[0], ffn[0].shape[0], ffn[0].shape[1]
    half = jax.ShapeDtypeStruct((4, 2, 2, fine, ff), BF)
    wq_shape, wo_shape = (2, 4, 2, 2, small, full), (2, 4, 2, 2, small, width)

    def like(shape, dtype):
        return jax.ShapeDtypeStruct(shape, dtype)

    out_shape = [half] * 6 + [
        like(wq_shape, BF), like(wo_shape, BF), like((rows, 2 * qk + hv), BF),
        like((rows, hv), BF), like((rows, hv), F32), like((rows, width), F32),
        like((rows, width), BF), STATE_SHAPES[0], STATE_SHAPES[1], like((8, width), F32),
    ]
    scratch = [
        pltpu.VMEM(wq_shape, BF), pltpu.VMEM(wo_shape, BF), pltpu.VMEM((rows, width), BF),
        pltpu.VMEM((rows, 2 * qk + hv), BF), pltpu.VMEM((rows, hv), F32),
        pltpu.VMEM((rows, hv), F32), pltpu.VMEM((rows, rows), F32), pltpu.VMEM((rows, hv), BF),
        pltpu.VMEM((rows, width), F32), pltpu.VMEM((rows, width), BF),
        pltpu.VMEM((PAIRS, FEATS, WIDE), BF), pltpu.VMEM((PAIRS, 8, FEATS), F32),
        pltpu.VMEM((8, width), F32),
    ] + exchange_shapes() + [
        pltpu.SemaphoreType.DMA((FWD_COPIES,)), pltpu.SemaphoreType.DMA((FWD_COPIES,)),
        pltpu.SemaphoreType.DMA((FWD_LOCALS,)),
    ]
    vmem = pl.BlockSpec(memory_space=pltpu.VMEM)
    return pl.pallas_call(
        forward_kernel,
        out_shape=out_shape,
        in_specs=[vmem] * 11 + [pl.BlockSpec(memory_space=pltpu.SMEM)],
        out_specs=[pl.BlockSpec(memory_space=pl.ANY)] * len(out_shape),
        scratch_shapes=scratch,
        compiler_params=pltpu.CompilerParams(
            collective_id=1, has_side_effects=True, vmem_limit_bytes=56 << 20
        ),
        cost_estimate=pl.CostEstimate(flops=8 << 30, bytes_accessed=64 << 20, transcendentals=0),
        name="forward",
    )(x, q_shard, o_shard, *ffn, row_ids, col_ids, first, last, table, gates)


def as_f32(ref, index):
    return ref[index].astype(F32)


class WideScatter:
    REMOTE, LOCAL = 7, 3

    def __init__(self, copies, links, own, other, bufs, out):
        n, y, c = links, links.y, links.c
        self.n, self.copies, self.out = n, copies, out
        a_own, a_oth, c_own, c_oth, xx, yy, zz, done = bufs
        self.bufs = bufs
        self.own_part, self.oth_part = own.at[:, :, c], other.at[:, :, c]
        self.core = [
            copies.remote(other.at[:, :, 1 - c], c_oth, n.core),
            copies.remote(own.at[:, :, 1 - c], c_own, n.core),
        ]
        self.cross = copies.remote(a_oth, xx, n.x)
        self.near = copies.remote(a_own.at[:, 1 - y], yy, n.near)
        self.far = [
            copies.remote(a_own.at[n.z ^ r, y], zz.at[r - 1], n.far[r]) for r in range(1, 4)
        ]

    def begin(self):
        a_own, a_oth = self.bufs[:2]
        self.copies.go(*self.core)
        self.loads = [
            self.copies.keep(self.oth_part, a_oth), self.copies.keep(self.own_part, a_own)
        ]

    def loaded(self, i):
        self.copies.finish(self.loads[i])

    def one(self):
        a_own, a_oth, c_own, c_oth, xx, yy, zz, done = self.bufs
        self.loaded(0)
        arrived(self.core[0])

        def add(i, carry):
            for at in ((i, 0), (i, 1)):
                a_oth[at] = (as_f32(a_oth, at) + as_f32(c_oth, at)).astype(BF)
            return carry

        lax.fori_loop(0, 4, add, 0)
        self.copies.go(self.cross)

    def two(self):
        a_own, a_oth, c_own, c_oth, xx, yy, zz, done = self.bufs
        self.loaded(1)
        arrived(self.core[1], self.cross)

        def add(i, carry):
            for at in ((i, 0), (i, 1)):
                total = as_f32(a_own, at) + as_f32(c_own, at) + as_f32(xx, at)
                a_own[at] = total.astype(BF)
            return carry

        lax.fori_loop(0, 4, add, 0)
        self.copies.go(self.near)

    def three(self):
        a_own, a_oth, c_own, c_oth, xx, yy, zz, done = self.bufs
        arrived(self.near)

        def add(i, carry):
            at = (i, self.n.y)
            a_own[at] = (as_f32(a_own, at) + as_f32(yy, i)).astype(BF)
            return carry

        lax.fori_loop(0, 4, add, 0)
        self.copies.go(*self.far)

    def four(self):
        a_own, a_oth, c_own, c_oth, xx, yy, zz, done = self.bufs
        arrived(*self.far)
        total = as_f32(a_own, (self.n.z, self.n.y))
        for r in range(3):
            total = total + as_f32(zz, r)
        done[...] = total
        self.copies.keep(done, self.out)

    @staticmethod
    def shapes(rows, cols):
        part = [pltpu.VMEM((4, 2, rows, cols), BF)]
        return part * 5 + [
            pltpu.VMEM((4, rows, cols), BF), pltpu.VMEM((3, rows, cols), BF),
            pltpu.VMEM((rows, cols), F32),
        ]


class TallScatter:
    REMOTE, LOCAL = 11, 3

    def __init__(self, copies, links, own, other, bufs, out):
        n, y, c = links, links.y, links.c
        self.n, self.copies, self.out, self.bufs = n, copies, out, bufs
        a, cc, yy, zz, xx, done = bufs
        both = (own, other)
        self.parts = [ref.at[:, :, c] for ref in both]
        self.core = [
            copies.remote(both[i].at[:, :, 1 - c], cc.at[i], n.core) for i in range(2)
        ]
        self.near = [copies.remote(a.at[i, :, 1 - y], yy.at[i], n.near) for i in range(2)]
        self.far = [
            copies.remote(a.at[i, n.z ^ r, y], zz.at[i, r - 1], n.far[r])
            for i in range(2)
            for r in range(1, 4)
        ]
        self.cross = copies.remote(a.at[1, n.z, y], xx, n.x)

    def begin(self):
        self.copies.go(*self.core)
        self.loads = [self.copies.keep(self.parts[i], self.bufs[0].at[i]) for i in range(2)]

    def one(self):
        a, cc, yy, zz, xx, done = self.bufs
        for i in range(2):
            self.copies.finish(self.loads[i])
            arrived(self.core[i])

            def add(k, carry, i=i):
                for at in ((i, k, 0), (i, k, 1)):
                    a[at] = (as_f32(a, at) + as_f32(cc, at)).astype(BF)
                return carry

            lax.fori_loop(0, 4, add, 0)
            self.copies.go(self.near[i])

    def two(self):
        a, cc, yy, zz, xx, done = self.bufs
        for i in range(2):
            arrived(self.near[i])

            def add(k, carry, i=i):
                at = (i, k, self.n.y)
                a[at] = (as_f32(a, at) + as_f32(yy, (i, k))).astype(BF)
                return carry

            lax.fori_loop(0, 4, add, 0)
            self.copies.go(*self.far[3 * i : 3 * i + 3])

    def total(self, i):
        a, cc, yy, zz, xx, done = self.bufs
        total = as_f32(a, (i, self.n.z, self.n.y))
        for r in range(3):
            total = total + as_f32(zz, (i, r))
        return total

    def three(self):
        a, cc, yy, zz, xx, done = self.bufs
        arrived(*self.far)
        a[1, self.n.z, self.n.y] = self.total(1).astype(BF)
        self.copies.go(self.cross)

    def four(self):
        a, cc, yy, zz, xx, done = self.bufs
        arrived(self.cross)
        done[...] = self.total(0) + xx[...].astype(F32)
        self.copies.keep(done, self.out)

    @staticmethod
    def shapes(rows, cols):
        return [
            pltpu.VMEM((2, 4, 2, rows, cols), BF), pltpu.VMEM((2, 4, 2, rows, cols), BF),
            pltpu.VMEM((2, 4, rows, cols), BF), pltpu.VMEM((2, 3, rows, cols), BF),
            pltpu.VMEM((rows, cols), BF), pltpu.VMEM((rows, cols), F32),
        ]


def prepare_pair(pair, grad, out, rden):
    rows = grad.shape[0]
    lanes = pair_lanes(pair)
    g = grad[:, lanes].astype(F32)
    r = rden[:, lanes]
    prod = g * out[:, lanes].astype(F32) * r
    low = half_mask(rows, 0)
    first = jnp.sum(jnp.where(low, prod, 0.0), axis=1, keepdims=True)
    second = jnp.sum(jnp.where(low, 0.0, prod), axis=1, keepdims=True)
    grad[:, lanes] = (g * r).astype(BF)
    rden[:, lanes] = jnp.where(low, first, second)


def delta_of(pair, part, deltas, where=slice(None)):
    return deltas[where, pair_lanes(pair)][:, part * VD : part * VD + 1]


def grad_state_pair(pair, table, query, first, dnum_ref, delta_ref, wide_ref, thin_ref):
    rows = query.shape[0]
    dnum = dnum_ref[:, pair_lanes(pair)]
    total = None
    for part in range(2):
        sel = selectors(table, 2 * pair + part)
        one, two = factors(query, table, sel)
        phi = one * two * (table[4:5, :] * first)
        new = mm(phi.astype(BF), keep(half_mask(rows, part), dnum), TN)
        total = new if total is None else total + new
        delta = delta_of(pair, part, delta_ref)
        thin_ref[pair, part : part + 1, :] = -jnp.sum(phi * delta, axis=0, keepdims=True)
    thin_ref[pair, 2:, :] = jnp.zeros((6, FEATS), F32)
    wide_ref[pair] = total.astype(BF)


def local_grad_pair(
    pair, table, qkv, first, dnum_ref, delta_ref, wide_ref, thin_ref, dq_acc, dk_acc, dv_ref,
    mask_ref,
):
    qk = HEADS * QD
    query, keys = qkv[:, :qk], qkv[:, qk : 2 * qk]
    rows = query.shape[0]
    tiles = rows // TILE
    scale = QD**-0.5
    lanes = pair_lanes(pair)
    values = qkv[:, pair_lanes(pair, 2 * qk)]
    dnum = dnum_ref[:, lanes]
    dv = [jnp.zeros((TILE, WIDE), F32) for _ in range(tiles)]
    for part in range(2):
        head = 2 * pair + part
        at_head = head_mask(rows, head)
        q_head = keep(at_head, query * scale)
        k_head = keep(at_head, keys * scale)
        d_head = keep(half_mask(rows, part), dnum)
        delta = delta_of(pair, part, delta_ref)
        for i in range(tiles):
            here = slice(i * TILE, (i + 1) * TILE)
            dq = dq_acc[here, :]
            for j in range(i + 1):
                there = slice(j * TILE, (j + 1) * TILE)
                s = mm(q_head[here], keys[there], NT)
                mask = mask_ref[here, there]
                w = ((1.0 + s + 0.5 * s * s) * mask).astype(BF)
                dp = mm(d_head[here], values[there], NT)
                ds = ((dp - delta[here]) * ((1.0 + s) * mask)).astype(BF)
                dq = dq + mm(ds, k_head[there], NN)
                dk_acc[there, :] += mm(ds, q_head[here], TN)
                dv[j] = dv[j] + mm(w, d_head[here], TN)
            dq_acc[here, :] = dq
        sel = selectors(table, head)
        one, two = factors(query, table, sel)
        dphi = mm(d_head, wide_ref[pair], NT) - delta * thin_ref[pair, part : part + 1, :]
        dphi = dphi * (table[4:5, :] * first)
        dq_acc[...] += mm((dphi * two).astype(BF), sel[0], NT) + mm(
            (dphi * one).astype(BF), sel[1], NT
        )
    for j in range(tiles):
        dv_ref[j * TILE : (j + 1) * TILE, lanes] = dv[j]


def finish_grad_pair(pair, table, qkv, last, wide_ref, thin_ref, dk_acc, dv_ref, grads):
    qk = HEADS * QD
    keys = qkv[:, qk : 2 * qk]
    rows = keys.shape[0]
    lanes = pair_lanes(pair)
    values = qkv[:, pair_lanes(pair, 2 * qk)]
    dv = dv_ref[:, lanes]
    for part in range(2):
        sel = selectors(table, 2 * pair + part)
        one, two = factors(keys, table, sel)
        mask = half_mask(rows, part)
        phi = one * two * last
        dv = dv + jnp.where(mask, mm(phi.astype(BF), wide_ref[pair], NN), 0.0)
        dphi = mm(keep(mask, values), wide_ref[pair], NT) + thin_ref[pair, part : part + 1, :]
        dphi = dphi * last
        dk_acc[...] += mm((dphi * two).astype(BF), sel[0], NT) + mm(
            (dphi * one).astype(BF), sel[1], NT
        )
    grads[:, pair_lanes(pair, 2 * qk)] = dv.astype(BF)


BWD_COPIES = 5 * WideScatter.REMOTE + TallScatter.REMOTE + EXCHANGE_COPIES
BWD_LOCALS = 6 * 3 + 12


def backward_kernel(
    gg_own, gg_oth, gu_own, gu_oth, gd_own, gd_oth, go_ref, grad_in, att_in, rden_in, qkv_in,
    wide_in, thin_in, wq_in, x_in, middle_in, gain_ref, dgain_ref, row_ids_ref, col_ids_ref,
    first_ref, last_ref, table_ref, gates_ref,
    dg_out, du_out, dd_out, do_out, dq_out, din_out,
    *rest,
):
    rest = list(rest)

    def take(count):
        got = rest[:count]
        del rest[:count]
        return got

    g_bufs, u_bufs, d_bufs, o_bufs = take(8), take(8), take(6), take(8)
    q_bufs = [take(8), take(8)]
    bufs = take(16)
    states = [(bufs[2 * i], bufs[2 * i + 1]) for i in range(8)]
    (
        grad, out, rden, mask, dq_acc, dk_acc, dv, before_wide, before_thin, wqg, qkv, grads,
        wide, thin, dgain, send, recv, local,
    ) = rest
    n = Links()
    copies = Copies(send, recv, local)
    rows, width = out.shape
    qk, hv = HEADS * QD, HEADS * VD
    table = table_ref[...]
    cut, full = 7 * 128, wqg.shape[-1]

    gates = WideScatter(copies, n, gg_own, gg_oth, g_bufs, dg_out)
    ups = WideScatter(copies, n, gu_own, gu_oth, u_bufs, du_out)
    downs = TallScatter(copies, n, gd_own, gd_oth, d_bufs, dd_out)
    outs = WideScatter(copies, n, go_ref.at[n.head], go_ref.at[1 - n.head], o_bufs, do_out)
    qs = []
    for bufs_of, (lo, hi) in zip(q_bufs, ((0, cut), (cut, full))):
        cols = pl.ds(lo, hi - lo)
        own = wqg.at[n.head, :, :, :, :, cols]
        oth = wqg.at[1 - n.head, :, :, :, :, cols]
        qs.append(WideScatter(copies, n, own, oth, bufs_of, dq_out.at[:, cols]))
    swap = Exchange(copies, n, gates_ref, 0, states, False)

    def fetch(*pairs):
        loads = [copies.keep(src, dst) for src, dst in pairs]

        def ready():
            for load in loads:
                copies.finish(load)

        return ready

    n.greet()

    ready = fetch(
        (grad_in, grad), (att_in, out), (rden_in, rden), (qkv_in, qkv),
        (wide_in, before_wide), (thin_in, before_thin),
    )
    gates.begin()
    ups.begin()
    downs.begin()
    outs.begin()
    visible_tile(mask, row_ids_ref, col_ids_ref, rows)
    dq_acc[...] = jnp.zeros_like(dq_acc)
    dk_acc[...] = jnp.zeros_like(dk_acc)
    ready()
    each_pair(0, PAIRS, lambda pair: prepare_pair(pair, grad, out, rden))
    ready_x = fetch((x_in, out), (wq_in, wqg))
    gates.one()

    def do_state(pair):
        grad_state_pair(
            pair, table, qkv[:, :qk], first_ref[...], grad, rden, states[0][0], states[0][1]
        )

    def do_local(pair):
        local_grad_pair(
            pair, table, qkv, first_ref[...], grad, rden, before_wide, before_thin, dq_acc,
            dk_acc, dv, mask,
        )

    def do_finish(pair):
        finish_grad_pair(pair, table, qkv, last_ref[...], wide, thin, dk_acc, dv, grads)

    each_pair(0, PAIRS, do_state)
    swap.begin()
    downs.one()
    ups.one()
    outs.one()
    each_pair(0, 2, do_local)
    swap.one()
    each_pair(2, 4, do_local)
    swap.two()
    downs.two()
    each_pair(4, 6, do_local)
    swap.three()
    gates.two()
    each_pair(6, PAIRS, do_local)
    ready_middle = fetch((middle_in, rden))
    grads[:, :qk] = dq_acc[...].astype(BF)
    swap.four((wide, thin))
    each_pair(0, PAIRS, do_finish)
    grads[:, qk : 2 * qk] = dk_acc[...].astype(BF)
    gates.three()
    downs.three()

    ready_x()
    ready_middle()
    wq, x_buf, middle, normed = wqg, out, rden, grad
    x = x_buf[...].astype(F32)
    scale = lax.rsqrt(jnp.mean(x * x, axis=-1, keepdims=True) + EPSILON)
    normed[...] = (x * scale * gain_ref[0:1, :]).astype(BF)
    dh = jnp.zeros((rows, width), F32)
    for lo in range(0, 2 * qk + hv, 512):
        weight = wq[..., lo : lo + 512].reshape(width, 512)
        dh = dh + mm(grads[:, lo : lo + 512], weight, NT)
    hat = x * scale
    dgain[...] = jnp.zeros_like(dgain)
    dgain[0:1, :] = jnp.sum(dh * hat, axis=0, keepdims=True)
    dgain[1:2, :] = dgain_ref[...]
    dhat = dh * gain_ref[0:1, :]
    inner = jnp.mean(dhat * hat, axis=-1, keepdims=True)
    middle[...] = middle[...] + (dhat - hat * inner) * scale
    copies.keep(middle, din_out)
    h1 = normed[...]
    for lo in range(0, 2 * qk + hv, 256):
        part = mm(h1, grads[:, lo : lo + 256], TN).astype(BF)
        wqg[..., lo : lo + 256] = part.reshape(wqg.shape[:-1] + (256,))
    spread = (
        lax.broadcasted_iota(jnp.int32, (8, GAIN_COLS), 0)
        == lax.broadcasted_iota(jnp.int32, (8, GAIN_COLS), 1)
    ).astype(F32).astype(BF)
    gain_part = mm(dgain[...].astype(BF), spread, TN).astype(BF)
    wqg[..., full - GAIN_COLS :] = gain_part.reshape(wqg.shape[:-1] + (GAIN_COLS,))
    for q in qs:
        q.begin()
    ups.two()
    for q in qs:
        q.one()
    downs.four()
    gates.four()
    ups.three()
    outs.two()
    outs.three()
    for q in qs:
        q.two()
    ups.four()
    outs.four()
    for q in qs:
        q.three()
    for q in qs:
        q.four()
    copies.drain()


def backward(
    ffn_grads, out_grad, grad, att, rden, qkv, before, wq, x, middle, gain, dgain, row_ids,
    col_ids, first, last, table, gates,
):
    rows, width = x.shape
    qk, hv = HEADS * QD, HEADS * VD
    fine, ff = ffn_grads[0].shape[-2:]
    small, full = wq.shape[-2:]
    cut = 7 * 128

    def like(shape, dtype):
        return jax.ShapeDtypeStruct(shape, dtype)

    out_shape = [like((fine, ff), F32)] * 3 + [
        like((small, width), F32), like((small, full), F32), like((rows, width), F32)
    ]
    scratch = (
        WideScatter.shapes(fine, ff) * 2 + TallScatter.shapes(fine, ff)
        + WideScatter.shapes(small, width)
        + WideScatter.shapes(small, cut) + WideScatter.shapes(small, full - cut)
        + exchange_shapes()
    )
    scratch += [
        pltpu.VMEM((rows, hv), BF), pltpu.VMEM((rows, width), BF), pltpu.VMEM((rows, hv), F32),
        pltpu.VMEM((rows, rows), F32), pltpu.VMEM((rows, qk), F32), pltpu.VMEM((rows, qk), F32),
        pltpu.VMEM((rows, hv), F32), pltpu.VMEM((PAIRS, FEATS, WIDE), BF),
        pltpu.VMEM((PAIRS, 8, FEATS), F32),
        pltpu.VMEM((2, 4, 2, 2, small, full), BF), pltpu.VMEM((rows, 2 * qk + hv), BF),
        pltpu.VMEM((rows, 2 * qk + hv), BF),
        pltpu.VMEM((PAIRS, FEATS, WIDE), BF), pltpu.VMEM((PAIRS, 8, FEATS), F32),
        pltpu.VMEM((8, width), F32),
        pltpu.SemaphoreType.DMA((BWD_COPIES,)), pltpu.SemaphoreType.DMA((BWD_COPIES,)),
        pltpu.SemaphoreType.DMA((BWD_LOCALS,)),
    ]
    vmem = pl.BlockSpec(memory_space=pltpu.VMEM)
    anywhere = pl.BlockSpec(memory_space=pl.ANY)
    return pl.pallas_call(
        backward_kernel,
        out_shape=out_shape,
        in_specs=[anywhere] * 16 + [vmem] * 7 + [pl.BlockSpec(memory_space=pltpu.SMEM)],
        out_specs=[anywhere] * len(out_shape),
        scratch_shapes=scratch,
        compiler_params=pltpu.CompilerParams(
            collective_id=2, has_side_effects=True, vmem_limit_bytes=62 << 20
        ),
        cost_estimate=pl.CostEstimate(flops=16 << 30, bytes_accessed=64 << 20, transcendentals=0),
        name="backward",
    )(
        *ffn_grads, out_grad, grad, att, rden, qkv, *before, wq, x, middle, gain, dgain, row_ids,
        col_ids, first, last, table, gates,
    )


def rms_scale(values, gain):
    return values * lax.rsqrt(jnp.mean(values * values, axis=-1, keepdims=True) + EPSILON) * gain


def swish_mix(gate, up_proj):
    return jax.nn.silu(gate) * up_proj


def dot_nn(a, b):
    return jnp.dot(a, b, preferred_element_type=F32)


def dot_nt(a, b):
    return lax.dot_general(a, b, (((1,), (1,)), ((), ())), preferred_element_type=F32)


def dot_tn(a, b):
    return lax.dot_general(a, b, (((0,), (0,)), ((), ())), preferred_element_type=F32)


def row_grads(left, right, by_head):
    head, core = lax.axis_index("head"), lax.axis_index("seq") % 2
    tokens = left.shape[0]
    chips = lax.axis_size("seq") // 2
    heads = 2 if by_head else 1
    rows = left.shape[1] // (heads * chips * 2)
    split = left.reshape(tokens, heads, chips, 2, rows)
    out = []
    for rel in range(heads):
        plane = pick(split, head ^ rel, 1) if by_head else split[:, 0]
        out.append([pick(plane, core ^ r, 2).reshape(tokens, chips * rows) for r in range(2)])
    if by_head:
        return [[dot_tn(part, right).astype(BF) for part in parts] for parts in out]
    return [[dot_tn(part, r).astype(BF) for part in out[0]] for r in right]


def plain_forward(
    inputs, segment_ids, norm1_gain, w_query, w_key, w_value, w_out, norm2_gain, w_gate, w_up,
    w_down, row_ids, col_ids, first, last, table,
):
    head, seq = lax.axis_index("head"), lax.axis_index("seq")
    n_seq = lax.axis_size("seq")
    rows, width = inputs.shape
    qk = HEADS * QD
    slot = head * n_seq + seq
    small = norm1_gain.shape[0]
    gains = jnp.zeros((2, width // small, small), F32)
    gains = lax.dynamic_update_slice(
        gains, jnp.stack([norm1_gain, norm2_gain]).astype(F32)[:, None, :], (0, slot, 0)
    ).reshape(2, width)
    gains = sum_everywhere(gains)
    gain_first, gain_second = gains[0], gains[1]

    qkv_full = gather_rows(jnp.concatenate([w_query, w_key, w_value], axis=1))
    out_full = gather_rows(w_out)
    gate_w = gather_halves(w_gate, False)
    up_w = gather_halves(w_up, False)
    down_w = gather_halves(w_down.T, True)

    normed_one = rms_scale(inputs, gain_first).astype(BF)
    qkv = dot_nn(normed_one, qkv_full).astype(BF)
    query, keys, values = qkv[:, :qk], qkv[:, qk : 2 * qk], qkv[:, 2 * qk :]
    vcols = HEADS * VD
    t_spec, q_spec = full_spec((8, FEATS)), full_spec((rows, qk))
    one_spec, row_spec = full_spec((rows, 1)), full_spec((1, rows))
    p_spec = pair_spec(rows)
    f32_like = jax.ShapeDtypeStruct((rows, vcols), F32)
    bf_like = jax.ShapeDtypeStruct((rows, vcols), BF)
    state = run(
        state_kernel,
        [t_spec, q_spec, p_spec, one_spec],
        state_specs(),
        STATE_SHAPES,
        (table, keys, values, last),
        flops=8 * rows * qk * FEATS * HEADS,
    )
    num, den = run(
        local_kernel,
        [q_spec, q_spec, p_spec, one_spec, row_spec],
        [p_spec, p_spec],
        [f32_like, f32_like],
        (query, keys, values, row_ids, col_ids),
        [pltpu.VMEM((rows, rows), F32)],
        flops=8 * rows * rows * qk * HEADS,
    )
    before = exchange(*state, segment_ids, rows, True)
    attended, rden = run(
        finish_kernel,
        [t_spec, q_spec, p_spec, p_spec, one_spec] + state_specs(),
        [p_spec, p_spec],
        [bf_like, f32_like],
        (table, query, num, den, first, *before),
        flops=8 * rows * qk * FEATS * HEADS,
    )
    residual = inputs + dot_nn(attended, out_full)
    normed_two = rms_scale(residual, gain_second).astype(BF)

    return (
        gate_w, up_w, down_w, qkv_full, out_full, gain_first, gain_second, normed_one,
        query, keys, values, attended, rden, residual, normed_two, before,
    )


def body(
    layer_input,
    segment_ids,
    norm1_gain,
    w_query,
    w_key,
    w_value,
    w_out,
    norm2_gain,
    w_gate,
    w_up,
    w_down,
    output_grad,
):
    rows = layer_input.shape[1]
    head, seq = lax.axis_index("head"), lax.axis_index("seq")
    n_seq = lax.axis_size("seq")
    qk = HEADS * QD
    inputs = layer_input[0].astype(F32)
    width = inputs.shape[1]

    segment = 2 * seq + head
    ids = lax.dynamic_slice_in_dim(segment_ids, segment * rows, rows)
    row_ids, col_ids = ids[:, None], ids[None, :]
    first = (row_ids == ids[0]).astype(F32)
    last = (row_ids == ids[rows - 1]).astype(F32)
    table = jnp.asarray(feature_table())
    vcols = HEADS * VD
    t_spec, q_spec = full_spec((8, FEATS)), full_spec((rows, qk))
    one_spec, row_spec = full_spec((rows, 1)), full_spec((1, rows))
    p_spec = pair_spec(rows)
    f32_like = jax.ShapeDtypeStruct((rows, vcols), F32)
    bf_like = jax.ShapeDtypeStruct((rows, vcols), BF)
    slot = head * n_seq + seq
    small = norm1_gain.shape[0]

    if n_seq == 16:
        gain_cols = jnp.stack([norm1_gain, norm2_gain], axis=1)
        gain_cols = jnp.pad(gain_cols, ((0, 0), (0, GAIN_COLS - 2)))
        (
            g_own, g_other, u_own, u_other, d_own, d_other, wq, wo, qkv, attended, rden,
            residual, normed_two, wide, thin, gains,
        ) = forward(
            layer_input[0],
            jnp.concatenate([w_query, w_key, w_value, gain_cols], axis=1),
            w_out,
            [w_gate, w_up, w_down.T],
            row_ids, col_ids, first, last, table, exchange_gates(segment_ids, rows, True),
        )

        def flat(weight):
            return weight.reshape(-1, weight.shape[-1])

        gate_w, up_w, down_w = (
            [flat(g_own), flat(g_other)], [flat(u_own), flat(u_other)], [flat(d_own), flat(d_other)],
        )
        qkv_full, out_full = flat(wq)[:, : 2 * qk + vcols], flat(wo)
        gain_first, gain_second = gains[0], gains[1]
        normed_one = rms_scale(inputs, gain_first).astype(BF)
        query, keys, values = qkv[:, :qk], qkv[:, qk : 2 * qk], qkv[:, 2 * qk :]
        before = (wide, thin)
    else:
        (
            gate_w, up_w, down_w, qkv_full, out_full, gain_first, gain_second, normed_one,
            query, keys, values, attended, rden, residual, normed_two, before,
        ) = plain_forward(
            inputs, segment_ids, norm1_gain, w_query, w_key, w_value, w_out, norm2_gain, w_gate,
            w_up, w_down, row_ids, col_ids, first, last, table,
        )

    grad_output = output_grad[0]
    outcome = residual
    grad_normed_two = None
    hiddens, grad_gates, grad_ups = [], [], []
    for w_g, w_u, w_d in zip(gate_w, up_w, down_w):
        gate = dot_nn(normed_two, w_g)
        up_proj = dot_nn(normed_two, w_u)
        grad_hidden = dot_nn(grad_output, w_d)
        hidden, mix_pull = jax.vjp(swish_mix, gate, up_proj)
        grad_gate, grad_up = mix_pull(grad_hidden)
        hiddens.append(hidden.astype(BF))
        grad_gates.append(grad_gate.astype(BF))
        grad_ups.append(grad_up.astype(BF))
        outcome = outcome + dot_nt(hiddens[-1], w_d)
        more = dot_nt(grad_gates[-1], w_g) + dot_nt(grad_ups[-1], w_u)
        grad_normed_two = more if grad_normed_two is None else grad_normed_two + more
    outcome = outcome.astype(BF)
    _, norm_pull = jax.vjp(rms_scale, residual, gain_second)
    grad_resid_two, grad_gain_two = norm_pull(grad_normed_two)
    grad_middle = grad_output.astype(F32) + grad_resid_two
    grad_middle_low = grad_middle.astype(BF)
    grad_attended = dot_nt(grad_middle_low, out_full).astype(BF)

    if n_seq == 16:
        chips = (4, 2, 2)

        def blocks(left, right):
            return dot_tn(left, right).astype(BF).reshape(chips + (-1, right.shape[1]))

        ffn_grads = (
            [blocks(normed_two, part) for part in grad_gates]
            + [blocks(normed_two, part) for part in grad_ups]
            + [blocks(grad_output, part) for part in hiddens]
        )
        out_grad = dot_tn(attended, grad_middle_low).astype(BF).reshape((2,) + chips + (-1, width))
        d_gate, d_up, d_down, d_out, d_qkv, grad_layer = backward(
            ffn_grads, out_grad, grad_attended, attended, rden, qkv, before, wq, layer_input[0],
            grad_middle, gains, grad_gain_two[None], row_ids, col_ids, first, last, table,
            exchange_gates(segment_ids, rows, False),
        )
        gain_at = 2 * qk + vcols
        return (
            outcome[None],
            grad_layer[None],
            d_qkv[:, gain_at],
            d_qkv[:, :qk],
            d_qkv[:, qk : 2 * qk],
            d_qkv[:, 2 * qk : gain_at],
            d_out,
            d_qkv[:, gain_at + 1],
            d_gate,
            d_up,
            d_down.T,
        )

    d_gate = scatter(row_grads(normed_two, grad_gates, False), True)
    d_up = scatter(row_grads(normed_two, grad_ups, False), True)
    d_down = scatter(row_grads(grad_output, hiddens, False), False).T

    d_out = scatter(row_grads(attended, grad_middle_low, True), True)

    grad_state = run(
        grad_state_kernel,
        [t_spec, q_spec, p_spec, p_spec, p_spec, one_spec],
        state_specs(),
        STATE_SHAPES,
        (table, query, grad_attended, attended, rden, first),
        flops=8 * rows * qk * FEATS * HEADS,
    )
    qk_f32 = jax.ShapeDtypeStruct((rows, qk), F32)
    qk_bf = jax.ShapeDtypeStruct((rows, qk), BF)
    grad_query, grad_key, grad_value = run(
        local_grad_kernel,
        [t_spec, q_spec, q_spec, p_spec, p_spec, p_spec, p_spec, one_spec, row_spec, one_spec]
        + state_specs(),
        [q_spec, q_spec, p_spec],
        [qk_bf, qk_f32, f32_like],
        (table, query, keys, values, grad_attended, attended, rden, row_ids, col_ids, first)
        + tuple(before),
        [pltpu.VMEM((rows, rows), F32), pltpu.VMEM((rows, qk), F32), pltpu.VMEM((rows, qk), F32)],
        flops=20 * rows * rows * qk * HEADS,
    )
    after = exchange(*grad_state, segment_ids, rows, False)
    grad_key, grad_value = run(
        finish_grad_kernel,
        [t_spec, q_spec, p_spec, q_spec, p_spec, one_spec] + state_specs(),
        [q_spec, p_spec],
        [qk_bf, bf_like],
        (table, keys, values, grad_key, grad_value, last, *after),
        [pltpu.VMEM((rows, qk), F32)],
        flops=16 * rows * qk * FEATS * HEADS,
    )
    grad_qkv = jnp.concatenate([grad_query, grad_key, grad_value], axis=1)
    d_qkv = scatter(row_grads(normed_one, grad_qkv, True), True)
    grad_normed_one = dot_nt(grad_qkv, qkv_full)
    _, first_pull = jax.vjp(rms_scale, inputs, gain_first)
    grad_inputs, grad_gain_one = first_pull(grad_normed_one)
    grad_layer = grad_middle + grad_inputs
    grad_gains = sum_everywhere(jnp.stack([grad_gain_one, grad_gain_two]))
    grad_gains = lax.dynamic_slice_in_dim(
        grad_gains.reshape(2, width // small, small), slot, 1, 1
    )[:, 0]
    return (
        outcome[None],
        grad_layer[None],
        grad_gains[0],
        d_qkv[:, :qk],
        d_qkv[:, qk : 2 * qk],
        d_qkv[:, 2 * qk :],
        d_out,
        grad_gains[1],
        d_gate,
        d_up,
        d_down,
    )


def solution(mesh):
    split = P(("head", "seq"))
    rows = P(("head", "seq"), None)
    block = P("seq", "head", None)
    wide, tall = P("seq", "head"), P("head", "seq")
    in_specs = (block, P(), split, rows, rows, rows, rows, split, wide, wide, tall, block)
    out_specs = (block, block, split, rows, rows, rows, rows, split, wide, wide, tall)
    return jax.shard_map(body, mesh=mesh, in_specs=in_specs, out_specs=out_specs, check_vma=False)
```

```python
import functools

import jax
import jax.numpy as jnp
import numpy as np
from jax import lax
from jax.experimental import pallas as pl
from jax.experimental.pallas import tpu as pltpu
from jax.sharding import PartitionSpec as P

HEADS = 16
QD = 16
VD = 64
DOC_MAX = 4096
EPSILON = 1e-05
PAIRS = HEADS // 2
WIDE = 2 * VD
FEATS = 160
TILE = 256

BF = jnp.bfloat16
F32 = jnp.float32


def flip_seq(value, code):
    n = lax.axis_size("seq")
    return lax.ppermute(value, "seq", [(i, i ^ code) for i in range(n)])


def flip_head(value):
    n = lax.axis_size("head")
    return lax.ppermute(value, "head", [(i, i ^ 1) for i in range(n)])


def shift_seq(value, distance):
    n = lax.axis_size("seq")
    return lax.ppermute(
        value, "seq", [(i, i + distance) for i in range(n) if 0 <= i + distance < n]
    )


def layout():
    chips = lax.axis_size("seq") // 2
    near = 2 if chips <= 8 else 8
    far = chips // near
    return far, near


def place_kernel(groups, count, *refs):
    pieces, out, sem = refs[:count], refs[count], refs[count + 1]
    me = lax.axis_index("seq")
    head = lax.axis_index("head")
    n = lax.axis_size("seq")
    copies = []
    for piece, blocks in zip(pieces, groups):
        for index, (rel_head, rel_seq) in blocks:
            place = me ^ rel_seq
            if rel_head is not None:
                place = place + (head ^ rel_head) * n
            copies.append(
                pltpu.make_async_copy(piece.at[index], out.at[place], sem.at[len(copies)])
            )
    for copy in copies:
        copy.start()
    for copy in copies:
        copy.wait()


def place(pieces, groups, blocks):
    rows, cols = pieces[0].shape[-2:]
    total = sum(len(g) for g in groups)
    out = pl.pallas_call(
        functools.partial(place_kernel, groups, len(pieces)),
        out_shape=jax.ShapeDtypeStruct((blocks, rows, cols), pieces[0].dtype),
        in_specs=[pl.BlockSpec(memory_space=pl.ANY)] * len(pieces),
        out_specs=pl.BlockSpec(memory_space=pltpu.VMEM),
        scratch_shapes=[pltpu.SemaphoreType.DMA((total,))],
        compiler_params=pltpu.CompilerParams(vmem_limit_bytes=16 << 20),
        cost_estimate=pl.CostEstimate(
            flops=0, bytes_accessed=4 * blocks * rows * cols, transcendentals=0
        ),
        name="place",
    )(*pieces)
    return out.reshape(blocks * rows, cols)


def gather(shard, head_first):
    far, near = layout()
    far_codes = [2 * near * r for r in range(far)]
    near_codes = [2 * r for r in range(near)]
    if head_first:
        shard = jnp.stack([shard, flip_head(shard)])
    column = jnp.stack([shard] + [flip_seq(shard, code) for code in far_codes[1:]])
    held = [(column, 0, 0)]
    held += [(flip_seq(column, code), 0, code) for code in near_codes[1:]]
    if not head_first:
        held += [(flip_head(buf), 1, code) for buf, _, code in held]
    held += [(flip_seq(buf, 1), rel, code + 1) for buf, rel, code in held]
    result = []
    for buf, rel, code in held:
        if head_first:
            blocks = [((r, g), (g, code + far_codes[r])) for r in range(far) for g in range(2)]
        else:
            blocks = [((r,), (rel, code + far_codes[r])) for r in range(far)]
        result.append((buf, blocks))
    return result


def gather_rows(shard):
    got = gather(shard, False)
    return place([b for b, _ in got], [g for _, g in got], 2 * lax.axis_size("seq"))


def gather_halves(shard, head_first):
    got = gather(shard, head_first)
    halves = []
    for rel in range(2):
        pieces, groups = [], []
        for buf, blocks in got:
            mine = [(i, (None, code)) for i, (r, code) in blocks if r == rel]
            if mine:
                pieces.append(buf)
                groups.append(mine)
        halves.append(place(pieces, groups, lax.axis_size("seq")))
    return halves


def add_low(*terms):
    total = terms[0].astype(F32)
    for term in terms[1:]:
        total = total + term.astype(F32)
    return total.astype(BF)


def pick(value, index, axis):
    return lax.dynamic_index_in_dim(value, index, axis, keepdims=False)


def scatter(grads, head_first):
    far, near = layout()
    seq = lax.axis_index("seq")
    far_at, near_at = seq // (2 * near), (seq // 2) % near
    both = [
        add_low(grads[rel][0], flip_seq(grads[rel][1], 1)) for rel in range(2)
    ]
    rows = both[0].shape[0] // (far * near)
    cols = both[0].shape[1]
    if head_first:
        whole = add_low(both[0], flip_head(both[1])).reshape(far, near, rows, cols)
    else:
        whole = jnp.stack(both).reshape(2, far, near, rows, cols).transpose(1, 2, 0, 3, 4)
    parts = [pick(whole, near_at, 1)]
    parts += [flip_seq(pick(whole, near_at ^ r, 1), 2 * r) for r in range(1, near)]
    column = add_low(*parts)
    parts = [pick(column, far_at, 0)]
    parts += [flip_seq(pick(column, far_at ^ r, 0), 2 * near * r) for r in range(1, far)]
    if head_first:
        return sum(part.astype(F32) for part in parts)
    both = add_low(*parts)
    return both[0].astype(F32) + flip_head(both[1]).astype(F32)


def sum_everywhere(value):
    value = value + flip_head(value)
    code = 1
    while code < lax.axis_size("seq"):
        value = value + flip_seq(value, code)
        code *= 2
    return value


def feature_table():
    first, second, one, two, scale = [], [], [], [], []
    for a in range(QD):
        for b in range(a, QD):
            first.append(a)
            second.append(b)
            one.append(0.0)
            two.append(0.0)
            scale.append((1.0 if a == b else 2.0) / (2.0 * QD))
    for a in range(QD):
        first.append(a)
        second.append(-1000)
        one.append(0.0)
        two.append(1.0)
        scale.append(QD**-0.5)
    first.append(-1000)
    second.append(-1000)
    one.append(1.0)
    two.append(1.0)
    scale.append(1.0)
    pad = FEATS - len(first)
    table = np.zeros((8, FEATS), np.float32)
    table[0] = np.array(first + [-1000] * pad)
    table[1] = np.array(second + [-1000] * pad)
    table[2] = np.array(one + [0.0] * pad)
    table[3] = np.array(two + [0.0] * pad)
    table[4] = np.array(scale + [0.0] * pad)
    return table


def mm(a, b, dims):
    return lax.dot_general(a, b, ((dims[0], dims[1]), ((), ())), preferred_element_type=F32)


NN = ((1,), (0,))
NT = ((1,), (1,))
TN = ((0,), (0,))


def selectors(table, head):
    lanes = HEADS * QD
    row = (lax.broadcasted_iota(jnp.int32, (lanes, FEATS), 0) - head * QD).astype(F32)
    one = (row == table[0:1, :]).astype(F32).astype(BF)
    two = (row == table[1:2, :]).astype(F32).astype(BF)
    return one, two


def factors(values, table, sel):
    return (
        mm(values, sel[0], NN) + table[2:3, :],
        mm(values, sel[1], NN) + table[3:4, :],
    )


def half_mask(rows, part):
    lane = lax.broadcasted_iota(jnp.int32, (rows, WIDE), 1)
    return (lane >= VD) if part else (lane < VD)


def head_mask(rows, head):
    lane = lax.broadcasted_iota(jnp.int32, (rows, HEADS * QD), 1)
    return (lane >= head * QD) & (lane < (head + 1) * QD)


def keep(mask, value):
    return jnp.where(mask, value.astype(F32), 0.0).astype(BF)


def state_kernel(table_ref, keys_ref, values_ref, last_ref, wide_ref, thin_ref):
    pair = pl.program_id(0)
    table = table_ref[...]
    keys = keys_ref[...]
    rows = keys.shape[0]
    last = last_ref[...]
    total = None
    for part in range(2):
        sel = selectors(table, 2 * pair + part)
        one, two = factors(keys, table, sel)
        phi = one * two * last
        value = keep(half_mask(rows, part), values_ref[...])
        new = mm(phi.astype(BF), value, TN)
        total = new if total is None else total + new
        thin_ref[0, part : part + 1, :] = jnp.sum(phi, axis=0, keepdims=True)
    thin_ref[0, 2:, :] = jnp.zeros((6, FEATS), F32)
    wide_ref[0] = total.astype(BF)


def visible_tile(mask_ref, row_ids_ref, col_ids_ref, rows):
    for i in range(rows // TILE):
        for j in range(i + 1):
            same = (
                row_ids_ref[i * TILE : (i + 1) * TILE, :]
                == col_ids_ref[:, j * TILE : (j + 1) * TILE]
            )
            if i == j:
                same = same & (
                    lax.broadcasted_iota(jnp.int32, (TILE, TILE), 1)
                    <= lax.broadcasted_iota(jnp.int32, (TILE, TILE), 0)
                )
            mask_ref[i * TILE : (i + 1) * TILE, j * TILE : (j + 1) * TILE] = same.astype(F32)


def local_kernel(
    query_ref, keys_ref, values_ref, row_ids_ref, col_ids_ref, num_ref, den_ref, mask_ref
):
    pair = pl.program_id(0)
    rows = query_ref.shape[0]

    @pl.when(pair == 0)
    def _():
        visible_tile(mask_ref, row_ids_ref, col_ids_ref, rows)

    for i in range(rows // TILE):
        here = slice(i * TILE, (i + 1) * TILE)
        num = jnp.zeros((TILE, WIDE), F32)
        dens = []
        for part in range(2):
            head = 2 * pair + part
            query = keep(head_mask(TILE, head), query_ref[here, :] * (QD**-0.5))
            den = jnp.zeros((TILE, 1), F32)
            for j in range(i + 1):
                there = slice(j * TILE, (j + 1) * TILE)
                s = mm(query, keys_ref[there, :], NT)
                w = (1.0 + s + 0.5 * s * s) * mask_ref[here, there]
                den = den + jnp.sum(w, axis=1, keepdims=True)
                num = num + mm(
                    w.astype(BF), keep(half_mask(TILE, part), values_ref[there, :]), NN
                )
            dens.append(den)
        num_ref[here, :] = num
        den_ref[here, :] = jnp.where(half_mask(TILE, 0), dens[0], dens[1])


def finish_kernel(
    table_ref, query_ref, num_ref, den_ref, first_ref, wide_ref, thin_ref, out_ref, rden_ref
):
    pair = pl.program_id(0)
    table = table_ref[...]
    query = query_ref[...]
    rows = query.shape[0]
    first = first_ref[...]
    num, den = num_ref[...], den_ref[...]
    for part in range(2):
        sel = selectors(table, 2 * pair + part)
        one, two = factors(query, table, sel)
        phi = one * two * (table[4:5, :] * first)
        mask = half_mask(rows, part)
        extra = mm(phi.astype(BF), wide_ref[0], NN)
        num = num + jnp.where(mask, extra, 0.0)
        more = jnp.sum(phi * thin_ref[0, part : part + 1, :], axis=1, keepdims=True)
        den = den + jnp.where(mask, more, 0.0)
    rden = 1.0 / den
    rden_ref[...] = rden
    out_ref[...] = (num * rden).astype(BF)


def prepare(grad_ref, out_ref, rden_ref):
    rows = grad_ref.shape[0]
    grad = grad_ref[...].astype(F32)
    rden = rden_ref[...]
    dnum = (grad * rden).astype(BF)
    prod = grad * out_ref[...].astype(F32) * rden
    deltas = [
        jnp.sum(jnp.where(half_mask(rows, part), prod, 0.0), axis=1, keepdims=True)
        for part in range(2)
    ]
    return dnum, deltas


def grad_state_kernel(
    table_ref, query_ref, grad_ref, out_ref, rden_ref, first_ref, wide_ref, thin_ref
):
    pair = pl.program_id(0)
    table = table_ref[...]
    query = query_ref[...]
    rows = query.shape[0]
    dnum, deltas = prepare(grad_ref, out_ref, rden_ref)
    total = None
    for part in range(2):
        sel = selectors(table, 2 * pair + part)
        one, two = factors(query, table, sel)
        phi = one * two * (table[4:5, :] * first_ref[...])
        new = mm(phi.astype(BF), keep(half_mask(rows, part), dnum), TN)
        total = new if total is None else total + new
        thin_ref[0, part : part + 1, :] = -jnp.sum(phi * deltas[part], axis=0, keepdims=True)
    thin_ref[0, 2:, :] = jnp.zeros((6, FEATS), F32)
    wide_ref[0] = total.astype(BF)


def local_grad_kernel(
    table_ref,
    query_ref,
    keys_ref,
    values_ref,
    grad_ref,
    out_ref,
    rden_ref,
    row_ids_ref,
    col_ids_ref,
    first_ref,
    wide_ref,
    thin_ref,
    dq_ref,
    dk_ref,
    dv_ref,
    mask_ref,
    dq_acc,
    dk_acc,
):
    pair = pl.program_id(0)
    table = table_ref[...]
    query = query_ref[...]
    keys = keys_ref[...]
    rows = query.shape[0]
    tiles = rows // TILE
    scale = QD**-0.5

    @pl.when(pair == 0)
    def _():
        visible_tile(mask_ref, row_ids_ref, col_ids_ref, rows)
        dq_acc[...] = jnp.zeros_like(dq_acc)
        dk_acc[...] = jnp.zeros_like(dk_acc)

    dnum, deltas = prepare(grad_ref, out_ref, rden_ref)
    dv = [jnp.zeros((TILE, WIDE), F32) for _ in range(tiles)]
    for part in range(2):
        head = 2 * pair + part
        at_head = head_mask(rows, head)
        q_head = keep(at_head, query * scale)
        k_head = keep(at_head, keys * scale)
        d_head = keep(half_mask(rows, part), dnum)
        for i in range(tiles):
            here = slice(i * TILE, (i + 1) * TILE)
            dq = dq_acc[here, :]
            for j in range(i + 1):
                there = slice(j * TILE, (j + 1) * TILE)
                s = mm(q_head[here], keys[there], NT)
                mask = mask_ref[here, there]
                w = ((1.0 + s + 0.5 * s * s) * mask).astype(BF)
                dp = mm(d_head[here], values_ref[there, :], NT)
                ds = ((dp - deltas[part][here]) * ((1.0 + s) * mask)).astype(BF)
                dq = dq + mm(ds, k_head[there], NN)
                dk_acc[there, :] += mm(ds, q_head[here], TN)
                dv[j] = dv[j] + mm(w, d_head[here], TN)
            dq_acc[here, :] = dq
        sel = selectors(table, head)
        one, two = factors(query, table, sel)
        dphi = mm(d_head, wide_ref[0], NT) - deltas[part] * thin_ref[0, part : part + 1, :]
        dphi = dphi * (table[4:5, :] * first_ref[...])
        dq_acc[...] += mm((dphi * two).astype(BF), sel[0], NT) + mm(
            (dphi * one).astype(BF), sel[1], NT
        )
    for j in range(tiles):
        dv_ref[j * TILE : (j + 1) * TILE, :] = dv[j]

    @pl.when(pair == PAIRS - 1)
    def _():
        dq_ref[...] = dq_acc[...].astype(BF)
        dk_ref[...] = dk_acc[...]


def finish_grad_kernel(
    table_ref, keys_ref, values_ref, dk_in_ref, dv_in_ref, last_ref, wide_ref, thin_ref,
    dk_ref, dv_ref, dk_acc,
):
    pair = pl.program_id(0)
    table = table_ref[...]
    keys = keys_ref[...]
    rows = keys.shape[0]
    last = last_ref[...]

    @pl.when(pair == 0)
    def _():
        dk_acc[...] = dk_in_ref[...]

    dv = dv_in_ref[...]
    for part in range(2):
        sel = selectors(table, 2 * pair + part)
        one, two = factors(keys, table, sel)
        mask = half_mask(rows, part)
        phi = one * two * last
        dv = dv + jnp.where(mask, mm(phi.astype(BF), wide_ref[0], NN), 0.0)
        dphi = mm(keep(mask, values_ref[...]), wide_ref[0], NT) + thin_ref[0, part : part + 1, :]
        dphi = dphi * last
        dk_acc[...] += mm((dphi * two).astype(BF), sel[0], NT) + mm(
            (dphi * one).astype(BF), sel[1], NT
        )
    dv_ref[...] = dv.astype(BF)

    @pl.when(pair == PAIRS - 1)
    def _():
        dk_ref[...] = dk_acc[...].astype(BF)


def full_spec(shape):
    return pl.BlockSpec(shape, lambda p: (0,) * len(shape))


def pair_spec(rows):
    return pl.BlockSpec((rows, WIDE), lambda p: (0, p))


def state_specs():
    return [
        pl.BlockSpec((1, FEATS, WIDE), lambda p: (p, 0, 0)),
        pl.BlockSpec((1, 8, FEATS), lambda p: (p, 0, 0)),
    ]


STATE_SHAPES = (
    jax.ShapeDtypeStruct((PAIRS, FEATS, WIDE), BF),
    jax.ShapeDtypeStruct((PAIRS, 8, FEATS), F32),
)


def run(kernel, in_specs, out_specs, out_shape, args, scratch=(), flops=0):
    moved = sum(a.size * a.dtype.itemsize for a in args)
    return pl.pallas_call(
        kernel,
        grid=(PAIRS,),
        in_specs=in_specs,
        out_specs=out_specs,
        out_shape=out_shape,
        scratch_shapes=scratch,
        compiler_params=pltpu.CompilerParams(vmem_limit_bytes=48 << 20),
        cost_estimate=pl.CostEstimate(flops=flops, bytes_accessed=moved, transcendentals=0),
        name=kernel.__name__,
    )(*args)


def exchange(wide, thin, ids, rows, forward):
    head, seq = lax.axis_index("head"), lax.axis_index("seq")
    n = lax.axis_size("seq")
    segments = 2 * n
    firsts = ids.reshape(segments, rows)[:, 0]
    lasts = ids.reshape(segments, rows)[:, rows - 1]
    step = 1 if forward else -1
    near_end, far_end = (lasts, firsts) if forward else (firsts, lasts)

    def end_of(which, segment):
        return which[jnp.clip(segment, 0, segments - 1)]

    seg = 2 * seq + head
    takes = end_of(far_end, seg)
    core = seq % 2
    late_head = head if forward else 1 - head
    late_core = core if forward else 1 - core

    def gate(flag):
        return jnp.where(flag, 1.0, 0.0).astype(F32)

    def wider(state):
        return [part.astype(F32) for part in state]

    def narrow(state):
        return [state[0].astype(BF), state[1]]

    def merge(own, other, late, other_takes, joined):
        gained = [part * (gate(other_takes) * late) for part in other]
        own_factor = jnp.where(late == 1, 1.0, gate(joined))
        other_factor = jnp.where(late == 1, gate(joined), 1.0)
        joint = [a * own_factor + b * other_factor for a, b in zip(own, other)]
        return gained, joint

    own = [wide, thin]
    other = [flip_head(part) for part in own]
    first_of, second_of = 2 * seq, 2 * seq + 1
    if not forward:
        first_of, second_of = second_of, first_of
    total, joint = merge(
        wider(own),
        wider(other),
        late_head,
        end_of(near_end, seg - step) == takes,
        end_of(near_end, first_of) == end_of(near_end, second_of),
    )
    joint = narrow(joint)
    other = [flip_seq(part, 1) for part in joint]
    base = 4 * (seq // 2)
    early_end, late_end = (base + 1, base + 3) if forward else (base + 2, base)
    gained, joint = merge(
        wider(joint),
        wider(other),
        late_core,
        end_of(near_end, early_end) == takes,
        end_of(near_end, early_end) == end_of(near_end, late_end),
    )
    total = [a + b for a, b in zip(total, gained)]
    joint = narrow(joint)
    half = PAIRS // 2
    mine = [lax.dynamic_slice_in_dim(part, core * half, half, 0) for part in joint]
    hops = -(-DOC_MAX // (4 * rows))
    far = None
    for hop in range(1, hops + 1):
        got = wider([shift_seq(part, 2 * hop * step) for part in mine])
        nearer, farther = late_end - 4 * step, late_end - 4 * step * hop
        joined = gate(end_of(near_end, nearer) == end_of(near_end, farther))
        got = [part * joined for part in got]
        far = got if far is None else [a + b for a, b in zip(far, got)]
    far = narrow(far)
    other = [flip_seq(part, 1) for part in far]
    comes = (seq // 2 >= 1) if forward else (seq // 2 < n // 2 - 1)
    use = gate(comes & (end_of(near_end, late_end - 4 * step) == takes))
    result = []
    for a, b, so_far in zip(far, other, total):
        low = jnp.where(core == 0, a, b).astype(F32)
        high = jnp.where(core == 0, b, a).astype(F32)
        result.append(so_far + use * jnp.concatenate([low, high], axis=0))
    return narrow(result)


MESH = pl.DeviceIdType.MESH
GAIN_COLS = 128


class Links:
    def __init__(self):
        self.head, self.seq = lax.axis_index("head"), lax.axis_index("seq")
        self.n = lax.axis_size("seq")
        self.z, self.y, self.c = self.seq // 4, (self.seq // 2) % 2, self.seq % 2
        self.core = self.at(self.head, self.seq ^ 1)
        self.x = self.at(1 - self.head, self.seq)
        self.near = self.at(self.head, self.seq ^ 2)
        self.far = [self.at(self.head, self.seq ^ (4 * r)) for r in range(4)]

    def at(self, head, seq):
        return {"head": head, "seq": seq}

    def shifted(self, distance):
        return self.at(self.head, lax.rem(self.seq + distance + self.n, self.n))

    def greet(self):
        barrier = pltpu.get_barrier_semaphore()
        partners = [self.core, self.x, self.near] + self.far[1:]
        partners += [self.shifted(d) for d in (2, 4, -2, -4)]
        for partner in partners:
            pl.semaphore_signal(barrier, inc=1, device_id=partner, device_id_type=MESH)
        pl.semaphore_wait(barrier, len(partners))


class Copies:
    def __init__(self, send, recv, local):
        self.send, self.recv, self.local = send, recv, local
        self.used, self.used_local = 0, 0
        self.started, self.started_local = [], []

    def remote(self, src, dst, partner):
        i = self.used
        self.used += 1
        return pltpu.make_async_remote_copy(
            src_ref=src,
            dst_ref=dst,
            send_sem=self.send.at[i],
            recv_sem=self.recv.at[i],
            device_id=partner,
            device_id_type=MESH,
        )

    def go(self, *copies):
        for copy in copies:
            copy.start()
            self.started.append(copy)

    def keep(self, src, dst):
        copy = pltpu.make_async_copy(src, dst, self.local.at[self.used_local])
        self.used_local += 1
        copy.start()
        self.started_local.append(copy)
        return copy

    def finish(self, copy):
        copy.wait()
        self.started_local = [other for other in self.started_local if other is not copy]

    def drain(self):
        for copy in self.started:
            copy.wait_send()
        for copy in self.started_local:
            copy.wait()


def arrived(*copies):
    for copy in copies:
        copy.wait_recv()


class WideGather:
    def __init__(self, copies, links, shard, own, other, other_there):
        n, y, c = links, links.y, links.c
        self.copies = copies
        self.place = own.at[n.z, y, c]
        self.shard = shard
        self.far = [copies.remote(shard, self.place, n.far[r]) for r in range(1, 4)]
        mine, theirs = own.at[:, y, c], own.at[:, 1 - y, c]
        self.near = copies.remote(mine, mine, n.near)
        self.cross = [
            copies.remote(mine, other_there.at[:, y, c], n.x),
            copies.remote(theirs, other_there.at[:, 1 - y, c], n.x),
        ]
        self.core = [
            copies.remote(part, part, n.core)
            for part in (mine, theirs, other.at[:, y, c], other.at[:, 1 - y, c])
        ]

    def begin(self):
        self.copies.go(*self.far)
        self.own = self.copies.keep(self.shard, self.place)

    def far_here(self):
        arrived(*self.far)
        self.copies.finish(self.own)

    def one(self):
        self.copies.go(self.near, self.cross[0], self.core[0])

    def two(self):
        arrived(self.near)
        self.copies.go(self.cross[1], self.core[1])

    def three(self):
        arrived(self.cross[0])
        self.copies.go(self.core[2])

    def four(self):
        arrived(self.cross[1])
        self.copies.go(self.core[3])

    def end(self):
        arrived(*self.core)


class PlaneGather:
    COPIES = 6

    def __init__(self, copies, links, shard, own):
        n, y, c = links, links.y, links.c
        self.copies, self.shard, self.place = copies, shard, own.at[n.z, y, c]
        self.far = [copies.remote(shard, self.place, n.far[r]) for r in range(1, 4)]
        mine, theirs = own.at[:, y, c], own.at[:, 1 - y, c]
        self.near = copies.remote(mine, mine, n.near)
        self.core = [copies.remote(part, part, n.core) for part in (mine, theirs)]

    def begin(self):
        self.copies.go(*self.far)
        self.own = self.copies.keep(self.shard, self.place)

    def far_here(self):
        arrived(*self.far)
        self.copies.finish(self.own)

    def one(self):
        self.copies.go(self.near, self.core[0])

    def two(self):
        arrived(self.near)
        self.copies.go(self.core[1])

    def end(self):
        arrived(*self.core)


class Exchange:
    def __init__(self, copies, links, gates, first, bufs, forward):
        n = links
        self.copies, self.gates, self.first, self.bufs = copies, gates, first, bufs
        half = PAIRS // 2
        step = 2 if forward else -2
        own, a, j, b, j2, r1, r2, far = bufs

        def both(src, dst, partner):
            return [copies.remote(s, d, partner) for s, d in zip(src, dst)]

        def halves(state):
            return [
                state[0].at[pl.ds(n.c * half, half)],
                state[1].at[pl.ds(n.c * half, half)],
            ]

        self.rounds = [
            both(own, a, n.x),
            both(j, b, n.core),
            both(halves(j2), r1, n.shifted(step)) + both(halves(j2), r2, n.shifted(2 * step)),
            both(halves(far), halves(far), n.core),
        ]
        self.halves = halves
        self.total = None

    def gate(self, i):
        return self.gates[self.first + i]

    def begin(self):
        self.copies.go(*self.rounds[0])

    def one(self):
        own, a, j, b, j2, r1, r2, far = self.bufs
        arrived(*self.rounds[0])
        for s, d, t in zip(own, a, j):
            t[...] = (
                s[...].astype(F32) * self.gate(1) + d[...].astype(F32) * self.gate(2)
            ).astype(t.dtype)
        self.copies.go(*self.rounds[1])

    def two(self):
        own, a, j, b, j2, r1, r2, far = self.bufs
        arrived(*self.rounds[1])
        for s, d, t in zip(j, b, j2):
            t[...] = (
                s[...].astype(F32) * self.gate(4) + d[...].astype(F32) * self.gate(5)
            ).astype(t.dtype)
        self.copies.go(*self.rounds[2])

    def three(self):
        own, a, j, b, j2, r1, r2, far = self.bufs
        arrived(*self.rounds[2])
        for s, d, t in zip(r1, r2, self.halves(far)):
            t[...] = (s[...].astype(F32) + d[...].astype(F32) * self.gate(6)).astype(t.dtype)
        self.copies.go(*self.rounds[3])

    def four(self, out):
        own, a, j, b, j2, r1, r2, far = self.bufs
        arrived(*self.rounds[3])
        for s, d, f, t in zip(a, b, far, out):
            t[...] = (
                s[...].astype(F32) * self.gate(0)
                + d[...].astype(F32) * self.gate(3)
                + f[...].astype(F32) * self.gate(7)
            ).astype(t.dtype)


def exchange_shapes():
    shapes = []
    for name in range(8):
        pairs = PAIRS // 2 if name in (5, 6) else PAIRS
        shapes += [pltpu.VMEM((pairs, FEATS, WIDE), BF), pltpu.VMEM((pairs, 8, FEATS), F32)]
    return shapes


def documents(ids_ref, ends_ref, links, mask, first, last):
    rows = ids_ref.shape[1]
    segment = 2 * links.seq + links.head
    row = ids_ref[pl.ds(segment, 1), :].astype(F32)
    column = jnp.transpose(jnp.broadcast_to(row, (128, rows)))[:, :1]
    visible_tile(mask, column, row, rows)
    first[...] = (column == ends_ref[segment].astype(F32)).astype(F32)
    last[...] = (column == ends_ref[2 * links.n + segment].astype(F32)).astype(F32)


def exchange_gates(ends_ref, links, forward):
    head, seq, core, n = links.head, links.seq, links.c, links.n
    segments = 2 * n
    step = 1 if forward else -1
    near_at, far_at = (segments, 0) if forward else (0, segments)
    seg = 2 * seq + head
    chip = seq // 2
    base = 4 * chip
    late_head = (head == 1) if forward else (head == 0)
    late_core = (core == 1) if forward else (core == 0)
    pair_early, pair_late = (2 * seq, 2 * seq + 1) if forward else (2 * seq + 1, 2 * seq)
    early_end, late_end = (base + 1, base + 3) if forward else (base + 2, base)
    near_ok = (chip >= 1) if forward else (chip < n // 2 - 1)
    far_ok = (chip >= 2) if forward else (chip < n // 2 - 2)

    def doc(segment):
        return ends_ref[near_at + jnp.minimum(jnp.maximum(segment, 0), segments - 1)]

    def factor(flag):
        return jnp.where(flag, 1.0, 0.0).astype(F32)

    takes = ends_ref[far_at + seg]
    joined = doc(pair_early) == doc(pair_late)
    joined2 = doc(early_end) == doc(late_end)
    nearer, farther = doc(late_end - 4 * step), doc(late_end - 8 * step)
    flags = [
        late_head & (doc(seg - step) == takes),
        late_head | joined,
        jnp.logical_not(late_head) | joined,
        late_core & (doc(early_end) == takes),
        late_core | joined2,
        jnp.logical_not(late_core) | joined2,
        far_ok & (nearer == farther),
        near_ok & (nearer == takes),
    ]
    return [factor(flag) for flag in flags]


def pair_lanes(pair, start=0):
    return pl.ds(pl.multiple_of(start + pair * WIDE, WIDE), WIDE)


def state_pair(pair, table, keys, value, last, wide_ref, thin_ref):
    rows = keys.shape[0]
    total = None
    for part in range(2):
        sel = selectors(table, 2 * pair + part)
        one, two = factors(keys, table, sel)
        phi = one * two * last
        new = mm(phi.astype(BF), keep(half_mask(rows, part), value), TN)
        total = new if total is None else total + new
        thin_ref[pair, part : part + 1, :] = jnp.sum(phi, axis=0, keepdims=True)
    thin_ref[pair, 2:, :] = jnp.zeros((6, FEATS), F32)
    wide_ref[pair] = total.astype(BF)


def local_pair(pair, qkv, num_ref, den_ref, mask_ref):
    rows = qkv.shape[0]
    qk = HEADS * QD
    for i in range(rows // TILE):
        here = slice(i * TILE, (i + 1) * TILE)
        num = jnp.zeros((TILE, WIDE), F32)
        dens = []
        for part in range(2):
            head = 2 * pair + part
            query = keep(head_mask(TILE, head), qkv[here, :qk] * (QD**-0.5))
            den = jnp.zeros((TILE, 1), F32)
            for j in range(i + 1):
                there = slice(j * TILE, (j + 1) * TILE)
                s = mm(query, qkv[there, qk : 2 * qk], NT)
                w = (1.0 + s + 0.5 * s * s) * mask_ref[here, there]
                den = den + jnp.sum(w, axis=1, keepdims=True)
                value = qkv[there, pair_lanes(pair, 2 * qk)]
                num = num + mm(w.astype(BF), keep(half_mask(TILE, part), value), NN)
            dens.append(den)
        num_ref[here, pair_lanes(pair)] = num
        den_ref[here, pair_lanes(pair)] = jnp.where(half_mask(TILE, 0), dens[0], dens[1])


def finish_pair(pair, table, query, first, num_ref, den_ref, wide_ref, thin_ref, out_ref):
    rows = query.shape[0]
    lanes = pair_lanes(pair)
    num, den = num_ref[:, lanes], den_ref[:, lanes]
    for part in range(2):
        sel = selectors(table, 2 * pair + part)
        one, two = factors(query, table, sel)
        phi = one * two * (table[4:5, :] * first)
        mask = half_mask(rows, part)
        num = num + jnp.where(mask, mm(phi.astype(BF), wide_ref[pair], NN), 0.0)
        more = jnp.sum(phi * thin_ref[pair, part : part + 1, :], axis=1, keepdims=True)
        den = den + jnp.where(mask, more, 0.0)
    rden = 1.0 / den
    den_ref[:, lanes] = rden
    out_ref[:, lanes] = (num * rden).astype(BF)


def each_pair(low, high, step):
    def one(pair, carry):
        step(pair)
        return carry

    lax.fori_loop(low, high, one, 0)


WIDE_COPIES, EXCHANGE_COPIES = 10, 10
FWD_COPIES = 3 * WIDE_COPIES + 4 * PlaneGather.COPIES + EXCHANGE_COPIES + 2
FWD_LOCALS = 20


def forward_kernel(
    x_ref, qs_ref, os_ref, gs_ref, us_ref, ds_ref, dy_ref, ids_ref, table_ref, ends_ref,
    g_own, u_own, d_own, dy_out, n2_other, wq_out, wo_out, qkv_out, att_out, rden_out,
    res_out, n2_out, wide_out, thin_out, gain_out,
    wq, wo, normed, qkv, num, den, mask, first_ref, last_ref, att, res, n2, wide, thin, gain,
    *rest,
):
    bufs, (send, recv, local) = rest[:16], rest[16:]
    states = [(bufs[2 * i], bufs[2 * i + 1]) for i in range(8)]
    n = Links()
    copies = Copies(send, recv, local)
    rows, width = x_ref.shape
    qk, hv = HEADS * QD, HEADS * VD
    cut = 7 * 128
    full = wq.shape[-1]

    def side(ref, head, lo=None, hi=None):
        return ref.at[head] if lo is None else ref.at[head, :, :, :, :, pl.ds(lo, hi - lo)]

    q_parts = []
    for lo, hi in ((0, cut), (cut, full)):
        shard = qs_ref.at[:, pl.ds(lo, hi - lo)]
        own, other = side(wq, n.head, lo, hi), side(wq, 1 - n.head, lo, hi)
        q_parts.append(WideGather(copies, n, shard, own, other, own))
    own, other = side(wo, n.head), side(wo, 1 - n.head)
    outs = WideGather(copies, n, os_ref, own, other, own)
    gates = PlaneGather(copies, n, gs_ref, g_own)
    ups = PlaneGather(copies, n, us_ref, u_own)
    middle = 6 * 128
    downs = []
    for lo, hi in ((0, middle), (middle, ds_ref.shape[-1])):
        part = d_own.at[:, :, :, :, pl.ds(lo, hi - lo)]
        downs.append(PlaneGather(copies, n, ds_ref.at[:, pl.ds(lo, hi - lo)], part))
    other_dy = copies.remote(dy_ref, dy_out, n.x)
    other_n2 = copies.remote(n2, n2_other, n.x)
    swap = Exchange(copies, n, exchange_gates(ends_ref, n, True), 0, states, True)

    n.greet()
    for part in q_parts:
        part.begin()

    table = table_ref[...]
    x = x_ref[...].astype(F32)
    scaled = x * lax.rsqrt(jnp.mean(x * x, axis=-1, keepdims=True) + EPSILON)
    documents(ids_ref, ends_ref, n, mask, first_ref, last_ref)
    for part in q_parts:
        part.far_here()
        part.one()
    outs.begin()
    for part in q_parts:
        part.two()
    outs.far_here()
    gates.begin()
    for part in q_parts:
        part.three()
    for part in q_parts:
        part.four()
    for part in q_parts:
        part.end()
    outs.one()

    pick_gain = (
        lax.broadcasted_iota(jnp.int32, (8, GAIN_COLS), 0)
        == lax.broadcasted_iota(jnp.int32, (8, GAIN_COLS), 1)
    ).astype(F32).astype(BF)
    gain[...] = mm(pick_gain, wq[..., full - GAIN_COLS :].reshape(width, GAIN_COLS), NT)
    normed[...] = (scaled * gain[0:1, :]).astype(BF)
    h1 = normed[...]
    for lo in range(0, 2 * qk + hv, 256):
        weight = wq[..., lo : lo + 256].reshape(width, 256)
        qkv[:, lo : lo + 256] = mm(h1, weight, NN).astype(BF)
    copies.keep(qkv, qkv_out)
    copies.keep(wq, wq_out)
    copies.keep(gain, gain_out)

    gates.far_here()
    gates.one()
    ups.begin()

    def do_state(pair):
        state_pair(
            pair, table, qkv[:, qk : 2 * qk], qkv[:, pair_lanes(pair, 2 * qk)], last_ref[...],
            states[0][0], states[0][1],
        )

    def do_local(pair):
        local_pair(pair, qkv, num, den, mask)

    def do_finish(pair):
        finish_pair(
            pair, table, qkv[:, :qk], first_ref[...], num, den, wide, thin, att
        )

    each_pair(0, PAIRS, do_state)
    swap.begin()
    outs.two()
    each_pair(0, 4, do_local)
    swap.one()
    outs.three()
    each_pair(4, 6, do_local)
    swap.two()
    ups.far_here()
    downs[0].begin()
    gates.two()
    ups.one()
    outs.four()
    copies.go(other_dy)
    each_pair(6, PAIRS, do_local)
    swap.three()
    swap.four((wide, thin))
    copies.keep(wide, wide_out)
    copies.keep(thin, thin_out)
    each_pair(0, 3, do_finish)
    downs[0].far_here()
    downs[1].begin()
    each_pair(3, PAIRS, do_finish)
    ups.two()
    downs[0].one()
    outs.end()
    copies.keep(wo, wo_out)
    copies.keep(att, att_out)
    copies.keep(den, rden_out)
    o = att[...]
    for lo in range(0, width, 256):
        weight = wo[..., lo : lo + 256].reshape(hv, 256)
        res[:, lo : lo + 256] = x_ref[:, lo : lo + 256].astype(F32) + mm(o, weight, NN)
    copies.keep(res, res_out)
    y1 = res[...]
    n2[...] = (
        y1 * lax.rsqrt(jnp.mean(y1 * y1, axis=-1, keepdims=True) + EPSILON) * gain[1:2, :]
    ).astype(BF)
    copies.keep(n2, n2_out)
    copies.go(other_n2)
    downs[1].far_here()
    downs[1].one()
    downs[0].two()
    downs[1].two()
    for part in (gates, ups, downs[0], downs[1]):
        part.end()
    arrived(other_dy, other_n2)
    copies.drain()


def forward(x, q_shard, o_shard, ffn, dy, ids, table, ends):
    rows, width = x.shape
    qk, hv = HEADS * QD, HEADS * VD
    full = q_shard.shape[-1]
    small, fine, ff = q_shard.shape[0], ffn[0].shape[0], ffn[0].shape[1]
    half = jax.ShapeDtypeStruct((4, 2, 2, fine, ff), BF)
    wq_shape, wo_shape = (2, 4, 2, 2, small, full), (2, 4, 2, 2, small, width)

    def like(shape, dtype):
        return jax.ShapeDtypeStruct(shape, dtype)

    out_shape = [half] * 3 + [
        like(dy.shape, BF), like(dy.shape, BF), like(wq_shape, BF), like(wo_shape, BF), like((rows, 2 * qk + hv), BF),
        like((rows, hv), BF), like((rows, hv), F32), like((rows, width), F32),
        like((rows, width), BF), STATE_SHAPES[0], STATE_SHAPES[1], like((8, width), F32),
    ]
    scratch = [
        pltpu.VMEM(wq_shape, BF), pltpu.VMEM(wo_shape, BF), pltpu.VMEM((rows, width), BF),
        pltpu.VMEM((rows, 2 * qk + hv), BF), pltpu.VMEM((rows, hv), F32),
        pltpu.VMEM((rows, hv), F32), pltpu.VMEM((rows, rows), F32), pltpu.VMEM((rows, 1), F32),
        pltpu.VMEM((rows, 1), F32), pltpu.VMEM((rows, hv), BF),
        pltpu.VMEM((rows, width), F32), pltpu.VMEM((rows, width), BF),
        pltpu.VMEM((PAIRS, FEATS, WIDE), BF), pltpu.VMEM((PAIRS, 8, FEATS), F32),
        pltpu.VMEM((8, width), F32),
    ] + exchange_shapes() + [
        pltpu.SemaphoreType.DMA((FWD_COPIES,)), pltpu.SemaphoreType.DMA((FWD_COPIES,)),
        pltpu.SemaphoreType.DMA((FWD_LOCALS,)),
    ]
    vmem = pl.BlockSpec(memory_space=pltpu.VMEM)
    return pl.pallas_call(
        forward_kernel,
        out_shape=out_shape,
        in_specs=[vmem] * 6
        + [pl.BlockSpec(memory_space=pl.ANY)]
        + [vmem] * 2
        + [pl.BlockSpec(memory_space=pltpu.SMEM)],
        out_specs=[pl.BlockSpec(memory_space=pl.ANY)] * len(out_shape),
        scratch_shapes=scratch,
        compiler_params=pltpu.CompilerParams(
            collective_id=1, has_side_effects=True, vmem_limit_bytes=56 << 20
        ),
        cost_estimate=pl.CostEstimate(flops=8 << 30, bytes_accessed=64 << 20, transcendentals=0),
        name="forward",
    )(x, q_shard, o_shard, *ffn, dy, ids, table, ends)


def as_f32(ref, index):
    return ref[index].astype(F32)


class WideScatter:
    REMOTE, LOCAL = 7, 3

    def __init__(self, copies, links, own, other, bufs, out):
        n, y, c = links, links.y, links.c
        self.n, self.copies, self.out = n, copies, out
        a_own, a_oth, c_own, c_oth, xx, yy, zz, done = bufs
        self.bufs = bufs
        self.own_part, self.oth_part = own.at[:, :, c], other.at[:, :, c]
        self.core = [
            copies.remote(other.at[:, :, 1 - c], c_oth, n.core),
            copies.remote(own.at[:, :, 1 - c], c_own, n.core),
        ]
        self.cross = copies.remote(a_oth, xx, n.x)
        self.near = copies.remote(a_own.at[:, 1 - y], yy, n.near)
        self.far = [
            copies.remote(a_own.at[n.z ^ r, y], zz.at[r - 1], n.far[r]) for r in range(1, 4)
        ]

    def begin(self):
        a_own, a_oth = self.bufs[:2]
        self.copies.go(*self.core)
        self.loads = [
            self.copies.keep(self.oth_part, a_oth), self.copies.keep(self.own_part, a_own)
        ]

    def loaded(self, i):
        self.copies.finish(self.loads[i])

    def one(self):
        a_own, a_oth, c_own, c_oth, xx, yy, zz, done = self.bufs
        self.loaded(0)
        arrived(self.core[0])

        def add(i, carry):
            for at in ((i, 0), (i, 1)):
                a_oth[at] = (as_f32(a_oth, at) + as_f32(c_oth, at)).astype(BF)
            return carry

        lax.fori_loop(0, 4, add, 0)
        self.copies.go(self.cross)

    def two(self):
        a_own, a_oth, c_own, c_oth, xx, yy, zz, done = self.bufs
        self.loaded(1)
        arrived(self.core[1], self.cross)

        def add(i, carry):
            for at in ((i, 0), (i, 1)):
                total = as_f32(a_own, at) + as_f32(c_own, at) + as_f32(xx, at)
                a_own[at] = total.astype(BF)
            return carry

        lax.fori_loop(0, 4, add, 0)
        self.copies.go(self.near)

    def three(self):
        a_own, a_oth, c_own, c_oth, xx, yy, zz, done = self.bufs
        arrived(self.near)

        def add(i, carry):
            at = (i, self.n.y)
            a_own[at] = (as_f32(a_own, at) + as_f32(yy, i)).astype(BF)
            return carry

        lax.fori_loop(0, 4, add, 0)
        self.copies.go(*self.far)

    def four(self):
        a_own, a_oth, c_own, c_oth, xx, yy, zz, done = self.bufs
        arrived(*self.far)
        total = as_f32(a_own, (self.n.z, self.n.y))
        for r in range(3):
            total = total + as_f32(zz, r)
        done[...] = total
        self.copies.keep(done, self.out)

    @staticmethod
    def shapes(rows, cols):
        part = [pltpu.VMEM((4, 2, rows, cols), BF)]
        return part * 5 + [
            pltpu.VMEM((4, rows, cols), BF), pltpu.VMEM((3, rows, cols), BF),
            pltpu.VMEM((rows, cols), F32),
        ]


class PlaneScatter:
    REMOTE = 5

    def __init__(self, copies, links, own, bufs, out):
        n, y, c = links, links.y, links.c
        self.n, self.copies, self.out, self.bufs = n, copies, out, bufs
        a, cc, yy, zz, done = bufs
        self.part = own.at[:, :, c]
        self.core = copies.remote(own.at[:, :, 1 - c], cc, n.core)
        self.near = copies.remote(a.at[:, 1 - y], yy, n.near)
        self.far = [copies.remote(a.at[n.z ^ r, y], zz.at[r - 1], n.far[r]) for r in range(1, 4)]

    def begin(self):
        self.copies.go(self.core)
        self.load = self.copies.keep(self.part, self.bufs[0])

    def one(self):
        a, cc, yy, zz, done = self.bufs
        self.copies.finish(self.load)
        arrived(self.core)

        def add(i, carry):
            for at in ((i, 0), (i, 1)):
                a[at] = (as_f32(a, at) + as_f32(cc, at)).astype(BF)
            return carry

        lax.fori_loop(0, 4, add, 0)
        self.copies.go(self.near)

    def two(self):
        a, cc, yy, zz, done = self.bufs
        arrived(self.near)

        def add(i, carry):
            at = (i, self.n.y)
            a[at] = (as_f32(a, at) + as_f32(yy, i)).astype(BF)
            return carry

        lax.fori_loop(0, 4, add, 0)
        self.copies.go(*self.far)

    def three(self):
        a, cc, yy, zz, done = self.bufs
        arrived(*self.far)
        total = as_f32(a, (self.n.z, self.n.y))
        for r in range(3):
            total = total + as_f32(zz, r)
        done[...] = total
        self.copies.keep(done, self.out)

    @staticmethod
    def shapes(rows, cols):
        return [pltpu.VMEM((4, 2, rows, cols), BF)] * 2 + [
            pltpu.VMEM((4, rows, cols), BF), pltpu.VMEM((3, rows, cols), BF),
            pltpu.VMEM((rows, cols), F32),
        ]


def prepare_pair(pair, grad, out, rden):
    rows = grad.shape[0]
    lanes = pair_lanes(pair)
    g = grad[:, lanes].astype(F32)
    r = rden[:, lanes]
    prod = g * out[:, lanes].astype(F32) * r
    low = half_mask(rows, 0)
    first = jnp.sum(jnp.where(low, prod, 0.0), axis=1, keepdims=True)
    second = jnp.sum(jnp.where(low, 0.0, prod), axis=1, keepdims=True)
    grad[:, lanes] = (g * r).astype(BF)
    rden[:, lanes] = jnp.where(low, first, second)


def delta_of(pair, part, deltas, where=slice(None)):
    return deltas[where, pair_lanes(pair)][:, part * VD : part * VD + 1]


def grad_state_pair(pair, table, query, first, dnum_ref, delta_ref, wide_ref, thin_ref):
    rows = query.shape[0]
    dnum = dnum_ref[:, pair_lanes(pair)]
    total = None
    for part in range(2):
        sel = selectors(table, 2 * pair + part)
        one, two = factors(query, table, sel)
        phi = one * two * (table[4:5, :] * first)
        new = mm(phi.astype(BF), keep(half_mask(rows, part), dnum), TN)
        total = new if total is None else total + new
        delta = delta_of(pair, part, delta_ref)
        thin_ref[pair, part : part + 1, :] = -jnp.sum(phi * delta, axis=0, keepdims=True)
    thin_ref[pair, 2:, :] = jnp.zeros((6, FEATS), F32)
    wide_ref[pair] = total.astype(BF)


def local_grad_pair(
    pair, table, qkv, first, dnum_ref, delta_ref, wide_ref, thin_ref, dq_acc, dk_acc, dv_ref,
    mask_ref,
):
    qk = HEADS * QD
    query, keys = qkv[:, :qk], qkv[:, qk : 2 * qk]
    rows = query.shape[0]
    tiles = rows // TILE
    scale = QD**-0.5
    lanes = pair_lanes(pair)
    values = qkv[:, pair_lanes(pair, 2 * qk)]
    dnum = dnum_ref[:, lanes]
    dv = [jnp.zeros((TILE, WIDE), F32) for _ in range(tiles)]
    for part in range(2):
        head = 2 * pair + part
        at_head = head_mask(rows, head)
        q_head = keep(at_head, query * scale)
        k_head = keep(at_head, keys * scale)
        d_head = keep(half_mask(rows, part), dnum)
        delta = delta_of(pair, part, delta_ref)
        for i in range(tiles):
            here = slice(i * TILE, (i + 1) * TILE)
            dq = dq_acc[here, :]
            for j in range(i + 1):
                there = slice(j * TILE, (j + 1) * TILE)
                s = mm(q_head[here], keys[there], NT)
                mask = mask_ref[here, there]
                w = ((1.0 + s + 0.5 * s * s) * mask).astype(BF)
                dp = mm(d_head[here], values[there], NT)
                ds = ((dp - delta[here]) * ((1.0 + s) * mask)).astype(BF)
                dq = dq + mm(ds, k_head[there], NN)
                dk_acc[there, :] += mm(ds, q_head[here], TN)
                dv[j] = dv[j] + mm(w, d_head[here], TN)
            dq_acc[here, :] = dq
        sel = selectors(table, head)
        one, two = factors(query, table, sel)
        dphi = mm(d_head, wide_ref[pair], NT) - delta * thin_ref[pair, part : part + 1, :]
        dphi = dphi * (table[4:5, :] * first)
        dq_acc[...] += mm((dphi * two).astype(BF), sel[0], NT) + mm(
            (dphi * one).astype(BF), sel[1], NT
        )
    for j in range(tiles):
        dv_ref[j * TILE : (j + 1) * TILE, lanes] = dv[j]


def finish_grad_pair(pair, table, qkv, last, wide_ref, thin_ref, dk_acc, dv_ref, grads):
    qk = HEADS * QD
    keys = qkv[:, qk : 2 * qk]
    rows = keys.shape[0]
    lanes = pair_lanes(pair)
    values = qkv[:, pair_lanes(pair, 2 * qk)]
    dv = dv_ref[:, lanes]
    for part in range(2):
        sel = selectors(table, 2 * pair + part)
        one, two = factors(keys, table, sel)
        mask = half_mask(rows, part)
        phi = one * two * last
        dv = dv + jnp.where(mask, mm(phi.astype(BF), wide_ref[pair], NN), 0.0)
        dphi = mm(keep(mask, values), wide_ref[pair], NT) + thin_ref[pair, part : part + 1, :]
        dphi = dphi * last
        dk_acc[...] += mm((dphi * two).astype(BF), sel[0], NT) + mm(
            (dphi * one).astype(BF), sel[1], NT
        )
    grads[:, pair_lanes(pair, 2 * qk)] = dv.astype(BF)


BWD_COPIES = 3 * WideScatter.REMOTE + 3 * PlaneScatter.REMOTE + EXCHANGE_COPIES + 1
BWD_LOCALS = 6 * 3 + 12


def backward_kernel(
    gg_own, gu_own, gd_own, go_ref, grad_in, att_in, rden_in, qkv_in,
    wide_in, thin_in, wq_in, x_in, middle_in, y_in, y_other_in, gain_ref, dgain_ref, ids_ref,
    table_ref, ends_ref,
    dg_out, du_out, dd_out, do_out, dq_out, din_out, outcome_out,
    *rest,
):
    rest = list(rest)

    def take(count):
        got = rest[:count]
        del rest[:count]
        return got

    g_bufs, u_bufs, d_bufs, o_bufs = take(5), take(5), take(5), take(8)
    q_bufs = [take(8), take(8)]
    bufs = take(16)
    states = [(bufs[2 * i], bufs[2 * i + 1]) for i in range(8)]
    (
        y_got, outcome, first_ref, last_ref, grad, out, rden, mask, dq_acc, dk_acc, dv, before_wide, before_thin, wqg, qkv, grads,
        wide, thin, dgain, send, recv, local,
    ) = rest
    n = Links()
    copies = Copies(send, recv, local)
    rows, width = out.shape
    qk, hv = HEADS * QD, HEADS * VD
    table = table_ref[...]
    cut, full = 7 * 128, wqg.shape[-1]

    gates = PlaneScatter(copies, n, gg_own, g_bufs, dg_out)
    ups = PlaneScatter(copies, n, gu_own, u_bufs, du_out)
    downs = PlaneScatter(copies, n, gd_own, d_bufs, dd_out)
    outs = WideScatter(copies, n, go_ref.at[n.head], go_ref.at[1 - n.head], o_bufs, do_out)
    qs = []
    for bufs_of, (lo, hi) in zip(q_bufs, ((0, cut), (cut, full))):
        cols = pl.ds(lo, hi - lo)
        own = wqg.at[n.head, :, :, :, :, cols]
        oth = wqg.at[1 - n.head, :, :, :, :, cols]
        qs.append(WideScatter(copies, n, own, oth, bufs_of, dq_out.at[:, cols]))
    swap = Exchange(copies, n, exchange_gates(ends_ref, n, False), 0, states, False)
    y_back = copies.remote(y_other_in, y_got, n.x)

    def fetch(*pairs):
        loads = [copies.keep(src, dst) for src, dst in pairs]

        def ready():
            for load in loads:
                copies.finish(load)

        return ready

    n.greet()

    ready = fetch(
        (grad_in, grad), (att_in, out), (rden_in, rden), (qkv_in, qkv),
        (wide_in, before_wide), (thin_in, before_thin),
    )
    gates.begin()
    ups.begin()
    downs.begin()
    outs.begin()
    documents(ids_ref, ends_ref, n, mask, first_ref, last_ref)
    dq_acc[...] = jnp.zeros_like(dq_acc)
    dk_acc[...] = jnp.zeros_like(dk_acc)
    ready()
    each_pair(0, PAIRS, lambda pair: prepare_pair(pair, grad, out, rden))
    ready_x = fetch((x_in, out), (wq_in, wqg))
    gates.one()

    def do_state(pair):
        grad_state_pair(
            pair, table, qkv[:, :qk], first_ref[...], grad, rden, states[0][0], states[0][1]
        )

    def do_local(pair):
        local_grad_pair(
            pair, table, qkv, first_ref[...], grad, rden, before_wide, before_thin, dq_acc,
            dk_acc, dv, mask,
        )

    def do_finish(pair):
        finish_grad_pair(pair, table, qkv, last_ref[...], wide, thin, dk_acc, dv, grads)

    each_pair(0, PAIRS, do_state)
    swap.begin()
    outs.one()
    each_pair(0, 2, do_local)
    swap.one()
    gates.two()
    ups.one()
    each_pair(2, 4, do_local)
    swap.two()
    outs.two()
    copies.go(y_back)
    each_pair(4, 6, do_local)
    swap.three()
    ups.two()
    downs.one()
    each_pair(6, PAIRS, do_local)
    ready_middle = fetch((middle_in, rden))
    grads[:, :qk] = dq_acc[...].astype(BF)
    swap.four((wide, thin))
    gates.three()
    outs.three()
    each_pair(0, 4, do_finish)
    each_pair(4, PAIRS, do_finish)
    ready_y = fetch((y_in, dv))
    grads[:, qk : 2 * qk] = dk_acc[...].astype(BF)
    downs.two()

    ready_x()
    ready_middle()
    wq, x_buf, middle, normed = wqg, out, rden, grad
    x = x_buf[...].astype(F32)
    scale = lax.rsqrt(jnp.mean(x * x, axis=-1, keepdims=True) + EPSILON)
    normed[...] = (x * scale * gain_ref[0:1, :]).astype(BF)
    dh = jnp.zeros((rows, width), F32)
    for lo in range(0, 2 * qk + hv, 512):
        weight = wq[..., lo : lo + 512].reshape(width, 512)
        dh = dh + mm(grads[:, lo : lo + 512], weight, NT)
    hat = x * scale
    dgain[...] = jnp.zeros_like(dgain)
    dgain[0:1, :] = jnp.sum(dh * hat, axis=0, keepdims=True)
    dgain[1:2, :] = dgain_ref[...]
    dhat = dh * gain_ref[0:1, :]
    inner = jnp.mean(dhat * hat, axis=-1, keepdims=True)
    middle[...] = middle[...] + (dhat - hat * inner) * scale
    copies.keep(middle, din_out)
    h1 = normed[...]
    for lo in range(0, 2 * qk + hv, 256):
        part = mm(h1, grads[:, lo : lo + 256], TN).astype(BF)
        wqg[..., lo : lo + 256] = part.reshape(wqg.shape[:-1] + (256,))
    spread = (
        lax.broadcasted_iota(jnp.int32, (8, GAIN_COLS), 0)
        == lax.broadcasted_iota(jnp.int32, (8, GAIN_COLS), 1)
    ).astype(F32).astype(BF)
    gain_part = mm(dgain[...].astype(BF), spread, TN).astype(BF)
    wqg[..., full - GAIN_COLS :] = gain_part.reshape(wqg.shape[:-1] + (GAIN_COLS,))
    for q in qs:
        q.begin()
    for q in qs:
        q.one()
    ups.three()
    outs.four()
    ready_y()
    arrived(y_back)
    outcome[...] = (dv[...] + y_got[...].astype(F32)).astype(BF)
    copies.keep(outcome, outcome_out)
    downs.three()
    for q in qs:
        q.two()
    for q in qs:
        q.three()
    for q in qs:
        q.four()
    copies.drain()


def swish_grads(gate, up, grad_hidden):
    sig = 1.0 / (1.0 + jnp.exp(-gate))
    silu = gate * sig
    grad_up = grad_hidden * silu
    grad_gate = grad_hidden * up * (sig * (1.0 + gate * (1.0 - sig)))
    return (silu * up).astype(BF), grad_gate.astype(BF), grad_up.astype(BF)


FFN_COPIES, FFN_LOCALS = 1, 24


def ffn_kernel(
    n2_in, n2_other_in, dy_in, dy_other_in, res_in, g_in, u_in, d_in, att_in, wo_in, gain_ref,
    dwg_out, dwu_out, dwd_out, dwo_out, do_out, middle_out, y_out, y_other_out, dgain_out,
    wg, wu, wd, n2, dy, flipped, acts, grad_gates, grad_ups, y_acc, h_acc, h_sent,
    h_got, res, att, wo, dwo, low, dgain, send, recv, local,
):
    n = Links()
    copies = Copies(send, recv, local)
    rows, width = res.shape
    ff = wg.shape[-1]

    def cols(ref, lo, hi):
        return ref[..., lo:hi].reshape(width, hi - lo)

    def fetch(*pairs):
        loads = [copies.keep(src, dst) for src, dst in pairs]

        def ready():
            for load in loads:
                copies.finish(load)

        return ready

    barrier = pltpu.get_barrier_semaphore()
    pl.semaphore_signal(barrier, inc=1, device_id=n.x, device_id_type=MESH)
    pl.semaphore_wait(barrier, 1)
    first = fetch(
        (n2_other_in, n2.at[1]), (g_in, wg), (u_in, wu), (dy_other_in, dy.at[1]), (d_in, wd)
    )
    later = fetch((n2_in, n2.at[0]), (dy_in, dy.at[0]))
    last = fetch((res_in, res), (att_in, att), (wo_in, wo))
    back = copies.remote(h_sent, h_got, n.x)
    first()
    steps = [(lo, min(lo + 512, ff)) for lo in range(0, ff, 512)]

    for t in (1, 0):
        here = slice(t * rows, (t + 1) * rows)
        if t == 0:
            later()
        for lo, hi in steps:
            w_g, w_u, w_d = cols(wg, lo, hi), cols(wu, lo, hi), cols(wd, lo, hi)
            gate = mm(n2[t], w_g, NN)
            up = mm(n2[t], w_u, NN)
            a, dg, du = swish_grads(gate, up, mm(dy[t], w_d, NN))
            acts[here, lo:hi] = a
            grad_gates[here, lo:hi] = dg
            grad_ups[here, lo:hi] = du
            more_h = mm(dg, w_g, NT) + mm(du, w_u, NT)
            more_y = mm(a, w_d, NT)
            if lo == 0:
                h_acc[t] = more_h
                y_acc[t] = more_y
            else:
                h_acc[t] += more_h
                y_acc[t] += more_y
        if t == 1:
            h_sent[...] = h_acc[1].astype(BF)
            copies.go(back)
            low[...] = y_acc[1].astype(BF)
            y_kept = copies.keep(low, y_other_out)
    last()
    y_acc[0] += res[...]
    copies.keep(y_acc.at[0], y_out)

    def flip(source):
        for t in range(2):
            for lo in range(0, width, 256):
                block = source[t, :, lo : lo + 256]
                flipped[lo : lo + 256, t * rows : (t + 1) * rows] = jnp.transpose(block)

    def weight_grad(right, weight, out):
        for lo, hi in steps:
            part = mm(flipped[...], right[:, lo:hi], NN).astype(BF)
            weight[..., lo:hi] = part.reshape(weight.shape[:-1] + (hi - lo,))
        copies.keep(weight, out)

    flip(n2)
    weight_grad(grad_gates, wg, dwg_out)
    weight_grad(grad_ups, wu, dwu_out)
    flip(dy)
    weight_grad(acts, wd, dwd_out)

    copies.finish(y_kept)
    arrived(back)
    gain = gain_ref[1:2, :]
    y1 = res[...]
    scale = lax.rsqrt(jnp.mean(y1 * y1, axis=-1, keepdims=True) + EPSILON)
    hat = y1 * scale
    dh = h_acc[0] + h_got[...].astype(F32)
    dgain[...] = jnp.sum(dh * hat, axis=0, keepdims=True)
    dhat = dh * gain
    inner = jnp.mean(dhat * hat, axis=-1, keepdims=True)
    middle = dy[0].astype(F32) + (dhat - hat * inner) * scale
    h_acc[0] = middle
    low[...] = middle.astype(BF)
    copies.keep(h_acc.at[0], middle_out)
    copies.keep(dgain, dgain_out)
    weight = wo[...].reshape(-1, width)
    h_sent_free = low[...]
    for lo in range(0, width, 256):
        dwo[..., lo : lo + 256] = (
            mm(att[...], h_sent_free[:, lo : lo + 256], TN)
            .astype(BF)
            .reshape(dwo.shape[:-1] + (256,))
        )
    copies.keep(dwo, dwo_out)
    n2[0] = mm(h_sent_free, weight, NT).astype(BF)
    copies.keep(n2.at[0], do_out)
    copies.drain()


def feed_forward(n2, n2_other, dy, dy_other, res, weights, att, wo, gain):
    rows, width = n2.shape
    full, ff = weights[0].shape, weights[0].shape[-1]

    def like(shape, dtype):
        return jax.ShapeDtypeStruct(shape, dtype)

    def scratch(shape, dtype):
        return pltpu.VMEM(shape, dtype)

    out_shape = [like(full, BF)] * 3 + [
        like(wo.shape, BF), like((rows, width), BF), like((rows, width), F32),
        like((rows, width), F32), like((rows, width), BF), like((1, width), F32),
    ]
    token = (rows, width)
    anywhere = pl.BlockSpec(memory_space=pl.ANY)
    return pl.pallas_call(
        ffn_kernel,
        out_shape=out_shape,
        in_specs=[anywhere] * 10 + [pl.BlockSpec(memory_space=pltpu.VMEM)],
        out_specs=[anywhere] * len(out_shape),
        scratch_shapes=[scratch(full, BF)] * 3
        + [scratch((2,) + token, BF)] * 2
        + [scratch((width, 2 * rows), BF)]
        + [scratch((2 * rows, ff), BF)] * 3
        + [scratch((2,) + token, F32)] * 2
        + [scratch(token, BF)] * 2
        + [scratch(token, F32), scratch(token, BF), scratch(wo.shape, BF), scratch(wo.shape, BF)]
        + [scratch(token, BF), scratch((1, width), F32)]
        + [
            pltpu.SemaphoreType.DMA((FFN_COPIES,)), pltpu.SemaphoreType.DMA((FFN_COPIES,)),
            pltpu.SemaphoreType.DMA((FFN_LOCALS,)),
        ],
        compiler_params=pltpu.CompilerParams(
            collective_id=3, has_side_effects=True, vmem_limit_bytes=62 << 20
        ),
        cost_estimate=pl.CostEstimate(flops=26 << 30, bytes_accessed=64 << 20, transcendentals=0),
        name="feed_forward",
    )(n2, n2_other, dy, dy_other, res, *weights, att, wo, gain)


def backward(
    ffn_grads, out_grad, grad, att, rden, qkv, before, wq, x, middle, y, y_other, gain, dgain, ids,
    table, ends,
):
    rows, width = x.shape
    qk, hv = HEADS * QD, HEADS * VD
    fine, ff = ffn_grads[0].shape[-2:]
    small, full = wq.shape[-2:]
    cut = 7 * 128

    def like(shape, dtype):
        return jax.ShapeDtypeStruct(shape, dtype)

    out_shape = [like((fine, ff), F32)] * 3 + [
        like((small, width), F32), like((small, full), F32), like((rows, width), F32),
        like((rows, width), BF),
    ]
    scratch = (
        PlaneScatter.shapes(fine, ff) * 3
        + WideScatter.shapes(small, width)
        + WideScatter.shapes(small, cut) + WideScatter.shapes(small, full - cut)
        + exchange_shapes()
    )
    scratch += [
        pltpu.VMEM((rows, width), BF), pltpu.VMEM((rows, width), BF), pltpu.VMEM((rows, 1), F32),
        pltpu.VMEM((rows, 1), F32),
        pltpu.VMEM((rows, hv), BF), pltpu.VMEM((rows, width), BF), pltpu.VMEM((rows, hv), F32),
        pltpu.VMEM((rows, rows), F32), pltpu.VMEM((rows, qk), F32), pltpu.VMEM((rows, qk), F32),
        pltpu.VMEM((rows, hv), F32), pltpu.VMEM((PAIRS, FEATS, WIDE), BF),
        pltpu.VMEM((PAIRS, 8, FEATS), F32),
        pltpu.VMEM((2, 4, 2, 2, small, full), BF), pltpu.VMEM((rows, 2 * qk + hv), BF),
        pltpu.VMEM((rows, 2 * qk + hv), BF),
        pltpu.VMEM((PAIRS, FEATS, WIDE), BF), pltpu.VMEM((PAIRS, 8, FEATS), F32),
        pltpu.VMEM((8, width), F32),
        pltpu.SemaphoreType.DMA((BWD_COPIES,)), pltpu.SemaphoreType.DMA((BWD_COPIES,)),
        pltpu.SemaphoreType.DMA((BWD_LOCALS,)),
    ]
    vmem = pl.BlockSpec(memory_space=pltpu.VMEM)
    anywhere = pl.BlockSpec(memory_space=pl.ANY)
    return pl.pallas_call(
        backward_kernel,
        out_shape=out_shape,
        in_specs=[anywhere] * 15 + [vmem] * 4 + [pl.BlockSpec(memory_space=pltpu.SMEM)],
        out_specs=[anywhere] * len(out_shape),
        scratch_shapes=scratch,
        compiler_params=pltpu.CompilerParams(
            collective_id=2, has_side_effects=True, vmem_limit_bytes=62 << 20
        ),
        cost_estimate=pl.CostEstimate(flops=16 << 30, bytes_accessed=64 << 20, transcendentals=0),
        name="backward",
    )(
        *ffn_grads, out_grad, grad, att, rden, qkv, *before, wq, x, middle, y, y_other, gain,
        dgain, ids, table, ends,
    )


def rms_scale(values, gain):
    return values * lax.rsqrt(jnp.mean(values * values, axis=-1, keepdims=True) + EPSILON) * gain


def swish_mix(gate, up_proj):
    return jax.nn.silu(gate) * up_proj


def dot_nn(a, b):
    return jnp.dot(a, b, preferred_element_type=F32)


def dot_nt(a, b):
    return lax.dot_general(a, b, (((1,), (1,)), ((), ())), preferred_element_type=F32)


def dot_tn(a, b):
    return lax.dot_general(a, b, (((0,), (0,)), ((), ())), preferred_element_type=F32)


def row_grads(left, right, by_head):
    head, core = lax.axis_index("head"), lax.axis_index("seq") % 2
    tokens = left.shape[0]
    chips = lax.axis_size("seq") // 2
    heads = 2 if by_head else 1
    rows = left.shape[1] // (heads * chips * 2)
    split = left.reshape(tokens, heads, chips, 2, rows)
    out = []
    for rel in range(heads):
        plane = pick(split, head ^ rel, 1) if by_head else split[:, 0]
        out.append([pick(plane, core ^ r, 2).reshape(tokens, chips * rows) for r in range(2)])
    if by_head:
        return [[dot_tn(part, right).astype(BF) for part in parts] for parts in out]
    return [[dot_tn(part, r).astype(BF) for part in out[0]] for r in right]


def plain_forward(
    inputs, segment_ids, norm1_gain, w_query, w_key, w_value, w_out, norm2_gain, w_gate, w_up,
    w_down, row_ids, col_ids, first, last, table,
):
    head, seq = lax.axis_index("head"), lax.axis_index("seq")
    n_seq = lax.axis_size("seq")
    rows, width = inputs.shape
    qk = HEADS * QD
    slot = head * n_seq + seq
    small = norm1_gain.shape[0]
    gains = jnp.zeros((2, width // small, small), F32)
    gains = lax.dynamic_update_slice(
        gains, jnp.stack([norm1_gain, norm2_gain]).astype(F32)[:, None, :], (0, slot, 0)
    ).reshape(2, width)
    gains = sum_everywhere(gains)
    gain_first, gain_second = gains[0], gains[1]

    qkv_full = gather_rows(jnp.concatenate([w_query, w_key, w_value], axis=1))
    out_full = gather_rows(w_out)
    gate_w = gather_halves(w_gate, False)
    up_w = gather_halves(w_up, False)
    down_w = gather_halves(w_down.T, True)

    normed_one = rms_scale(inputs, gain_first).astype(BF)
    qkv = dot_nn(normed_one, qkv_full).astype(BF)
    query, keys, values = qkv[:, :qk], qkv[:, qk : 2 * qk], qkv[:, 2 * qk :]
    vcols = HEADS * VD
    t_spec, q_spec = full_spec((8, FEATS)), full_spec((rows, qk))
    one_spec, row_spec = full_spec((rows, 1)), full_spec((1, rows))
    p_spec = pair_spec(rows)
    f32_like = jax.ShapeDtypeStruct((rows, vcols), F32)
    bf_like = jax.ShapeDtypeStruct((rows, vcols), BF)
    state = run(
        state_kernel,
        [t_spec, q_spec, p_spec, one_spec],
        state_specs(),
        STATE_SHAPES,
        (table, keys, values, last),
        flops=8 * rows * qk * FEATS * HEADS,
    )
    num, den = run(
        local_kernel,
        [q_spec, q_spec, p_spec, one_spec, row_spec],
        [p_spec, p_spec],
        [f32_like, f32_like],
        (query, keys, values, row_ids, col_ids),
        [pltpu.VMEM((rows, rows), F32)],
        flops=8 * rows * rows * qk * HEADS,
    )
    before = exchange(*state, segment_ids, rows, True)
    attended, rden = run(
        finish_kernel,
        [t_spec, q_spec, p_spec, p_spec, one_spec] + state_specs(),
        [p_spec, p_spec],
        [bf_like, f32_like],
        (table, query, num, den, first, *before),
        flops=8 * rows * qk * FEATS * HEADS,
    )
    residual = inputs + dot_nn(attended, out_full)
    normed_two = rms_scale(residual, gain_second).astype(BF)

    return (
        gate_w, up_w, down_w, qkv_full, out_full, gain_first, gain_second, normed_one,
        query, keys, values, attended, rden, residual, normed_two, before,
    )


def body(
    layer_input,
    segment_ids,
    norm1_gain,
    w_query,
    w_key,
    w_value,
    w_out,
    norm2_gain,
    w_gate,
    w_up,
    w_down,
    output_grad,
):
    rows = layer_input.shape[1]
    head, seq = lax.axis_index("head"), lax.axis_index("seq")
    n_seq = lax.axis_size("seq")
    qk = HEADS * QD
    inputs = layer_input[0].astype(F32)
    width = inputs.shape[1]

    table = jnp.asarray(feature_table())
    vcols = HEADS * VD
    t_spec, q_spec = full_spec((8, FEATS)), full_spec((rows, qk))
    one_spec, row_spec = full_spec((rows, 1)), full_spec((1, rows))
    p_spec = pair_spec(rows)
    f32_like = jax.ShapeDtypeStruct((rows, vcols), F32)
    bf_like = jax.ShapeDtypeStruct((rows, vcols), BF)
    slot = head * n_seq + seq
    small = norm1_gain.shape[0]

    if n_seq == 16:
        gain_cols = jnp.stack([norm1_gain, norm2_gain], axis=1)
        gain_cols = jnp.pad(gain_cols, ((0, 0), (0, GAIN_COLS - 2)))
        ids = segment_ids.reshape(2 * n_seq, rows)
        ends = jnp.concatenate([ids[:, 0], ids[:, rows - 1]])
        (
            g_own, u_own, d_own, dy_other, n2_other, wq, wo, qkv, attended, rden, residual,
            normed_two, wide, thin, gains,
        ) = forward(
            layer_input[0],
            jnp.concatenate([w_query, w_key, w_value, gain_cols], axis=1),
            w_out,
            [w_gate, w_up, w_down.T],
            output_grad[0],
            ids, table, ends,
        )
        d_gate, d_up, d_down, d_out, grad_attended, grad_middle, y, y_other, grad_gain = (
            feed_forward(
                normed_two, n2_other, output_grad[0], dy_other, residual, [g_own, u_own, d_own],
                attended, wo, gains,
            )
        )
        d_gate, d_up, d_down, d_out, d_qkv, grad_layer, outcome = backward(
            [d_gate, d_up, d_down], d_out, grad_attended, attended, rden, qkv, (wide, thin), wq,
            layer_input[0], grad_middle, y, y_other, gains, grad_gain, ids, table, ends,
        )
        gain_at = 2 * qk + vcols
        return (
            outcome[None],
            grad_layer[None],
            d_qkv[:, gain_at],
            d_qkv[:, :qk],
            d_qkv[:, qk : 2 * qk],
            d_qkv[:, 2 * qk : gain_at],
            d_out,
            d_qkv[:, gain_at + 1],
            d_gate,
            d_up,
            d_down.T,
        )

    segment = 2 * seq + head
    ids = lax.dynamic_slice_in_dim(segment_ids, segment * rows, rows)
    row_ids, col_ids = ids[:, None], ids[None, :]
    first = (row_ids == ids[0]).astype(F32)
    last = (row_ids == ids[rows - 1]).astype(F32)
    (
        gate_w, up_w, down_w, qkv_full, out_full, gain_first, gain_second, normed_one,
        query, keys, values, attended, rden, residual, normed_two, before,
    ) = plain_forward(
        inputs, segment_ids, norm1_gain, w_query, w_key, w_value, w_out, norm2_gain, w_gate,
        w_up, w_down, row_ids, col_ids, first, last, table,
    )

    grad_output = output_grad[0]
    outcome = residual
    grad_normed_two = None
    hiddens, grad_gates, grad_ups = [], [], []
    for w_g, w_u, w_d in zip(gate_w, up_w, down_w):
        gate = dot_nn(normed_two, w_g)
        up_proj = dot_nn(normed_two, w_u)
        grad_hidden = dot_nn(grad_output, w_d)
        hidden, mix_pull = jax.vjp(swish_mix, gate, up_proj)
        grad_gate, grad_up = mix_pull(grad_hidden)
        hiddens.append(hidden.astype(BF))
        grad_gates.append(grad_gate.astype(BF))
        grad_ups.append(grad_up.astype(BF))
        outcome = outcome + dot_nt(hiddens[-1], w_d)
        more = dot_nt(grad_gates[-1], w_g) + dot_nt(grad_ups[-1], w_u)
        grad_normed_two = more if grad_normed_two is None else grad_normed_two + more
    outcome = outcome.astype(BF)
    _, norm_pull = jax.vjp(rms_scale, residual, gain_second)
    grad_resid_two, grad_gain_two = norm_pull(grad_normed_two)
    grad_middle = grad_output.astype(F32) + grad_resid_two
    grad_middle_low = grad_middle.astype(BF)
    grad_attended = dot_nt(grad_middle_low, out_full).astype(BF)

    d_gate = scatter(row_grads(normed_two, grad_gates, False), True)
    d_up = scatter(row_grads(normed_two, grad_ups, False), True)
    d_down = scatter(row_grads(grad_output, hiddens, False), False).T

    d_out = scatter(row_grads(attended, grad_middle_low, True), True)

    grad_state = run(
        grad_state_kernel,
        [t_spec, q_spec, p_spec, p_spec, p_spec, one_spec],
        state_specs(),
        STATE_SHAPES,
        (table, query, grad_attended, attended, rden, first),
        flops=8 * rows * qk * FEATS * HEADS,
    )
    qk_f32 = jax.ShapeDtypeStruct((rows, qk), F32)
    qk_bf = jax.ShapeDtypeStruct((rows, qk), BF)
    grad_query, grad_key, grad_value = run(
        local_grad_kernel,
        [t_spec, q_spec, q_spec, p_spec, p_spec, p_spec, p_spec, one_spec, row_spec, one_spec]
        + state_specs(),
        [q_spec, q_spec, p_spec],
        [qk_bf, qk_f32, f32_like],
        (table, query, keys, values, grad_attended, attended, rden, row_ids, col_ids, first)
        + tuple(before),
        [pltpu.VMEM((rows, rows), F32), pltpu.VMEM((rows, qk), F32), pltpu.VMEM((rows, qk), F32)],
        flops=20 * rows * rows * qk * HEADS,
    )
    after = exchange(*grad_state, segment_ids, rows, False)
    grad_key, grad_value = run(
        finish_grad_kernel,
        [t_spec, q_spec, p_spec, q_spec, p_spec, one_spec] + state_specs(),
        [q_spec, p_spec],
        [qk_bf, bf_like],
        (table, keys, values, grad_key, grad_value, last, *after),
        [pltpu.VMEM((rows, qk), F32)],
        flops=16 * rows * qk * FEATS * HEADS,
    )
    grad_qkv = jnp.concatenate([grad_query, grad_key, grad_value], axis=1)
    d_qkv = scatter(row_grads(normed_one, grad_qkv, True), True)
    grad_normed_one = dot_nt(grad_qkv, qkv_full)
    _, first_pull = jax.vjp(rms_scale, inputs, gain_first)
    grad_inputs, grad_gain_one = first_pull(grad_normed_one)
    grad_layer = grad_middle + grad_inputs
    grad_gains = sum_everywhere(jnp.stack([grad_gain_one, grad_gain_two]))
    grad_gains = lax.dynamic_slice_in_dim(
        grad_gains.reshape(2, width // small, small), slot, 1, 1
    )[:, 0]
    return (
        outcome[None],
        grad_layer[None],
        grad_gains[0],
        d_qkv[:, :qk],
        d_qkv[:, qk : 2 * qk],
        d_qkv[:, 2 * qk :],
        d_out,
        grad_gains[1],
        d_gate,
        d_up,
        d_down,
    )


def solution(mesh):
    split = P(("head", "seq"))
    rows = P(("head", "seq"), None)
    block = P("seq", "head", None)
    wide, tall = P("seq", "head"), P("head", "seq")
    in_specs = (block, P(), split, rows, rows, rows, rows, split, wide, wide, tall, block)
    out_specs = (block, block, split, rows, rows, rows, rows, split, wide, wide, tall)
    return jax.shard_map(body, mesh=mesh, in_specs=in_specs, out_specs=out_specs, check_vma=False)
```

```python
import functools

import jax
import jax.numpy as jnp
import numpy as np
from jax import lax
from jax.experimental import pallas as pl
from jax.experimental.pallas import tpu as pltpu
from jax.sharding import PartitionSpec as P

HEADS = 16
QD = 16
VD = 64
DOC_MAX = 4096
EPSILON = 1e-05
PAIRS = HEADS // 2
WIDE = 2 * VD
FEATS = 160
TILE = 256
LANES = 128

BF = jnp.bfloat16
F32 = jnp.float32


def flip_seq(value, code):
    n = lax.axis_size("seq")
    return lax.ppermute(value, "seq", [(i, i ^ code) for i in range(n)])


def flip_head(value):
    n = lax.axis_size("head")
    return lax.ppermute(value, "head", [(i, i ^ 1) for i in range(n)])


def shift_seq(value, distance):
    n = lax.axis_size("seq")
    return lax.ppermute(
        value, "seq", [(i, i + distance) for i in range(n) if 0 <= i + distance < n]
    )


def layout():
    chips = lax.axis_size("seq") // 2
    near = 2 if chips <= 8 else 8
    far = chips // near
    return far, near


def place_kernel(groups, count, *refs):
    pieces, out, sem = refs[:count], refs[count], refs[count + 1]
    me = lax.axis_index("seq")
    head = lax.axis_index("head")
    n = lax.axis_size("seq")
    copies = []
    for piece, blocks in zip(pieces, groups):
        for index, (rel_head, rel_seq) in blocks:
            place = me ^ rel_seq
            if rel_head is not None:
                place = place + (head ^ rel_head) * n
            copies.append(
                pltpu.make_async_copy(piece.at[index], out.at[place], sem.at[len(copies)])
            )
    for copy in copies:
        copy.start()
    for copy in copies:
        copy.wait()


def place(pieces, groups, blocks):
    rows, cols = pieces[0].shape[-2:]
    total = sum(len(g) for g in groups)
    out = pl.pallas_call(
        functools.partial(place_kernel, groups, len(pieces)),
        out_shape=jax.ShapeDtypeStruct((blocks, rows, cols), pieces[0].dtype),
        in_specs=[pl.BlockSpec(memory_space=pl.ANY)] * len(pieces),
        out_specs=pl.BlockSpec(memory_space=pltpu.VMEM),
        scratch_shapes=[pltpu.SemaphoreType.DMA((total,))],
        compiler_params=pltpu.CompilerParams(vmem_limit_bytes=16 << 20),
        cost_estimate=pl.CostEstimate(
            flops=0, bytes_accessed=4 * blocks * rows * cols, transcendentals=0
        ),
        name="place",
    )(*pieces)
    return out.reshape(blocks * rows, cols)


def gather(shard, head_first):
    far, near = layout()
    far_codes = [2 * near * r for r in range(far)]
    near_codes = [2 * r for r in range(near)]
    if head_first:
        shard = jnp.stack([shard, flip_head(shard)])
    column = jnp.stack([shard] + [flip_seq(shard, code) for code in far_codes[1:]])
    held = [(column, 0, 0)]
    held += [(flip_seq(column, code), 0, code) for code in near_codes[1:]]
    if not head_first:
        held += [(flip_head(buf), 1, code) for buf, _, code in held]
    held += [(flip_seq(buf, 1), rel, code + 1) for buf, rel, code in held]
    result = []
    for buf, rel, code in held:
        if head_first:
            blocks = [((r, g), (g, code + far_codes[r])) for r in range(far) for g in range(2)]
        else:
            blocks = [((r,), (rel, code + far_codes[r])) for r in range(far)]
        result.append((buf, blocks))
    return result


def gather_rows(shard):
    got = gather(shard, False)
    return place([b for b, _ in got], [g for _, g in got], 2 * lax.axis_size("seq"))


def gather_halves(shard, head_first):
    got = gather(shard, head_first)
    halves = []
    for rel in range(2):
        pieces, groups = [], []
        for buf, blocks in got:
            mine = [(i, (None, code)) for i, (r, code) in blocks if r == rel]
            if mine:
                pieces.append(buf)
                groups.append(mine)
        halves.append(place(pieces, groups, lax.axis_size("seq")))
    return halves


def add_low(*terms):
    total = terms[0].astype(F32)
    for term in terms[1:]:
        total = total + term.astype(F32)
    return total.astype(BF)


def pick(value, index, axis):
    return lax.dynamic_index_in_dim(value, index, axis, keepdims=False)


def scatter(grads, head_first):
    far, near = layout()
    seq = lax.axis_index("seq")
    far_at, near_at = seq // (2 * near), (seq // 2) % near
    both = [
        add_low(grads[rel][0], flip_seq(grads[rel][1], 1)) for rel in range(2)
    ]
    rows = both[0].shape[0] // (far * near)
    cols = both[0].shape[1]
    if head_first:
        whole = add_low(both[0], flip_head(both[1])).reshape(far, near, rows, cols)
    else:
        whole = jnp.stack(both).reshape(2, far, near, rows, cols).transpose(1, 2, 0, 3, 4)
    parts = [pick(whole, near_at, 1)]
    parts += [flip_seq(pick(whole, near_at ^ r, 1), 2 * r) for r in range(1, near)]
    column = add_low(*parts)
    parts = [pick(column, far_at, 0)]
    parts += [flip_seq(pick(column, far_at ^ r, 0), 2 * near * r) for r in range(1, far)]
    if head_first:
        return sum(part.astype(F32) for part in parts)
    both = add_low(*parts)
    return both[0].astype(F32) + flip_head(both[1]).astype(F32)


def sum_everywhere(value):
    value = value + flip_head(value)
    code = 1
    while code < lax.axis_size("seq"):
        value = value + flip_seq(value, code)
        code *= 2
    return value


def feature_table():
    first, second, one, two, scale = [], [], [], [], []
    for a in range(QD):
        for b in range(a, QD):
            first.append(a)
            second.append(b)
            one.append(0.0)
            two.append(0.0)
            scale.append((1.0 if a == b else 2.0) / (2.0 * QD))
    for a in range(QD):
        first.append(a)
        second.append(-1000)
        one.append(0.0)
        two.append(1.0)
        scale.append(QD**-0.5)
    first.append(-1000)
    second.append(-1000)
    one.append(1.0)
    two.append(1.0)
    scale.append(1.0)
    pad = FEATS - len(first)
    table = np.zeros((8, FEATS), np.float32)
    table[0] = np.array(first + [-1000] * pad)
    table[1] = np.array(second + [-1000] * pad)
    table[2] = np.array(one + [0.0] * pad)
    table[3] = np.array(two + [0.0] * pad)
    table[4] = np.array(scale + [0.0] * pad)
    return table


def mm(a, b, dims):
    return lax.dot_general(a, b, ((dims[0], dims[1]), ((), ())), preferred_element_type=F32)


NN = ((1,), (0,))
NT = ((1,), (1,))
TN = ((0,), (0,))


def selectors(table, head, lanes=HEADS * QD):
    row = (lax.broadcasted_iota(jnp.int32, (lanes, FEATS), 0) - head * QD).astype(F32)
    one = (row == table[0:1, :]).astype(F32).astype(BF)
    two = (row == table[1:2, :]).astype(F32).astype(BF)
    return one, two


def factors(values, table, sel):
    return (
        mm(values, sel[0], NN) + table[2:3, :],
        mm(values, sel[1], NN) + table[3:4, :],
    )


def half_mask(rows, part):
    lane = lax.broadcasted_iota(jnp.int32, (rows, WIDE), 1)
    return (lane >= VD) if part else (lane < VD)


def head_mask(rows, head, lanes=HEADS * QD):
    lane = lax.broadcasted_iota(jnp.int32, (rows, lanes), 1)
    return (lane >= head * QD) & (lane < (head + 1) * QD)


def keep(mask, value):
    return jnp.where(mask, value.astype(F32), 0.0).astype(BF)


def state_kernel(table_ref, keys_ref, values_ref, last_ref, wide_ref, thin_ref):
    pair = pl.program_id(0)
    table = table_ref[...]
    keys = keys_ref[...]
    rows = keys.shape[0]
    last = last_ref[...]
    total = None
    for part in range(2):
        sel = selectors(table, 2 * pair + part)
        one, two = factors(keys, table, sel)
        phi = one * two * last
        value = keep(half_mask(rows, part), values_ref[...])
        new = mm(phi.astype(BF), value, TN)
        total = new if total is None else total + new
        thin_ref[0, part : part + 1, :] = jnp.sum(phi, axis=0, keepdims=True)
    thin_ref[0, 2:, :] = jnp.zeros((6, FEATS), F32)
    wide_ref[0] = total.astype(BF)


def visible_tile(mask_ref, row_ids_ref, col_ids_ref, rows):
    for i in range(rows // TILE):
        for j in range(i + 1):
            same = (
                row_ids_ref[i * TILE : (i + 1) * TILE, :]
                == col_ids_ref[:, j * TILE : (j + 1) * TILE]
            )
            if i == j:
                same = same & (
                    lax.broadcasted_iota(jnp.int32, (TILE, TILE), 1)
                    <= lax.broadcasted_iota(jnp.int32, (TILE, TILE), 0)
                )
            mask_ref[i * TILE : (i + 1) * TILE, j * TILE : (j + 1) * TILE] = same.astype(F32)


def local_kernel(
    query_ref, keys_ref, values_ref, row_ids_ref, col_ids_ref, num_ref, den_ref, mask_ref
):
    pair = pl.program_id(0)
    rows = query_ref.shape[0]

    @pl.when(pair == 0)
    def _():
        visible_tile(mask_ref, row_ids_ref, col_ids_ref, rows)

    for i in range(rows // TILE):
        here = slice(i * TILE, (i + 1) * TILE)
        num = jnp.zeros((TILE, WIDE), F32)
        dens = []
        for part in range(2):
            head = 2 * pair + part
            query = keep(head_mask(TILE, head), query_ref[here, :] * (QD**-0.5))
            den = jnp.zeros((TILE, 1), F32)
            for j in range(i + 1):
                there = slice(j * TILE, (j + 1) * TILE)
                s = mm(query, keys_ref[there, :], NT)
                w = (1.0 + s + 0.5 * s * s) * mask_ref[here, there]
                den = den + jnp.sum(w, axis=1, keepdims=True)
                num = num + mm(
                    w.astype(BF), keep(half_mask(TILE, part), values_ref[there, :]), NN
                )
            dens.append(den)
        num_ref[here, :] = num
        den_ref[here, :] = jnp.where(half_mask(TILE, 0), dens[0], dens[1])


def finish_kernel(
    table_ref, query_ref, num_ref, den_ref, first_ref, wide_ref, thin_ref, out_ref, rden_ref
):
    pair = pl.program_id(0)
    table = table_ref[...]
    query = query_ref[...]
    rows = query.shape[0]
    first = first_ref[...]
    num, den = num_ref[...], den_ref[...]
    for part in range(2):
        sel = selectors(table, 2 * pair + part)
        one, two = factors(query, table, sel)
        phi = one * two * (table[4:5, :] * first)
        mask = half_mask(rows, part)
        extra = mm(phi.astype(BF), wide_ref[0], NN)
        num = num + jnp.where(mask, extra, 0.0)
        more = jnp.sum(phi * thin_ref[0, part : part + 1, :], axis=1, keepdims=True)
        den = den + jnp.where(mask, more, 0.0)
    rden = 1.0 / den
    rden_ref[...] = rden
    out_ref[...] = (num * rden).astype(BF)


def prepare(grad_ref, out_ref, rden_ref):
    rows = grad_ref.shape[0]
    grad = grad_ref[...].astype(F32)
    rden = rden_ref[...]
    dnum = (grad * rden).astype(BF)
    prod = grad * out_ref[...].astype(F32) * rden
    deltas = [
        jnp.sum(jnp.where(half_mask(rows, part), prod, 0.0), axis=1, keepdims=True)
        for part in range(2)
    ]
    return dnum, deltas


def grad_state_kernel(
    table_ref, query_ref, grad_ref, out_ref, rden_ref, first_ref, wide_ref, thin_ref
):
    pair = pl.program_id(0)
    table = table_ref[...]
    query = query_ref[...]
    rows = query.shape[0]
    dnum, deltas = prepare(grad_ref, out_ref, rden_ref)
    total = None
    for part in range(2):
        sel = selectors(table, 2 * pair + part)
        one, two = factors(query, table, sel)
        phi = one * two * (table[4:5, :] * first_ref[...])
        new = mm(phi.astype(BF), keep(half_mask(rows, part), dnum), TN)
        total = new if total is None else total + new
        thin_ref[0, part : part + 1, :] = -jnp.sum(phi * deltas[part], axis=0, keepdims=True)
    thin_ref[0, 2:, :] = jnp.zeros((6, FEATS), F32)
    wide_ref[0] = total.astype(BF)


def local_grad_kernel(
    table_ref,
    query_ref,
    keys_ref,
    values_ref,
    grad_ref,
    out_ref,
    rden_ref,
    row_ids_ref,
    col_ids_ref,
    first_ref,
    wide_ref,
    thin_ref,
    dq_ref,
    dk_ref,
    dv_ref,
    mask_ref,
    dq_acc,
    dk_acc,
):
    pair = pl.program_id(0)
    table = table_ref[...]
    query = query_ref[...]
    keys = keys_ref[...]
    rows = query.shape[0]
    tiles = rows // TILE
    scale = QD**-0.5

    @pl.when(pair == 0)
    def _():
        visible_tile(mask_ref, row_ids_ref, col_ids_ref, rows)
        dq_acc[...] = jnp.zeros_like(dq_acc)
        dk_acc[...] = jnp.zeros_like(dk_acc)

    dnum, deltas = prepare(grad_ref, out_ref, rden_ref)
    dv = [jnp.zeros((TILE, WIDE), F32) for _ in range(tiles)]
    for part in range(2):
        head = 2 * pair + part
        at_head = head_mask(rows, head)
        q_head = keep(at_head, query * scale)
        k_head = keep(at_head, keys * scale)
        d_head = keep(half_mask(rows, part), dnum)
        for i in range(tiles):
            here = slice(i * TILE, (i + 1) * TILE)
            dq = dq_acc[here, :]
            for j in range(i + 1):
                there = slice(j * TILE, (j + 1) * TILE)
                s = mm(q_head[here], keys[there], NT)
                mask = mask_ref[here, there]
                w = ((1.0 + s + 0.5 * s * s) * mask).astype(BF)
                dp = mm(d_head[here], values_ref[there, :], NT)
                ds = ((dp - deltas[part][here]) * ((1.0 + s) * mask)).astype(BF)
                dq = dq + mm(ds, k_head[there], NN)
                dk_acc[there, :] += mm(ds, q_head[here], TN)
                dv[j] = dv[j] + mm(w, d_head[here], TN)
            dq_acc[here, :] = dq
        sel = selectors(table, head)
        one, two = factors(query, table, sel)
        dphi = mm(d_head, wide_ref[0], NT) - deltas[part] * thin_ref[0, part : part + 1, :]
        dphi = dphi * (table[4:5, :] * first_ref[...])
        dq_acc[...] += mm((dphi * two).astype(BF), sel[0], NT) + mm(
            (dphi * one).astype(BF), sel[1], NT
        )
    for j in range(tiles):
        dv_ref[j * TILE : (j + 1) * TILE, :] = dv[j]

    @pl.when(pair == PAIRS - 1)
    def _():
        dq_ref[...] = dq_acc[...].astype(BF)
        dk_ref[...] = dk_acc[...]


def finish_grad_kernel(
    table_ref, keys_ref, values_ref, dk_in_ref, dv_in_ref, last_ref, wide_ref, thin_ref,
    dk_ref, dv_ref, dk_acc,
):
    pair = pl.program_id(0)
    table = table_ref[...]
    keys = keys_ref[...]
    rows = keys.shape[0]
    last = last_ref[...]

    @pl.when(pair == 0)
    def _():
        dk_acc[...] = dk_in_ref[...]

    dv = dv_in_ref[...]
    for part in range(2):
        sel = selectors(table, 2 * pair + part)
        one, two = factors(keys, table, sel)
        mask = half_mask(rows, part)
        phi = one * two * last
        dv = dv + jnp.where(mask, mm(phi.astype(BF), wide_ref[0], NN), 0.0)
        dphi = mm(keep(mask, values_ref[...]), wide_ref[0], NT) + thin_ref[0, part : part + 1, :]
        dphi = dphi * last
        dk_acc[...] += mm((dphi * two).astype(BF), sel[0], NT) + mm(
            (dphi * one).astype(BF), sel[1], NT
        )
    dv_ref[...] = dv.astype(BF)

    @pl.when(pair == PAIRS - 1)
    def _():
        dk_ref[...] = dk_acc[...].astype(BF)


def full_spec(shape):
    return pl.BlockSpec(shape, lambda p: (0,) * len(shape))


def pair_spec(rows):
    return pl.BlockSpec((rows, WIDE), lambda p: (0, p))


def state_specs():
    return [
        pl.BlockSpec((1, FEATS, WIDE), lambda p: (p, 0, 0)),
        pl.BlockSpec((1, 8, FEATS), lambda p: (p, 0, 0)),
    ]


STATE_SHAPES = (
    jax.ShapeDtypeStruct((PAIRS, FEATS, WIDE), BF),
    jax.ShapeDtypeStruct((PAIRS, 8, FEATS), F32),
)


def run(kernel, in_specs, out_specs, out_shape, args, scratch=(), flops=0):
    moved = sum(a.size * a.dtype.itemsize for a in args)
    return pl.pallas_call(
        kernel,
        grid=(PAIRS,),
        in_specs=in_specs,
        out_specs=out_specs,
        out_shape=out_shape,
        scratch_shapes=scratch,
        compiler_params=pltpu.CompilerParams(vmem_limit_bytes=48 << 20),
        cost_estimate=pl.CostEstimate(flops=flops, bytes_accessed=moved, transcendentals=0),
        name=kernel.__name__,
    )(*args)


def exchange(wide, thin, ids, rows, forward):
    head, seq = lax.axis_index("head"), lax.axis_index("seq")
    n = lax.axis_size("seq")
    segments = 2 * n
    firsts = ids.reshape(segments, rows)[:, 0]
    lasts = ids.reshape(segments, rows)[:, rows - 1]
    step = 1 if forward else -1
    near_end, far_end = (lasts, firsts) if forward else (firsts, lasts)

    def end_of(which, segment):
        return which[jnp.clip(segment, 0, segments - 1)]

    seg = 2 * seq + head
    takes = end_of(far_end, seg)
    core = seq % 2
    late_head = head if forward else 1 - head
    late_core = core if forward else 1 - core

    def gate(flag):
        return jnp.where(flag, 1.0, 0.0).astype(F32)

    def wider(state):
        return [part.astype(F32) for part in state]

    def narrow(state):
        return [state[0].astype(BF), state[1]]

    def merge(own, other, late, other_takes, joined):
        gained = [part * (gate(other_takes) * late) for part in other]
        own_factor = jnp.where(late == 1, 1.0, gate(joined))
        other_factor = jnp.where(late == 1, gate(joined), 1.0)
        joint = [a * own_factor + b * other_factor for a, b in zip(own, other)]
        return gained, joint

    own = [wide, thin]
    other = [flip_head(part) for part in own]
    first_of, second_of = 2 * seq, 2 * seq + 1
    if not forward:
        first_of, second_of = second_of, first_of
    total, joint = merge(
        wider(own),
        wider(other),
        late_head,
        end_of(near_end, seg - step) == takes,
        end_of(near_end, first_of) == end_of(near_end, second_of),
    )
    joint = narrow(joint)
    other = [flip_seq(part, 1) for part in joint]
    base = 4 * (seq // 2)
    early_end, late_end = (base + 1, base + 3) if forward else (base + 2, base)
    gained, joint = merge(
        wider(joint),
        wider(other),
        late_core,
        end_of(near_end, early_end) == takes,
        end_of(near_end, early_end) == end_of(near_end, late_end),
    )
    total = [a + b for a, b in zip(total, gained)]
    joint = narrow(joint)
    half = PAIRS // 2
    mine = [lax.dynamic_slice_in_dim(part, core * half, half, 0) for part in joint]
    hops = -(-DOC_MAX // (4 * rows))
    far = None
    for hop in range(1, hops + 1):
        got = wider([shift_seq(part, 2 * hop * step) for part in mine])
        nearer, farther = late_end - 4 * step, late_end - 4 * step * hop
        joined = gate(end_of(near_end, nearer) == end_of(near_end, farther))
        got = [part * joined for part in got]
        far = got if far is None else [a + b for a, b in zip(far, got)]
    far = narrow(far)
    other = [flip_seq(part, 1) for part in far]
    comes = (seq // 2 >= 1) if forward else (seq // 2 < n // 2 - 1)
    use = gate(comes & (end_of(near_end, late_end - 4 * step) == takes))
    result = []
    for a, b, so_far in zip(far, other, total):
        low = jnp.where(core == 0, a, b).astype(F32)
        high = jnp.where(core == 0, b, a).astype(F32)
        result.append(so_far + use * jnp.concatenate([low, high], axis=0))
    return narrow(result)


MESH = pl.DeviceIdType.MESH
GAIN_COLS = 128


class Links:
    def __init__(self):
        self.head, self.seq = lax.axis_index("head"), lax.axis_index("seq")
        self.n = lax.axis_size("seq")
        self.z, self.y, self.c = self.seq // 4, (self.seq // 2) % 2, self.seq % 2
        self.core = self.at(self.head, self.seq ^ 1)
        self.x = self.at(1 - self.head, self.seq)
        self.near = self.at(self.head, self.seq ^ 2)
        self.far = [self.at(self.head, self.seq ^ (4 * r)) for r in range(4)]

    def at(self, head, seq):
        return {"head": head, "seq": seq}

    def shifted(self, distance):
        return self.at(self.head, lax.rem(self.seq + distance + self.n, self.n))

    def greet(self):
        barrier = pltpu.get_barrier_semaphore()
        partners = [self.core, self.x, self.near] + self.far[1:]
        partners += [self.shifted(d) for d in (2, 4, -2, -4)]
        for partner in partners:
            pl.semaphore_signal(barrier, inc=1, device_id=partner, device_id_type=MESH)
        pl.semaphore_wait(barrier, len(partners))


class Copies:
    def __init__(self, send, recv, local):
        self.send, self.recv, self.local = send, recv, local
        self.used, self.used_local = 0, 0
        self.started, self.started_local = [], []

    def remote(self, src, dst, partner):
        i = self.used
        self.used += 1
        return pltpu.make_async_remote_copy(
            src_ref=src,
            dst_ref=dst,
            send_sem=self.send.at[i],
            recv_sem=self.recv.at[i],
            device_id=partner,
            device_id_type=MESH,
        )

    def go(self, *copies):
        for copy in copies:
            copy.start()
            self.started.append(copy)

    def keep(self, src, dst):
        copy = pltpu.make_async_copy(src, dst, self.local.at[self.used_local])
        self.used_local += 1
        copy.start()
        self.started_local.append(copy)
        return copy

    def finish(self, copy):
        copy.wait()
        self.started_local = [other for other in self.started_local if other is not copy]

    def drain(self):
        for copy in self.started:
            copy.wait_send()
        for copy in self.started_local:
            copy.wait()


def arrived(*copies):
    for copy in copies:
        copy.wait_recv()


class WideGather:
    def __init__(self, copies, links, shard, own, other, other_there, near_last=False):
        n, y, c = links, links.y, links.c
        self.copies, self.near_last = copies, near_last
        self.place = own.at[n.z, y, c]
        self.shard = shard
        self.far = [copies.remote(shard, self.place, n.far[r]) for r in range(1, 4)]
        mine, theirs = own.at[:, y, c], own.at[:, 1 - y, c]
        self.near = copies.remote(mine, mine, n.near)
        across = other.at[:, y, c]
        self.cross = copies.remote(mine, other_there.at[:, y, c], n.x)
        if near_last:
            self.last = copies.remote(across, across, n.near)
        else:
            self.last = copies.remote(theirs, other_there.at[:, 1 - y, c], n.x)
        self.core = [
            copies.remote(part, part, n.core)
            for part in (mine, theirs, other.at[:, y, c], other.at[:, 1 - y, c])
        ]

    def begin(self):
        self.copies.go(*self.far)
        self.own = self.copies.keep(self.shard, self.place)

    def far_here(self):
        arrived(*self.far)
        self.copies.finish(self.own)

    def one(self):
        self.copies.go(self.near, self.cross, self.core[0])

    def two(self):
        arrived(self.near)
        if not self.near_last:
            self.copies.go(self.last)
        self.copies.go(self.core[1])

    def three(self):
        arrived(self.cross)
        if self.near_last:
            self.copies.go(self.last)
        self.copies.go(self.core[2])

    def four(self):
        arrived(self.last)
        self.copies.go(self.core[3])

    def end(self):
        arrived(*self.core)


class PlaneGather:
    COPIES = 6

    def __init__(self, copies, links, shard, own):
        n, y, c = links, links.y, links.c
        self.copies, self.shard, self.place = copies, shard, own.at[n.z, y, c]
        self.far = [copies.remote(shard, self.place, n.far[r]) for r in range(1, 4)]
        mine, theirs = own.at[:, y, c], own.at[:, 1 - y, c]
        self.near = copies.remote(mine, mine, n.near)
        self.core = [copies.remote(part, part, n.core) for part in (mine, theirs)]

    def begin(self):
        self.copies.go(*self.far)
        self.own = self.copies.keep(self.shard, self.place)

    def far_here(self):
        arrived(*self.far)
        self.copies.finish(self.own)

    def one(self):
        self.copies.go(self.near, self.core[0])

    def two(self):
        arrived(self.near)
        self.copies.go(self.core[1])

    def end(self):
        arrived(*self.core)


class Exchange:
    def __init__(self, copies, links, gates, first, bufs, forward):
        n = links
        self.copies, self.gates, self.first, self.bufs = copies, gates, first, bufs
        half = PAIRS // 2
        step = 2 if forward else -2
        own, a, j, b, j2, r1, r2, far = bufs

        def both(src, dst, partner, groups=4):
            size = src[0].shape[0] // groups
            cuts = [pl.ds(i * size, size) for i in range(groups)]
            made = [copies.remote(src[0].at[cut], dst[0].at[cut], partner) for cut in cuts]
            return made + [copies.remote(src[1], dst[1], partner)]

        def halves(state):
            return [
                state[0].at[pl.ds(n.c * half, half)],
                state[1].at[pl.ds(n.c * half, half)],
            ]

        self.rounds = [
            both(own, a, n.x),
            both(j, b, n.core, 1),
            both(halves(j2), r1, n.shifted(step)) + both(halves(j2), r2, n.shifted(2 * step)),
            both(halves(far), halves(far), n.core, 1),
        ]
        self.halves = halves
        self.total = None

    def gate(self, i):
        return self.gates[self.first + i]

    def begin(self):
        self.copies.go(*self.rounds[0])

    def one(self):
        own, a, j, b, j2, r1, r2, far = self.bufs
        arrived(*self.rounds[0])
        for s, d, t in zip(own, a, j):
            t[...] = (
                s[...].astype(F32) * self.gate(1) + d[...].astype(F32) * self.gate(2)
            ).astype(t.dtype)
        self.copies.go(*self.rounds[1])

    def two(self):
        own, a, j, b, j2, r1, r2, far = self.bufs
        arrived(*self.rounds[1])
        for s, d, t in zip(j, b, j2):
            t[...] = (
                s[...].astype(F32) * self.gate(4) + d[...].astype(F32) * self.gate(5)
            ).astype(t.dtype)
        self.copies.go(*self.rounds[2])

    def three(self):
        own, a, j, b, j2, r1, r2, far = self.bufs
        arrived(*self.rounds[2])
        for s, d, t in zip(r1, r2, self.halves(far)):
            t[...] = (s[...].astype(F32) + d[...].astype(F32) * self.gate(6)).astype(t.dtype)
        self.copies.go(*self.rounds[3])

    def four(self, out):
        own, a, j, b, j2, r1, r2, far = self.bufs
        arrived(*self.rounds[3])
        for s, d, f, t in zip(a, b, far, out):
            t[...] = (
                s[...].astype(F32) * self.gate(0)
                + d[...].astype(F32) * self.gate(3)
                + f[...].astype(F32) * self.gate(7)
            ).astype(t.dtype)


def exchange_shapes():
    shapes = []
    for name in range(8):
        pairs = PAIRS // 2 if name in (5, 6) else PAIRS
        shapes += [pltpu.VMEM((pairs, FEATS, WIDE), BF), pltpu.VMEM((pairs, 8, FEATS), F32)]
    return shapes


def documents(ids_ref, ends_ref, links, mask, first, last):
    rows = ids_ref.shape[1]
    segment = 2 * links.seq + links.head
    row = ids_ref[pl.ds(segment, 1), :].astype(F32)
    column = jnp.transpose(jnp.broadcast_to(row, (128, rows)))[:, :1]
    visible_tile(mask, column, row, rows)
    first[...] = (column == ends_ref[segment].astype(F32)).astype(F32)
    last[...] = (column == ends_ref[2 * links.n + segment].astype(F32)).astype(F32)


def exchange_gates(ends_ref, links, forward):
    head, seq, core, n = links.head, links.seq, links.c, links.n
    segments = 2 * n
    step = 1 if forward else -1
    near_at, far_at = (segments, 0) if forward else (0, segments)
    seg = 2 * seq + head
    chip = seq // 2
    base = 4 * chip
    late_head = (head == 1) if forward else (head == 0)
    late_core = (core == 1) if forward else (core == 0)
    pair_early, pair_late = (2 * seq, 2 * seq + 1) if forward else (2 * seq + 1, 2 * seq)
    early_end, late_end = (base + 1, base + 3) if forward else (base + 2, base)
    near_ok = (chip >= 1) if forward else (chip < n // 2 - 1)
    far_ok = (chip >= 2) if forward else (chip < n // 2 - 2)

    def doc(segment):
        return ends_ref[near_at + jnp.minimum(jnp.maximum(segment, 0), segments - 1)]

    def factor(flag):
        return jnp.where(flag, 1.0, 0.0).astype(F32)

    takes = ends_ref[far_at + seg]
    joined = doc(pair_early) == doc(pair_late)
    joined2 = doc(early_end) == doc(late_end)
    nearer, farther = doc(late_end - 4 * step), doc(late_end - 8 * step)
    flags = [
        late_head & (doc(seg - step) == takes),
        late_head | joined,
        jnp.logical_not(late_head) | joined,
        late_core & (doc(early_end) == takes),
        late_core | joined2,
        jnp.logical_not(late_core) | joined2,
        far_ok & (nearer == farther),
        near_ok & (nearer == takes),
    ]
    return [factor(flag) for flag in flags]


def pair_lanes(pair, start=0):
    return pl.ds(pl.multiple_of(start + pair * WIDE, WIDE), WIDE)


def head_tile(pair, part):
    tile = pair // (LANES // (2 * QD))
    return tile, 2 * pair + part - tile * (LANES // QD)


def tile_lanes(pair, start=0):
    return pl.ds(pl.multiple_of(start + head_tile(pair, 0)[0] * LANES, LANES), LANES)


def state_pair(pair, table, qkv, last, wide_ref, thin_ref):
    rows = qkv.shape[0]
    qk = HEADS * QD
    keys, value = qkv[:, tile_lanes(pair, qk)], qkv[:, pair_lanes(pair, 2 * qk)]
    total = None
    for part in range(2):
        sel = selectors(table, head_tile(pair, part)[1], LANES)
        one, two = factors(keys, table, sel)
        phi = one * two * last
        new = mm(phi.astype(BF), keep(half_mask(rows, part), value), TN)
        total = new if total is None else total + new
        thin_ref[pair, part : part + 1, :] = jnp.sum(phi, axis=0, keepdims=True)
    thin_ref[pair, 2:, :] = jnp.zeros((6, FEATS), F32)
    wide_ref[pair] = total.astype(BF)


def local_pair(pair, qkv, num_ref, den_ref, mask_ref):
    rows = qkv.shape[0]
    qk = HEADS * QD
    for i in range(rows // TILE):
        here = slice(i * TILE, (i + 1) * TILE)
        num = jnp.zeros((TILE, WIDE), F32)
        dens = []
        for part in range(2):
            head = head_tile(pair, part)[1]
            query = keep(
                head_mask(TILE, head, LANES), qkv[here, tile_lanes(pair)] * (QD**-0.5)
            )
            den = jnp.zeros((TILE, 1), F32)
            for j in range(i + 1):
                there = slice(j * TILE, (j + 1) * TILE)
                s = mm(query, qkv[there, tile_lanes(pair, qk)], NT)
                w = (1.0 + s + 0.5 * s * s) * mask_ref[here, there]
                den = den + jnp.sum(w, axis=1, keepdims=True)
                value = qkv[there, pair_lanes(pair, 2 * qk)]
                num = num + mm(w.astype(BF), keep(half_mask(TILE, part), value), NN)
            dens.append(den)
        num_ref[here, pair_lanes(pair)] = num
        den_ref[here, pair_lanes(pair)] = jnp.where(half_mask(TILE, 0), dens[0], dens[1])


def finish_pair(pair, table, qkv, first, num_ref, den_ref, wide_ref, thin_ref, out_ref):
    rows = qkv.shape[0]
    query = qkv[:, tile_lanes(pair)]
    lanes = pair_lanes(pair)
    num, den = num_ref[:, lanes], den_ref[:, lanes]
    for part in range(2):
        sel = selectors(table, head_tile(pair, part)[1], LANES)
        one, two = factors(query, table, sel)
        phi = one * two * (table[4:5, :] * first)
        mask = half_mask(rows, part)
        num = num + jnp.where(mask, mm(phi.astype(BF), wide_ref[pair], NN), 0.0)
        more = jnp.sum(phi * thin_ref[pair, part : part + 1, :], axis=1, keepdims=True)
        den = den + jnp.where(mask, more, 0.0)
    rden = 1.0 / den
    den_ref[:, lanes] = rden
    out_ref[:, lanes] = (num * rden).astype(BF)


def each_pair(low, high, step):
    def one(pair, carry):
        step(pair)
        return carry

    lax.fori_loop(low, high, one, 0)


WIDE_COPIES, EXCHANGE_COPIES = 10, 19
FWD_COPIES = 3 * WIDE_COPIES + 6 * PlaneGather.COPIES + EXCHANGE_COPIES + 1
FWD_LOCALS = 20


def forward_kernel(
    x_ref, wq_ref, wk_ref, wv_ref, gs_in, os_ref, gs_ref, us_ref, ds_ref, ids_ref, table_ref,
    dy_ref, ends_ref,
    g_own, u_own, d_own, dy_out, wq_out, wo_out, qkv_out, att_out, rden_out,
    res_out, n2_out, wide_out, thin_out, gain_out,
    wq, wo, normed, qkv, num, den, mask, first_ref, last_ref, att, res, n2, wide, thin, gain,
    qs_ref, *rest,
):
    bufs, (send, recv, local) = rest[:16], rest[16:]
    states = [(bufs[2 * i], bufs[2 * i + 1]) for i in range(8)]
    n = Links()
    copies = Copies(send, recv, local)
    rows, width = x_ref.shape
    qk, hv = HEADS * QD, HEADS * VD
    cut = 7 * 128
    full = wq.shape[-1]

    def side(ref, head, lo=None, hi=None):
        return ref.at[head] if lo is None else ref.at[head, :, :, :, :, pl.ds(lo, hi - lo)]

    q_parts = []
    for lo, hi in ((0, cut), (cut, full)):
        shard = qs_ref.at[:, pl.ds(lo, hi - lo)]
        own, other = side(wq, n.head, lo, hi), side(wq, 1 - n.head, lo, hi)
        q_parts.append(WideGather(copies, n, shard, own, other, own, near_last=lo > 0))
    own, other = side(wo, n.head), side(wo, 1 - n.head)
    outs = WideGather(copies, n, os_ref, own, other, own)
    middle, ff = 6 * 128, ds_ref.shape[-1]
    ffn = []
    for shard, own in ((gs_ref, g_own), (us_ref, u_own), (ds_ref, d_own)):
        for lo, hi in ((0, middle), (middle, ff)):
            part = own.at[:, :, :, :, pl.ds(lo, hi - lo)]
            ffn.append(PlaneGather(copies, n, shard.at[:, pl.ds(lo, hi - lo)], part))

    def pass_on(i):
        ffn[i].far_here()
        ffn[i].one()
        if i + 2 < len(ffn):
            ffn[i + 2].begin()
        if i >= 2:
            ffn[i - 2].two()

    other_dy = copies.remote(dy_ref, dy_out, n.x)
    swap = Exchange(copies, n, exchange_gates(ends_ref, n, True), 0, states, True)

    qs_ref[:, :qk] = wq_ref[...]
    qs_ref[:, qk : 2 * qk] = wk_ref[...]
    qs_ref[:, 2 * qk : 2 * qk + hv] = wv_ref[...]
    qs_ref[:, 2 * qk + hv :] = gs_in[...]
    n.greet()
    for part in q_parts:
        part.begin()

    table = table_ref[...]
    x = x_ref[...].astype(F32)
    scaled = x * lax.rsqrt(jnp.mean(x * x, axis=-1, keepdims=True) + EPSILON)
    documents(ids_ref, ends_ref, n, mask, first_ref, last_ref)
    for part in q_parts:
        part.far_here()
        part.one()
    outs.begin()
    ffn[0].begin()
    q_parts[0].two()
    q_parts[1].three()
    q_parts[1].two()
    q_parts[0].three()
    outs.far_here()
    ffn[1].begin()
    for part in q_parts:
        part.four()
    outs.one()
    for part in q_parts:
        part.end()
    pass_on(0)

    pick_gain = (
        lax.broadcasted_iota(jnp.int32, (8, GAIN_COLS), 0)
        == lax.broadcasted_iota(jnp.int32, (8, GAIN_COLS), 1)
    ).astype(F32).astype(BF)
    gain[...] = mm(pick_gain, wq[..., full - GAIN_COLS :].reshape(width, GAIN_COLS), NT)
    normed[...] = (scaled * gain[0:1, :]).astype(BF)

    def project(i):
        at = pl.ds(pl.multiple_of(i * 512, 512), 512)
        weight = wq[:, :, :, :, :, at].reshape(width, 512)
        qkv[:, at] = mm(normed[...], weight, NN).astype(BF)

    each_pair(0, (2 * qk + hv) // 512, project)
    copies.keep(qkv, qkv_out)
    copies.keep(wq, wq_out)
    copies.keep(gain, gain_out)

    def do_state(pair):
        state_pair(
            pair, table, qkv, last_ref[...], states[0][0], states[0][1]
        )

    def do_local(pair):
        local_pair(pair, qkv, num, den, mask)

    def do_finish(pair):
        finish_pair(
            pair, table, qkv, first_ref[...], num, den, wide, thin, att
        )

    each_pair(0, PAIRS // 2, do_state)
    outs.two()
    outs.three()
    pass_on(1)
    each_pair(PAIRS // 2, PAIRS, do_state)
    swap.begin()
    outs.four()
    each_pair(0, 4, do_local)
    swap.one()
    pass_on(2)
    each_pair(4, 5, do_local)
    swap.two()
    copies.go(other_dy)
    each_pair(5, PAIRS, do_local)
    pass_on(3)
    swap.three()
    swap.four((wide, thin))
    copies.keep(wide, wide_out)
    copies.keep(thin, thin_out)
    each_pair(0, 4, do_finish)
    pass_on(4)
    each_pair(4, PAIRS, do_finish)
    outs.end()
    copies.keep(wo, wo_out)
    copies.keep(att, att_out)
    copies.keep(den, rden_out)

    def leave(i):
        at = pl.ds(pl.multiple_of(i * 512, 512), 512)
        weight = wo[:, :, :, :, :, at].reshape(hv, 512)
        res[:, at] = x_ref[:, at].astype(F32) + mm(att[...], weight, NN)

    each_pair(0, width // 512, leave)
    copies.keep(res, res_out)
    y1 = res[...]
    n2[...] = (
        y1 * lax.rsqrt(jnp.mean(y1 * y1, axis=-1, keepdims=True) + EPSILON) * gain[1:2, :]
    ).astype(BF)
    copies.keep(n2, n2_out)
    pass_on(5)
    ffn[4].two()
    ffn[5].two()
    for part in ffn:
        part.end()
    arrived(other_dy)
    copies.drain()


def forward(x, projections, o_shard, ffn, dy, ids, table, ends):
    rows, width = x.shape
    qk, hv = HEADS * QD, HEADS * VD
    full = sum(part.shape[1] for part in projections)
    small, fine, ff = o_shard.shape[0], ffn[0].shape[0], ffn[0].shape[1]
    half = jax.ShapeDtypeStruct((4, 2, 2, fine, ff), BF)
    wq_shape, wo_shape = (2, 4, 2, 2, small, full), (2, 4, 2, 2, small, width)

    def like(shape, dtype):
        return jax.ShapeDtypeStruct(shape, dtype)

    out_shape = [half] * 3 + [
        like(dy.shape, BF), like(wq_shape, BF), like(wo_shape, BF), like((rows, 2 * qk + hv), BF),
        like((rows, hv), BF), like((rows, hv), F32), like((rows, width), F32),
        like((rows, width), BF), STATE_SHAPES[0], STATE_SHAPES[1], like((8, width), F32),
    ]
    scratch = [
        pltpu.VMEM(wq_shape, BF), pltpu.VMEM(wo_shape, BF), pltpu.VMEM((rows, width), BF),
        pltpu.VMEM((rows, 2 * qk + hv), BF), pltpu.VMEM((rows, hv), F32),
        pltpu.VMEM((rows, hv), F32), pltpu.VMEM((rows, rows), F32), pltpu.VMEM((rows, 1), F32),
        pltpu.VMEM((rows, 1), F32), pltpu.VMEM((rows, hv), BF),
        pltpu.VMEM((rows, width), F32), pltpu.VMEM((rows, width), BF),
        pltpu.VMEM((PAIRS, FEATS, WIDE), BF), pltpu.VMEM((PAIRS, 8, FEATS), F32),
        pltpu.VMEM((8, width), F32), pltpu.VMEM((small, full), BF),
    ] + exchange_shapes() + [
        pltpu.SemaphoreType.DMA((FWD_COPIES,)), pltpu.SemaphoreType.DMA((FWD_COPIES,)),
        pltpu.SemaphoreType.DMA((FWD_LOCALS,)),
    ]
    vmem = pl.BlockSpec(memory_space=pltpu.VMEM)
    return pl.pallas_call(
        forward_kernel,
        out_shape=out_shape,
        in_specs=[vmem] * 11
        + [pl.BlockSpec(memory_space=pl.ANY)]
        + [pl.BlockSpec(memory_space=pltpu.SMEM)],
        out_specs=[pl.BlockSpec(memory_space=pl.ANY)] * len(out_shape),
        scratch_shapes=scratch,
        compiler_params=pltpu.CompilerParams(
            collective_id=1, has_side_effects=True, vmem_limit_bytes=56 << 20
        ),
        cost_estimate=pl.CostEstimate(flops=8 << 30, bytes_accessed=64 << 20, transcendentals=0),
        name="forward",
    )(x, *projections, o_shard, *ffn, ids, table, dy, ends)


def as_f32(ref, index):
    return ref[index].astype(F32)


class WideScatter:
    REMOTE, LOCAL = 7, 3

    def __init__(self, copies, links, own, other, bufs, out):
        n, y, c = links, links.y, links.c
        self.n, self.copies, self.out = n, copies, out
        a_own, a_oth, c_own, c_oth, xx, yy, zz, done = bufs
        self.bufs = bufs
        self.own_part, self.oth_part = own.at[:, :, c], other.at[:, :, c]
        self.core = [
            copies.remote(other.at[:, :, 1 - c], c_oth, n.core),
            copies.remote(own.at[:, :, 1 - c], c_own, n.core),
        ]
        self.cross = copies.remote(a_oth, xx, n.x)
        self.near = copies.remote(a_own.at[:, 1 - y], yy, n.near)
        self.far = [
            copies.remote(a_own.at[n.z ^ r, y], zz.at[r - 1], n.far[r]) for r in range(1, 4)
        ]

    def begin(self):
        a_own, a_oth = self.bufs[:2]
        self.copies.go(*self.core)
        self.loads = [
            self.copies.keep(self.oth_part, a_oth), self.copies.keep(self.own_part, a_own)
        ]

    def loaded(self, i):
        self.copies.finish(self.loads[i])

    def one(self):
        a_own, a_oth, c_own, c_oth, xx, yy, zz, done = self.bufs
        self.loaded(0)
        arrived(self.core[0])

        def add(i, carry):
            for at in ((i, 0), (i, 1)):
                a_oth[at] = (as_f32(a_oth, at) + as_f32(c_oth, at)).astype(BF)
            return carry

        lax.fori_loop(0, 4, add, 0)
        self.copies.go(self.cross)

    def two(self):
        a_own, a_oth, c_own, c_oth, xx, yy, zz, done = self.bufs
        self.loaded(1)
        arrived(self.core[1], self.cross)

        def add(i, carry):
            for at in ((i, 0), (i, 1)):
                total = as_f32(a_own, at) + as_f32(c_own, at) + as_f32(xx, at)
                a_own[at] = total.astype(BF)
            return carry

        lax.fori_loop(0, 4, add, 0)
        self.copies.go(self.near)

    def three(self):
        a_own, a_oth, c_own, c_oth, xx, yy, zz, done = self.bufs
        arrived(self.near)

        def add(i, carry):
            at = (i, self.n.y)
            a_own[at] = (as_f32(a_own, at) + as_f32(yy, i)).astype(BF)
            return carry

        lax.fori_loop(0, 4, add, 0)
        self.copies.go(*self.far)

    def four(self):
        a_own, a_oth, c_own, c_oth, xx, yy, zz, done = self.bufs
        arrived(*self.far)
        total = as_f32(a_own, (self.n.z, self.n.y))
        for r in range(3):
            total = total + as_f32(zz, r)
        done[...] = total
        if self.out is not None:
            self.copies.keep(done, self.out)

    @staticmethod
    def shapes(rows, cols):
        part = [pltpu.VMEM((4, 2, rows, cols), BF)]
        return part * 5 + [
            pltpu.VMEM((4, rows, cols), BF), pltpu.VMEM((3, rows, cols), BF),
            pltpu.VMEM((rows, cols), F32),
        ]


class PlaneScatter:
    REMOTE = 5

    def __init__(self, copies, links, own, bufs, out):
        n, y, c = links, links.y, links.c
        self.n, self.copies, self.out, self.bufs = n, copies, out, bufs
        a, cc, yy, zz, done = bufs
        self.part = own.at[:, :, c]
        self.core = copies.remote(own.at[:, :, 1 - c], cc, n.core)
        self.near = copies.remote(a.at[:, 1 - y], yy, n.near)
        self.far = [copies.remote(a.at[n.z ^ r, y], zz.at[r - 1], n.far[r]) for r in range(1, 4)]

    def begin(self):
        self.copies.go(self.core)
        self.load = self.copies.keep(self.part, self.bufs[0])

    def one(self):
        a, cc, yy, zz, done = self.bufs
        self.copies.finish(self.load)
        arrived(self.core)

        def add(i, carry):
            for at in ((i, 0), (i, 1)):
                a[at] = (as_f32(a, at) + as_f32(cc, at)).astype(BF)
            return carry

        lax.fori_loop(0, 4, add, 0)
        self.copies.go(self.near)

    def two(self):
        a, cc, yy, zz, done = self.bufs
        arrived(self.near)

        def add(i, carry):
            at = (i, self.n.y)
            a[at] = (as_f32(a, at) + as_f32(yy, i)).astype(BF)
            return carry

        lax.fori_loop(0, 4, add, 0)
        self.copies.go(*self.far)

    def three(self):
        a, cc, yy, zz, done = self.bufs
        arrived(*self.far)
        total = as_f32(a, (self.n.z, self.n.y))
        for r in range(3):
            total = total + as_f32(zz, r)
        done[...] = total
        self.copies.keep(done, self.out)

    @staticmethod
    def shapes(rows, cols):
        return [pltpu.VMEM((4, 2, rows, cols), BF)] * 2 + [
            pltpu.VMEM((4, rows, cols), BF), pltpu.VMEM((3, rows, cols), BF),
            pltpu.VMEM((rows, cols), F32),
        ]


def prepare_pair(pair, grad, out, rden):
    rows = grad.shape[0]
    lanes = pair_lanes(pair)
    g = grad[:, lanes].astype(F32)
    r = rden[:, lanes]
    prod = g * out[:, lanes].astype(F32) * r
    low = half_mask(rows, 0)
    first = jnp.sum(jnp.where(low, prod, 0.0), axis=1, keepdims=True)
    second = jnp.sum(jnp.where(low, 0.0, prod), axis=1, keepdims=True)
    grad[:, lanes] = (g * r).astype(BF)
    rden[:, lanes] = jnp.where(low, first, second)


def delta_of(pair, part, deltas, where=slice(None)):
    return deltas[where, pair_lanes(pair)][:, part * VD : part * VD + 1]


def grad_state_pair(pair, table, qkv, first, dnum_ref, delta_ref, wide_ref, thin_ref):
    rows = qkv.shape[0]
    query = qkv[:, tile_lanes(pair)]
    dnum = dnum_ref[:, pair_lanes(pair)]
    total = None
    for part in range(2):
        sel = selectors(table, head_tile(pair, part)[1], LANES)
        one, two = factors(query, table, sel)
        phi = one * two * (table[4:5, :] * first)
        new = mm(phi.astype(BF), keep(half_mask(rows, part), dnum), TN)
        total = new if total is None else total + new
        delta = delta_of(pair, part, delta_ref)
        thin_ref[pair, part : part + 1, :] = -jnp.sum(phi * delta, axis=0, keepdims=True)
    thin_ref[pair, 2:, :] = jnp.zeros((6, FEATS), F32)
    wide_ref[pair] = total.astype(BF)


def local_grad_pair(
    pair, table, qkv, first, dnum_ref, delta_ref, wide_ref, thin_ref, dq_acc, dk_acc, dv_ref,
    mask_ref,
):
    qk = HEADS * QD
    at_tile = tile_lanes(pair)
    query, keys = qkv[:, at_tile], qkv[:, tile_lanes(pair, qk)]
    rows = query.shape[0]
    tiles = rows // TILE
    scale = QD**-0.5
    lanes = pair_lanes(pair)
    values = qkv[:, pair_lanes(pair, 2 * qk)]
    dnum = dnum_ref[:, lanes]
    dv = [jnp.zeros((TILE, WIDE), F32) for _ in range(tiles)]
    for part in range(2):
        head = head_tile(pair, part)[1]
        at_head = head_mask(rows, head, LANES)
        q_head = keep(at_head, query * scale)
        k_head = keep(at_head, keys * scale)
        d_head = keep(half_mask(rows, part), dnum)
        delta = delta_of(pair, part, delta_ref)
        for i in range(tiles):
            here = slice(i * TILE, (i + 1) * TILE)
            dq = dq_acc[here, at_tile]
            for j in range(i + 1):
                there = slice(j * TILE, (j + 1) * TILE)
                s = mm(q_head[here], keys[there], NT)
                mask = mask_ref[here, there]
                w = ((1.0 + s + 0.5 * s * s) * mask).astype(BF)
                dp = mm(d_head[here], values[there], NT)
                ds = ((dp - delta[here]) * ((1.0 + s) * mask)).astype(BF)
                dq = dq + mm(ds, k_head[there], NN)
                dk_acc[there, at_tile] += mm(ds, q_head[here], TN)
                dv[j] = dv[j] + mm(w, d_head[here], TN)
            dq_acc[here, at_tile] = dq
        sel = selectors(table, head, LANES)
        one, two = factors(query, table, sel)
        dphi = mm(d_head, wide_ref[pair], NT) - delta * thin_ref[pair, part : part + 1, :]
        dphi = dphi * (table[4:5, :] * first)
        dq_acc[:, at_tile] += mm((dphi * two).astype(BF), sel[0], NT) + mm(
            (dphi * one).astype(BF), sel[1], NT
        )
    for j in range(tiles):
        dv_ref[j * TILE : (j + 1) * TILE, lanes] = dv[j]


def finish_grad_pair(pair, table, qkv, last, wide_ref, thin_ref, dk_acc, dv_ref, grads):
    qk = HEADS * QD
    at_tile = tile_lanes(pair)
    keys = qkv[:, tile_lanes(pair, qk)]
    rows = keys.shape[0]
    lanes = pair_lanes(pair)
    values = qkv[:, pair_lanes(pair, 2 * qk)]
    dv = dv_ref[:, lanes]
    for part in range(2):
        sel = selectors(table, head_tile(pair, part)[1], LANES)
        one, two = factors(keys, table, sel)
        mask = half_mask(rows, part)
        phi = one * two * last
        dv = dv + jnp.where(mask, mm(phi.astype(BF), wide_ref[pair], NN), 0.0)
        dphi = mm(keep(mask, values), wide_ref[pair], NT) + thin_ref[pair, part : part + 1, :]
        dphi = dphi * last
        dk_acc[:, at_tile] += mm((dphi * two).astype(BF), sel[0], NT) + mm(
            (dphi * one).astype(BF), sel[1], NT
        )
    grads[:, pair_lanes(pair, 2 * qk)] = dv.astype(BF)


def projection_chunks(qk, hv, full):
    return ((0, qk), (2 * qk + hv // 2, 2 * qk + hv), (qk, 2 * qk + hv // 2), (2 * qk + hv, full))


BWD_COPIES = 5 * WideScatter.REMOTE + 3 * PlaneScatter.REMOTE + EXCHANGE_COPIES + 1
BWD_LOCALS = 8 * 3 + 16


def backward_kernel(
    gg_own, gu_own, gd_own, go_ref, grad_in, att_in, rden_in, qkv_in,
    wide_in, thin_in, wq_in, x_in, middle_in, y_in, y_other_in, gain_ref, dgain_ref, ids_ref,
    table_ref, ends_ref,
    dg_out, du_out, dd_out, do_out, dq_out, dk_out, dv_out, dgains_out, din_out, outcome_out,
    *rest,
):
    rest = list(rest)

    def take(count):
        got = rest[:count]
        del rest[:count]
        return got

    g_bufs, u_bufs, d_bufs, o_bufs = take(5), take(5), take(5), take(8)
    q_bufs = [take(8) for _ in range(4)]
    bufs = take(16)
    states = [(bufs[2 * i], bufs[2 * i + 1]) for i in range(8)]
    (
        y_got, outcome, wq, first_ref, last_ref, grad, out, rden, mask, dq_acc, dk_acc, dv, before_wide, before_thin, wqg, qkv, grads,
        wide, thin, dgain, turned, send, recv, local,
    ) = rest
    n = Links()
    copies = Copies(send, recv, local)
    rows, width = out.shape
    qk, hv = HEADS * QD, HEADS * VD
    table = table_ref[...]
    full = wqg.shape[-1]

    gates = PlaneScatter(copies, n, gg_own, g_bufs, dg_out)
    ups = PlaneScatter(copies, n, gu_own, u_bufs, du_out)
    downs = PlaneScatter(copies, n, gd_own, d_bufs, dd_out)
    outs = WideScatter(copies, n, go_ref.at[n.head], go_ref.at[1 - n.head], o_bufs, do_out)
    qs = []
    for bufs_of, (lo, hi) in zip(q_bufs, projection_chunks(qk, hv, full)):
        cols = pl.ds(lo, hi - lo)
        own = wqg.at[n.head, :, :, :, :, cols]
        oth = wqg.at[1 - n.head, :, :, :, :, cols]
        qs.append(WideScatter(copies, n, own, oth, bufs_of, None))
    q_grad, v_late, kv_rest, gain_grad = qs
    swap = Exchange(copies, n, exchange_gates(ends_ref, n, False), 0, states, False)
    y_back = copies.remote(y_other_in, y_got, n.x)

    def fetch(*pairs):
        loads = [copies.keep(src, dst) for src, dst in pairs]

        def ready():
            for load in loads:
                copies.finish(load)

        return ready

    n.greet()

    ready = fetch(
        (grad_in, grad), (att_in, out), (rden_in, rden), (qkv_in, qkv),
        (wide_in, before_wide), (thin_in, before_thin),
    )
    gates.begin()
    ups.begin()
    downs.begin()
    outs.begin()
    documents(ids_ref, ends_ref, n, mask, first_ref, last_ref)
    dq_acc[...] = jnp.zeros_like(dq_acc)
    dk_acc[...] = jnp.zeros_like(dk_acc)
    ready()
    each_pair(0, PAIRS, lambda pair: prepare_pair(pair, grad, out, rden))
    ready_x = fetch((x_in, out), (wq_in, wq))
    gates.one()

    def do_state(pair):
        grad_state_pair(
            pair, table, qkv, first_ref[...], grad, rden, states[0][0], states[0][1]
        )

    def do_local(pair):
        local_grad_pair(
            pair, table, qkv, first_ref[...], grad, rden, before_wide, before_thin, dq_acc,
            dk_acc, dv, mask,
        )

    def do_finish(pair):
        finish_grad_pair(pair, table, qkv, last_ref[...], wide, thin, dk_acc, dv, grads)

    each_pair(0, PAIRS, do_state)
    swap.begin()
    each_pair(0, 1, do_local)
    swap.one()
    outs.one()
    each_pair(1, 2, do_local)
    swap.two()
    gates.two()
    ups.one()
    each_pair(2, 4, do_local)
    outs.two()
    swap.three()
    copies.go(y_back)
    each_pair(4, 6, do_local)
    ups.two()
    downs.one()
    each_pair(6, PAIRS, do_local)
    ready_middle = fetch((middle_in, rden))
    swap.four((wide, thin))
    gates.three()
    outs.three()

    ready_x()
    x_buf, middle = out, rden
    x = x_buf[...].astype(F32)
    scale = lax.rsqrt(jnp.mean(x * x, axis=-1, keepdims=True) + EPSILON)
    normed = (x * scale * gain_ref[0:1, :]).astype(BF)
    turned[...] = jnp.transpose(normed)
    grads[:, :qk] = dq_acc[...].astype(BF)

    def project(lo, hi):
        def rows_step(half):
            left = turned[pl.ds(pl.multiple_of(half * 512, 512), 512), :]
            part = mm(left, grads[:, lo:hi], NN).astype(BF)
            wqg[half, :, :, :, :, lo:hi] = part.reshape(wqg.shape[1:-1] + (hi - lo,))

        each_pair(0, 2, rows_step)

    project(0, qk)
    q_grad.begin()
    each_pair(PAIRS // 2, PAIRS, do_finish)
    q_grad.one()
    project(2 * qk + hv // 2, 2 * qk + hv)
    v_late.begin()
    downs.two()
    each_pair(0, PAIRS // 2, do_finish)
    v_late.one()
    grads[:, qk : 2 * qk] = dk_acc[...].astype(BF)
    project(qk, 2 * qk + hv // 2)
    kv_rest.begin()
    q_grad.two()
    kv_rest.one()
    ups.three()

    ready_middle()
    dv[...] = jnp.zeros_like(dv)

    def back_step(i):
        at = pl.ds(pl.multiple_of(i * 512, 512), 512)
        weight = wq[:, :, :, :, :, at].reshape(width, 512)
        dv[...] += mm(grads[:, at], weight, NT)

    each_pair(0, (2 * qk + hv) // 512, back_step)
    v_late.two()
    q_grad.three()
    dh = dv[...]
    hat = x_buf[...].astype(F32) * scale
    dgain[...] = jnp.zeros_like(dgain)
    dgain[0:1, :] = jnp.sum(dh * hat, axis=0, keepdims=True)
    dgain[1:2, :] = dgain_ref[...]
    spread = (
        lax.broadcasted_iota(jnp.int32, (8, GAIN_COLS), 0)
        == lax.broadcasted_iota(jnp.int32, (8, GAIN_COLS), 1)
    ).astype(F32).astype(BF)
    gain_part = mm(dgain[...].astype(BF), spread, TN).astype(BF)
    wqg[:, :, :, :, :, full - GAIN_COLS :] = gain_part.reshape(wqg.shape[:-1] + (GAIN_COLS,))
    gain_grad.begin()
    dhat = dh * gain_ref[0:1, :]
    inner = jnp.mean(dhat * hat, axis=-1, keepdims=True)
    middle[...] = middle[...] + (dhat - hat * inner) * scale
    copies.keep(middle, din_out)
    ready_y = fetch((y_in, dv))
    gain_grad.one()
    kv_rest.two()
    v_late.three()
    outs.four()
    ready_y()
    arrived(y_back)
    outcome[...] = (dv[...] + y_got[...].astype(F32)).astype(BF)
    copies.keep(outcome, outcome_out)
    downs.three()
    q_grad.four()
    copies.keep(q_bufs[0][7], dq_out)
    gain_grad.two()
    kv_rest.three()
    gain_grad.three()
    v_late.four()
    late, rest_done = q_bufs[1][7], q_bufs[2][7]
    copies.keep(late, dv_out.at[:, pl.ds(hv // 2, hv // 2)])
    kv_rest.four()
    copies.keep(rest_done.at[:, pl.ds(0, qk)], dk_out)
    copies.keep(rest_done.at[:, pl.ds(qk, hv // 2)], dv_out.at[:, pl.ds(0, hv // 2)])
    gain_grad.four()
    copies.keep(q_bufs[3][7], dgains_out)
    copies.drain()


def swish_grads(gate, up, grad_hidden):
    sig = 1.0 / (1.0 + jnp.exp(-gate))
    silu = gate * sig
    grad_up = grad_hidden * silu
    grad_gate = grad_hidden * up * (sig * (1.0 + gate * (1.0 - sig)))
    return (silu * up).astype(BF), grad_gate.astype(BF), grad_up.astype(BF)


FFN_COPIES, FFN_LOCALS = 4, 32


def ffn_kernel(
    n2_in, dy_in, dy_other_in, res_in, g_in, u_in, d_in, att_in, wo_in, gain_ref,
    dwg_out, dwu_out, dwd_out, dwo_out, do_out, middle_out, y_out, y_other_out, dgain_out,
    wg, wu, wd, n2, dy, flipped, acts, grad_gates, grad_ups, y_acc, h_acc, h_sent,
    h_got, res, att, wo, dwo, low, dgain, send, recv, local,
):
    n = Links()
    copies = Copies(send, recv, local)
    rows, width = res.shape
    ff = wg.shape[-1]

    def cols(ref, lo, hi):
        return ref[..., lo:hi].reshape(width, hi - lo)

    def fetch(*pairs):
        loads = [copies.keep(src, dst) for src, dst in pairs]

        def ready():
            for load in loads:
                copies.finish(load)

        return ready

    barrier = pltpu.get_barrier_semaphore()
    pl.semaphore_signal(barrier, inc=1, device_id=n.x, device_id_type=MESH)
    pl.semaphore_wait(barrier, 1)
    part = rows // 2
    halves = [pl.ds(0, part), pl.ds(part, part)]
    tokens = [copies.remote(n2_in.at[half], n2.at[1, half], n.x) for half in halves]
    back = [copies.remote(h_sent.at[half], h_got.at[half], n.x) for half in halves]
    tokens[0].start()
    steps = [(lo, min(lo + 512, ff)) for lo in range(0, ff, 512)]
    first = fetch((n2_in, n2.at[0]), (dy_in, dy.at[0]))
    weight_loads = []
    for lo, hi in steps:
        at = pl.ds(lo, hi - lo)
        loads = []
        for src, dst in ((g_in, wg), (u_in, wu), (d_in, wd)):
            i = copies.used_local
            copies.used_local += 1
            loads.append(
                pltpu.make_async_copy(
                    src.at[:, :, :, :, at], dst.at[:, :, :, :, at], local.at[i]
                )
            )
            loads[-1].start()
        weight_loads.append(loads)
    later_loads = []
    for src, dst in ((dy_other_in, dy.at[1]), (res_in, res), (att_in, att), (wo_in, wo)):
        i = copies.used_local
        copies.used_local += 1
        later_loads.append(pltpu.make_async_copy(src, dst, local.at[i]))
        later_loads[-1].start()
    first()

    def tokens_step(unit, carry):
        side, row = unit // 2, unit - 2 * (unit // 2)
        here = pl.ds(pl.multiple_of(row * part, part), part)
        there = pl.ds(pl.multiple_of(unit * part, part), part)

        @pl.when(unit == 2)
        def _():
            tokens[0].wait_recv()
            for load in later_loads:
                load.wait()

        @pl.when(unit == 3)
        def _():
            tokens[1].wait()

        n2_here, dy_here = n2[side, here, :], dy[side, here, :]
        for step, (lo, hi) in enumerate(steps):
            @pl.when(unit == 0)
            def _(step=step):
                for load in weight_loads[step]:
                    load.wait()

            w_g, w_u, w_d = cols(wg, lo, hi), cols(wu, lo, hi), cols(wd, lo, hi)
            gate = mm(n2_here, w_g, NN)
            up = mm(n2_here, w_u, NN)
            a, dg, du = swish_grads(gate, up, mm(dy_here, w_d, NN))
            acts[there, lo:hi] = a
            grad_gates[there, lo:hi] = dg
            grad_ups[there, lo:hi] = du
            more_h = mm(dg, w_g, NT) + mm(du, w_u, NT)
            more_y = mm(a, w_d, NT)
            if lo == 0:
                h_acc[side, here, :] = more_h
                y_acc[side, here, :] = more_y

                @pl.when(unit == 1)
                def _():
                    tokens[0].wait_send()
                    tokens[1].start()
            else:
                h_acc[side, here, :] += more_h
                y_acc[side, here, :] += more_y

        @pl.when(unit == 2)
        def _():
            h_sent[halves[0], :] = h_acc[1, halves[0], :].astype(BF)
            back[0].start()

        @pl.when(unit == 3)
        def _():
            h_sent[halves[1], :] = h_acc[1, halves[1], :].astype(BF)
            back[1].start()

        return carry

    lax.fori_loop(0, 4, tokens_step, 0)
    low[...] = y_acc[1].astype(BF)
    y_kept = copies.keep(low, y_other_out)
    y_acc[0] += res[...]
    copies.keep(y_acc.at[0], y_out)

    def flip(source):
        for t in range(2):
            def block_step(i, t=t):
                at = pl.ds(pl.multiple_of(i * 256, 256), 256)
                flipped[at, t * rows : (t + 1) * rows] = jnp.transpose(source[t, :, at])

            each_pair(0, width // 256, block_step)

    def weight_grad(right, weight, out):
        def rows_step(z):
            left = flipped[pl.ds(pl.multiple_of(z * 256, 256), 256), :]
            for lo, hi in steps:
                total = mm(left, right[:, lo:hi], NN).astype(BF)
                weight[z, :, :, :, lo:hi] = total.reshape(weight.shape[1:-1] + (hi - lo,))

        each_pair(0, 4, rows_step)
        copies.keep(weight, out)

    flip(n2)
    weight_grad(grad_gates, wg, dwg_out)
    weight_grad(grad_ups, wu, dwu_out)
    flip(dy)
    weight_grad(acts, wd, dwd_out)

    copies.finish(y_kept)
    for copy in back:
        copy.wait()
    gain = gain_ref[1:2, :]
    y1 = res[...]
    scale = lax.rsqrt(jnp.mean(y1 * y1, axis=-1, keepdims=True) + EPSILON)
    hat = y1 * scale
    dh = h_acc[0] + h_got[...].astype(F32)
    dgain[...] = jnp.sum(dh * hat, axis=0, keepdims=True)
    dhat = dh * gain
    inner = jnp.mean(dhat * hat, axis=-1, keepdims=True)
    middle = dy[0].astype(F32) + (dhat - hat * inner) * scale
    h_acc[0] = middle
    low[...] = middle.astype(BF)
    copies.keep(h_acc.at[0], middle_out)
    copies.keep(dgain, dgain_out)
    weight = wo[...].reshape(-1, width)

    def out_step(i):
        at = pl.ds(pl.multiple_of(i * 256, 256), 256)
        total = mm(att[...], low[:, at], TN).astype(BF)
        dwo[:, :, :, :, :, at] = total.reshape(dwo.shape[:-1] + (256,))

    each_pair(0, width // 256, out_step)
    copies.keep(dwo, dwo_out)
    n2[0] = mm(low[...], weight, NT).astype(BF)
    copies.keep(n2.at[0], do_out)
    copies.drain()


def feed_forward(n2, dy, dy_other, res, weights, att, wo, gain):
    rows, width = n2.shape
    full, ff = weights[0].shape, weights[0].shape[-1]

    def like(shape, dtype):
        return jax.ShapeDtypeStruct(shape, dtype)

    def scratch(shape, dtype):
        return pltpu.VMEM(shape, dtype)

    out_shape = [like(full, BF)] * 3 + [
        like(wo.shape, BF), like((rows, width), BF), like((rows, width), F32),
        like((rows, width), F32), like((rows, width), BF), like((1, width), F32),
    ]
    token = (rows, width)
    anywhere = pl.BlockSpec(memory_space=pl.ANY)
    return pl.pallas_call(
        ffn_kernel,
        out_shape=out_shape,
        in_specs=[anywhere] * 9 + [pl.BlockSpec(memory_space=pltpu.VMEM)],
        out_specs=[anywhere] * len(out_shape),
        scratch_shapes=[scratch(full, BF)] * 3
        + [scratch((2,) + token, BF)] * 2
        + [scratch((width, 2 * rows), BF)]
        + [scratch((2 * rows, ff), BF)] * 3
        + [scratch((2,) + token, F32)] * 2
        + [scratch(token, BF)] * 2
        + [scratch(token, F32), scratch(token, BF), scratch(wo.shape, BF), scratch(wo.shape, BF)]
        + [scratch(token, BF), scratch((1, width), F32)]
        + [
            pltpu.SemaphoreType.DMA((FFN_COPIES,)), pltpu.SemaphoreType.DMA((FFN_COPIES,)),
            pltpu.SemaphoreType.DMA((FFN_LOCALS,)),
        ],
        compiler_params=pltpu.CompilerParams(
            collective_id=3, has_side_effects=True, vmem_limit_bytes=62 << 20
        ),
        cost_estimate=pl.CostEstimate(flops=26 << 30, bytes_accessed=64 << 20, transcendentals=0),
        name="feed_forward",
    )(n2, dy, dy_other, res, *weights, att, wo, gain)


def backward(
    ffn_grads, out_grad, grad, att, rden, qkv, before, wq, x, middle, y, y_other, gain, dgain, ids,
    table, ends,
):
    rows, width = x.shape
    qk, hv = HEADS * QD, HEADS * VD
    fine, ff = ffn_grads[0].shape[-2:]
    small, full = wq.shape[-2:]

    def like(shape, dtype):
        return jax.ShapeDtypeStruct(shape, dtype)

    out_shape = [like((fine, ff), F32)] * 3 + [
        like((small, width), F32), like((small, qk), F32), like((small, qk), F32),
        like((small, hv), F32), like((small, GAIN_COLS), F32), like((rows, width), F32),
        like((rows, width), BF),
    ]
    scratch = (
        PlaneScatter.shapes(fine, ff) * 3
        + WideScatter.shapes(small, width)
    )
    for lo, hi in projection_chunks(qk, hv, full):
        scratch += WideScatter.shapes(small, hi - lo)
    scratch += exchange_shapes()
    scratch += [
        pltpu.VMEM((rows, width), BF), pltpu.VMEM((rows, width), BF),
        pltpu.VMEM((2, 4, 2, 2, small, full), BF), pltpu.VMEM((rows, 1), F32),
        pltpu.VMEM((rows, 1), F32),
        pltpu.VMEM((rows, hv), BF), pltpu.VMEM((rows, width), BF), pltpu.VMEM((rows, hv), F32),
        pltpu.VMEM((rows, rows), F32), pltpu.VMEM((rows, qk), F32), pltpu.VMEM((rows, qk), F32),
        pltpu.VMEM((rows, hv), F32), pltpu.VMEM((PAIRS, FEATS, WIDE), BF),
        pltpu.VMEM((PAIRS, 8, FEATS), F32),
        pltpu.VMEM((2, 4, 2, 2, small, full), BF), pltpu.VMEM((rows, 2 * qk + hv), BF),
        pltpu.VMEM((rows, 2 * qk + hv), BF),
        pltpu.VMEM((PAIRS, FEATS, WIDE), BF), pltpu.VMEM((PAIRS, 8, FEATS), F32),
        pltpu.VMEM((8, width), F32), pltpu.VMEM((width, rows), BF),
        pltpu.SemaphoreType.DMA((BWD_COPIES,)), pltpu.SemaphoreType.DMA((BWD_COPIES,)),
        pltpu.SemaphoreType.DMA((BWD_LOCALS,)),
    ]
    vmem = pl.BlockSpec(memory_space=pltpu.VMEM)
    anywhere = pl.BlockSpec(memory_space=pl.ANY)
    return pl.pallas_call(
        backward_kernel,
        out_shape=out_shape,
        in_specs=[anywhere] * 15 + [vmem] * 4 + [pl.BlockSpec(memory_space=pltpu.SMEM)],
        out_specs=[anywhere] * len(out_shape),
        scratch_shapes=scratch,
        compiler_params=pltpu.CompilerParams(
            collective_id=2, has_side_effects=True, vmem_limit_bytes=62 << 20
        ),
        cost_estimate=pl.CostEstimate(flops=16 << 30, bytes_accessed=64 << 20, transcendentals=0),
        name="backward",
    )(
        *ffn_grads, out_grad, grad, att, rden, qkv, *before, wq, x, middle, y, y_other, gain,
        dgain, ids, table, ends,
    )


def deliver_kernel(count, *refs):
    ins, rest = refs[:count], refs[count:]
    down_in, gains_in, rest = rest[0], rest[1], rest[2:]
    outs, rest = rest[:count], rest[count:]
    down_out, one_out, two_out, rest = rest[0], rest[1], rest[2], rest[3:]
    bufs, (sem_in, sem_out) = rest[:count], rest[count:]
    loads, stores = [], []
    for i in range(count):
        loads.append(pltpu.make_async_copy(ins[i], bufs[i], sem_in.at[i]))
        stores.append(pltpu.make_async_copy(bufs[i], outs[i], sem_out.at[i]))
        loads[-1].start()
    down_out[...] = jnp.transpose(down_in[...])
    turned = jnp.transpose(gains_in[...])
    one_out[...] = turned[0:1, :]
    two_out[...] = turned[1:2, :]
    for load, store in zip(loads, stores):
        load.wait()
        store.start()
    for store in stores:
        store.wait()


def deliver(plain, down, gains):
    count = len(plain)
    far, vmem = pl.BlockSpec(memory_space=pltpu.HBM), pl.BlockSpec(memory_space=pltpu.VMEM)
    small = gains.shape[0]
    return pl.pallas_call(
        functools.partial(deliver_kernel, count),
        out_shape=[jax.ShapeDtypeStruct(a.shape, a.dtype) for a in plain]
        + [jax.ShapeDtypeStruct(down.shape[::-1], F32)]
        + [jax.ShapeDtypeStruct((1, small), F32)] * 2,
        in_specs=[far] * count + [vmem] * 2,
        out_specs=[far] * count + [vmem] * 3,
        scratch_shapes=[pltpu.VMEM(a.shape, a.dtype) for a in plain]
        + [pltpu.SemaphoreType.DMA((count,))] * 2,
        compiler_params=pltpu.CompilerParams(vmem_limit_bytes=62 << 20),
        name="deliver",
    )(*plain, down, gains)


def rms_scale(values, gain):
    return values * lax.rsqrt(jnp.mean(values * values, axis=-1, keepdims=True) + EPSILON) * gain


def swish_mix(gate, up_proj):
    return jax.nn.silu(gate) * up_proj


def dot_nn(a, b):
    return jnp.dot(a, b, preferred_element_type=F32)


def dot_nt(a, b):
    return lax.dot_general(a, b, (((1,), (1,)), ((), ())), preferred_element_type=F32)


def dot_tn(a, b):
    return lax.dot_general(a, b, (((0,), (0,)), ((), ())), preferred_element_type=F32)


def row_grads(left, right, by_head):
    head, core = lax.axis_index("head"), lax.axis_index("seq") % 2
    tokens = left.shape[0]
    chips = lax.axis_size("seq") // 2
    heads = 2 if by_head else 1
    rows = left.shape[1] // (heads * chips * 2)
    split = left.reshape(tokens, heads, chips, 2, rows)
    out = []
    for rel in range(heads):
        plane = pick(split, head ^ rel, 1) if by_head else split[:, 0]
        out.append([pick(plane, core ^ r, 2).reshape(tokens, chips * rows) for r in range(2)])
    if by_head:
        return [[dot_tn(part, right).astype(BF) for part in parts] for parts in out]
    return [[dot_tn(part, r).astype(BF) for part in out[0]] for r in right]


def plain_forward(
    inputs, segment_ids, norm1_gain, w_query, w_key, w_value, w_out, norm2_gain, w_gate, w_up,
    w_down, row_ids, col_ids, first, last, table,
):
    head, seq = lax.axis_index("head"), lax.axis_index("seq")
    n_seq = lax.axis_size("seq")
    rows, width = inputs.shape
    qk = HEADS * QD
    slot = head * n_seq + seq
    small = norm1_gain.shape[0]
    gains = jnp.zeros((2, width // small, small), F32)
    gains = lax.dynamic_update_slice(
        gains, jnp.stack([norm1_gain, norm2_gain]).astype(F32)[:, None, :], (0, slot, 0)
    ).reshape(2, width)
    gains = sum_everywhere(gains)
    gain_first, gain_second = gains[0], gains[1]

    qkv_full = gather_rows(jnp.concatenate([w_query, w_key, w_value], axis=1))
    out_full = gather_rows(w_out)
    gate_w = gather_halves(w_gate, False)
    up_w = gather_halves(w_up, False)
    down_w = gather_halves(w_down.T, True)

    normed_one = rms_scale(inputs, gain_first).astype(BF)
    qkv = dot_nn(normed_one, qkv_full).astype(BF)
    query, keys, values = qkv[:, :qk], qkv[:, qk : 2 * qk], qkv[:, 2 * qk :]
    vcols = HEADS * VD
    t_spec, q_spec = full_spec((8, FEATS)), full_spec((rows, qk))
    one_spec, row_spec = full_spec((rows, 1)), full_spec((1, rows))
    p_spec = pair_spec(rows)
    f32_like = jax.ShapeDtypeStruct((rows, vcols), F32)
    bf_like = jax.ShapeDtypeStruct((rows, vcols), BF)
    state = run(
        state_kernel,
        [t_spec, q_spec, p_spec, one_spec],
        state_specs(),
        STATE_SHAPES,
        (table, keys, values, last),
        flops=8 * rows * qk * FEATS * HEADS,
    )
    num, den = run(
        local_kernel,
        [q_spec, q_spec, p_spec, one_spec, row_spec],
        [p_spec, p_spec],
        [f32_like, f32_like],
        (query, keys, values, row_ids, col_ids),
        [pltpu.VMEM((rows, rows), F32)],
        flops=8 * rows * rows * qk * HEADS,
    )
    before = exchange(*state, segment_ids, rows, True)
    attended, rden = run(
        finish_kernel,
        [t_spec, q_spec, p_spec, p_spec, one_spec] + state_specs(),
        [p_spec, p_spec],
        [bf_like, f32_like],
        (table, query, num, den, first, *before),
        flops=8 * rows * qk * FEATS * HEADS,
    )
    residual = inputs + dot_nn(attended, out_full)
    normed_two = rms_scale(residual, gain_second).astype(BF)

    return (
        gate_w, up_w, down_w, qkv_full, out_full, gain_first, gain_second, normed_one,
        query, keys, values, attended, rden, residual, normed_two, before,
    )


def body(
    layer_input,
    segment_ids,
    norm1_gain,
    w_query,
    w_key,
    w_value,
    w_out,
    norm2_gain,
    w_gate,
    w_up,
    w_down,
    output_grad,
):
    rows = layer_input.shape[1]
    head, seq = lax.axis_index("head"), lax.axis_index("seq")
    n_seq = lax.axis_size("seq")
    qk = HEADS * QD
    inputs = layer_input[0].astype(F32)
    width = inputs.shape[1]

    table = jnp.asarray(feature_table())
    vcols = HEADS * VD
    t_spec, q_spec = full_spec((8, FEATS)), full_spec((rows, qk))
    one_spec, row_spec = full_spec((rows, 1)), full_spec((1, rows))
    p_spec = pair_spec(rows)
    f32_like = jax.ShapeDtypeStruct((rows, vcols), F32)
    bf_like = jax.ShapeDtypeStruct((rows, vcols), BF)
    slot = head * n_seq + seq
    small = norm1_gain.shape[0]

    if n_seq == 16:
        gain_cols = jnp.stack([norm1_gain, norm2_gain], axis=1)
        gain_cols = jnp.pad(gain_cols, ((0, 0), (0, GAIN_COLS - 2)))
        ids = segment_ids.reshape(2 * n_seq, rows)
        ends = jnp.concatenate([ids[:, 0], ids[:, rows - 1]])
        (
            g_own, u_own, d_own, dy_other, wq, wo, qkv, attended, rden, residual,
            normed_two, wide, thin, gains,
        ) = forward(
            layer_input[0],
            [w_query, w_key, w_value, gain_cols],
            w_out,
            [w_gate, w_up, w_down.T],
            output_grad[0],
            ids, table, ends,
        )
        d_gate, d_up, d_down, d_out, grad_attended, grad_middle, y, y_other, grad_gain = (
            feed_forward(
                normed_two, output_grad[0], dy_other, residual, [g_own, u_own, d_own],
                attended, wo, gains,
            )
        )
        d_gate, d_up, d_down, d_out, d_q, d_k, d_v, d_gains, grad_layer, outcome = backward(
            [d_gate, d_up, d_down], d_out, grad_attended, attended, rden, qkv, (wide, thin), wq,
            layer_input[0], grad_middle, y, y_other, gains, grad_gain, ids, table, ends,
        )
        (
            grad_layer, outcome, d_gate, d_up, d_v, d_out, d_q, d_k, d_down, gain_one, gain_two,
        ) = deliver(
            [grad_layer, outcome, d_gate, d_up, d_v, d_out, d_q, d_k], d_down, d_gains
        )
        return (
            outcome[None], grad_layer[None], gain_one[0], d_q, d_k, d_v, d_out, gain_two[0],
            d_gate, d_up, d_down,
        )

    segment = 2 * seq + head
    ids = lax.dynamic_slice_in_dim(segment_ids, segment * rows, rows)
    row_ids, col_ids = ids[:, None], ids[None, :]
    first = (row_ids == ids[0]).astype(F32)
    last = (row_ids == ids[rows - 1]).astype(F32)
    (
        gate_w, up_w, down_w, qkv_full, out_full, gain_first, gain_second, normed_one,
        query, keys, values, attended, rden, residual, normed_two, before,
    ) = plain_forward(
        inputs, segment_ids, norm1_gain, w_query, w_key, w_value, w_out, norm2_gain, w_gate,
        w_up, w_down, row_ids, col_ids, first, last, table,
    )

    grad_output = output_grad[0]
    outcome = residual
    grad_normed_two = None
    hiddens, grad_gates, grad_ups = [], [], []
    for w_g, w_u, w_d in zip(gate_w, up_w, down_w):
        gate = dot_nn(normed_two, w_g)
        up_proj = dot_nn(normed_two, w_u)
        grad_hidden = dot_nn(grad_output, w_d)
        hidden, mix_pull = jax.vjp(swish_mix, gate, up_proj)
        grad_gate, grad_up = mix_pull(grad_hidden)
        hiddens.append(hidden.astype(BF))
        grad_gates.append(grad_gate.astype(BF))
        grad_ups.append(grad_up.astype(BF))
        outcome = outcome + dot_nt(hiddens[-1], w_d)
        more = dot_nt(grad_gates[-1], w_g) + dot_nt(grad_ups[-1], w_u)
        grad_normed_two = more if grad_normed_two is None else grad_normed_two + more
    outcome = outcome.astype(BF)
    _, norm_pull = jax.vjp(rms_scale, residual, gain_second)
    grad_resid_two, grad_gain_two = norm_pull(grad_normed_two)
    grad_middle = grad_output.astype(F32) + grad_resid_two
    grad_middle_low = grad_middle.astype(BF)
    grad_attended = dot_nt(grad_middle_low, out_full).astype(BF)

    d_gate = scatter(row_grads(normed_two, grad_gates, False), True)
    d_up = scatter(row_grads(normed_two, grad_ups, False), True)
    d_down = scatter(row_grads(grad_output, hiddens, False), False).T

    d_out = scatter(row_grads(attended, grad_middle_low, True), True)

    grad_state = run(
        grad_state_kernel,
        [t_spec, q_spec, p_spec, p_spec, p_spec, one_spec],
        state_specs(),
        STATE_SHAPES,
        (table, query, grad_attended, attended, rden, first),
        flops=8 * rows * qk * FEATS * HEADS,
    )
    qk_f32 = jax.ShapeDtypeStruct((rows, qk), F32)
    qk_bf = jax.ShapeDtypeStruct((rows, qk), BF)
    grad_query, grad_key, grad_value = run(
        local_grad_kernel,
        [t_spec, q_spec, q_spec, p_spec, p_spec, p_spec, p_spec, one_spec, row_spec, one_spec]
        + state_specs(),
        [q_spec, q_spec, p_spec],
        [qk_bf, qk_f32, f32_like],
        (table, query, keys, values, grad_attended, attended, rden, row_ids, col_ids, first)
        + tuple(before),
        [pltpu.VMEM((rows, rows), F32), pltpu.VMEM((rows, qk), F32), pltpu.VMEM((rows, qk), F32)],
        flops=20 * rows * rows * qk * HEADS,
    )
    after = exchange(*grad_state, segment_ids, rows, False)
    grad_key, grad_value = run(
        finish_grad_kernel,
        [t_spec, q_spec, p_spec, q_spec, p_spec, one_spec] + state_specs(),
        [q_spec, p_spec],
        [qk_bf, bf_like],
        (table, keys, values, grad_key, grad_value, last, *after),
        [pltpu.VMEM((rows, qk), F32)],
        flops=16 * rows * qk * FEATS * HEADS,
    )
    grad_qkv = jnp.concatenate([grad_query, grad_key, grad_value], axis=1)
    d_qkv = scatter(row_grads(normed_one, grad_qkv, True), True)
    grad_normed_one = dot_nt(grad_qkv, qkv_full)
    _, first_pull = jax.vjp(rms_scale, inputs, gain_first)
    grad_inputs, grad_gain_one = first_pull(grad_normed_one)
    grad_layer = grad_middle + grad_inputs
    grad_gains = sum_everywhere(jnp.stack([grad_gain_one, grad_gain_two]))
    grad_gains = lax.dynamic_slice_in_dim(
        grad_gains.reshape(2, width // small, small), slot, 1, 1
    )[:, 0]
    return (
        outcome[None],
        grad_layer[None],
        grad_gains[0],
        d_qkv[:, :qk],
        d_qkv[:, qk : 2 * qk],
        d_qkv[:, 2 * qk :],
        d_out,
        grad_gains[1],
        d_gate,
        d_up,
        d_down,
    )


def solution(mesh):
    split = P(("head", "seq"))
    rows = P(("head", "seq"), None)
    block = P("seq", "head", None)
    wide, tall = P("seq", "head"), P("head", "seq")
    in_specs = (block, P(), split, rows, rows, rows, rows, split, wide, wide, tall, block)
    out_specs = (block, block, split, rows, rows, rows, rows, split, wide, wide, tall)
    return jax.shard_map(body, mesh=mesh, in_specs=in_specs, out_specs=out_specs, check_vma=False)
```

```python
import functools

import jax
import jax.numpy as jnp
import numpy as np
from jax import lax
from jax.experimental import pallas as pl
from jax.experimental.pallas import tpu as pltpu
from jax.sharding import PartitionSpec as P

HEADS = 16
QD = 16
VD = 64
DOC_MAX = 4096
EPSILON = 1e-05
PAIRS = HEADS // 2
WIDE = 2 * VD
FEATS = 160
TILE = 256
LANES = 128

BF = jnp.bfloat16
F32 = jnp.float32


def flip_seq(value, code):
    n = lax.axis_size("seq")
    return lax.ppermute(value, "seq", [(i, i ^ code) for i in range(n)])


def flip_head(value):
    n = lax.axis_size("head")
    return lax.ppermute(value, "head", [(i, i ^ 1) for i in range(n)])


def shift_seq(value, distance):
    n = lax.axis_size("seq")
    return lax.ppermute(
        value, "seq", [(i, i + distance) for i in range(n) if 0 <= i + distance < n]
    )


def layout():
    chips = lax.axis_size("seq") // 2
    near = 2 if chips <= 8 else 8
    far = chips // near
    return far, near


def place_kernel(groups, count, *refs):
    pieces, out, sem = refs[:count], refs[count], refs[count + 1]
    me = lax.axis_index("seq")
    head = lax.axis_index("head")
    n = lax.axis_size("seq")
    copies = []
    for piece, blocks in zip(pieces, groups):
        for index, (rel_head, rel_seq) in blocks:
            place = me ^ rel_seq
            if rel_head is not None:
                place = place + (head ^ rel_head) * n
            copies.append(
                pltpu.make_async_copy(piece.at[index], out.at[place], sem.at[len(copies)])
            )
    for copy in copies:
        copy.start()
    for copy in copies:
        copy.wait()


def place(pieces, groups, blocks):
    rows, cols = pieces[0].shape[-2:]
    total = sum(len(g) for g in groups)
    out = pl.pallas_call(
        functools.partial(place_kernel, groups, len(pieces)),
        out_shape=jax.ShapeDtypeStruct((blocks, rows, cols), pieces[0].dtype),
        in_specs=[pl.BlockSpec(memory_space=pl.ANY)] * len(pieces),
        out_specs=pl.BlockSpec(memory_space=pltpu.VMEM),
        scratch_shapes=[pltpu.SemaphoreType.DMA((total,))],
        compiler_params=pltpu.CompilerParams(vmem_limit_bytes=16 << 20),
        cost_estimate=pl.CostEstimate(
            flops=0, bytes_accessed=4 * blocks * rows * cols, transcendentals=0
        ),
        name="place",
    )(*pieces)
    return out.reshape(blocks * rows, cols)


def gather(shard, head_first):
    far, near = layout()
    far_codes = [2 * near * r for r in range(far)]
    near_codes = [2 * r for r in range(near)]
    if head_first:
        shard = jnp.stack([shard, flip_head(shard)])
    column = jnp.stack([shard] + [flip_seq(shard, code) for code in far_codes[1:]])
    held = [(column, 0, 0)]
    held += [(flip_seq(column, code), 0, code) for code in near_codes[1:]]
    if not head_first:
        held += [(flip_head(buf), 1, code) for buf, _, code in held]
    held += [(flip_seq(buf, 1), rel, code + 1) for buf, rel, code in held]
    result = []
    for buf, rel, code in held:
        if head_first:
            blocks = [((r, g), (g, code + far_codes[r])) for r in range(far) for g in range(2)]
        else:
            blocks = [((r,), (rel, code + far_codes[r])) for r in range(far)]
        result.append((buf, blocks))
    return result


def gather_rows(shard):
    got = gather(shard, False)
    return place([b for b, _ in got], [g for _, g in got], 2 * lax.axis_size("seq"))


def gather_halves(shard, head_first):
    got = gather(shard, head_first)
    halves = []
    for rel in range(2):
        pieces, groups = [], []
        for buf, blocks in got:
            mine = [(i, (None, code)) for i, (r, code) in blocks if r == rel]
            if mine:
                pieces.append(buf)
                groups.append(mine)
        halves.append(place(pieces, groups, lax.axis_size("seq")))
    return halves


def add_low(*terms):
    total = terms[0].astype(F32)
    for term in terms[1:]:
        total = total + term.astype(F32)
    return total.astype(BF)


def pick(value, index, axis):
    return lax.dynamic_index_in_dim(value, index, axis, keepdims=False)


def scatter(grads, head_first):
    far, near = layout()
    seq = lax.axis_index("seq")
    far_at, near_at = seq // (2 * near), (seq // 2) % near
    both = [
        add_low(grads[rel][0], flip_seq(grads[rel][1], 1)) for rel in range(2)
    ]
    rows = both[0].shape[0] // (far * near)
    cols = both[0].shape[1]
    if head_first:
        whole = add_low(both[0], flip_head(both[1])).reshape(far, near, rows, cols)
    else:
        whole = jnp.stack(both).reshape(2, far, near, rows, cols).transpose(1, 2, 0, 3, 4)
    parts = [pick(whole, near_at, 1)]
    parts += [flip_seq(pick(whole, near_at ^ r, 1), 2 * r) for r in range(1, near)]
    column = add_low(*parts)
    parts = [pick(column, far_at, 0)]
    parts += [flip_seq(pick(column, far_at ^ r, 0), 2 * near * r) for r in range(1, far)]
    if head_first:
        return sum(part.astype(F32) for part in parts)
    both = add_low(*parts)
    return both[0].astype(F32) + flip_head(both[1]).astype(F32)


def sum_everywhere(value):
    value = value + flip_head(value)
    code = 1
    while code < lax.axis_size("seq"):
        value = value + flip_seq(value, code)
        code *= 2
    return value


def feature_table():
    first, second, one, two, scale = [], [], [], [], []
    for a in range(QD):
        for b in range(a, QD):
            first.append(a)
            second.append(b)
            one.append(0.0)
            two.append(0.0)
            scale.append((1.0 if a == b else 2.0) / (2.0 * QD))
    for a in range(QD):
        first.append(a)
        second.append(-1000)
        one.append(0.0)
        two.append(1.0)
        scale.append(QD**-0.5)
    first.append(-1000)
    second.append(-1000)
    one.append(1.0)
    two.append(1.0)
    scale.append(1.0)
    pad = FEATS - len(first)
    table = np.zeros((8, FEATS), np.float32)
    table[0] = np.array(first + [-1000] * pad)
    table[1] = np.array(second + [-1000] * pad)
    table[2] = np.array(one + [0.0] * pad)
    table[3] = np.array(two + [0.0] * pad)
    table[4] = np.array(scale + [0.0] * pad)
    return table


def mm(a, b, dims):
    return lax.dot_general(a, b, ((dims[0], dims[1]), ((), ())), preferred_element_type=F32)


NN = ((1,), (0,))
NT = ((1,), (1,))
TN = ((0,), (0,))


def selectors(table, head, lanes=HEADS * QD):
    row = (lax.broadcasted_iota(jnp.int32, (lanes, FEATS), 0) - head * QD).astype(F32)
    one = (row == table[0:1, :]).astype(F32).astype(BF)
    two = (row == table[1:2, :]).astype(F32).astype(BF)
    return one, two


def factors(values, table, sel):
    return (
        mm(values, sel[0], NN) + table[2:3, :],
        mm(values, sel[1], NN) + table[3:4, :],
    )


def half_mask(rows, part):
    lane = lax.broadcasted_iota(jnp.int32, (rows, WIDE), 1)
    return (lane >= VD) if part else (lane < VD)


def head_mask(rows, head, lanes=HEADS * QD):
    lane = lax.broadcasted_iota(jnp.int32, (rows, lanes), 1)
    return (lane >= head * QD) & (lane < (head + 1) * QD)


def keep(mask, value):
    return jnp.where(mask, value.astype(F32), 0.0).astype(BF)


def state_kernel(table_ref, keys_ref, values_ref, last_ref, wide_ref, thin_ref):
    pair = pl.program_id(0)
    table = table_ref[...]
    keys = keys_ref[...]
    rows = keys.shape[0]
    last = last_ref[...]
    total = None
    for part in range(2):
        sel = selectors(table, 2 * pair + part)
        one, two = factors(keys, table, sel)
        phi = one * two * last
        value = keep(half_mask(rows, part), values_ref[...])
        new = mm(phi.astype(BF), value, TN)
        total = new if total is None else total + new
        thin_ref[0, part : part + 1, :] = jnp.sum(phi, axis=0, keepdims=True)
    thin_ref[0, 2:, :] = jnp.zeros((6, FEATS), F32)
    wide_ref[0] = total.astype(BF)


def visible_tile(mask_ref, row_ids_ref, col_ids_ref, rows):
    for i in range(rows // TILE):
        for j in range(i + 1):
            same = (
                row_ids_ref[i * TILE : (i + 1) * TILE, :]
                == col_ids_ref[:, j * TILE : (j + 1) * TILE]
            )
            if i == j:
                same = same & (
                    lax.broadcasted_iota(jnp.int32, (TILE, TILE), 1)
                    <= lax.broadcasted_iota(jnp.int32, (TILE, TILE), 0)
                )
            mask_ref[i * TILE : (i + 1) * TILE, j * TILE : (j + 1) * TILE] = same.astype(F32)


def local_kernel(
    query_ref, keys_ref, values_ref, row_ids_ref, col_ids_ref, num_ref, den_ref, mask_ref
):
    pair = pl.program_id(0)
    rows = query_ref.shape[0]

    @pl.when(pair == 0)
    def _():
        visible_tile(mask_ref, row_ids_ref, col_ids_ref, rows)

    for i in range(rows // TILE):
        here = slice(i * TILE, (i + 1) * TILE)
        num = jnp.zeros((TILE, WIDE), F32)
        dens = []
        for part in range(2):
            head = 2 * pair + part
            query = keep(head_mask(TILE, head), query_ref[here, :] * (QD**-0.5))
            den = jnp.zeros((TILE, 1), F32)
            for j in range(i + 1):
                there = slice(j * TILE, (j + 1) * TILE)
                s = mm(query, keys_ref[there, :], NT)
                w = (1.0 + s + 0.5 * s * s) * mask_ref[here, there]
                den = den + jnp.sum(w, axis=1, keepdims=True)
                num = num + mm(
                    w.astype(BF), keep(half_mask(TILE, part), values_ref[there, :]), NN
                )
            dens.append(den)
        num_ref[here, :] = num
        den_ref[here, :] = jnp.where(half_mask(TILE, 0), dens[0], dens[1])


def finish_kernel(
    table_ref, query_ref, num_ref, den_ref, first_ref, wide_ref, thin_ref, out_ref, rden_ref
):
    pair = pl.program_id(0)
    table = table_ref[...]
    query = query_ref[...]
    rows = query.shape[0]
    first = first_ref[...]
    num, den = num_ref[...], den_ref[...]
    for part in range(2):
        sel = selectors(table, 2 * pair + part)
        one, two = factors(query, table, sel)
        phi = one * two * (table[4:5, :] * first)
        mask = half_mask(rows, part)
        extra = mm(phi.astype(BF), wide_ref[0], NN)
        num = num + jnp.where(mask, extra, 0.0)
        more = jnp.sum(phi * thin_ref[0, part : part + 1, :], axis=1, keepdims=True)
        den = den + jnp.where(mask, more, 0.0)
    rden = 1.0 / den
    rden_ref[...] = rden
    out_ref[...] = (num * rden).astype(BF)


def prepare(grad_ref, out_ref, rden_ref):
    rows = grad_ref.shape[0]
    grad = grad_ref[...].astype(F32)
    rden = rden_ref[...]
    dnum = (grad * rden).astype(BF)
    prod = grad * out_ref[...].astype(F32) * rden
    deltas = [
        jnp.sum(jnp.where(half_mask(rows, part), prod, 0.0), axis=1, keepdims=True)
        for part in range(2)
    ]
    return dnum, deltas


def grad_state_kernel(
    table_ref, query_ref, grad_ref, out_ref, rden_ref, first_ref, wide_ref, thin_ref
):
    pair = pl.program_id(0)
    table = table_ref[...]
    query = query_ref[...]
    rows = query.shape[0]
    dnum, deltas = prepare(grad_ref, out_ref, rden_ref)
    total = None
    for part in range(2):
        sel = selectors(table, 2 * pair + part)
        one, two = factors(query, table, sel)
        phi = one * two * (table[4:5, :] * first_ref[...])
        new = mm(phi.astype(BF), keep(half_mask(rows, part), dnum), TN)
        total = new if total is None else total + new
        thin_ref[0, part : part + 1, :] = -jnp.sum(phi * deltas[part], axis=0, keepdims=True)
    thin_ref[0, 2:, :] = jnp.zeros((6, FEATS), F32)
    wide_ref[0] = total.astype(BF)


def local_grad_kernel(
    table_ref,
    query_ref,
    keys_ref,
    values_ref,
    grad_ref,
    out_ref,
    rden_ref,
    row_ids_ref,
    col_ids_ref,
    first_ref,
    wide_ref,
    thin_ref,
    dq_ref,
    dk_ref,
    dv_ref,
    mask_ref,
    dq_acc,
    dk_acc,
):
    pair = pl.program_id(0)
    table = table_ref[...]
    query = query_ref[...]
    keys = keys_ref[...]
    rows = query.shape[0]
    tiles = rows // TILE
    scale = QD**-0.5

    @pl.when(pair == 0)
    def _():
        visible_tile(mask_ref, row_ids_ref, col_ids_ref, rows)
        dq_acc[...] = jnp.zeros_like(dq_acc)
        dk_acc[...] = jnp.zeros_like(dk_acc)

    dnum, deltas = prepare(grad_ref, out_ref, rden_ref)
    dv = [jnp.zeros((TILE, WIDE), F32) for _ in range(tiles)]
    for part in range(2):
        head = 2 * pair + part
        at_head = head_mask(rows, head)
        q_head = keep(at_head, query * scale)
        k_head = keep(at_head, keys * scale)
        d_head = keep(half_mask(rows, part), dnum)
        for i in range(tiles):
            here = slice(i * TILE, (i + 1) * TILE)
            dq = dq_acc[here, :]
            for j in range(i + 1):
                there = slice(j * TILE, (j + 1) * TILE)
                s = mm(q_head[here], keys[there], NT)
                mask = mask_ref[here, there]
                w = ((1.0 + s + 0.5 * s * s) * mask).astype(BF)
                dp = mm(d_head[here], values_ref[there, :], NT)
                ds = ((dp - deltas[part][here]) * ((1.0 + s) * mask)).astype(BF)
                dq = dq + mm(ds, k_head[there], NN)
                dk_acc[there, :] += mm(ds, q_head[here], TN)
                dv[j] = dv[j] + mm(w, d_head[here], TN)
            dq_acc[here, :] = dq
        sel = selectors(table, head)
        one, two = factors(query, table, sel)
        dphi = mm(d_head, wide_ref[0], NT) - deltas[part] * thin_ref[0, part : part + 1, :]
        dphi = dphi * (table[4:5, :] * first_ref[...])
        dq_acc[...] += mm((dphi * two).astype(BF), sel[0], NT) + mm(
            (dphi * one).astype(BF), sel[1], NT
        )
    for j in range(tiles):
        dv_ref[j * TILE : (j + 1) * TILE, :] = dv[j]

    @pl.when(pair == PAIRS - 1)
    def _():
        dq_ref[...] = dq_acc[...].astype(BF)
        dk_ref[...] = dk_acc[...]


def finish_grad_kernel(
    table_ref, keys_ref, values_ref, dk_in_ref, dv_in_ref, last_ref, wide_ref, thin_ref,
    dk_ref, dv_ref, dk_acc,
):
    pair = pl.program_id(0)
    table = table_ref[...]
    keys = keys_ref[...]
    rows = keys.shape[0]
    last = last_ref[...]

    @pl.when(pair == 0)
    def _():
        dk_acc[...] = dk_in_ref[...]

    dv = dv_in_ref[...]
    for part in range(2):
        sel = selectors(table, 2 * pair + part)
        one, two = factors(keys, table, sel)
        mask = half_mask(rows, part)
        phi = one * two * last
        dv = dv + jnp.where(mask, mm(phi.astype(BF), wide_ref[0], NN), 0.0)
        dphi = mm(keep(mask, values_ref[...]), wide_ref[0], NT) + thin_ref[0, part : part + 1, :]
        dphi = dphi * last
        dk_acc[...] += mm((dphi * two).astype(BF), sel[0], NT) + mm(
            (dphi * one).astype(BF), sel[1], NT
        )
    dv_ref[...] = dv.astype(BF)

    @pl.when(pair == PAIRS - 1)
    def _():
        dk_ref[...] = dk_acc[...].astype(BF)


def full_spec(shape):
    return pl.BlockSpec(shape, lambda p: (0,) * len(shape))


def pair_spec(rows):
    return pl.BlockSpec((rows, WIDE), lambda p: (0, p))


def state_specs():
    return [
        pl.BlockSpec((1, FEATS, WIDE), lambda p: (p, 0, 0)),
        pl.BlockSpec((1, 8, FEATS), lambda p: (p, 0, 0)),
    ]


STATE_SHAPES = (
    jax.ShapeDtypeStruct((PAIRS, FEATS, WIDE), BF),
    jax.ShapeDtypeStruct((PAIRS, 8, FEATS), F32),
)


def run(kernel, in_specs, out_specs, out_shape, args, scratch=(), flops=0):
    moved = sum(a.size * a.dtype.itemsize for a in args)
    return pl.pallas_call(
        kernel,
        grid=(PAIRS,),
        in_specs=in_specs,
        out_specs=out_specs,
        out_shape=out_shape,
        scratch_shapes=scratch,
        compiler_params=pltpu.CompilerParams(vmem_limit_bytes=48 << 20),
        cost_estimate=pl.CostEstimate(flops=flops, bytes_accessed=moved, transcendentals=0),
        name=kernel.__name__,
    )(*args)


def exchange(wide, thin, ids, rows, forward):
    head, seq = lax.axis_index("head"), lax.axis_index("seq")
    n = lax.axis_size("seq")
    segments = 2 * n
    firsts = ids.reshape(segments, rows)[:, 0]
    lasts = ids.reshape(segments, rows)[:, rows - 1]
    step = 1 if forward else -1
    near_end, far_end = (lasts, firsts) if forward else (firsts, lasts)

    def end_of(which, segment):
        return which[jnp.clip(segment, 0, segments - 1)]

    seg = 2 * seq + head
    takes = end_of(far_end, seg)
    core = seq % 2
    late_head = head if forward else 1 - head
    late_core = core if forward else 1 - core

    def gate(flag):
        return jnp.where(flag, 1.0, 0.0).astype(F32)

    def wider(state):
        return [part.astype(F32) for part in state]

    def narrow(state):
        return [state[0].astype(BF), state[1]]

    def merge(own, other, late, other_takes, joined):
        gained = [part * (gate(other_takes) * late) for part in other]
        own_factor = jnp.where(late == 1, 1.0, gate(joined))
        other_factor = jnp.where(late == 1, gate(joined), 1.0)
        joint = [a * own_factor + b * other_factor for a, b in zip(own, other)]
        return gained, joint

    own = [wide, thin]
    other = [flip_head(part) for part in own]
    first_of, second_of = 2 * seq, 2 * seq + 1
    if not forward:
        first_of, second_of = second_of, first_of
    total, joint = merge(
        wider(own),
        wider(other),
        late_head,
        end_of(near_end, seg - step) == takes,
        end_of(near_end, first_of) == end_of(near_end, second_of),
    )
    joint = narrow(joint)
    other = [flip_seq(part, 1) for part in joint]
    base = 4 * (seq // 2)
    early_end, late_end = (base + 1, base + 3) if forward else (base + 2, base)
    gained, joint = merge(
        wider(joint),
        wider(other),
        late_core,
        end_of(near_end, early_end) == takes,
        end_of(near_end, early_end) == end_of(near_end, late_end),
    )
    total = [a + b for a, b in zip(total, gained)]
    joint = narrow(joint)
    half = PAIRS // 2
    mine = [lax.dynamic_slice_in_dim(part, core * half, half, 0) for part in joint]
    hops = -(-DOC_MAX // (4 * rows))
    far = None
    for hop in range(1, hops + 1):
        got = wider([shift_seq(part, 2 * hop * step) for part in mine])
        nearer, farther = late_end - 4 * step, late_end - 4 * step * hop
        joined = gate(end_of(near_end, nearer) == end_of(near_end, farther))
        got = [part * joined for part in got]
        far = got if far is None else [a + b for a, b in zip(far, got)]
    far = narrow(far)
    other = [flip_seq(part, 1) for part in far]
    comes = (seq // 2 >= 1) if forward else (seq // 2 < n // 2 - 1)
    use = gate(comes & (end_of(near_end, late_end - 4 * step) == takes))
    result = []
    for a, b, so_far in zip(far, other, total):
        low = jnp.where(core == 0, a, b).astype(F32)
        high = jnp.where(core == 0, b, a).astype(F32)
        result.append(so_far + use * jnp.concatenate([low, high], axis=0))
    return narrow(result)


MESH = pl.DeviceIdType.MESH
GAIN_COLS = 128


class Links:
    def __init__(self):
        self.head, self.seq = lax.axis_index("head"), lax.axis_index("seq")
        self.n = lax.axis_size("seq")
        self.z, self.y, self.c = self.seq // 4, (self.seq // 2) % 2, self.seq % 2
        self.core = self.at(self.head, self.seq ^ 1)
        self.x = self.at(1 - self.head, self.seq)
        self.near = self.at(self.head, self.seq ^ 2)
        self.far = [self.at(self.head, self.seq ^ (4 * r)) for r in range(4)]

    def at(self, head, seq):
        return {"head": head, "seq": seq}

    def shifted(self, distance):
        return self.at(self.head, lax.rem(self.seq + distance + self.n, self.n))

    def greet(self):
        barrier = pltpu.get_barrier_semaphore()
        partners = [self.core, self.x, self.near] + self.far[1:]
        partners += [self.shifted(d) for d in (2, 4, -2, -4)]
        for partner in partners:
            pl.semaphore_signal(barrier, inc=1, device_id=partner, device_id_type=MESH)
        pl.semaphore_wait(barrier, len(partners))


class Copies:
    def __init__(self, send, recv, local):
        self.send, self.recv, self.local = send, recv, local
        self.used, self.used_local = 0, 0
        self.started, self.started_local = [], []

    def remote(self, src, dst, partner):
        i = self.used
        self.used += 1
        return pltpu.make_async_remote_copy(
            src_ref=src,
            dst_ref=dst,
            send_sem=self.send.at[i],
            recv_sem=self.recv.at[i],
            device_id=partner,
            device_id_type=MESH,
        )

    def go(self, *copies):
        for copy in copies:
            copy.start()
            self.started.append(copy)

    def keep(self, src, dst):
        copy = pltpu.make_async_copy(src, dst, self.local.at[self.used_local])
        self.used_local += 1
        copy.start()
        self.started_local.append(copy)
        return copy

    def finish(self, copy):
        copy.wait()
        self.started_local = [other for other in self.started_local if other is not copy]

    def drain(self):
        for copy in self.started:
            copy.wait_send()
        for copy in self.started_local:
            copy.wait()


def arrived(*copies):
    for copy in copies:
        copy.wait_recv()


class WideGather:
    def __init__(self, copies, links, shard, own, other, other_there, near_last=False):
        n, y, c = links, links.y, links.c
        self.copies, self.near_last = copies, near_last
        self.place = own.at[n.z, y, c]
        self.shard = shard
        self.far = [copies.remote(shard, self.place, n.far[r]) for r in range(1, 4)]
        mine, theirs = own.at[:, y, c], own.at[:, 1 - y, c]
        self.near = copies.remote(mine, mine, n.near)
        across = other.at[:, y, c]
        self.cross = copies.remote(mine, other_there.at[:, y, c], n.x)
        if near_last:
            self.last = copies.remote(across, across, n.near)
        else:
            self.last = copies.remote(theirs, other_there.at[:, 1 - y, c], n.x)
        self.core = [
            copies.remote(part, part, n.core)
            for part in (mine, theirs, other.at[:, y, c], other.at[:, 1 - y, c])
        ]

    def begin(self):
        self.copies.go(*self.far)
        self.own = self.copies.keep(self.shard, self.place)

    def far_here(self):
        arrived(*self.far)
        self.copies.finish(self.own)

    def one(self):
        self.copies.go(self.near, self.cross, self.core[0])

    def two(self):
        arrived(self.near)
        if not self.near_last:
            self.copies.go(self.last)
        self.copies.go(self.core[1])

    def three(self):
        arrived(self.cross)
        if self.near_last:
            self.copies.go(self.last)
        self.copies.go(self.core[2])

    def four(self):
        arrived(self.last)
        self.copies.go(self.core[3])

    def end(self):
        arrived(*self.core)


class PlaneGather:
    COPIES = 6

    def __init__(self, copies, links, shard, own):
        n, y, c = links, links.y, links.c
        self.copies, self.shard, self.place = copies, shard, own.at[n.z, y, c]
        self.far = [copies.remote(shard, self.place, n.far[r]) for r in range(1, 4)]
        mine, theirs = own.at[:, y, c], own.at[:, 1 - y, c]
        self.near = copies.remote(mine, mine, n.near)
        self.core = [copies.remote(part, part, n.core) for part in (mine, theirs)]

    def begin(self):
        self.copies.go(*self.far)
        self.own = self.copies.keep(self.shard, self.place)

    def far_here(self):
        arrived(*self.far)
        self.copies.finish(self.own)

    def one(self):
        self.copies.go(self.near, self.core[0])

    def two(self):
        arrived(self.near)
        self.copies.go(self.core[1])

    def end(self):
        arrived(*self.core)


class Exchange:
    def __init__(self, copies, links, gates, first, bufs, forward):
        n = links
        self.copies, self.gates, self.first, self.bufs = copies, gates, first, bufs
        half = PAIRS // 2
        step = 2 if forward else -2
        own, a, j, b, j2, r1, r2, far = bufs

        def both(src, dst, partner, groups=4):
            size = src[0].shape[0] // groups
            cuts = [pl.ds(i * size, size) for i in range(groups)]
            made = [copies.remote(src[0].at[cut], dst[0].at[cut], partner) for cut in cuts]
            return made + [copies.remote(src[1], dst[1], partner)]

        def halves(state):
            return [
                state[0].at[pl.ds(n.c * half, half)],
                state[1].at[pl.ds(n.c * half, half)],
            ]

        self.rounds = [
            both(own, a, n.x),
            both(j, b, n.core, 1),
            both(halves(j2), r1, n.shifted(step)) + both(halves(j2), r2, n.shifted(2 * step)),
            both(halves(far), halves(far), n.core, 1),
        ]
        self.halves = halves
        self.total = None

    def gate(self, i):
        return self.gates[self.first + i]

    def begin(self):
        self.copies.go(*self.rounds[0])

    def one(self):
        own, a, j, b, j2, r1, r2, far = self.bufs
        arrived(*self.rounds[0])
        for s, d, t in zip(own, a, j):
            t[...] = (
                s[...].astype(F32) * self.gate(1) + d[...].astype(F32) * self.gate(2)
            ).astype(t.dtype)
        self.copies.go(*self.rounds[1])

    def two(self):
        own, a, j, b, j2, r1, r2, far = self.bufs
        arrived(*self.rounds[1])
        for s, d, t in zip(j, b, j2):
            t[...] = (
                s[...].astype(F32) * self.gate(4) + d[...].astype(F32) * self.gate(5)
            ).astype(t.dtype)
        self.copies.go(*self.rounds[2])

    def three(self):
        own, a, j, b, j2, r1, r2, far = self.bufs
        arrived(*self.rounds[2])
        for s, d, t in zip(r1, r2, self.halves(far)):
            t[...] = (s[...].astype(F32) + d[...].astype(F32) * self.gate(6)).astype(t.dtype)
        self.copies.go(*self.rounds[3])

    def four(self, out):
        own, a, j, b, j2, r1, r2, far = self.bufs
        arrived(*self.rounds[3])
        for s, d, f, t in zip(a, b, far, out):
            t[...] = (
                s[...].astype(F32) * self.gate(0)
                + d[...].astype(F32) * self.gate(3)
                + f[...].astype(F32) * self.gate(7)
            ).astype(t.dtype)


def exchange_shapes():
    shapes = []
    for name in range(8):
        pairs = PAIRS // 2 if name in (5, 6) else PAIRS
        shapes += [pltpu.VMEM((pairs, FEATS, WIDE), BF), pltpu.VMEM((pairs, 8, FEATS), F32)]
    return shapes


def documents(ids_ref, ends_ref, links, mask, first, last):
    rows = ids_ref.shape[1]
    segment = 2 * links.seq + links.head
    row = ids_ref[pl.ds(segment, 1), :].astype(F32)
    column = jnp.transpose(jnp.broadcast_to(row, (128, rows)))[:, :1]
    visible_tile(mask, column, row, rows)
    first[...] = (column == ends_ref[segment].astype(F32)).astype(F32)
    last[...] = (column == ends_ref[2 * links.n + segment].astype(F32)).astype(F32)


def exchange_gates(ends_ref, links, forward):
    head, seq, core, n = links.head, links.seq, links.c, links.n
    segments = 2 * n
    step = 1 if forward else -1
    near_at, far_at = (segments, 0) if forward else (0, segments)
    seg = 2 * seq + head
    chip = seq // 2
    base = 4 * chip
    late_head = (head == 1) if forward else (head == 0)
    late_core = (core == 1) if forward else (core == 0)
    pair_early, pair_late = (2 * seq, 2 * seq + 1) if forward else (2 * seq + 1, 2 * seq)
    early_end, late_end = (base + 1, base + 3) if forward else (base + 2, base)
    near_ok = (chip >= 1) if forward else (chip < n // 2 - 1)
    far_ok = (chip >= 2) if forward else (chip < n // 2 - 2)

    def doc(segment):
        return ends_ref[near_at + jnp.minimum(jnp.maximum(segment, 0), segments - 1)]

    def factor(flag):
        return jnp.where(flag, 1.0, 0.0).astype(F32)

    takes = ends_ref[far_at + seg]
    joined = doc(pair_early) == doc(pair_late)
    joined2 = doc(early_end) == doc(late_end)
    nearer, farther = doc(late_end - 4 * step), doc(late_end - 8 * step)
    flags = [
        late_head & (doc(seg - step) == takes),
        late_head | joined,
        jnp.logical_not(late_head) | joined,
        late_core & (doc(early_end) == takes),
        late_core | joined2,
        jnp.logical_not(late_core) | joined2,
        far_ok & (nearer == farther),
        near_ok & (nearer == takes),
    ]
    return [factor(flag) for flag in flags]


def pair_lanes(pair, start=0):
    return pl.ds(pl.multiple_of(start + pair * WIDE, WIDE), WIDE)


def head_tile(pair, part):
    tile = pair // (LANES // (2 * QD))
    return tile, 2 * pair + part - tile * (LANES // QD)


def tile_lanes(pair, start=0):
    return pl.ds(pl.multiple_of(start + head_tile(pair, 0)[0] * LANES, LANES), LANES)


def state_pair(pair, table, qkv, last, wide_ref, thin_ref):
    rows = qkv.shape[0]
    qk = HEADS * QD
    keys, value = qkv[:, tile_lanes(pair, qk)], qkv[:, pair_lanes(pair, 2 * qk)]
    total = None
    for part in range(2):
        sel = selectors(table, head_tile(pair, part)[1], LANES)
        one, two = factors(keys, table, sel)
        phi = one * two * last
        new = mm(phi.astype(BF), keep(half_mask(rows, part), value), TN)
        total = new if total is None else total + new
        thin_ref[pair, part : part + 1, :] = jnp.sum(phi, axis=0, keepdims=True)
    thin_ref[pair, 2:, :] = jnp.zeros((6, FEATS), F32)
    wide_ref[pair] = total.astype(BF)


def local_pair(pair, qkv, num_ref, den_ref, mask_ref):
    rows = qkv.shape[0]
    qk = HEADS * QD
    for i in range(rows // TILE):
        here = slice(i * TILE, (i + 1) * TILE)
        num = jnp.zeros((TILE, WIDE), F32)
        dens = []
        for part in range(2):
            head = head_tile(pair, part)[1]
            query = keep(
                head_mask(TILE, head, LANES), qkv[here, tile_lanes(pair)] * (QD**-0.5)
            )
            den = jnp.zeros((TILE, 1), F32)
            for j in range(i + 1):
                there = slice(j * TILE, (j + 1) * TILE)
                s = mm(query, qkv[there, tile_lanes(pair, qk)], NT)
                mask = mask_ref[here, there]
                t = (1.0 + s) * mask
                w = t * t + mask
                den = den + jnp.sum(w, axis=1, keepdims=True)
                value = qkv[there, pair_lanes(pair, 2 * qk)]
                num = num + mm(w.astype(BF), keep(half_mask(TILE, part), value), NN)
            dens.append(den)
        num_ref[here, pair_lanes(pair)] = 0.5 * num
        den_ref[here, pair_lanes(pair)] = 0.5 * jnp.where(half_mask(TILE, 0), dens[0], dens[1])


def finish_pair(pair, table, qkv, first, num_ref, den_ref, wide_ref, thin_ref, out_ref):
    rows = qkv.shape[0]
    query = qkv[:, tile_lanes(pair)]
    lanes = pair_lanes(pair)
    num, den = num_ref[:, lanes], den_ref[:, lanes]
    for part in range(2):
        sel = selectors(table, head_tile(pair, part)[1], LANES)
        one, two = factors(query, table, sel)
        phi = one * two * (table[4:5, :] * first)
        mask = half_mask(rows, part)
        num = num + jnp.where(mask, mm(phi.astype(BF), wide_ref[pair], NN), 0.0)
        more = jnp.sum(phi * thin_ref[pair, part : part + 1, :], axis=1, keepdims=True)
        den = den + jnp.where(mask, more, 0.0)
    rden = 1.0 / den
    den_ref[:, lanes] = rden
    out_ref[:, lanes] = (num * rden).astype(BF)


def each_pair(low, high, step):
    def one(pair, carry):
        step(pair)
        return carry

    lax.fori_loop(low, high, one, 0)


WIDE_COPIES, EXCHANGE_COPIES = 10, 19
FWD_COPIES = 3 * WIDE_COPIES + 6 * PlaneGather.COPIES + EXCHANGE_COPIES + 1
FWD_LOCALS = 20


def forward_kernel(
    x_ref, wq_ref, wk_ref, wv_ref, gs_in, os_ref, gs_ref, us_ref, ds_ref, ids_ref, table_ref,
    dy_ref, ends_ref,
    g_own, u_own, d_own, dy_out, wq_out, wo_out, qkv_out, att_out, rden_out,
    res_out, n2_out, wide_out, thin_out, gain_out,
    wq, wo, normed, qkv, num, den, mask, first_ref, last_ref, att, res, n2, wide, thin, gain,
    qs_ref, *rest,
):
    bufs, (send, recv, local) = rest[:16], rest[16:]
    states = [(bufs[2 * i], bufs[2 * i + 1]) for i in range(8)]
    n = Links()
    copies = Copies(send, recv, local)
    rows, width = x_ref.shape
    qk, hv = HEADS * QD, HEADS * VD
    cut = 7 * 128
    full = wq.shape[-1]

    def side(ref, head, lo=None, hi=None):
        return ref.at[head] if lo is None else ref.at[head, :, :, :, :, pl.ds(lo, hi - lo)]

    q_parts = []
    for lo, hi in ((0, cut), (cut, full)):
        shard = qs_ref.at[:, pl.ds(lo, hi - lo)]
        own, other = side(wq, n.head, lo, hi), side(wq, 1 - n.head, lo, hi)
        q_parts.append(WideGather(copies, n, shard, own, other, own, near_last=lo > 0))
    own, other = side(wo, n.head), side(wo, 1 - n.head)
    outs = WideGather(copies, n, os_ref, own, other, own)
    ffn = []
    for shard, own in ((gs_ref, g_own), (us_ref, u_own), (ds_ref, d_own)):
        for lo, hi in half_columns(ds_ref.shape[-1]):
            part = own.at[:, :, :, :, pl.ds(lo, hi - lo)]
            ffn.append(PlaneGather(copies, n, shard.at[:, pl.ds(lo, hi - lo)], part))

    def pass_on(i):
        ffn[i].far_here()
        ffn[i].one()
        if i + 2 < len(ffn):
            ffn[i + 2].begin()
        if i >= 2:
            ffn[i - 2].two()

    other_dy = copies.remote(dy_ref, dy_out, n.x)
    swap = Exchange(copies, n, exchange_gates(ends_ref, n, True), 0, states, True)

    qs_ref[:, :qk] = wq_ref[...]
    qs_ref[:, qk : 2 * qk] = wk_ref[...]
    qs_ref[:, 2 * qk : 2 * qk + hv] = wv_ref[...]
    qs_ref[:, 2 * qk + hv :] = gs_in[...]
    n.greet()
    for part in q_parts:
        part.begin()

    table = table_ref[...]
    x = x_ref[...].astype(F32)
    scaled = x * lax.rsqrt(jnp.mean(x * x, axis=-1, keepdims=True) + EPSILON)
    documents(ids_ref, ends_ref, n, mask, first_ref, last_ref)
    for part in q_parts:
        part.far_here()
        part.one()
    outs.begin()
    ffn[0].begin()
    q_parts[0].two()
    q_parts[1].three()
    q_parts[1].two()
    q_parts[0].three()
    outs.far_here()
    ffn[1].begin()
    for part in q_parts:
        part.four()
    outs.one()
    for part in q_parts:
        part.end()
    pass_on(0)

    pick_gain = (
        lax.broadcasted_iota(jnp.int32, (8, GAIN_COLS), 0)
        == lax.broadcasted_iota(jnp.int32, (8, GAIN_COLS), 1)
    ).astype(F32).astype(BF)
    gain[...] = mm(pick_gain, wq[..., full - GAIN_COLS :].reshape(width, GAIN_COLS), NT)
    normed[...] = (scaled * gain[0:1, :]).astype(BF)

    def project(i):
        at = pl.ds(pl.multiple_of(i * 512, 512), 512)
        weight = wq[:, :, :, :, :, at].reshape(width, 512)
        qkv[:, at] = mm(normed[...], weight, NN).astype(BF)

    each_pair(0, (2 * qk + hv) // 512, project)
    copies.keep(qkv, qkv_out)
    copies.keep(wq, wq_out)
    copies.keep(gain, gain_out)

    def do_state(pair):
        state_pair(
            pair, table, qkv, last_ref[...], states[0][0], states[0][1]
        )

    def do_local(pair):
        local_pair(pair, qkv, num, den, mask)

    def do_finish(pair):
        finish_pair(
            pair, table, qkv, first_ref[...], num, den, wide, thin, att
        )

    each_pair(0, PAIRS // 2, do_state)
    outs.two()
    outs.three()
    pass_on(1)
    each_pair(PAIRS // 2, PAIRS, do_state)
    swap.begin()
    outs.four()
    each_pair(0, 4, do_local)
    swap.one()
    pass_on(2)
    each_pair(4, 5, do_local)
    swap.two()
    copies.go(other_dy)
    each_pair(5, PAIRS, do_local)
    pass_on(3)
    swap.three()
    swap.four((wide, thin))
    copies.keep(wide, wide_out)
    copies.keep(thin, thin_out)
    each_pair(0, 4, do_finish)
    pass_on(4)
    each_pair(4, PAIRS, do_finish)
    outs.end()
    copies.keep(wo, wo_out)
    copies.keep(att, att_out)
    copies.keep(den, rden_out)

    def leave(i):
        at = pl.ds(pl.multiple_of(i * 512, 512), 512)
        weight = wo[:, :, :, :, :, at].reshape(hv, 512)
        res[:, at] = x_ref[:, at].astype(F32) + mm(att[...], weight, NN)

    each_pair(0, width // 512, leave)
    copies.keep(res, res_out)
    y1 = res[...]
    n2[...] = (
        y1 * lax.rsqrt(jnp.mean(y1 * y1, axis=-1, keepdims=True) + EPSILON) * gain[1:2, :]
    ).astype(BF)
    copies.keep(n2, n2_out)
    pass_on(5)
    ffn[4].two()
    ffn[5].two()
    for part in ffn:
        part.end()
    arrived(other_dy)
    copies.drain()


def forward(x, projections, o_shard, ffn, dy, ids, table, ends):
    rows, width = x.shape
    qk, hv = HEADS * QD, HEADS * VD
    full = sum(part.shape[1] for part in projections)
    small, fine, ff = o_shard.shape[0], ffn[0].shape[0], ffn[0].shape[1]
    half = jax.ShapeDtypeStruct((4, 2, 2, fine, ff), BF)
    wq_shape, wo_shape = (2, 4, 2, 2, small, full), (2, 4, 2, 2, small, width)

    def like(shape, dtype):
        return jax.ShapeDtypeStruct(shape, dtype)

    out_shape = [half] * 3 + [
        like(dy.shape, BF), like(wq_shape, BF), like(wo_shape, BF), like((rows, 2 * qk + hv), BF),
        like((rows, hv), BF), like((rows, hv), F32), like((rows, width), F32),
        like((rows, width), BF), STATE_SHAPES[0], STATE_SHAPES[1], like((8, width), F32),
    ]
    scratch = [
        pltpu.VMEM(wq_shape, BF), pltpu.VMEM(wo_shape, BF), pltpu.VMEM((rows, width), BF),
        pltpu.VMEM((rows, 2 * qk + hv), BF), pltpu.VMEM((rows, hv), F32),
        pltpu.VMEM((rows, hv), F32), pltpu.VMEM((rows, rows), F32), pltpu.VMEM((rows, 1), F32),
        pltpu.VMEM((rows, 1), F32), pltpu.VMEM((rows, hv), BF),
        pltpu.VMEM((rows, width), F32), pltpu.VMEM((rows, width), BF),
        pltpu.VMEM((PAIRS, FEATS, WIDE), BF), pltpu.VMEM((PAIRS, 8, FEATS), F32),
        pltpu.VMEM((8, width), F32), pltpu.VMEM((small, full), BF),
    ] + exchange_shapes() + [
        pltpu.SemaphoreType.DMA((FWD_COPIES,)), pltpu.SemaphoreType.DMA((FWD_COPIES,)),
        pltpu.SemaphoreType.DMA((FWD_LOCALS,)),
    ]
    vmem = pl.BlockSpec(memory_space=pltpu.VMEM)
    return pl.pallas_call(
        forward_kernel,
        out_shape=out_shape,
        in_specs=[vmem] * 11
        + [pl.BlockSpec(memory_space=pl.ANY)]
        + [pl.BlockSpec(memory_space=pltpu.SMEM)],
        out_specs=[pl.BlockSpec(memory_space=pl.ANY)] * len(out_shape),
        scratch_shapes=scratch,
        compiler_params=pltpu.CompilerParams(
            collective_id=1, has_side_effects=True, vmem_limit_bytes=56 << 20
        ),
        cost_estimate=pl.CostEstimate(flops=8 << 30, bytes_accessed=64 << 20, transcendentals=0),
        name="forward",
    )(x, *projections, o_shard, *ffn, ids, table, dy, ends)


def as_f32(ref, index):
    return ref[index].astype(F32)


class WideScatter:
    REMOTE, LOCAL = 7, 3

    def __init__(self, copies, links, own, other, bufs, out):
        n, y, c = links, links.y, links.c
        self.n, self.copies, self.out = n, copies, out
        a_own, a_oth, c_own, c_oth, xx, yy, zz, done = bufs
        self.bufs = bufs
        self.own_part, self.oth_part = own.at[:, :, c], other.at[:, :, c]
        self.core = [
            copies.remote(other.at[:, :, 1 - c], c_oth, n.core),
            copies.remote(own.at[:, :, 1 - c], c_own, n.core),
        ]
        self.cross = copies.remote(a_oth, xx, n.x)
        self.near = copies.remote(a_own.at[:, 1 - y], yy, n.near)
        self.far = [
            copies.remote(a_own.at[n.z ^ r, y], zz.at[r - 1], n.far[r]) for r in range(1, 4)
        ]

    def begin(self):
        a_own, a_oth = self.bufs[:2]
        self.copies.go(*self.core)
        self.loads = [
            self.copies.keep(self.oth_part, a_oth), self.copies.keep(self.own_part, a_own)
        ]

    def loaded(self, i):
        self.copies.finish(self.loads[i])

    def one(self):
        a_own, a_oth, c_own, c_oth, xx, yy, zz, done = self.bufs
        self.loaded(0)
        arrived(self.core[0])

        def add(i, carry):
            for at in ((i, 0), (i, 1)):
                a_oth[at] = (as_f32(a_oth, at) + as_f32(c_oth, at)).astype(BF)
            return carry

        lax.fori_loop(0, 4, add, 0)
        self.copies.go(self.cross)

    def two(self):
        a_own, a_oth, c_own, c_oth, xx, yy, zz, done = self.bufs
        self.loaded(1)
        arrived(self.core[1], self.cross)

        def add(i, carry):
            for at in ((i, 0), (i, 1)):
                total = as_f32(a_own, at) + as_f32(c_own, at) + as_f32(xx, at)
                a_own[at] = total.astype(BF)
            return carry

        lax.fori_loop(0, 4, add, 0)
        self.copies.go(self.near)

    def three(self):
        a_own, a_oth, c_own, c_oth, xx, yy, zz, done = self.bufs
        arrived(self.near)

        def add(i, carry):
            at = (i, self.n.y)
            a_own[at] = (as_f32(a_own, at) + as_f32(yy, i)).astype(BF)
            return carry

        lax.fori_loop(0, 4, add, 0)
        self.copies.go(*self.far)

    def four(self):
        a_own, a_oth, c_own, c_oth, xx, yy, zz, done = self.bufs
        arrived(*self.far)
        total = as_f32(a_own, (self.n.z, self.n.y))
        for r in range(3):
            total = total + as_f32(zz, r)
        done[...] = total
        if self.out is not None:
            self.copies.keep(done, self.out)

    @staticmethod
    def shapes(rows, cols):
        part = [pltpu.VMEM((4, 2, rows, cols), BF)]
        return part * 5 + [
            pltpu.VMEM((4, rows, cols), BF), pltpu.VMEM((3, rows, cols), BF),
            pltpu.VMEM((rows, cols), F32),
        ]


class PlaneScatter:
    REMOTE = 5

    def __init__(self, copies, links, own, bufs, out):
        n, y, c = links, links.y, links.c
        self.n, self.copies, self.out, self.bufs = n, copies, out, bufs
        a, cc, yy, zz, done = bufs
        self.part = own.at[:, :, c]
        self.core = copies.remote(own.at[:, :, 1 - c], cc, n.core)
        self.near = copies.remote(a.at[:, 1 - y], yy, n.near)
        self.far = [copies.remote(a.at[n.z ^ r, y], zz.at[r - 1], n.far[r]) for r in range(1, 4)]

    def begin(self):
        self.copies.go(self.core)
        self.load = self.copies.keep(self.part, self.bufs[0])

    def one(self):
        a, cc, yy, zz, done = self.bufs
        self.copies.finish(self.load)
        arrived(self.core)

        def add(i, carry):
            for at in ((i, 0), (i, 1)):
                a[at] = (as_f32(a, at) + as_f32(cc, at)).astype(BF)
            return carry

        lax.fori_loop(0, 4, add, 0)
        self.copies.go(self.near)

    def two(self):
        a, cc, yy, zz, done = self.bufs
        arrived(self.near)

        def add(i, carry):
            at = (i, self.n.y)
            a[at] = (as_f32(a, at) + as_f32(yy, i)).astype(BF)
            return carry

        lax.fori_loop(0, 4, add, 0)
        self.copies.go(*self.far)

    def three(self):
        a, cc, yy, zz, done = self.bufs
        arrived(*self.far)
        total = as_f32(a, (self.n.z, self.n.y))
        for r in range(3):
            total = total + as_f32(zz, r)
        done[...] = total
        self.copies.keep(done, self.out)

    @staticmethod
    def shapes(rows, cols):
        return [pltpu.VMEM((4, 2, rows, cols), BF)] * 2 + [
            pltpu.VMEM((4, rows, cols), BF), pltpu.VMEM((3, rows, cols), BF),
            pltpu.VMEM((rows, cols), F32),
        ]


def prepare_pair(pair, grad, out, rden):
    rows = grad.shape[0]
    lanes = pair_lanes(pair)
    g = grad[:, lanes].astype(F32)
    r = rden[:, lanes]
    prod = g * out[:, lanes].astype(F32) * r
    low = half_mask(rows, 0)
    first = jnp.sum(jnp.where(low, prod, 0.0), axis=1, keepdims=True)
    second = jnp.sum(jnp.where(low, 0.0, prod), axis=1, keepdims=True)
    grad[:, lanes] = (g * r).astype(BF)
    rden[:, lanes] = jnp.where(low, first, second)


def delta_of(pair, part, deltas, where=slice(None)):
    return deltas[where, pair_lanes(pair)][:, part * VD : part * VD + 1]


def grad_state_pair(pair, table, qkv, first, dnum_ref, delta_ref, wide_ref, thin_ref):
    rows = qkv.shape[0]
    query = qkv[:, tile_lanes(pair)]
    dnum = dnum_ref[:, pair_lanes(pair)]
    total = None
    for part in range(2):
        sel = selectors(table, head_tile(pair, part)[1], LANES)
        one, two = factors(query, table, sel)
        phi = one * two * (table[4:5, :] * first)
        new = mm(phi.astype(BF), keep(half_mask(rows, part), dnum), TN)
        total = new if total is None else total + new
        delta = delta_of(pair, part, delta_ref)
        thin_ref[pair, part : part + 1, :] = -jnp.sum(phi * delta, axis=0, keepdims=True)
    thin_ref[pair, 2:, :] = jnp.zeros((6, FEATS), F32)
    wide_ref[pair] = total.astype(BF)


def local_grad_pair(
    pair, table, qkv, first, dnum_ref, delta_ref, wide_ref, thin_ref, dq_acc, dk_acc, dv_ref,
    mask_ref,
):
    qk = HEADS * QD
    at_tile = tile_lanes(pair)
    query, keys = qkv[:, at_tile], qkv[:, tile_lanes(pair, qk)]
    rows = query.shape[0]
    tiles = rows // TILE
    scale = QD**-0.5
    lanes = pair_lanes(pair)
    values = qkv[:, pair_lanes(pair, 2 * qk)]
    dnum = dnum_ref[:, lanes]
    dv = [jnp.zeros((TILE, WIDE), F32) for _ in range(tiles)]
    for part in range(2):
        head = head_tile(pair, part)[1]
        at_head = head_mask(rows, head, LANES)
        q_head = keep(at_head, query * scale)
        k_head = keep(at_head, keys * scale)
        d_head = keep(half_mask(rows, part), dnum)
        delta = delta_of(pair, part, delta_ref)
        for i in range(tiles):
            here = slice(i * TILE, (i + 1) * TILE)
            dq = dq_acc[here, at_tile]
            for j in range(i + 1):
                there = slice(j * TILE, (j + 1) * TILE)
                s = mm(q_head[here], keys[there], NT)
                mask = mask_ref[here, there]
                t = (1.0 + s) * mask
                w = (t * t + mask).astype(BF)
                dp = mm(d_head[here], values[there], NT)
                ds = ((dp - delta[here]) * t).astype(BF)
                dq = dq + mm(ds, k_head[there], NN)
                dk_acc[there, at_tile] += mm(ds, q_head[here], TN)
                dv[j] = dv[j] + mm(w, d_head[here], TN)
            dq_acc[here, at_tile] = dq
        sel = selectors(table, head, LANES)
        one, two = factors(query, table, sel)
        dphi = mm(d_head, wide_ref[pair], NT) - delta * thin_ref[pair, part : part + 1, :]
        dphi = dphi * (table[4:5, :] * first)
        dq_acc[:, at_tile] += mm((dphi * two).astype(BF), sel[0], NT) + mm(
            (dphi * one).astype(BF), sel[1], NT
        )
    for j in range(tiles):
        dv_ref[j * TILE : (j + 1) * TILE, lanes] = 0.5 * dv[j]


def finish_grad_pair(pair, table, qkv, last, wide_ref, thin_ref, dk_acc, dv_ref, grads):
    qk = HEADS * QD
    at_tile = tile_lanes(pair)
    keys = qkv[:, tile_lanes(pair, qk)]
    rows = keys.shape[0]
    lanes = pair_lanes(pair)
    values = qkv[:, pair_lanes(pair, 2 * qk)]
    dv = dv_ref[:, lanes]
    for part in range(2):
        sel = selectors(table, head_tile(pair, part)[1], LANES)
        one, two = factors(keys, table, sel)
        mask = half_mask(rows, part)
        phi = one * two * last
        dv = dv + jnp.where(mask, mm(phi.astype(BF), wide_ref[pair], NN), 0.0)
        dphi = mm(keep(mask, values), wide_ref[pair], NT) + thin_ref[pair, part : part + 1, :]
        dphi = dphi * last
        dk_acc[:, at_tile] += mm((dphi * two).astype(BF), sel[0], NT) + mm(
            (dphi * one).astype(BF), sel[1], NT
        )
    grads[:, pair_lanes(pair, 2 * qk)] = dv.astype(BF)


def half_columns(ff):
    middle = -(-ff // 256) * 128
    return ((0, middle), (middle, ff))


def projection_chunks(qk, hv, full):
    middle = (3 * qk + hv // 2) // 2
    return (
        (0, qk), (2 * qk + hv // 2, 2 * qk + hv), (qk, middle), (middle, 2 * qk + hv // 2),
        (2 * qk + hv, full),
    )


BWD_COPIES = 6 * WideScatter.REMOTE + 6 * PlaneScatter.REMOTE + EXCHANGE_COPIES + 4
BWD_LOCALS = 12 * 3 + 16


def backward_kernel(
    gg_own, gu_own, gd_own, go_ref, grad_in, att_in, rden_in, qkv_in,
    wide_in, thin_in, wq_in, x_in, middle_in, y_in, y_other_in, gain_ref, dgain_ref, ids_ref,
    table_ref, ends_ref,
    dg_out, du_out, dd_out, do_out, dq_out, dk_out, dv_out, dgains_out, din_out, outcome_out,
    *rest,
):
    rest = list(rest)

    def take(count):
        got = rest[:count]
        del rest[:count]
        return got

    f_bufs = [take(5) for _ in range(6)]
    o_bufs = take(8)
    q_bufs = [take(8) for _ in range(5)]
    bufs = take(16)
    states = [(bufs[2 * i], bufs[2 * i + 1]) for i in range(8)]
    (
        y_got, outcome, wq, first_ref, last_ref, grad, out, rden, mask, dq_acc, dk_acc, dv, before_wide, before_thin, wqg, qkv, grads,
        wide, thin, dgain, turned, send, recv, local,
    ) = rest
    n = Links()
    copies = Copies(send, recv, local)
    rows, width = out.shape
    qk, hv = HEADS * QD, HEADS * VD
    table = table_ref[...]
    full = wqg.shape[-1]

    ffn = []
    for grad_ref, result in ((gg_own, dg_out), (gu_own, du_out), (gd_own, dd_out)):
        for lo, hi in half_columns(result.shape[-1]):
            cols = pl.ds(lo, hi - lo)
            part = grad_ref.at[:, :, :, :, cols]
            ffn.append(PlaneScatter(copies, n, part, f_bufs[len(ffn)], result.at[:, cols]))

    def pass_on(i):
        ffn[i].two()
        if i + 2 < len(ffn):
            ffn[i + 2].one()
        if i >= 2:
            ffn[i - 2].three()

    outs = WideScatter(copies, n, go_ref.at[n.head], go_ref.at[1 - n.head], o_bufs, do_out)
    qs = []
    for bufs_of, (lo, hi) in zip(q_bufs, projection_chunks(qk, hv, full)):
        cols = pl.ds(lo, hi - lo)
        own = wqg.at[n.head, :, :, :, :, cols]
        oth = wqg.at[1 - n.head, :, :, :, :, cols]
        qs.append(WideScatter(copies, n, own, oth, bufs_of, None))
    q_grad, v_late, kv_low, kv_high, gain_grad = qs
    middle_at = projection_chunks(qk, hv, full)[2][1]
    swap = Exchange(copies, n, exchange_gates(ends_ref, n, False), 0, states, False)
    piece = rows // 4
    y_back = [
        copies.remote(y_other_in.at[pl.ds(i * piece, piece)], y_got.at[pl.ds(i * piece, piece)], n.x)
        for i in range(4)
    ]

    def fetch(*pairs):
        loads = [copies.keep(src, dst) for src, dst in pairs]

        def ready():
            for load in loads:
                copies.finish(load)

        return ready

    n.greet()

    ready = fetch(
        (grad_in, grad), (att_in, out), (rden_in, rden), (qkv_in, qkv),
        (wide_in, before_wide), (thin_in, before_thin),
    )
    for part in ffn:
        part.begin()
    outs.begin()
    documents(ids_ref, ends_ref, n, mask, first_ref, last_ref)
    dq_acc[...] = jnp.zeros_like(dq_acc)
    dk_acc[...] = jnp.zeros_like(dk_acc)
    ready()
    each_pair(0, PAIRS, lambda pair: prepare_pair(pair, grad, out, rden))
    ready_x = fetch((x_in, out), (wq_in, wq))
    ffn[0].one()
    ffn[1].one()

    def do_state(pair):
        grad_state_pair(
            pair, table, qkv, first_ref[...], grad, rden, states[0][0], states[0][1]
        )

    def do_local(pair):
        local_grad_pair(
            pair, table, qkv, first_ref[...], grad, rden, before_wide, before_thin, dq_acc,
            dk_acc, dv, mask,
        )

    def do_finish(pair):
        finish_grad_pair(pair, table, qkv, last_ref[...], wide, thin, dk_acc, dv, grads)

    each_pair(0, PAIRS, do_state)
    swap.begin()
    each_pair(0, 2, do_local)
    swap.one()
    pass_on(0)
    each_pair(2, 3, do_local)
    swap.two()
    copies.go(*y_back[0:1])
    outs.one()
    pass_on(1)
    each_pair(3, 5, do_local)
    swap.three()
    pass_on(2)
    copies.go(*y_back[1:2])
    each_pair(5, 6, do_local)
    outs.two()
    pass_on(3)
    copies.go(*y_back[2:3])
    each_pair(6, PAIRS, do_local)
    ready_middle = fetch((middle_in, rden))
    swap.four((wide, thin))
    outs.three()
    copies.go(*y_back[3:4])

    ready_x()
    x_buf, middle = out, rden
    x = x_buf[...].astype(F32)
    scale = lax.rsqrt(jnp.mean(x * x, axis=-1, keepdims=True) + EPSILON)
    normed = (x * scale * gain_ref[0:1, :]).astype(BF)
    turned[...] = jnp.transpose(normed)
    grads[:, :qk] = dq_acc[...].astype(BF)

    def project(lo, hi):
        def rows_step(half):
            left = turned[pl.ds(pl.multiple_of(half * 512, 512), 512), :]
            part = mm(left, grads[:, lo:hi], NN).astype(BF)
            wqg[half, :, :, :, :, lo:hi] = part.reshape(wqg.shape[1:-1] + (hi - lo,))

        each_pair(0, 2, rows_step)

    project(0, qk)
    q_grad.begin()
    each_pair(PAIRS // 2, PAIRS, do_finish)
    q_grad.one()
    project(2 * qk + hv // 2, 2 * qk + hv)
    v_late.begin()
    pass_on(4)
    each_pair(0, PAIRS // 2, do_finish)
    v_late.one()
    grads[:, qk : 2 * qk] = dk_acc[...].astype(BF)
    project(qk, middle_at)
    kv_low.begin()
    q_grad.two()
    project(middle_at, 2 * qk + hv // 2)
    kv_high.begin()
    kv_low.one()
    pass_on(5)
    kv_high.one()

    ready_middle()
    dv[...] = jnp.zeros_like(dv)

    def back_step(i):
        at = pl.ds(pl.multiple_of(i * 512, 512), 512)
        weight = wq[:, :, :, :, :, at].reshape(width, 512)
        dv[...] += mm(grads[:, at], weight, NT)

    each_pair(0, (2 * qk + hv) // 512, back_step)
    v_late.two()
    q_grad.three()
    dh = dv[...]
    hat = x_buf[...].astype(F32) * scale
    dgain[...] = jnp.zeros_like(dgain)
    dgain[0:1, :] = jnp.sum(dh * hat, axis=0, keepdims=True)
    dgain[1:2, :] = dgain_ref[...]
    spread = (
        lax.broadcasted_iota(jnp.int32, (8, GAIN_COLS), 0)
        == lax.broadcasted_iota(jnp.int32, (8, GAIN_COLS), 1)
    ).astype(F32).astype(BF)
    gain_part = mm(dgain[...].astype(BF), spread, TN).astype(BF)
    wqg[:, :, :, :, :, full - GAIN_COLS :] = gain_part.reshape(wqg.shape[:-1] + (GAIN_COLS,))
    gain_grad.begin()
    dhat = dh * gain_ref[0:1, :]
    inner = jnp.mean(dhat * hat, axis=-1, keepdims=True)
    middle[...] = middle[...] + (dhat - hat * inner) * scale
    copies.keep(middle, din_out)
    ready_y = fetch((y_in, dv))
    gain_grad.one()
    kv_low.two()
    v_late.three()
    kv_high.two()
    outs.four()
    ready_y()
    arrived(*y_back)
    outcome[...] = (dv[...] + y_got[...].astype(F32)).astype(BF)
    copies.keep(outcome, outcome_out)
    ffn[4].three()
    ffn[5].three()
    q_grad.four()
    copies.keep(q_bufs[0][7], dq_out)
    gain_grad.two()
    kv_low.three()
    kv_high.three()
    gain_grad.three()
    v_late.four()
    copies.keep(q_bufs[1][7], dv_out.at[:, pl.ds(hv // 2, hv // 2)])
    kv_low.four()
    low, high = q_bufs[2][7], q_bufs[3][7]
    early = middle_at - 2 * qk
    copies.keep(low.at[:, pl.ds(0, qk)], dk_out)
    copies.keep(low.at[:, pl.ds(qk, early)], dv_out.at[:, pl.ds(0, early)])
    kv_high.four()
    copies.keep(high, dv_out.at[:, pl.ds(early, hv // 2 - early)])
    gain_grad.four()
    copies.keep(q_bufs[4][7], dgains_out)
    copies.drain()


def swish_grads(gate, up, grad_hidden):
    sig = 1.0 / (1.0 + jnp.exp(-gate))
    silu = gate * sig
    grad_up = grad_hidden * silu
    grad_gate = grad_hidden * up * (sig * (1.0 + gate * (1.0 - sig)))
    return (silu * up).astype(BF), grad_gate.astype(BF), grad_up.astype(BF)


FFN_COPIES, FFN_LOCALS = 4, 32


def ffn_kernel(
    n2_in, dy_in, dy_other_in, res_in, g_in, u_in, d_in, att_in, wo_in, gain_ref,
    dwg_out, dwu_out, dwd_out, dwo_out, do_out, middle_out, y_out, y_other_out, dgain_out,
    weights, n2, dy, flipped, inner_grads, y_acc, h_acc, h_sent,
    h_got, res, att, wo, dwo, low, dgain, send, recv, local,
):
    n = Links()
    copies = Copies(send, recv, local)
    rows, width = res.shape
    ff = weights.shape[-1]
    wg, wu, wd = weights.at[0], weights.at[1], weights.at[2]
    grad_gates, grad_ups, acts = inner_grads.at[0], inner_grads.at[1], inner_grads.at[2]

    def cols(ref, lo, hi):
        return ref[..., lo:hi].reshape(width, hi - lo)

    def fetch(*pairs):
        loads = [copies.keep(src, dst) for src, dst in pairs]

        def ready():
            for load in loads:
                copies.finish(load)

        return ready

    barrier = pltpu.get_barrier_semaphore()
    pl.semaphore_signal(barrier, inc=1, device_id=n.x, device_id_type=MESH)
    pl.semaphore_wait(barrier, 1)
    part = rows // 2
    halves = [pl.ds(0, part), pl.ds(part, part)]
    tokens = [copies.remote(n2_in.at[half], n2.at[1, half], n.x) for half in halves]
    back = [copies.remote(h_sent.at[half], h_got.at[half], n.x) for half in halves]
    tokens[0].start()
    steps = [(lo, min(lo + 512, ff)) for lo in range(0, ff, 512)]
    first = fetch((n2_in, n2.at[0]), (dy_in, dy.at[0]))
    weight_loads = []
    for lo, hi in steps:
        at = pl.ds(lo, hi - lo)
        loads = []
        for src, dst in ((g_in, wg), (u_in, wu), (d_in, wd)):
            i = copies.used_local
            copies.used_local += 1
            loads.append(
                pltpu.make_async_copy(
                    src.at[:, :, :, :, at], dst.at[:, :, :, :, at], local.at[i]
                )
            )
            loads[-1].start()
        weight_loads.append(loads)
    later_loads = []
    for src, dst in ((dy_other_in, dy.at[1]), (res_in, res), (att_in, att), (wo_in, wo)):
        i = copies.used_local
        copies.used_local += 1
        later_loads.append(pltpu.make_async_copy(src, dst, local.at[i]))
        later_loads[-1].start()
    first()

    def tokens_step(unit, carry):
        side, row = unit // 2, unit - 2 * (unit // 2)
        here = pl.ds(pl.multiple_of(row * part, part), part)
        there = pl.ds(pl.multiple_of(unit * part, part), part)

        @pl.when(unit == 2)
        def _():
            tokens[0].wait_recv()
            for load in later_loads:
                load.wait()

        @pl.when(unit == 3)
        def _():
            tokens[1].wait()

        n2_here, dy_here = n2[side, here, :], dy[side, here, :]
        for step, (lo, hi) in enumerate(steps):
            @pl.when(unit == 0)
            def _(step=step):
                for load in weight_loads[step]:
                    load.wait()

            w_g, w_u, w_d = cols(wg, lo, hi), cols(wu, lo, hi), cols(wd, lo, hi)
            gate = mm(n2_here, w_g, NN)
            up = mm(n2_here, w_u, NN)
            a, dg, du = swish_grads(gate, up, mm(dy_here, w_d, NN))
            acts[there, lo:hi] = a
            grad_gates[there, lo:hi] = dg
            grad_ups[there, lo:hi] = du
            more_h = mm(dg, w_g, NT) + mm(du, w_u, NT)
            more_y = mm(a, w_d, NT)
            if lo == 0:
                h_acc[side, here, :] = more_h
                y_acc[side, here, :] = more_y

                @pl.when(unit == 1)
                def _():
                    tokens[0].wait_send()
                    tokens[1].start()
            else:
                h_acc[side, here, :] += more_h
                y_acc[side, here, :] += more_y

        @pl.when(unit == 2)
        def _():
            h_sent[halves[0], :] = h_acc[1, halves[0], :].astype(BF)
            back[0].start()

        @pl.when(unit == 3)
        def _():
            h_sent[halves[1], :] = h_acc[1, halves[1], :].astype(BF)
            back[1].start()

        return carry

    lax.fori_loop(0, 4, tokens_step, 0)
    low[...] = y_acc[1].astype(BF)
    y_kept = copies.keep(low, y_other_out)
    y_acc[0] += res[...]
    copies.keep(y_acc.at[0], y_out)

    for side, source in enumerate((n2, dy)):
        for t in range(2):
            def flip(i, side=side, source=source, t=t):
                at = pl.ds(pl.multiple_of(i * 256, 256), 256)
                flipped[side, at, t * rows : (t + 1) * rows] = jnp.transpose(source[t, :, at])

            each_pair(0, width // 256, flip)

    def weight_grad(m):
        def rows_step(z):
            left = flipped[m // 2, pl.ds(pl.multiple_of(z * 256, 256), 256), :]
            for lo, hi in steps:
                total = mm(left, inner_grads[m, :, lo:hi], NN).astype(BF)
                weights[m, z, :, :, :, lo:hi] = total.reshape(weights.shape[2:-1] + (hi - lo,))

        each_pair(0, 4, rows_step)

    each_pair(0, 3, weight_grad)
    for m, out in enumerate((dwg_out, dwu_out, dwd_out)):
        copies.keep(weights.at[m], out)

    copies.finish(y_kept)
    for copy in back:
        copy.wait()
    gain = gain_ref[1:2, :]
    y1 = res[...]
    scale = lax.rsqrt(jnp.mean(y1 * y1, axis=-1, keepdims=True) + EPSILON)
    hat = y1 * scale
    dh = h_acc[0] + h_got[...].astype(F32)
    dgain[...] = jnp.sum(dh * hat, axis=0, keepdims=True)
    dhat = dh * gain
    inner = jnp.mean(dhat * hat, axis=-1, keepdims=True)
    middle = dy[0].astype(F32) + (dhat - hat * inner) * scale
    h_acc[0] = middle
    low[...] = middle.astype(BF)
    copies.keep(h_acc.at[0], middle_out)
    copies.keep(dgain, dgain_out)
    weight = wo[...].reshape(-1, width)

    def out_step(i):
        at = pl.ds(pl.multiple_of(i * 256, 256), 256)
        total = mm(att[...], low[:, at], TN).astype(BF)
        dwo[:, :, :, :, :, at] = total.reshape(dwo.shape[:-1] + (256,))

    each_pair(0, width // 256, out_step)
    copies.keep(dwo, dwo_out)
    n2[0] = mm(low[...], weight, NT).astype(BF)
    copies.keep(n2.at[0], do_out)
    copies.drain()


def feed_forward(n2, dy, dy_other, res, weights, att, wo, gain):
    rows, width = n2.shape
    full, ff = weights[0].shape, weights[0].shape[-1]

    def like(shape, dtype):
        return jax.ShapeDtypeStruct(shape, dtype)

    def scratch(shape, dtype):
        return pltpu.VMEM(shape, dtype)

    out_shape = [like(full, BF)] * 3 + [
        like(wo.shape, BF), like((rows, width), BF), like((rows, width), F32),
        like((rows, width), F32), like((rows, width), BF), like((1, width), F32),
    ]
    token = (rows, width)
    anywhere = pl.BlockSpec(memory_space=pl.ANY)
    return pl.pallas_call(
        ffn_kernel,
        out_shape=out_shape,
        in_specs=[anywhere] * 9 + [pl.BlockSpec(memory_space=pltpu.VMEM)],
        out_specs=[anywhere] * len(out_shape),
        scratch_shapes=[scratch((3,) + full, BF)]
        + [scratch((2,) + token, BF)] * 2
        + [scratch((2, width, 2 * rows), BF)]
        + [scratch((3, 2 * rows, ff), BF)]
        + [scratch((2,) + token, F32)] * 2
        + [scratch(token, BF)] * 2
        + [scratch(token, F32), scratch(token, BF), scratch(wo.shape, BF), scratch(wo.shape, BF)]
        + [scratch(token, BF), scratch((1, width), F32)]
        + [
            pltpu.SemaphoreType.DMA((FFN_COPIES,)), pltpu.SemaphoreType.DMA((FFN_COPIES,)),
            pltpu.SemaphoreType.DMA((FFN_LOCALS,)),
        ],
        compiler_params=pltpu.CompilerParams(
            collective_id=3, has_side_effects=True, vmem_limit_bytes=62 << 20
        ),
        cost_estimate=pl.CostEstimate(flops=26 << 30, bytes_accessed=64 << 20, transcendentals=0),
        name="feed_forward",
    )(n2, dy, dy_other, res, *weights, att, wo, gain)


def backward(
    ffn_grads, out_grad, grad, att, rden, qkv, before, wq, x, middle, y, y_other, gain, dgain, ids,
    table, ends,
):
    rows, width = x.shape
    qk, hv = HEADS * QD, HEADS * VD
    fine, ff = ffn_grads[0].shape[-2:]
    small, full = wq.shape[-2:]

    def like(shape, dtype):
        return jax.ShapeDtypeStruct(shape, dtype)

    out_shape = [like((fine, ff), F32)] * 3 + [
        like((small, width), F32), like((small, qk), F32), like((small, qk), F32),
        like((small, hv), F32), like((small, GAIN_COLS), F32), like((rows, width), F32),
        like((rows, width), BF),
    ]
    scratch = []
    for _ in range(3):
        for lo, hi in half_columns(ff):
            scratch += PlaneScatter.shapes(fine, hi - lo)
    scratch += WideScatter.shapes(small, width)
    for lo, hi in projection_chunks(qk, hv, full):
        scratch += WideScatter.shapes(small, hi - lo)
    scratch += exchange_shapes()
    scratch += [
        pltpu.VMEM((rows, width), BF), pltpu.VMEM((rows, width), BF),
        pltpu.VMEM((2, 4, 2, 2, small, full), BF), pltpu.VMEM((rows, 1), F32),
        pltpu.VMEM((rows, 1), F32),
        pltpu.VMEM((rows, hv), BF), pltpu.VMEM((rows, width), BF), pltpu.VMEM((rows, hv), F32),
        pltpu.VMEM((rows, rows), F32), pltpu.VMEM((rows, qk), F32), pltpu.VMEM((rows, qk), F32),
        pltpu.VMEM((rows, hv), F32), pltpu.VMEM((PAIRS, FEATS, WIDE), BF),
        pltpu.VMEM((PAIRS, 8, FEATS), F32),
        pltpu.VMEM((2, 4, 2, 2, small, full), BF), pltpu.VMEM((rows, 2 * qk + hv), BF),
        pltpu.VMEM((rows, 2 * qk + hv), BF),
        pltpu.VMEM((PAIRS, FEATS, WIDE), BF), pltpu.VMEM((PAIRS, 8, FEATS), F32),
        pltpu.VMEM((8, width), F32), pltpu.VMEM((width, rows), BF),
        pltpu.SemaphoreType.DMA((BWD_COPIES,)), pltpu.SemaphoreType.DMA((BWD_COPIES,)),
        pltpu.SemaphoreType.DMA((BWD_LOCALS,)),
    ]
    vmem = pl.BlockSpec(memory_space=pltpu.VMEM)
    anywhere = pl.BlockSpec(memory_space=pl.ANY)
    return pl.pallas_call(
        backward_kernel,
        out_shape=out_shape,
        in_specs=[anywhere] * 15 + [vmem] * 4 + [pl.BlockSpec(memory_space=pltpu.SMEM)],
        out_specs=[anywhere] * len(out_shape),
        scratch_shapes=scratch,
        compiler_params=pltpu.CompilerParams(
            collective_id=2, has_side_effects=True, vmem_limit_bytes=62 << 20
        ),
        cost_estimate=pl.CostEstimate(flops=16 << 30, bytes_accessed=64 << 20, transcendentals=0),
        name="backward",
    )(
        *ffn_grads, out_grad, grad, att, rden, qkv, *before, wq, x, middle, y, y_other, gain,
        dgain, ids, table, ends,
    )


def deliver_kernel(count, *refs):
    ins, rest = refs[:count], refs[count:]
    down_in, gains_in, rest = rest[0], rest[1], rest[2:]
    outs, rest = rest[:count], rest[count:]
    down_out, one_out, two_out, rest = rest[0], rest[1], rest[2], rest[3:]
    bufs, (down, sem_in, sem_out) = rest[:count], rest[count:]
    loads, stores = [], []
    for i in range(count):
        loads.append(pltpu.make_async_copy(ins[i], bufs[i], sem_in.at[i]))
        stores.append(pltpu.make_async_copy(bufs[i], outs[i], sem_out.at[i]))
        loads[-1].start()
    down[...] = jnp.transpose(down_in[...])
    stores.append(pltpu.make_async_copy(down, down_out, sem_out.at[count]))
    stores[-1].start()
    turned = jnp.transpose(gains_in[...])
    one_out[...] = turned[0:1, :]
    two_out[...] = turned[1:2, :]
    for load, store in zip(loads, stores):
        load.wait()
        store.start()
    for store in stores:
        store.wait()


def deliver(plain, down, gains):
    count = len(plain)
    far, vmem = pl.BlockSpec(memory_space=pltpu.HBM), pl.BlockSpec(memory_space=pltpu.VMEM)
    small = gains.shape[0]
    return pl.pallas_call(
        functools.partial(deliver_kernel, count),
        out_shape=[jax.ShapeDtypeStruct(a.shape, a.dtype) for a in plain]
        + [jax.ShapeDtypeStruct(down.shape[::-1], F32)]
        + [jax.ShapeDtypeStruct((1, small), F32)] * 2,
        in_specs=[far] * count + [vmem] * 2,
        out_specs=[far] * (count + 1) + [vmem] * 2,
        scratch_shapes=[pltpu.VMEM(a.shape, a.dtype) for a in plain]
        + [pltpu.VMEM(down.shape[::-1], F32)]
        + [pltpu.SemaphoreType.DMA((count + 1,))] * 2,
        compiler_params=pltpu.CompilerParams(vmem_limit_bytes=62 << 20),
        name="deliver",
    )(*plain, down, gains)


def rms_scale(values, gain):
    return values * lax.rsqrt(jnp.mean(values * values, axis=-1, keepdims=True) + EPSILON) * gain


def swish_mix(gate, up_proj):
    return jax.nn.silu(gate) * up_proj


def dot_nn(a, b):
    return jnp.dot(a, b, preferred_element_type=F32)


def dot_nt(a, b):
    return lax.dot_general(a, b, (((1,), (1,)), ((), ())), preferred_element_type=F32)


def dot_tn(a, b):
    return lax.dot_general(a, b, (((0,), (0,)), ((), ())), preferred_element_type=F32)


def row_grads(left, right, by_head):
    head, core = lax.axis_index("head"), lax.axis_index("seq") % 2
    tokens = left.shape[0]
    chips = lax.axis_size("seq") // 2
    heads = 2 if by_head else 1
    rows = left.shape[1] // (heads * chips * 2)
    split = left.reshape(tokens, heads, chips, 2, rows)
    out = []
    for rel in range(heads):
        plane = pick(split, head ^ rel, 1) if by_head else split[:, 0]
        out.append([pick(plane, core ^ r, 2).reshape(tokens, chips * rows) for r in range(2)])
    if by_head:
        return [[dot_tn(part, right).astype(BF) for part in parts] for parts in out]
    return [[dot_tn(part, r).astype(BF) for part in out[0]] for r in right]


def plain_forward(
    inputs, segment_ids, norm1_gain, w_query, w_key, w_value, w_out, norm2_gain, w_gate, w_up,
    w_down, row_ids, col_ids, first, last, table,
):
    head, seq = lax.axis_index("head"), lax.axis_index("seq")
    n_seq = lax.axis_size("seq")
    rows, width = inputs.shape
    qk = HEADS * QD
    slot = head * n_seq + seq
    small = norm1_gain.shape[0]
    gains = jnp.zeros((2, width // small, small), F32)
    gains = lax.dynamic_update_slice(
        gains, jnp.stack([norm1_gain, norm2_gain]).astype(F32)[:, None, :], (0, slot, 0)
    ).reshape(2, width)
    gains = sum_everywhere(gains)
    gain_first, gain_second = gains[0], gains[1]

    qkv_full = gather_rows(jnp.concatenate([w_query, w_key, w_value], axis=1))
    out_full = gather_rows(w_out)
    gate_w = gather_halves(w_gate, False)
    up_w = gather_halves(w_up, False)
    down_w = gather_halves(w_down.T, True)

    normed_one = rms_scale(inputs, gain_first).astype(BF)
    qkv = dot_nn(normed_one, qkv_full).astype(BF)
    query, keys, values = qkv[:, :qk], qkv[:, qk : 2 * qk], qkv[:, 2 * qk :]
    vcols = HEADS * VD
    t_spec, q_spec = full_spec((8, FEATS)), full_spec((rows, qk))
    one_spec, row_spec = full_spec((rows, 1)), full_spec((1, rows))
    p_spec = pair_spec(rows)
    f32_like = jax.ShapeDtypeStruct((rows, vcols), F32)
    bf_like = jax.ShapeDtypeStruct((rows, vcols), BF)
    state = run(
        state_kernel,
        [t_spec, q_spec, p_spec, one_spec],
        state_specs(),
        STATE_SHAPES,
        (table, keys, values, last),
        flops=8 * rows * qk * FEATS * HEADS,
    )
    num, den = run(
        local_kernel,
        [q_spec, q_spec, p_spec, one_spec, row_spec],
        [p_spec, p_spec],
        [f32_like, f32_like],
        (query, keys, values, row_ids, col_ids),
        [pltpu.VMEM((rows, rows), F32)],
        flops=8 * rows * rows * qk * HEADS,
    )
    before = exchange(*state, segment_ids, rows, True)
    attended, rden = run(
        finish_kernel,
        [t_spec, q_spec, p_spec, p_spec, one_spec] + state_specs(),
        [p_spec, p_spec],
        [bf_like, f32_like],
        (table, query, num, den, first, *before),
        flops=8 * rows * qk * FEATS * HEADS,
    )
    residual = inputs + dot_nn(attended, out_full)
    normed_two = rms_scale(residual, gain_second).astype(BF)

    return (
        gate_w, up_w, down_w, qkv_full, out_full, gain_first, gain_second, normed_one,
        query, keys, values, attended, rden, residual, normed_two, before,
    )


def body(
    layer_input,
    segment_ids,
    norm1_gain,
    w_query,
    w_key,
    w_value,
    w_out,
    norm2_gain,
    w_gate,
    w_up,
    w_down,
    output_grad,
):
    rows = layer_input.shape[1]
    head, seq = lax.axis_index("head"), lax.axis_index("seq")
    n_seq = lax.axis_size("seq")
    qk = HEADS * QD
    inputs = layer_input[0].astype(F32)
    width = inputs.shape[1]

    table = jnp.asarray(feature_table())
    vcols = HEADS * VD
    t_spec, q_spec = full_spec((8, FEATS)), full_spec((rows, qk))
    one_spec, row_spec = full_spec((rows, 1)), full_spec((1, rows))
    p_spec = pair_spec(rows)
    f32_like = jax.ShapeDtypeStruct((rows, vcols), F32)
    bf_like = jax.ShapeDtypeStruct((rows, vcols), BF)
    slot = head * n_seq + seq
    small = norm1_gain.shape[0]

    if n_seq == 16:
        gain_cols = jnp.stack([norm1_gain, norm2_gain], axis=1)
        gain_cols = jnp.pad(gain_cols, ((0, 0), (0, GAIN_COLS - 2)))
        ids = segment_ids.reshape(2 * n_seq, rows)
        ends = jnp.concatenate([ids[:, 0], ids[:, rows - 1]])
        (
            g_own, u_own, d_own, dy_other, wq, wo, qkv, attended, rden, residual,
            normed_two, wide, thin, gains,
        ) = forward(
            layer_input[0],
            [w_query, w_key, w_value, gain_cols],
            w_out,
            [w_gate, w_up, w_down.T],
            output_grad[0],
            ids, table, ends,
        )
        d_gate, d_up, d_down, d_out, grad_attended, grad_middle, y, y_other, grad_gain = (
            feed_forward(
                normed_two, output_grad[0], dy_other, residual, [g_own, u_own, d_own],
                attended, wo, gains,
            )
        )
        d_gate, d_up, d_down, d_out, d_q, d_k, d_v, d_gains, grad_layer, outcome = backward(
            [d_gate, d_up, d_down], d_out, grad_attended, attended, rden, qkv, (wide, thin), wq,
            layer_input[0], grad_middle, y, y_other, gains, grad_gain, ids, table, ends,
        )
        (
            grad_layer, outcome, d_gate, d_up, d_v, d_out, d_q, d_k, d_down, gain_one, gain_two,
        ) = deliver(
            [grad_layer, outcome, d_gate, d_up, d_v, d_out, d_q, d_k], d_down, d_gains
        )
        return (
            outcome[None], grad_layer[None], gain_one[0], d_q, d_k, d_v, d_out, gain_two[0],
            d_gate, d_up, d_down,
        )

    segment = 2 * seq + head
    ids = lax.dynamic_slice_in_dim(segment_ids, segment * rows, rows)
    row_ids, col_ids = ids[:, None], ids[None, :]
    first = (row_ids == ids[0]).astype(F32)
    last = (row_ids == ids[rows - 1]).astype(F32)
    (
        gate_w, up_w, down_w, qkv_full, out_full, gain_first, gain_second, normed_one,
        query, keys, values, attended, rden, residual, normed_two, before,
    ) = plain_forward(
        inputs, segment_ids, norm1_gain, w_query, w_key, w_value, w_out, norm2_gain, w_gate,
        w_up, w_down, row_ids, col_ids, first, last, table,
    )

    grad_output = output_grad[0]
    outcome = residual
    grad_normed_two = None
    hiddens, grad_gates, grad_ups = [], [], []
    for w_g, w_u, w_d in zip(gate_w, up_w, down_w):
        gate = dot_nn(normed_two, w_g)
        up_proj = dot_nn(normed_two, w_u)
        grad_hidden = dot_nn(grad_output, w_d)
        hidden, mix_pull = jax.vjp(swish_mix, gate, up_proj)
        grad_gate, grad_up = mix_pull(grad_hidden)
        hiddens.append(hidden.astype(BF))
        grad_gates.append(grad_gate.astype(BF))
        grad_ups.append(grad_up.astype(BF))
        outcome = outcome + dot_nt(hiddens[-1], w_d)
        more = dot_nt(grad_gates[-1], w_g) + dot_nt(grad_ups[-1], w_u)
        grad_normed_two = more if grad_normed_two is None else grad_normed_two + more
    outcome = outcome.astype(BF)
    _, norm_pull = jax.vjp(rms_scale, residual, gain_second)
    grad_resid_two, grad_gain_two = norm_pull(grad_normed_two)
    grad_middle = grad_output.astype(F32) + grad_resid_two
    grad_middle_low = grad_middle.astype(BF)
    grad_attended = dot_nt(grad_middle_low, out_full).astype(BF)

    d_gate = scatter(row_grads(normed_two, grad_gates, False), True)
    d_up = scatter(row_grads(normed_two, grad_ups, False), True)
    d_down = scatter(row_grads(grad_output, hiddens, False), False).T

    d_out = scatter(row_grads(attended, grad_middle_low, True), True)

    grad_state = run(
        grad_state_kernel,
        [t_spec, q_spec, p_spec, p_spec, p_spec, one_spec],
        state_specs(),
        STATE_SHAPES,
        (table, query, grad_attended, attended, rden, first),
        flops=8 * rows * qk * FEATS * HEADS,
    )
    qk_f32 = jax.ShapeDtypeStruct((rows, qk), F32)
    qk_bf = jax.ShapeDtypeStruct((rows, qk), BF)
    grad_query, grad_key, grad_value = run(
        local_grad_kernel,
        [t_spec, q_spec, q_spec, p_spec, p_spec, p_spec, p_spec, one_spec, row_spec, one_spec]
        + state_specs(),
        [q_spec, q_spec, p_spec],
        [qk_bf, qk_f32, f32_like],
        (table, query, keys, values, grad_attended, attended, rden, row_ids, col_ids, first)
        + tuple(before),
        [pltpu.VMEM((rows, rows), F32), pltpu.VMEM((rows, qk), F32), pltpu.VMEM((rows, qk), F32)],
        flops=20 * rows * rows * qk * HEADS,
    )
    after = exchange(*grad_state, segment_ids, rows, False)
    grad_key, grad_value = run(
        finish_grad_kernel,
        [t_spec, q_spec, p_spec, q_spec, p_spec, one_spec] + state_specs(),
        [q_spec, p_spec],
        [qk_bf, bf_like],
        (table, keys, values, grad_key, grad_value, last, *after),
        [pltpu.VMEM((rows, qk), F32)],
        flops=16 * rows * qk * FEATS * HEADS,
    )
    grad_qkv = jnp.concatenate([grad_query, grad_key, grad_value], axis=1)
    d_qkv = scatter(row_grads(normed_one, grad_qkv, True), True)
    grad_normed_one = dot_nt(grad_qkv, qkv_full)
    _, first_pull = jax.vjp(rms_scale, inputs, gain_first)
    grad_inputs, grad_gain_one = first_pull(grad_normed_one)
    grad_layer = grad_middle + grad_inputs
    grad_gains = sum_everywhere(jnp.stack([grad_gain_one, grad_gain_two]))
    grad_gains = lax.dynamic_slice_in_dim(
        grad_gains.reshape(2, width // small, small), slot, 1, 1
    )[:, 0]
    return (
        outcome[None],
        grad_layer[None],
        grad_gains[0],
        d_qkv[:, :qk],
        d_qkv[:, qk : 2 * qk],
        d_qkv[:, 2 * qk :],
        d_out,
        grad_gains[1],
        d_gate,
        d_up,
        d_down,
    )


def solution(mesh):
    split = P(("head", "seq"))
    rows = P(("head", "seq"), None)
    block = P("seq", "head", None)
    wide, tall = P("seq", "head"), P("head", "seq")
    in_specs = (block, P(), split, rows, rows, rows, rows, split, wide, wide, tall, block)
    out_specs = (block, block, split, rows, rows, rows, rows, split, wide, wide, tall)
    return jax.shard_map(body, mesh=mesh, in_specs=in_specs, out_specs=out_specs, check_vma=False)
```

```python
import functools

import jax
import jax.numpy as jnp
import numpy as np
from jax import lax
from jax.experimental import pallas as pl
from jax.experimental.pallas import tpu as pltpu
from jax.sharding import PartitionSpec as P

HEADS = 16
QD = 16
VD = 64
DOC_MAX = 4096
EPSILON = 1e-05
PAIRS = HEADS // 2
WIDE = 2 * VD
FEATS = 160
TILE = 256
LANES = 128

BF = jnp.bfloat16
F32 = jnp.float32


def flip_seq(value, code):
    n = lax.axis_size("seq")
    return lax.ppermute(value, "seq", [(i, i ^ code) for i in range(n)])


def flip_head(value):
    n = lax.axis_size("head")
    return lax.ppermute(value, "head", [(i, i ^ 1) for i in range(n)])


def shift_seq(value, distance):
    n = lax.axis_size("seq")
    return lax.ppermute(
        value, "seq", [(i, i + distance) for i in range(n) if 0 <= i + distance < n]
    )


def layout():
    chips = lax.axis_size("seq") // 2
    near = 2 if chips <= 8 else 8
    far = chips // near
    return far, near


def place_kernel(groups, count, *refs):
    pieces, out, sem = refs[:count], refs[count], refs[count + 1]
    me = lax.axis_index("seq")
    head = lax.axis_index("head")
    n = lax.axis_size("seq")
    copies = []
    for piece, blocks in zip(pieces, groups):
        for index, (rel_head, rel_seq) in blocks:
            place = me ^ rel_seq
            if rel_head is not None:
                place = place + (head ^ rel_head) * n
            copies.append(
                pltpu.make_async_copy(piece.at[index], out.at[place], sem.at[len(copies)])
            )
    for copy in copies:
        copy.start()
    for copy in copies:
        copy.wait()


def place(pieces, groups, blocks):
    rows, cols = pieces[0].shape[-2:]
    total = sum(len(g) for g in groups)
    out = pl.pallas_call(
        functools.partial(place_kernel, groups, len(pieces)),
        out_shape=jax.ShapeDtypeStruct((blocks, rows, cols), pieces[0].dtype),
        in_specs=[pl.BlockSpec(memory_space=pl.ANY)] * len(pieces),
        out_specs=pl.BlockSpec(memory_space=pltpu.VMEM),
        scratch_shapes=[pltpu.SemaphoreType.DMA((total,))],
        compiler_params=pltpu.CompilerParams(vmem_limit_bytes=16 << 20),
        cost_estimate=pl.CostEstimate(
            flops=0, bytes_accessed=4 * blocks * rows * cols, transcendentals=0
        ),
        name="place",
    )(*pieces)
    return out.reshape(blocks * rows, cols)


def gather(shard, head_first):
    far, near = layout()
    far_codes = [2 * near * r for r in range(far)]
    near_codes = [2 * r for r in range(near)]
    if head_first:
        shard = jnp.stack([shard, flip_head(shard)])
    column = jnp.stack([shard] + [flip_seq(shard, code) for code in far_codes[1:]])
    held = [(column, 0, 0)]
    held += [(flip_seq(column, code), 0, code) for code in near_codes[1:]]
    if not head_first:
        held += [(flip_head(buf), 1, code) for buf, _, code in held]
    held += [(flip_seq(buf, 1), rel, code + 1) for buf, rel, code in held]
    result = []
    for buf, rel, code in held:
        if head_first:
            blocks = [((r, g), (g, code + far_codes[r])) for r in range(far) for g in range(2)]
        else:
            blocks = [((r,), (rel, code + far_codes[r])) for r in range(far)]
        result.append((buf, blocks))
    return result


def gather_rows(shard):
    got = gather(shard, False)
    return place([b for b, _ in got], [g for _, g in got], 2 * lax.axis_size("seq"))


def gather_halves(shard, head_first):
    got = gather(shard, head_first)
    halves = []
    for rel in range(2):
        pieces, groups = [], []
        for buf, blocks in got:
            mine = [(i, (None, code)) for i, (r, code) in blocks if r == rel]
            if mine:
                pieces.append(buf)
                groups.append(mine)
        halves.append(place(pieces, groups, lax.axis_size("seq")))
    return halves


def add_low(*terms):
    total = terms[0].astype(F32)
    for term in terms[1:]:
        total = total + term.astype(F32)
    return total.astype(BF)


def pick(value, index, axis):
    return lax.dynamic_index_in_dim(value, index, axis, keepdims=False)


def scatter(grads, head_first):
    far, near = layout()
    seq = lax.axis_index("seq")
    far_at, near_at = seq // (2 * near), (seq // 2) % near
    both = [
        add_low(grads[rel][0], flip_seq(grads[rel][1], 1)) for rel in range(2)
    ]
    rows = both[0].shape[0] // (far * near)
    cols = both[0].shape[1]
    if head_first:
        whole = add_low(both[0], flip_head(both[1])).reshape(far, near, rows, cols)
    else:
        whole = jnp.stack(both).reshape(2, far, near, rows, cols).transpose(1, 2, 0, 3, 4)
    parts = [pick(whole, near_at, 1)]
    parts += [flip_seq(pick(whole, near_at ^ r, 1), 2 * r) for r in range(1, near)]
    column = add_low(*parts)
    parts = [pick(column, far_at, 0)]
    parts += [flip_seq(pick(column, far_at ^ r, 0), 2 * near * r) for r in range(1, far)]
    if head_first:
        return sum(part.astype(F32) for part in parts)
    both = add_low(*parts)
    return both[0].astype(F32) + flip_head(both[1]).astype(F32)


def sum_everywhere(value):
    value = value + flip_head(value)
    code = 1
    while code < lax.axis_size("seq"):
        value = value + flip_seq(value, code)
        code *= 2
    return value


def feature_table():
    first, second, one, two, scale = [], [], [], [], []
    for a in range(QD):
        for b in range(a, QD):
            first.append(a)
            second.append(b)
            one.append(0.0)
            two.append(0.0)
            scale.append((1.0 if a == b else 2.0) / (2.0 * QD))
    for a in range(QD):
        first.append(a)
        second.append(-1000)
        one.append(0.0)
        two.append(1.0)
        scale.append(QD**-0.5)
    first.append(-1000)
    second.append(-1000)
    one.append(1.0)
    two.append(1.0)
    scale.append(1.0)
    pad = FEATS - len(first)
    table = np.zeros((8, FEATS), np.float32)
    table[0] = np.array(first + [-1000] * pad)
    table[1] = np.array(second + [-1000] * pad)
    table[2] = np.array(one + [0.0] * pad)
    table[3] = np.array(two + [0.0] * pad)
    table[4] = np.array(scale + [0.0] * pad)
    return table


def mm(a, b, dims):
    return lax.dot_general(a, b, ((dims[0], dims[1]), ((), ())), preferred_element_type=F32)


NN = ((1,), (0,))
NT = ((1,), (1,))
TN = ((0,), (0,))


def selectors(table, head, lanes=HEADS * QD):
    row = (lax.broadcasted_iota(jnp.int32, (lanes, FEATS), 0) - head * QD).astype(F32)
    one = (row == table[0:1, :]).astype(F32).astype(BF)
    two = (row == table[1:2, :]).astype(F32).astype(BF)
    return one, two


def factors(values, table, sel):
    return (
        mm(values, sel[0], NN) + table[2:3, :],
        mm(values, sel[1], NN) + table[3:4, :],
    )


def half_mask(rows, part):
    lane = lax.broadcasted_iota(jnp.int32, (rows, WIDE), 1)
    return (lane >= VD) if part else (lane < VD)


def head_mask(rows, head, lanes=HEADS * QD):
    lane = lax.broadcasted_iota(jnp.int32, (rows, lanes), 1)
    return (lane >= head * QD) & (lane < (head + 1) * QD)


def keep(mask, value):
    return jnp.where(mask, value.astype(F32), 0.0).astype(BF)


def state_kernel(table_ref, keys_ref, values_ref, last_ref, wide_ref, thin_ref):
    pair = pl.program_id(0)
    table = table_ref[...]
    keys = keys_ref[...]
    rows = keys.shape[0]
    last = last_ref[...]
    total = None
    for part in range(2):
        sel = selectors(table, 2 * pair + part)
        one, two = factors(keys, table, sel)
        phi = one * two * last
        value = keep(half_mask(rows, part), values_ref[...])
        new = mm(phi.astype(BF), value, TN)
        total = new if total is None else total + new
        thin_ref[0, part : part + 1, :] = jnp.sum(phi, axis=0, keepdims=True)
    thin_ref[0, 2:, :] = jnp.zeros((6, FEATS), F32)
    wide_ref[0] = total.astype(BF)


def visible_tile(mask_ref, row_ids_ref, col_ids_ref, rows):
    for i in range(rows // TILE):
        for j in range(i + 1):
            same = (
                row_ids_ref[i * TILE : (i + 1) * TILE, :]
                == col_ids_ref[:, j * TILE : (j + 1) * TILE]
            )
            if i == j:
                same = same & (
                    lax.broadcasted_iota(jnp.int32, (TILE, TILE), 1)
                    <= lax.broadcasted_iota(jnp.int32, (TILE, TILE), 0)
                )
            mask_ref[i * TILE : (i + 1) * TILE, j * TILE : (j + 1) * TILE] = same.astype(F32)


def local_kernel(
    query_ref, keys_ref, values_ref, row_ids_ref, col_ids_ref, num_ref, den_ref, mask_ref
):
    pair = pl.program_id(0)
    rows = query_ref.shape[0]

    @pl.when(pair == 0)
    def _():
        visible_tile(mask_ref, row_ids_ref, col_ids_ref, rows)

    for i in range(rows // TILE):
        here = slice(i * TILE, (i + 1) * TILE)
        num = jnp.zeros((TILE, WIDE), F32)
        dens = []
        for part in range(2):
            head = 2 * pair + part
            query = keep(head_mask(TILE, head), query_ref[here, :] * (QD**-0.5))
            den = jnp.zeros((TILE, 1), F32)
            for j in range(i + 1):
                there = slice(j * TILE, (j + 1) * TILE)
                s = mm(query, keys_ref[there, :], NT)
                w = (1.0 + s + 0.5 * s * s) * mask_ref[here, there]
                den = den + jnp.sum(w, axis=1, keepdims=True)
                num = num + mm(
                    w.astype(BF), keep(half_mask(TILE, part), values_ref[there, :]), NN
                )
            dens.append(den)
        num_ref[here, :] = num
        den_ref[here, :] = jnp.where(half_mask(TILE, 0), dens[0], dens[1])


def finish_kernel(
    table_ref, query_ref, num_ref, den_ref, first_ref, wide_ref, thin_ref, out_ref, rden_ref
):
    pair = pl.program_id(0)
    table = table_ref[...]
    query = query_ref[...]
    rows = query.shape[0]
    first = first_ref[...]
    num, den = num_ref[...], den_ref[...]
    for part in range(2):
        sel = selectors(table, 2 * pair + part)
        one, two = factors(query, table, sel)
        phi = one * two * (table[4:5, :] * first)
        mask = half_mask(rows, part)
        extra = mm(phi.astype(BF), wide_ref[0], NN)
        num = num + jnp.where(mask, extra, 0.0)
        more = jnp.sum(phi * thin_ref[0, part : part + 1, :], axis=1, keepdims=True)
        den = den + jnp.where(mask, more, 0.0)
    rden = 1.0 / den
    rden_ref[...] = rden
    out_ref[...] = (num * rden).astype(BF)


def prepare(grad_ref, out_ref, rden_ref):
    rows = grad_ref.shape[0]
    grad = grad_ref[...].astype(F32)
    rden = rden_ref[...]
    dnum = (grad * rden).astype(BF)
    prod = grad * out_ref[...].astype(F32) * rden
    deltas = [
        jnp.sum(jnp.where(half_mask(rows, part), prod, 0.0), axis=1, keepdims=True)
        for part in range(2)
    ]
    return dnum, deltas


def grad_state_kernel(
    table_ref, query_ref, grad_ref, out_ref, rden_ref, first_ref, wide_ref, thin_ref
):
    pair = pl.program_id(0)
    table = table_ref[...]
    query = query_ref[...]
    rows = query.shape[0]
    dnum, deltas = prepare(grad_ref, out_ref, rden_ref)
    total = None
    for part in range(2):
        sel = selectors(table, 2 * pair + part)
        one, two = factors(query, table, sel)
        phi = one * two * (table[4:5, :] * first_ref[...])
        new = mm(phi.astype(BF), keep(half_mask(rows, part), dnum), TN)
        total = new if total is None else total + new
        thin_ref[0, part : part + 1, :] = -jnp.sum(phi * deltas[part], axis=0, keepdims=True)
    thin_ref[0, 2:, :] = jnp.zeros((6, FEATS), F32)
    wide_ref[0] = total.astype(BF)


def local_grad_kernel(
    table_ref,
    query_ref,
    keys_ref,
    values_ref,
    grad_ref,
    out_ref,
    rden_ref,
    row_ids_ref,
    col_ids_ref,
    first_ref,
    wide_ref,
    thin_ref,
    dq_ref,
    dk_ref,
    dv_ref,
    mask_ref,
    dq_acc,
    dk_acc,
):
    pair = pl.program_id(0)
    table = table_ref[...]
    query = query_ref[...]
    keys = keys_ref[...]
    rows = query.shape[0]
    tiles = rows // TILE
    scale = QD**-0.5

    @pl.when(pair == 0)
    def _():
        visible_tile(mask_ref, row_ids_ref, col_ids_ref, rows)
        dq_acc[...] = jnp.zeros_like(dq_acc)
        dk_acc[...] = jnp.zeros_like(dk_acc)

    dnum, deltas = prepare(grad_ref, out_ref, rden_ref)
    dv = [jnp.zeros((TILE, WIDE), F32) for _ in range(tiles)]
    for part in range(2):
        head = 2 * pair + part
        at_head = head_mask(rows, head)
        q_head = keep(at_head, query * scale)
        k_head = keep(at_head, keys * scale)
        d_head = keep(half_mask(rows, part), dnum)
        for i in range(tiles):
            here = slice(i * TILE, (i + 1) * TILE)
            dq = dq_acc[here, :]
            for j in range(i + 1):
                there = slice(j * TILE, (j + 1) * TILE)
                s = mm(q_head[here], keys[there], NT)
                mask = mask_ref[here, there]
                w = ((1.0 + s + 0.5 * s * s) * mask).astype(BF)
                dp = mm(d_head[here], values_ref[there, :], NT)
                ds = ((dp - deltas[part][here]) * ((1.0 + s) * mask)).astype(BF)
                dq = dq + mm(ds, k_head[there], NN)
                dk_acc[there, :] += mm(ds, q_head[here], TN)
                dv[j] = dv[j] + mm(w, d_head[here], TN)
            dq_acc[here, :] = dq
        sel = selectors(table, head)
        one, two = factors(query, table, sel)
        dphi = mm(d_head, wide_ref[0], NT) - deltas[part] * thin_ref[0, part : part + 1, :]
        dphi = dphi * (table[4:5, :] * first_ref[...])
        dq_acc[...] += mm((dphi * two).astype(BF), sel[0], NT) + mm(
            (dphi * one).astype(BF), sel[1], NT
        )
    for j in range(tiles):
        dv_ref[j * TILE : (j + 1) * TILE, :] = dv[j]

    @pl.when(pair == PAIRS - 1)
    def _():
        dq_ref[...] = dq_acc[...].astype(BF)
        dk_ref[...] = dk_acc[...]


def finish_grad_kernel(
    table_ref, keys_ref, values_ref, dk_in_ref, dv_in_ref, last_ref, wide_ref, thin_ref,
    dk_ref, dv_ref, dk_acc,
):
    pair = pl.program_id(0)
    table = table_ref[...]
    keys = keys_ref[...]
    rows = keys.shape[0]
    last = last_ref[...]

    @pl.when(pair == 0)
    def _():
        dk_acc[...] = dk_in_ref[...]

    dv = dv_in_ref[...]
    for part in range(2):
        sel = selectors(table, 2 * pair + part)
        one, two = factors(keys, table, sel)
        mask = half_mask(rows, part)
        phi = one * two * last
        dv = dv + jnp.where(mask, mm(phi.astype(BF), wide_ref[0], NN), 0.0)
        dphi = mm(keep(mask, values_ref[...]), wide_ref[0], NT) + thin_ref[0, part : part + 1, :]
        dphi = dphi * last
        dk_acc[...] += mm((dphi * two).astype(BF), sel[0], NT) + mm(
            (dphi * one).astype(BF), sel[1], NT
        )
    dv_ref[...] = dv.astype(BF)

    @pl.when(pair == PAIRS - 1)
    def _():
        dk_ref[...] = dk_acc[...].astype(BF)


def full_spec(shape):
    return pl.BlockSpec(shape, lambda p: (0,) * len(shape))


def pair_spec(rows):
    return pl.BlockSpec((rows, WIDE), lambda p: (0, p))


def state_specs():
    return [
        pl.BlockSpec((1, FEATS, WIDE), lambda p: (p, 0, 0)),
        pl.BlockSpec((1, 8, FEATS), lambda p: (p, 0, 0)),
    ]


STATE_SHAPES = (
    jax.ShapeDtypeStruct((PAIRS, FEATS, WIDE), BF),
    jax.ShapeDtypeStruct((PAIRS, 8, FEATS), F32),
)


def run(kernel, in_specs, out_specs, out_shape, args, scratch=(), flops=0):
    moved = sum(a.size * a.dtype.itemsize for a in args)
    return pl.pallas_call(
        kernel,
        grid=(PAIRS,),
        in_specs=in_specs,
        out_specs=out_specs,
        out_shape=out_shape,
        scratch_shapes=scratch,
        compiler_params=pltpu.CompilerParams(vmem_limit_bytes=48 << 20),
        cost_estimate=pl.CostEstimate(flops=flops, bytes_accessed=moved, transcendentals=0),
        name=kernel.__name__,
    )(*args)


def exchange(wide, thin, ids, rows, forward):
    head, seq = lax.axis_index("head"), lax.axis_index("seq")
    n = lax.axis_size("seq")
    segments = 2 * n
    firsts = ids.reshape(segments, rows)[:, 0]
    lasts = ids.reshape(segments, rows)[:, rows - 1]
    step = 1 if forward else -1
    near_end, far_end = (lasts, firsts) if forward else (firsts, lasts)

    def end_of(which, segment):
        return which[jnp.clip(segment, 0, segments - 1)]

    seg = 2 * seq + head
    takes = end_of(far_end, seg)
    core = seq % 2
    late_head = head if forward else 1 - head
    late_core = core if forward else 1 - core

    def gate(flag):
        return jnp.where(flag, 1.0, 0.0).astype(F32)

    def wider(state):
        return [part.astype(F32) for part in state]

    def narrow(state):
        return [state[0].astype(BF), state[1]]

    def merge(own, other, late, other_takes, joined):
        gained = [part * (gate(other_takes) * late) for part in other]
        own_factor = jnp.where(late == 1, 1.0, gate(joined))
        other_factor = jnp.where(late == 1, gate(joined), 1.0)
        joint = [a * own_factor + b * other_factor for a, b in zip(own, other)]
        return gained, joint

    own = [wide, thin]
    other = [flip_head(part) for part in own]
    first_of, second_of = 2 * seq, 2 * seq + 1
    if not forward:
        first_of, second_of = second_of, first_of
    total, joint = merge(
        wider(own),
        wider(other),
        late_head,
        end_of(near_end, seg - step) == takes,
        end_of(near_end, first_of) == end_of(near_end, second_of),
    )
    joint = narrow(joint)
    other = [flip_seq(part, 1) for part in joint]
    base = 4 * (seq // 2)
    early_end, late_end = (base + 1, base + 3) if forward else (base + 2, base)
    gained, joint = merge(
        wider(joint),
        wider(other),
        late_core,
        end_of(near_end, early_end) == takes,
        end_of(near_end, early_end) == end_of(near_end, late_end),
    )
    total = [a + b for a, b in zip(total, gained)]
    joint = narrow(joint)
    half = PAIRS // 2
    mine = [lax.dynamic_slice_in_dim(part, core * half, half, 0) for part in joint]
    hops = -(-DOC_MAX // (4 * rows))
    far = None
    for hop in range(1, hops + 1):
        got = wider([shift_seq(part, 2 * hop * step) for part in mine])
        nearer, farther = late_end - 4 * step, late_end - 4 * step * hop
        joined = gate(end_of(near_end, nearer) == end_of(near_end, farther))
        got = [part * joined for part in got]
        far = got if far is None else [a + b for a, b in zip(far, got)]
    far = narrow(far)
    other = [flip_seq(part, 1) for part in far]
    comes = (seq // 2 >= 1) if forward else (seq // 2 < n // 2 - 1)
    use = gate(comes & (end_of(near_end, late_end - 4 * step) == takes))
    result = []
    for a, b, so_far in zip(far, other, total):
        low = jnp.where(core == 0, a, b).astype(F32)
        high = jnp.where(core == 0, b, a).astype(F32)
        result.append(so_far + use * jnp.concatenate([low, high], axis=0))
    return narrow(result)


MESH = pl.DeviceIdType.MESH
GAIN_COLS = 128


class Links:
    def __init__(self):
        self.head, self.seq = lax.axis_index("head"), lax.axis_index("seq")
        self.n = lax.axis_size("seq")
        self.z, self.y, self.c = self.seq // 4, (self.seq // 2) % 2, self.seq % 2
        self.core = self.at(self.head, self.seq ^ 1)
        self.x = self.at(1 - self.head, self.seq)
        self.near = self.at(self.head, self.seq ^ 2)
        self.far = [self.at(self.head, self.seq ^ (4 * r)) for r in range(4)]

    def at(self, head, seq):
        return {"head": head, "seq": seq}

    def shifted(self, distance):
        return self.at(self.head, lax.rem(self.seq + distance + self.n, self.n))

    def greet(self):
        barrier = pltpu.get_barrier_semaphore()
        partners = [self.core, self.x, self.near] + self.far[1:]
        partners += [self.shifted(d) for d in (2, 4, -2, -4)]
        for partner in partners:
            pl.semaphore_signal(barrier, inc=1, device_id=partner, device_id_type=MESH)
        pl.semaphore_wait(barrier, len(partners))


class Copies:
    def __init__(self, send, recv, local):
        self.send, self.recv, self.local = send, recv, local
        self.used, self.used_local = 0, 0
        self.started, self.started_local = [], []

    def remote(self, src, dst, partner):
        i = self.used
        self.used += 1
        return pltpu.make_async_remote_copy(
            src_ref=src,
            dst_ref=dst,
            send_sem=self.send.at[i],
            recv_sem=self.recv.at[i],
            device_id=partner,
            device_id_type=MESH,
        )

    def go(self, *copies):
        for copy in copies:
            copy.start()
            self.started.append(copy)

    def keep(self, src, dst):
        copy = pltpu.make_async_copy(src, dst, self.local.at[self.used_local])
        self.used_local += 1
        copy.start()
        self.started_local.append(copy)
        return copy

    def finish(self, copy):
        copy.wait()
        self.started_local = [other for other in self.started_local if other is not copy]

    def drain(self):
        for copy in self.started:
            copy.wait_send()
        for copy in self.started_local:
            copy.wait()


def arrived(*copies):
    for copy in copies:
        copy.wait_recv()


class WideGather:
    def __init__(self, copies, links, shard, own, other, other_there, near_last=False):
        n, y, c = links, links.y, links.c
        self.copies, self.near_last = copies, near_last
        self.place = own.at[n.z, y, c]
        self.shard = shard
        self.far = [copies.remote(shard, self.place, n.far[r]) for r in range(1, 4)]
        mine, theirs = own.at[:, y, c], own.at[:, 1 - y, c]
        self.near = copies.remote(mine, mine, n.near)
        across = other.at[:, y, c]
        self.cross = copies.remote(mine, other_there.at[:, y, c], n.x)
        if near_last:
            self.last = copies.remote(across, across, n.near)
        else:
            self.last = copies.remote(theirs, other_there.at[:, 1 - y, c], n.x)
        self.core = [
            copies.remote(part, part, n.core)
            for part in (mine, theirs, other.at[:, y, c], other.at[:, 1 - y, c])
        ]

    def begin(self):
        self.copies.go(*self.far)
        self.own = self.copies.keep(self.shard, self.place)

    def far_here(self):
        arrived(*self.far)
        self.copies.finish(self.own)

    def one(self):
        self.copies.go(self.near, self.cross, self.core[0])

    def two(self):
        arrived(self.near)
        if not self.near_last:
            self.copies.go(self.last)
        self.copies.go(self.core[1])

    def three(self):
        arrived(self.cross)
        if self.near_last:
            self.copies.go(self.last)
        self.copies.go(self.core[2])

    def four(self):
        arrived(self.last)
        self.copies.go(self.core[3])

    def end(self):
        arrived(*self.core)


class PlaneGather:
    COPIES = 6

    def __init__(self, copies, links, shard, own):
        n, y, c = links, links.y, links.c
        self.copies, self.shard, self.place = copies, shard, own.at[n.z, y, c]
        self.far = [copies.remote(shard, self.place, n.far[r]) for r in range(1, 4)]
        mine, theirs = own.at[:, y, c], own.at[:, 1 - y, c]
        self.near = copies.remote(mine, mine, n.near)
        self.core = [copies.remote(part, part, n.core) for part in (mine, theirs)]

    def begin(self):
        self.copies.go(*self.far)
        self.own = self.copies.keep(self.shard, self.place)

    def far_here(self):
        arrived(*self.far)
        self.copies.finish(self.own)

    def one(self):
        self.copies.go(self.near, self.core[0])

    def two(self):
        arrived(self.near)
        self.copies.go(self.core[1])

    def end(self):
        arrived(*self.core)


class Exchange:
    def __init__(self, copies, links, gates, first, bufs, forward):
        n = links
        self.copies, self.gates, self.first, self.bufs = copies, gates, first, bufs
        half = PAIRS // 2
        step = 2 if forward else -2
        own, a, j, b, j2, r1, r2, far = bufs

        def both(src, dst, partner, groups=4):
            size = src[0].shape[0] // groups
            cuts = [pl.ds(i * size, size) for i in range(groups)]
            made = [copies.remote(src[0].at[cut], dst[0].at[cut], partner) for cut in cuts]
            return made + [copies.remote(src[1], dst[1], partner)]

        def halves(state):
            return [
                state[0].at[pl.ds(n.c * half, half)],
                state[1].at[pl.ds(n.c * half, half)],
            ]

        self.rounds = [
            both(own, a, n.x),
            both(j, b, n.core, 1),
            both(halves(j2), r1, n.shifted(step)) + both(halves(j2), r2, n.shifted(2 * step)),
            both(halves(far), halves(far), n.core, 1),
        ]
        self.halves = halves
        self.total = None

    def gate(self, i):
        return self.gates[self.first + i]

    def begin(self):
        self.copies.go(*self.rounds[0])

    def one(self):
        own, a, j, b, j2, r1, r2, far = self.bufs
        arrived(*self.rounds[0])
        for s, d, t in zip(own, a, j):
            t[...] = (
                s[...].astype(F32) * self.gate(1) + d[...].astype(F32) * self.gate(2)
            ).astype(t.dtype)
        self.copies.go(*self.rounds[1])

    def two(self):
        own, a, j, b, j2, r1, r2, far = self.bufs
        arrived(*self.rounds[1])
        for s, d, t in zip(j, b, j2):
            t[...] = (
                s[...].astype(F32) * self.gate(4) + d[...].astype(F32) * self.gate(5)
            ).astype(t.dtype)
        self.copies.go(*self.rounds[2])

    def three(self):
        own, a, j, b, j2, r1, r2, far = self.bufs
        arrived(*self.rounds[2])
        for s, d, t in zip(r1, r2, self.halves(far)):
            t[...] = (s[...].astype(F32) + d[...].astype(F32) * self.gate(6)).astype(t.dtype)
        self.copies.go(*self.rounds[3])

    def four(self, out):
        own, a, j, b, j2, r1, r2, far = self.bufs
        arrived(*self.rounds[3])
        for s, d, f, t in zip(a, b, far, out):
            t[...] = (
                s[...].astype(F32) * self.gate(0)
                + d[...].astype(F32) * self.gate(3)
                + f[...].astype(F32) * self.gate(7)
            ).astype(t.dtype)


def exchange_shapes():
    shapes = []
    for name in range(8):
        pairs = PAIRS // 2 if name in (5, 6) else PAIRS
        shapes += [pltpu.VMEM((pairs, FEATS, WIDE), BF), pltpu.VMEM((pairs, 8, FEATS), F32)]
    return shapes


def documents(ids_ref, ends_ref, links, mask, first, last):
    rows = ids_ref.shape[1]
    segment = 2 * links.seq + links.head
    row = ids_ref[pl.ds(segment, 1), :].astype(F32)
    column = jnp.transpose(jnp.broadcast_to(row, (128, rows)))[:, :1]
    visible_tile(mask, column, row, rows)
    first[...] = (column == ends_ref[segment].astype(F32)).astype(F32)
    last[...] = (column == ends_ref[2 * links.n + segment].astype(F32)).astype(F32)


def exchange_gates(ends_ref, links, forward):
    head, seq, core, n = links.head, links.seq, links.c, links.n
    segments = 2 * n
    step = 1 if forward else -1
    near_at, far_at = (segments, 0) if forward else (0, segments)
    seg = 2 * seq + head
    chip = seq // 2
    base = 4 * chip
    late_head = (head == 1) if forward else (head == 0)
    late_core = (core == 1) if forward else (core == 0)
    pair_early, pair_late = (2 * seq, 2 * seq + 1) if forward else (2 * seq + 1, 2 * seq)
    early_end, late_end = (base + 1, base + 3) if forward else (base + 2, base)
    near_ok = (chip >= 1) if forward else (chip < n // 2 - 1)
    far_ok = (chip >= 2) if forward else (chip < n // 2 - 2)

    def doc(segment):
        return ends_ref[near_at + jnp.minimum(jnp.maximum(segment, 0), segments - 1)]

    def factor(flag):
        return jnp.where(flag, 1.0, 0.0).astype(F32)

    takes = ends_ref[far_at + seg]
    joined = doc(pair_early) == doc(pair_late)
    joined2 = doc(early_end) == doc(late_end)
    nearer, farther = doc(late_end - 4 * step), doc(late_end - 8 * step)
    flags = [
        late_head & (doc(seg - step) == takes),
        late_head | joined,
        jnp.logical_not(late_head) | joined,
        late_core & (doc(early_end) == takes),
        late_core | joined2,
        jnp.logical_not(late_core) | joined2,
        far_ok & (nearer == farther),
        near_ok & (nearer == takes),
    ]
    return [factor(flag) for flag in flags]


def pair_lanes(pair, start=0):
    return pl.ds(pl.multiple_of(start + pair * WIDE, WIDE), WIDE)


def head_tile(pair, part):
    tile = pair // (LANES // (2 * QD))
    return tile, 2 * pair + part - tile * (LANES // QD)


def tile_lanes(pair, start=0):
    return pl.ds(pl.multiple_of(start + head_tile(pair, 0)[0] * LANES, LANES), LANES)


def state_pair(pair, table, qkv, last, wide_ref, thin_ref):
    rows = qkv.shape[0]
    qk = HEADS * QD
    keys, value = qkv[:, tile_lanes(pair, qk)], qkv[:, pair_lanes(pair, 2 * qk)]
    total = None
    for part in range(2):
        sel = selectors(table, head_tile(pair, part)[1], LANES)
        one, two = factors(keys, table, sel)
        phi = one * two * last
        new = mm(phi.astype(BF), keep(half_mask(rows, part), value), TN)
        total = new if total is None else total + new
        thin_ref[pair, part : part + 1, :] = jnp.sum(phi, axis=0, keepdims=True)
    thin_ref[pair, 2:, :] = jnp.zeros((6, FEATS), F32)
    wide_ref[pair] = total.astype(BF)


def local_pair(pair, qkv, num_ref, den_ref, mask_ref):
    rows = qkv.shape[0]
    qk = HEADS * QD
    for i in range(rows // TILE):
        here = slice(i * TILE, (i + 1) * TILE)
        num = jnp.zeros((TILE, WIDE), F32)
        dens = []
        for part in range(2):
            head = head_tile(pair, part)[1]
            query = keep(
                head_mask(TILE, head, LANES), qkv[here, tile_lanes(pair)] * (QD**-0.5)
            )
            den = jnp.zeros((TILE, 1), F32)
            for j in range(i + 1):
                there = slice(j * TILE, (j + 1) * TILE)
                s = mm(query, qkv[there, tile_lanes(pair, qk)], NT)
                mask = mask_ref[here, there]
                t = (1.0 + s) * mask
                w = t * t + mask
                den = den + jnp.sum(w, axis=1, keepdims=True)
                value = qkv[there, pair_lanes(pair, 2 * qk)]
                num = num + mm(w.astype(BF), keep(half_mask(TILE, part), value), NN)
            dens.append(den)
        num_ref[here, pair_lanes(pair)] = 0.5 * num
        den_ref[here, pair_lanes(pair)] = 0.5 * jnp.where(half_mask(TILE, 0), dens[0], dens[1])


def finish_pair(pair, table, qkv, first, num_ref, den_ref, wide_ref, thin_ref, out_ref):
    rows = qkv.shape[0]
    query = qkv[:, tile_lanes(pair)]
    lanes = pair_lanes(pair)
    num, den = num_ref[:, lanes], den_ref[:, lanes]
    for part in range(2):
        sel = selectors(table, head_tile(pair, part)[1], LANES)
        one, two = factors(query, table, sel)
        phi = one * two * (table[4:5, :] * first)
        mask = half_mask(rows, part)
        num = num + jnp.where(mask, mm(phi.astype(BF), wide_ref[pair], NN), 0.0)
        more = jnp.sum(phi * thin_ref[pair, part : part + 1, :], axis=1, keepdims=True)
        den = den + jnp.where(mask, more, 0.0)
    rden = 1.0 / den
    den_ref[:, lanes] = rden
    out_ref[:, lanes] = (num * rden).astype(BF)


def each_pair(low, high, step):
    def one(pair, carry):
        step(pair)
        return carry

    lax.fori_loop(low, high, one, 0)


WIDE_COPIES, EXCHANGE_COPIES = 10, 19
FWD_COPIES = 3 * WIDE_COPIES + 6 * PlaneGather.COPIES + EXCHANGE_COPIES + 1
FWD_LOCALS = 20


def forward_kernel(
    x_ref, wq_ref, wk_ref, wv_ref, gs_in, os_ref, gs_ref, us_ref, ds_ref, ids_ref, table_ref,
    dy_ref, ends_ref,
    g_own, u_own, d_own, dy_out, wq_out, wo_out, qkv_out, att_out, rden_out,
    res_out, n2_out, wide_out, thin_out, gain_out,
    wq, wo, normed, qkv, num, den, mask, first_ref, last_ref, att, res, n2, wide, thin, gain,
    qs_ref, *rest,
):
    bufs, (send, recv, local) = rest[:16], rest[16:]
    states = [(bufs[2 * i], bufs[2 * i + 1]) for i in range(8)]
    n = Links()
    copies = Copies(send, recv, local)
    rows, width = x_ref.shape
    qk, hv = HEADS * QD, HEADS * VD
    cut = 7 * 128
    full = wq.shape[-1]

    def side(ref, head, lo=None, hi=None):
        return ref.at[head] if lo is None else ref.at[head, :, :, :, :, pl.ds(lo, hi - lo)]

    q_parts = []
    for lo, hi in ((0, cut), (cut, full)):
        shard = qs_ref.at[:, pl.ds(lo, hi - lo)]
        own, other = side(wq, n.head, lo, hi), side(wq, 1 - n.head, lo, hi)
        q_parts.append(WideGather(copies, n, shard, own, other, own, near_last=lo > 0))
    own, other = side(wo, n.head), side(wo, 1 - n.head)
    outs = WideGather(copies, n, os_ref, own, other, own)
    ffn = []
    for shard, own in ((gs_ref, g_own), (us_ref, u_own), (ds_ref, d_own)):
        for lo, hi in half_columns(ds_ref.shape[-1]):
            part = own.at[:, :, :, :, pl.ds(lo, hi - lo)]
            ffn.append(PlaneGather(copies, n, shard.at[:, pl.ds(lo, hi - lo)], part))

    def pass_on(i):
        ffn[i].far_here()
        ffn[i].one()
        if i + 2 < len(ffn):
            ffn[i + 2].begin()
        if i >= 2:
            ffn[i - 2].two()

    other_dy = copies.remote(dy_ref, dy_out, n.x)
    swap = Exchange(copies, n, exchange_gates(ends_ref, n, True), 0, states, True)

    qs_ref[:, :qk] = wq_ref[...]
    qs_ref[:, qk : 2 * qk] = wk_ref[...]
    qs_ref[:, 2 * qk : 2 * qk + hv] = wv_ref[...]
    qs_ref[:, 2 * qk + hv :] = gs_in[...]
    n.greet()
    for part in q_parts:
        part.begin()

    table = table_ref[...]
    x = x_ref[...].astype(F32)
    scaled = x * lax.rsqrt(jnp.mean(x * x, axis=-1, keepdims=True) + EPSILON)
    documents(ids_ref, ends_ref, n, mask, first_ref, last_ref)
    for part in q_parts:
        part.far_here()
        part.one()
    outs.begin()
    ffn[0].begin()
    q_parts[0].two()
    q_parts[1].three()
    q_parts[1].two()
    q_parts[0].three()
    outs.far_here()
    ffn[1].begin()
    for part in q_parts:
        part.four()
    outs.one()
    for part in q_parts:
        part.end()
    pass_on(0)

    pick_gain = (
        lax.broadcasted_iota(jnp.int32, (8, GAIN_COLS), 0)
        == lax.broadcasted_iota(jnp.int32, (8, GAIN_COLS), 1)
    ).astype(F32).astype(BF)
    gain[...] = mm(pick_gain, wq[..., full - GAIN_COLS :].reshape(width, GAIN_COLS), NT)
    normed[...] = (scaled * gain[0:1, :]).astype(BF)

    def project(i):
        at = pl.ds(pl.multiple_of(i * 512, 512), 512)
        weight = wq[:, :, :, :, :, at].reshape(width, 512)
        qkv[:, at] = mm(normed[...], weight, NN).astype(BF)

    each_pair(0, (2 * qk + hv) // 512, project)
    copies.keep(qkv, qkv_out)
    copies.keep(wq, wq_out)
    copies.keep(gain, gain_out)

    def do_state(pair):
        state_pair(
            pair, table, qkv, last_ref[...], states[0][0], states[0][1]
        )

    def do_local(pair):
        local_pair(pair, qkv, num, den, mask)

    def do_finish(pair):
        finish_pair(
            pair, table, qkv, first_ref[...], num, den, wide, thin, att
        )

    each_pair(0, PAIRS // 2, do_state)
    outs.two()
    outs.three()
    pass_on(1)
    each_pair(PAIRS // 2, PAIRS, do_state)
    swap.begin()
    outs.four()
    each_pair(0, 4, do_local)
    swap.one()
    pass_on(2)
    each_pair(4, 5, do_local)
    swap.two()
    copies.go(other_dy)
    each_pair(5, PAIRS, do_local)
    pass_on(3)
    swap.three()
    swap.four((wide, thin))
    copies.keep(wide, wide_out)
    copies.keep(thin, thin_out)
    each_pair(0, 4, do_finish)
    pass_on(4)
    each_pair(4, PAIRS, do_finish)
    outs.end()
    copies.keep(wo, wo_out)
    copies.keep(att, att_out)
    copies.keep(den, rden_out)

    def leave(i):
        at = pl.ds(pl.multiple_of(i * 512, 512), 512)
        weight = wo[:, :, :, :, :, at].reshape(hv, 512)
        res[:, at] = x_ref[:, at].astype(F32) + mm(att[...], weight, NN)

    each_pair(0, width // 512, leave)
    copies.keep(res, res_out)
    y1 = res[...]
    n2[...] = (
        y1 * lax.rsqrt(jnp.mean(y1 * y1, axis=-1, keepdims=True) + EPSILON) * gain[1:2, :]
    ).astype(BF)
    copies.keep(n2, n2_out)
    pass_on(5)
    ffn[4].two()
    ffn[5].two()
    for part in ffn:
        part.end()
    arrived(other_dy)
    copies.drain()


def forward(x, projections, o_shard, ffn, dy, ids, table, ends):
    rows, width = x.shape
    qk, hv = HEADS * QD, HEADS * VD
    full = sum(part.shape[1] for part in projections)
    small, fine, ff = o_shard.shape[0], ffn[0].shape[0], ffn[0].shape[1]
    half = jax.ShapeDtypeStruct((4, 2, 2, fine, ff), BF)
    wq_shape, wo_shape = (2, 4, 2, 2, small, full), (2, 4, 2, 2, small, width)

    def like(shape, dtype):
        return jax.ShapeDtypeStruct(shape, dtype)

    out_shape = [half] * 3 + [
        like(dy.shape, BF), like(wq_shape, BF), like(wo_shape, BF), like((rows, 2 * qk + hv), BF),
        like((rows, hv), BF), like((rows, hv), F32), like((rows, width), F32),
        like((rows, width), BF), STATE_SHAPES[0], STATE_SHAPES[1], like((8, width), F32),
    ]
    scratch = [
        pltpu.VMEM(wq_shape, BF), pltpu.VMEM(wo_shape, BF), pltpu.VMEM((rows, width), BF),
        pltpu.VMEM((rows, 2 * qk + hv), BF), pltpu.VMEM((rows, hv), F32),
        pltpu.VMEM((rows, hv), F32), pltpu.VMEM((rows, rows), F32), pltpu.VMEM((rows, 1), F32),
        pltpu.VMEM((rows, 1), F32), pltpu.VMEM((rows, hv), BF),
        pltpu.VMEM((rows, width), F32), pltpu.VMEM((rows, width), BF),
        pltpu.VMEM((PAIRS, FEATS, WIDE), BF), pltpu.VMEM((PAIRS, 8, FEATS), F32),
        pltpu.VMEM((8, width), F32), pltpu.VMEM((small, full), BF),
    ] + exchange_shapes() + [
        pltpu.SemaphoreType.DMA((FWD_COPIES,)), pltpu.SemaphoreType.DMA((FWD_COPIES,)),
        pltpu.SemaphoreType.DMA((FWD_LOCALS,)),
    ]
    vmem = pl.BlockSpec(memory_space=pltpu.VMEM)
    return pl.pallas_call(
        forward_kernel,
        out_shape=out_shape,
        in_specs=[vmem] * 11
        + [pl.BlockSpec(memory_space=pl.ANY)]
        + [pl.BlockSpec(memory_space=pltpu.SMEM)],
        out_specs=[pl.BlockSpec(memory_space=pl.ANY)] * len(out_shape),
        scratch_shapes=scratch,
        compiler_params=pltpu.CompilerParams(
            collective_id=1, has_side_effects=True, vmem_limit_bytes=56 << 20
        ),
        cost_estimate=pl.CostEstimate(flops=8 << 30, bytes_accessed=64 << 20, transcendentals=0),
        name="forward",
    )(x, *projections, o_shard, *ffn, ids, table, dy, ends)


def as_f32(ref, index):
    return ref[index].astype(F32)


class WideScatter:
    REMOTE, LOCAL = 7, 3

    def __init__(self, copies, links, own, other, bufs, out):
        n, y, c = links, links.y, links.c
        self.n, self.copies, self.out = n, copies, out
        a_own, a_oth, c_own, c_oth, xx, yy, zz, done = bufs
        self.bufs = bufs
        self.own_part, self.oth_part = own.at[:, :, c], other.at[:, :, c]
        self.core = [
            copies.remote(other.at[:, :, 1 - c], c_oth, n.core),
            copies.remote(own.at[:, :, 1 - c], c_own, n.core),
        ]
        self.cross = copies.remote(a_oth, xx, n.x)
        self.near = copies.remote(a_own.at[:, 1 - y], yy, n.near)
        self.far = [
            copies.remote(a_own.at[n.z ^ r, y], zz.at[r - 1], n.far[r]) for r in range(1, 4)
        ]

    def begin(self):
        a_own, a_oth = self.bufs[:2]
        self.copies.go(*self.core)
        self.loads = [
            self.copies.keep(self.oth_part, a_oth), self.copies.keep(self.own_part, a_own)
        ]

    def loaded(self, i):
        self.copies.finish(self.loads[i])

    def one(self):
        a_own, a_oth, c_own, c_oth, xx, yy, zz, done = self.bufs
        self.loaded(0)
        arrived(self.core[0])

        def add(i, carry):
            for at in ((i, 0), (i, 1)):
                a_oth[at] = (as_f32(a_oth, at) + as_f32(c_oth, at)).astype(BF)
            return carry

        lax.fori_loop(0, 4, add, 0)
        self.copies.go(self.cross)

    def two(self):
        a_own, a_oth, c_own, c_oth, xx, yy, zz, done = self.bufs
        self.loaded(1)
        arrived(self.core[1], self.cross)

        def add(i, carry):
            for at in ((i, 0), (i, 1)):
                total = as_f32(a_own, at) + as_f32(c_own, at) + as_f32(xx, at)
                a_own[at] = total.astype(BF)
            return carry

        lax.fori_loop(0, 4, add, 0)
        self.copies.go(self.near)

    def three(self):
        a_own, a_oth, c_own, c_oth, xx, yy, zz, done = self.bufs
        arrived(self.near)

        def add(i, carry):
            at = (i, self.n.y)
            a_own[at] = (as_f32(a_own, at) + as_f32(yy, i)).astype(BF)
            return carry

        lax.fori_loop(0, 4, add, 0)
        self.copies.go(*self.far)

    def four(self):
        a_own, a_oth, c_own, c_oth, xx, yy, zz, done = self.bufs
        arrived(*self.far)
        total = as_f32(a_own, (self.n.z, self.n.y))
        for r in range(3):
            total = total + as_f32(zz, r)
        done[...] = total
        if self.out is not None:
            self.copies.keep(done, self.out)

    @staticmethod
    def shapes(rows, cols):
        part = [pltpu.VMEM((4, 2, rows, cols), BF)]
        return part * 5 + [
            pltpu.VMEM((4, rows, cols), BF), pltpu.VMEM((3, rows, cols), BF),
            pltpu.VMEM((rows, cols), F32),
        ]


class PlaneScatter:
    REMOTE = 5

    def __init__(self, copies, links, own, bufs, out):
        n, y, c = links, links.y, links.c
        self.n, self.copies, self.out, self.bufs = n, copies, out, bufs
        a, cc, yy, zz, done = bufs
        self.part = own.at[:, :, c]
        self.core = copies.remote(own.at[:, :, 1 - c], cc, n.core)
        self.near = copies.remote(a.at[:, 1 - y], yy, n.near)
        self.far = [copies.remote(a.at[n.z ^ r, y], zz.at[r - 1], n.far[r]) for r in range(1, 4)]

    def begin(self):
        self.copies.go(self.core)
        self.load = self.copies.keep(self.part, self.bufs[0])

    def one(self):
        a, cc, yy, zz, done = self.bufs
        self.copies.finish(self.load)
        arrived(self.core)

        def add(i, carry):
            for at in ((i, 0), (i, 1)):
                a[at] = (as_f32(a, at) + as_f32(cc, at)).astype(BF)
            return carry

        lax.fori_loop(0, 4, add, 0)
        self.copies.go(self.near)

    def two(self):
        a, cc, yy, zz, done = self.bufs
        arrived(self.near)

        def add(i, carry):
            at = (i, self.n.y)
            a[at] = (as_f32(a, at) + as_f32(yy, i)).astype(BF)
            return carry

        lax.fori_loop(0, 4, add, 0)
        self.copies.go(*self.far)

    def three(self):
        a, cc, yy, zz, done = self.bufs
        arrived(*self.far)
        total = as_f32(a, (self.n.z, self.n.y))
        for r in range(3):
            total = total + as_f32(zz, r)
        done[...] = total
        self.copies.keep(done, self.out)

    @staticmethod
    def shapes(rows, cols):
        return [pltpu.VMEM((4, 2, rows, cols), BF)] * 2 + [
            pltpu.VMEM((4, rows, cols), BF), pltpu.VMEM((3, rows, cols), BF),
            pltpu.VMEM((rows, cols), F32),
        ]


def prepare_pair(pair, grad, out, rden):
    rows = grad.shape[0]
    lanes = pair_lanes(pair)
    g = grad[:, lanes].astype(F32)
    r = rden[:, lanes]
    prod = g * out[:, lanes].astype(F32) * r
    low = half_mask(rows, 0)
    first = jnp.sum(jnp.where(low, prod, 0.0), axis=1, keepdims=True)
    second = jnp.sum(jnp.where(low, 0.0, prod), axis=1, keepdims=True)
    grad[:, lanes] = (g * r).astype(BF)
    rden[:, lanes] = jnp.where(low, first, second)


def delta_of(pair, part, deltas, where=slice(None)):
    return deltas[where, pair_lanes(pair)][:, part * VD : part * VD + 1]


def grad_state_pair(pair, table, qkv, first, dnum_ref, delta_ref, wide_ref, thin_ref):
    rows = qkv.shape[0]
    query = qkv[:, tile_lanes(pair)]
    dnum = dnum_ref[:, pair_lanes(pair)]
    total = None
    for part in range(2):
        sel = selectors(table, head_tile(pair, part)[1], LANES)
        one, two = factors(query, table, sel)
        phi = one * two * (table[4:5, :] * first)
        new = mm(phi.astype(BF), keep(half_mask(rows, part), dnum), TN)
        total = new if total is None else total + new
        delta = delta_of(pair, part, delta_ref)
        thin_ref[pair, part : part + 1, :] = -jnp.sum(phi * delta, axis=0, keepdims=True)
    thin_ref[pair, 2:, :] = jnp.zeros((6, FEATS), F32)
    wide_ref[pair] = total.astype(BF)


def local_grad_pair(
    pair, table, qkv, first, dnum_ref, delta_ref, wide_ref, thin_ref, dq_acc, dk_acc, dv_ref,
    mask_ref,
):
    qk = HEADS * QD
    at_tile = tile_lanes(pair)
    query, keys = qkv[:, at_tile], qkv[:, tile_lanes(pair, qk)]
    rows = query.shape[0]
    tiles = rows // TILE
    scale = QD**-0.5
    lanes = pair_lanes(pair)
    values = qkv[:, pair_lanes(pair, 2 * qk)]
    dnum = dnum_ref[:, lanes]
    dv = [jnp.zeros((TILE, WIDE), F32) for _ in range(tiles)]
    for part in range(2):
        head = head_tile(pair, part)[1]
        at_head = head_mask(rows, head, LANES)
        q_head = keep(at_head, query * scale)
        k_head = keep(at_head, keys * scale)
        d_head = keep(half_mask(rows, part), dnum)
        delta = delta_of(pair, part, delta_ref)
        for i in range(tiles):
            here = slice(i * TILE, (i + 1) * TILE)
            dq = dq_acc[here, at_tile]
            for j in range(i + 1):
                there = slice(j * TILE, (j + 1) * TILE)
                s = mm(q_head[here], keys[there], NT)
                mask = mask_ref[here, there]
                t = (1.0 + s) * mask
                w = (t * t + mask).astype(BF)
                dp = mm(d_head[here], values[there], NT)
                ds = ((dp - delta[here]) * t).astype(BF)
                dq = dq + mm(ds, k_head[there], NN)
                dk_acc[there, at_tile] += mm(ds, q_head[here], TN)
                dv[j] = dv[j] + mm(w, d_head[here], TN)
            dq_acc[here, at_tile] = dq
        sel = selectors(table, head, LANES)
        one, two = factors(query, table, sel)
        dphi = mm(d_head, wide_ref[pair], NT) - delta * thin_ref[pair, part : part + 1, :]
        dphi = dphi * (table[4:5, :] * first)
        dq_acc[:, at_tile] += mm((dphi * two).astype(BF), sel[0], NT) + mm(
            (dphi * one).astype(BF), sel[1], NT
        )
    for j in range(tiles):
        dv_ref[j * TILE : (j + 1) * TILE, lanes] = 0.5 * dv[j]


def finish_grad_pair(pair, table, qkv, last, wide_ref, thin_ref, dk_acc, dv_ref, grads):
    qk = HEADS * QD
    at_tile = tile_lanes(pair)
    keys = qkv[:, tile_lanes(pair, qk)]
    rows = keys.shape[0]
    lanes = pair_lanes(pair)
    values = qkv[:, pair_lanes(pair, 2 * qk)]
    dv = dv_ref[:, lanes]
    for part in range(2):
        sel = selectors(table, head_tile(pair, part)[1], LANES)
        one, two = factors(keys, table, sel)
        mask = half_mask(rows, part)
        phi = one * two * last
        dv = dv + jnp.where(mask, mm(phi.astype(BF), wide_ref[pair], NN), 0.0)
        dphi = mm(keep(mask, values), wide_ref[pair], NT) + thin_ref[pair, part : part + 1, :]
        dphi = dphi * last
        dk_acc[:, at_tile] += mm((dphi * two).astype(BF), sel[0], NT) + mm(
            (dphi * one).astype(BF), sel[1], NT
        )
    grads[:, pair_lanes(pair, 2 * qk)] = dv.astype(BF)


def half_columns(ff):
    middle = -(-ff // 256) * 128
    return ((0, middle), (middle, ff))


def projection_chunks(qk, hv, full):
    middle = (3 * qk + hv // 2) // 2
    return (
        (0, qk), (2 * qk + hv // 2, 2 * qk + hv), (qk, middle), (middle, 2 * qk + hv // 2),
        (2 * qk + hv, full),
    )


BWD_COPIES = 6 * WideScatter.REMOTE + 6 * PlaneScatter.REMOTE + EXCHANGE_COPIES + 4
BWD_LOCALS = 12 * 3 + 16


def backward_kernel(
    gg_own, gu_own, gd_own, go_ref, grad_in, att_in, rden_in, qkv_in,
    wide_in, thin_in, wq_in, x_in, middle_in, y_in, y_other_in, gain_ref, dgain_ref, ids_ref,
    table_ref, ends_ref,
    dg_out, du_out, dd_out, do_out, dq_out, dk_out, dv_out, dgains_out, din_out, outcome_out,
    *rest,
):
    rest = list(rest)

    def take(count):
        got = rest[:count]
        del rest[:count]
        return got

    f_bufs = [take(5) for _ in range(6)]
    o_bufs = take(8)
    q_bufs = [take(8) for _ in range(5)]
    bufs = take(16)
    states = [(bufs[2 * i], bufs[2 * i + 1]) for i in range(8)]
    (
        y_got, outcome, wq, first_ref, last_ref, grad, out, rden, mask, dq_acc, dk_acc, dv, before_wide, before_thin, wqg, qkv, grads,
        wide, thin, dgain, turned, send, recv, local,
    ) = rest
    n = Links()
    copies = Copies(send, recv, local)
    rows, width = out.shape
    qk, hv = HEADS * QD, HEADS * VD
    table = table_ref[...]
    full = wqg.shape[-1]

    ffn = []
    for grad_ref, result in ((gg_own, dg_out), (gu_own, du_out), (gd_own, dd_out)):
        for lo, hi in half_columns(result.shape[-1]):
            cols = pl.ds(lo, hi - lo)
            part = grad_ref.at[:, :, :, :, cols]
            ffn.append(PlaneScatter(copies, n, part, f_bufs[len(ffn)], result.at[:, cols]))

    def pass_on(i):
        ffn[i].two()
        if i + 2 < len(ffn):
            ffn[i + 2].one()
        if i >= 2:
            ffn[i - 2].three()

    outs = WideScatter(copies, n, go_ref.at[n.head], go_ref.at[1 - n.head], o_bufs, do_out)
    qs = []
    for bufs_of, (lo, hi) in zip(q_bufs, projection_chunks(qk, hv, full)):
        cols = pl.ds(lo, hi - lo)
        own = wqg.at[n.head, :, :, :, :, cols]
        oth = wqg.at[1 - n.head, :, :, :, :, cols]
        qs.append(WideScatter(copies, n, own, oth, bufs_of, None))
    q_grad, v_late, kv_low, kv_high, gain_grad = qs
    middle_at = projection_chunks(qk, hv, full)[2][1]
    swap = Exchange(copies, n, exchange_gates(ends_ref, n, False), 0, states, False)
    piece = rows // 4
    y_back = [
        copies.remote(y_other_in.at[pl.ds(i * piece, piece)], y_got.at[pl.ds(i * piece, piece)], n.x)
        for i in range(4)
    ]

    def fetch(*pairs):
        loads = [copies.keep(src, dst) for src, dst in pairs]

        def ready():
            for load in loads:
                copies.finish(load)

        return ready

    n.greet()

    ready = fetch(
        (grad_in, grad), (att_in, out), (rden_in, rden), (qkv_in, qkv),
        (wide_in, before_wide), (thin_in, before_thin),
    )
    for part in ffn:
        part.begin()
    outs.begin()
    documents(ids_ref, ends_ref, n, mask, first_ref, last_ref)
    dq_acc[...] = jnp.zeros_like(dq_acc)
    dk_acc[...] = jnp.zeros_like(dk_acc)
    ready()
    each_pair(0, PAIRS, lambda pair: prepare_pair(pair, grad, out, rden))
    ready_x = fetch((x_in, out), (wq_in, wq))
    ffn[0].one()
    ffn[1].one()

    def do_state(pair):
        grad_state_pair(
            pair, table, qkv, first_ref[...], grad, rden, states[0][0], states[0][1]
        )

    def do_local(pair):
        local_grad_pair(
            pair, table, qkv, first_ref[...], grad, rden, before_wide, before_thin, dq_acc,
            dk_acc, dv, mask,
        )

    def do_finish(pair):
        finish_grad_pair(pair, table, qkv, last_ref[...], wide, thin, dk_acc, dv, grads)

    each_pair(0, PAIRS, do_state)
    swap.begin()
    each_pair(0, 2, do_local)
    swap.one()
    pass_on(0)
    each_pair(2, 3, do_local)
    swap.two()
    copies.go(*y_back[0:1])
    outs.one()
    pass_on(1)
    each_pair(3, 5, do_local)
    swap.three()
    pass_on(2)
    copies.go(*y_back[1:2])
    each_pair(5, 6, do_local)
    outs.two()
    pass_on(3)
    copies.go(*y_back[2:3])
    each_pair(6, PAIRS, do_local)
    ready_middle = fetch((middle_in, rden))
    swap.four((wide, thin))
    outs.three()
    copies.go(*y_back[3:4])

    ready_x()
    x_buf, middle = out, rden
    x = x_buf[...].astype(F32)
    scale = lax.rsqrt(jnp.mean(x * x, axis=-1, keepdims=True) + EPSILON)
    normed = (x * scale * gain_ref[0:1, :]).astype(BF)
    turned[...] = jnp.transpose(normed)
    grads[:, :qk] = dq_acc[...].astype(BF)

    def project(lo, hi):
        def rows_step(half):
            left = turned[pl.ds(pl.multiple_of(half * 512, 512), 512), :]
            part = mm(left, grads[:, lo:hi], NN).astype(BF)
            wqg[half, :, :, :, :, lo:hi] = part.reshape(wqg.shape[1:-1] + (hi - lo,))

        each_pair(0, 2, rows_step)

    project(0, qk)
    q_grad.begin()
    each_pair(PAIRS // 2, PAIRS, do_finish)
    q_grad.one()
    project(2 * qk + hv // 2, 2 * qk + hv)
    v_late.begin()
    pass_on(4)
    each_pair(0, PAIRS // 2, do_finish)
    v_late.one()
    grads[:, qk : 2 * qk] = dk_acc[...].astype(BF)
    project(qk, middle_at)
    kv_low.begin()
    q_grad.two()
    project(middle_at, 2 * qk + hv // 2)
    kv_high.begin()
    kv_low.one()
    pass_on(5)
    kv_high.one()

    ready_middle()
    dv[...] = jnp.zeros_like(dv)

    def back_step(i):
        at = pl.ds(pl.multiple_of(i * 512, 512), 512)
        weight = wq[:, :, :, :, :, at].reshape(width, 512)
        dv[...] += mm(grads[:, at], weight, NT)

    each_pair(0, (2 * qk + hv) // 512, back_step)
    v_late.two()
    q_grad.three()
    dh = dv[...]
    hat = x_buf[...].astype(F32) * scale
    dgain[...] = jnp.zeros_like(dgain)
    dgain[0:1, :] = jnp.sum(dh * hat, axis=0, keepdims=True)
    dgain[1:2, :] = dgain_ref[...]
    spread = (
        lax.broadcasted_iota(jnp.int32, (8, GAIN_COLS), 0)
        == lax.broadcasted_iota(jnp.int32, (8, GAIN_COLS), 1)
    ).astype(F32).astype(BF)
    gain_part = mm(dgain[...].astype(BF), spread, TN).astype(BF)
    wqg[:, :, :, :, :, full - GAIN_COLS :] = gain_part.reshape(wqg.shape[:-1] + (GAIN_COLS,))
    gain_grad.begin()
    dhat = dh * gain_ref[0:1, :]
    inner = jnp.mean(dhat * hat, axis=-1, keepdims=True)
    middle[...] = middle[...] + (dhat - hat * inner) * scale
    copies.keep(middle, din_out)
    ready_y = fetch((y_in, dv))
    gain_grad.one()
    kv_low.two()
    v_late.three()
    kv_high.two()
    outs.four()
    ready_y()
    arrived(*y_back)
    outcome[...] = (dv[...] + y_got[...].astype(F32)).astype(BF)
    copies.keep(outcome, outcome_out)
    ffn[4].three()
    ffn[5].three()
    q_grad.four()
    copies.keep(q_bufs[0][7], dq_out)
    gain_grad.two()
    kv_low.three()
    kv_high.three()
    gain_grad.three()
    v_late.four()
    copies.keep(q_bufs[1][7], dv_out.at[:, pl.ds(hv // 2, hv // 2)])
    kv_low.four()
    low, high = q_bufs[2][7], q_bufs[3][7]
    early = middle_at - 2 * qk
    copies.keep(low.at[:, pl.ds(0, qk)], dk_out)
    copies.keep(low.at[:, pl.ds(qk, early)], dv_out.at[:, pl.ds(0, early)])
    kv_high.four()
    copies.keep(high, dv_out.at[:, pl.ds(early, hv // 2 - early)])
    gain_grad.four()
    copies.keep(q_bufs[4][7], dgains_out)
    copies.drain()


def swish_grads(gate, up, grad_hidden):
    sig = 1.0 / (1.0 + jnp.exp(-gate))
    silu = gate * sig
    grad_up = grad_hidden * silu
    grad_gate = grad_hidden * up * (sig * (1.0 + gate * (1.0 - sig)))
    return (silu * up).astype(BF), grad_gate.astype(BF), grad_up.astype(BF)


FFN_COPIES, FFN_LOCALS = 4, 32


def ffn_kernel(
    n2_in, dy_in, dy_other_in, res_in, g_in, u_in, d_in, att_in, wo_in, gain_ref,
    dwg_out, dwu_out, dwd_out, dwo_out, do_out, middle_out, y_out, y_other_out, dgain_out,
    weights, n2, dy, flipped, inner_grads, y_acc, h_acc, h_sent,
    h_got, res, att, wo, dwo, low, dgain, send, recv, local,
):
    n = Links()
    copies = Copies(send, recv, local)
    rows, width = res.shape
    ff = weights.shape[-1]
    wg, wu, wd = weights.at[0], weights.at[1], weights.at[2]
    grad_gates, grad_ups, acts = inner_grads.at[0], inner_grads.at[1], inner_grads.at[2]

    def cols(ref, lo, hi):
        return ref[..., lo:hi].reshape(width, hi - lo)

    def fetch(*pairs):
        loads = [copies.keep(src, dst) for src, dst in pairs]

        def ready():
            for load in loads:
                copies.finish(load)

        return ready

    barrier = pltpu.get_barrier_semaphore()
    pl.semaphore_signal(barrier, inc=1, device_id=n.x, device_id_type=MESH)
    pl.semaphore_wait(barrier, 1)
    part = rows // 2
    halves = [pl.ds(0, part), pl.ds(part, part)]
    tokens = [copies.remote(n2_in.at[half], n2.at[1, half], n.x) for half in halves]
    back = [copies.remote(h_sent.at[half], h_got.at[half], n.x) for half in halves]
    tokens[0].start()
    steps = [(lo, min(lo + 512, ff)) for lo in range(0, ff, 512)]
    first = fetch((n2_in, n2.at[0]), (dy_in, dy.at[0]))
    weight_loads = []
    for lo, hi in steps:
        at = pl.ds(lo, hi - lo)
        loads = []
        for src, dst in ((g_in, wg), (u_in, wu), (d_in, wd)):
            i = copies.used_local
            copies.used_local += 1
            loads.append(
                pltpu.make_async_copy(
                    src.at[:, :, :, :, at], dst.at[:, :, :, :, at], local.at[i]
                )
            )
            loads[-1].start()
        weight_loads.append(loads)
    later_loads = []
    for src, dst in ((dy_other_in, dy.at[1]), (res_in, res), (att_in, att), (wo_in, wo)):
        i = copies.used_local
        copies.used_local += 1
        later_loads.append(pltpu.make_async_copy(src, dst, local.at[i]))
        later_loads[-1].start()
    first()

    def tokens_step(unit, carry):
        side, row = unit // 2, unit - 2 * (unit // 2)
        here = pl.ds(pl.multiple_of(row * part, part), part)
        there = pl.ds(pl.multiple_of(unit * part, part), part)

        @pl.when(unit == 2)
        def _():
            tokens[0].wait_recv()
            for load in later_loads:
                load.wait()

        @pl.when(unit == 3)
        def _():
            tokens[1].wait()

        n2_here, dy_here = n2[side, here, :], dy[side, here, :]
        for step, (lo, hi) in enumerate(steps):
            @pl.when(unit == 0)
            def _(step=step):
                for load in weight_loads[step]:
                    load.wait()

            w_g, w_u, w_d = cols(wg, lo, hi), cols(wu, lo, hi), cols(wd, lo, hi)
            gate = mm(n2_here, w_g, NN)
            up = mm(n2_here, w_u, NN)
            a, dg, du = swish_grads(gate, up, mm(dy_here, w_d, NN))
            acts[there, lo:hi] = a
            grad_gates[there, lo:hi] = dg
            grad_ups[there, lo:hi] = du
            more_h = mm(dg, w_g, NT) + mm(du, w_u, NT)
            more_y = mm(a, w_d, NT)
            if lo == 0:
                h_acc[side, here, :] = more_h
                y_acc[side, here, :] = more_y

                @pl.when(unit == 1)
                def _():
                    tokens[0].wait_send()
                    tokens[1].start()
            else:
                h_acc[side, here, :] += more_h
                y_acc[side, here, :] += more_y

        @pl.when(unit == 2)
        def _():
            h_sent[halves[0], :] = h_acc[1, halves[0], :].astype(BF)
            back[0].start()

        @pl.when(unit == 3)
        def _():
            h_sent[halves[1], :] = h_acc[1, halves[1], :].astype(BF)
            back[1].start()

        return carry

    lax.fori_loop(0, 4, tokens_step, 0)
    low[...] = y_acc[1].astype(BF)
    y_kept = copies.keep(low, y_other_out)
    y_acc[0] += res[...]
    copies.keep(y_acc.at[0], y_out)

    for side, source in enumerate((n2, dy)):
        for t in range(2):
            def flip(i, side=side, source=source, t=t):
                at = pl.ds(pl.multiple_of(i * 256, 256), 256)
                flipped[side, at, t * rows : (t + 1) * rows] = jnp.transpose(source[t, :, at])

            each_pair(0, width // 256, flip)

    def weight_grad(m):
        def rows_step(z):
            left = flipped[m // 2, pl.ds(pl.multiple_of(z * 256, 256), 256), :]
            for lo, hi in steps:
                total = mm(left, inner_grads[m, :, lo:hi], NN).astype(BF)
                weights[m, z, :, :, :, lo:hi] = total.reshape(weights.shape[2:-1] + (hi - lo,))

        each_pair(0, 4, rows_step)

    each_pair(0, 3, weight_grad)
    for m, out in enumerate((dwg_out, dwu_out, dwd_out)):
        copies.keep(weights.at[m], out)

    copies.finish(y_kept)
    for copy in back:
        copy.wait()
    gain = gain_ref[1:2, :]
    y1 = res[...]
    scale = lax.rsqrt(jnp.mean(y1 * y1, axis=-1, keepdims=True) + EPSILON)
    hat = y1 * scale
    dh = h_acc[0] + h_got[...].astype(F32)
    dgain[...] = jnp.sum(dh * hat, axis=0, keepdims=True)
    dhat = dh * gain
    inner = jnp.mean(dhat * hat, axis=-1, keepdims=True)
    middle = dy[0].astype(F32) + (dhat - hat * inner) * scale
    h_acc[0] = middle
    low[...] = middle.astype(BF)
    copies.keep(h_acc.at[0], middle_out)
    copies.keep(dgain, dgain_out)
    weight = wo[...].reshape(-1, width)

    def out_step(i):
        at = pl.ds(pl.multiple_of(i * 256, 256), 256)
        total = mm(att[...], low[:, at], TN).astype(BF)
        dwo[:, :, :, :, :, at] = total.reshape(dwo.shape[:-1] + (256,))

    each_pair(0, width // 256, out_step)
    copies.keep(dwo, dwo_out)
    n2[0] = mm(low[...], weight, NT).astype(BF)
    copies.keep(n2.at[0], do_out)
    copies.drain()


def feed_forward(n2, dy, dy_other, res, weights, att, wo, gain):
    rows, width = n2.shape
    full, ff = weights[0].shape, weights[0].shape[-1]

    def like(shape, dtype):
        return jax.ShapeDtypeStruct(shape, dtype)

    def scratch(shape, dtype):
        return pltpu.VMEM(shape, dtype)

    out_shape = [like(full, BF)] * 3 + [
        like(wo.shape, BF), like((rows, width), BF), like((rows, width), F32),
        like((rows, width), F32), like((rows, width), BF), like((1, width), F32),
    ]
    token = (rows, width)
    anywhere = pl.BlockSpec(memory_space=pl.ANY)
    return pl.pallas_call(
        ffn_kernel,
        out_shape=out_shape,
        in_specs=[anywhere] * 9 + [pl.BlockSpec(memory_space=pltpu.VMEM)],
        out_specs=[anywhere] * len(out_shape),
        scratch_shapes=[scratch((3,) + full, BF)]
        + [scratch((2,) + token, BF)] * 2
        + [scratch((2, width, 2 * rows), BF)]
        + [scratch((3, 2 * rows, ff), BF)]
        + [scratch((2,) + token, F32)] * 2
        + [scratch(token, BF)] * 2
        + [scratch(token, F32), scratch(token, BF), scratch(wo.shape, BF), scratch(wo.shape, BF)]
        + [scratch(token, BF), scratch((1, width), F32)]
        + [
            pltpu.SemaphoreType.DMA((FFN_COPIES,)), pltpu.SemaphoreType.DMA((FFN_COPIES,)),
            pltpu.SemaphoreType.DMA((FFN_LOCALS,)),
        ],
        compiler_params=pltpu.CompilerParams(
            collective_id=3, has_side_effects=True, vmem_limit_bytes=62 << 20
        ),
        cost_estimate=pl.CostEstimate(flops=26 << 30, bytes_accessed=64 << 20, transcendentals=0),
        name="feed_forward",
    )(n2, dy, dy_other, res, *weights, att, wo, gain)


def backward(
    ffn_grads, out_grad, grad, att, rden, qkv, before, wq, x, middle, y, y_other, gain, dgain, ids,
    table, ends,
):
    rows, width = x.shape
    qk, hv = HEADS * QD, HEADS * VD
    fine, ff = ffn_grads[0].shape[-2:]
    small, full = wq.shape[-2:]

    def like(shape, dtype):
        return jax.ShapeDtypeStruct(shape, dtype)

    out_shape = [like((fine, ff), F32)] * 3 + [
        like((small, width), F32), like((small, qk), F32), like((small, qk), F32),
        like((small, hv), F32), like((small, GAIN_COLS), F32), like((rows, width), F32),
        like((rows, width), BF),
    ]
    scratch = []
    for _ in range(3):
        for lo, hi in half_columns(ff):
            scratch += PlaneScatter.shapes(fine, hi - lo)
    scratch += WideScatter.shapes(small, width)
    for lo, hi in projection_chunks(qk, hv, full):
        scratch += WideScatter.shapes(small, hi - lo)
    scratch += exchange_shapes()
    scratch += [
        pltpu.VMEM((rows, width), BF), pltpu.VMEM((rows, width), BF),
        pltpu.VMEM((2, 4, 2, 2, small, full), BF), pltpu.VMEM((rows, 1), F32),
        pltpu.VMEM((rows, 1), F32),
        pltpu.VMEM((rows, hv), BF), pltpu.VMEM((rows, width), BF), pltpu.VMEM((rows, hv), F32),
        pltpu.VMEM((rows, rows), F32), pltpu.VMEM((rows, qk), F32), pltpu.VMEM((rows, qk), F32),
        pltpu.VMEM((rows, hv), F32), pltpu.VMEM((PAIRS, FEATS, WIDE), BF),
        pltpu.VMEM((PAIRS, 8, FEATS), F32),
        pltpu.VMEM((2, 4, 2, 2, small, full), BF), pltpu.VMEM((rows, 2 * qk + hv), BF),
        pltpu.VMEM((rows, 2 * qk + hv), BF),
        pltpu.VMEM((PAIRS, FEATS, WIDE), BF), pltpu.VMEM((PAIRS, 8, FEATS), F32),
        pltpu.VMEM((8, width), F32), pltpu.VMEM((width, rows), BF),
        pltpu.SemaphoreType.DMA((BWD_COPIES,)), pltpu.SemaphoreType.DMA((BWD_COPIES,)),
        pltpu.SemaphoreType.DMA((BWD_LOCALS,)),
    ]
    vmem = pl.BlockSpec(memory_space=pltpu.VMEM)
    anywhere = pl.BlockSpec(memory_space=pl.ANY)
    return pl.pallas_call(
        backward_kernel,
        out_shape=out_shape,
        in_specs=[anywhere] * 15 + [vmem] * 4 + [pl.BlockSpec(memory_space=pltpu.SMEM)],
        out_specs=[anywhere] * len(out_shape),
        scratch_shapes=scratch,
        compiler_params=pltpu.CompilerParams(
            collective_id=2, has_side_effects=True, vmem_limit_bytes=62 << 20
        ),
        cost_estimate=pl.CostEstimate(flops=16 << 30, bytes_accessed=64 << 20, transcendentals=0),
        name="backward",
    )(
        *ffn_grads, out_grad, grad, att, rden, qkv, *before, wq, x, middle, y, y_other, gain,
        dgain, ids, table, ends,
    )


def result_pieces(shape):
    parts = 4 if shape[0] % 64 == 0 and shape[0] >= 512 else 1
    size = shape[0] // parts
    return [pl.ds(i * size, size) for i in range(parts)]


def deliver_kernel(count, *refs):
    ins, gains_in, rest = refs[:count], refs[count], refs[count + 1 :]
    outs, one_out, two_out, rest = rest[:count], rest[count], rest[count + 1], rest[count + 2 :]
    bufs, (sem_in, sem_out) = rest[:count], rest[count:]
    loads, stores = [], []
    for i in range(count):
        pieces = result_pieces(ins[i].shape)
        for at in pieces:
            k = len(loads)
            loads.append(pltpu.make_async_copy(ins[i].at[at], bufs[i].at[at], sem_in.at[k]))
            stores.append(pltpu.make_async_copy(bufs[i].at[at], outs[i].at[at], sem_out.at[k]))
            loads[-1].start()
    turned = jnp.transpose(gains_in[...])
    one_out[...] = turned[0:1, :]
    two_out[...] = turned[1:2, :]
    for load, store in zip(loads, stores):
        load.wait()
        store.start()
    for store in stores:
        store.wait()


def deliver(plain, gains):
    count = len(plain)
    far, vmem = pl.BlockSpec(memory_space=pltpu.HBM), pl.BlockSpec(memory_space=pltpu.VMEM)
    small = gains.shape[0]
    return pl.pallas_call(
        functools.partial(deliver_kernel, count),
        out_shape=[jax.ShapeDtypeStruct(a.shape, a.dtype) for a in plain]
        + [jax.ShapeDtypeStruct((1, small), F32)] * 2,
        in_specs=[far] * count + [vmem],
        out_specs=[far] * count + [vmem] * 2,
        scratch_shapes=[pltpu.VMEM(a.shape, a.dtype) for a in plain]
        + [pltpu.SemaphoreType.DMA((sum(len(result_pieces(a.shape)) for a in plain),))] * 2,
        compiler_params=pltpu.CompilerParams(vmem_limit_bytes=62 << 20),
        name="deliver",
    )(*plain, gains)


def rms_scale(values, gain):
    return values * lax.rsqrt(jnp.mean(values * values, axis=-1, keepdims=True) + EPSILON) * gain


def swish_mix(gate, up_proj):
    return jax.nn.silu(gate) * up_proj


def dot_nn(a, b):
    return jnp.dot(a, b, preferred_element_type=F32)


def dot_nt(a, b):
    return lax.dot_general(a, b, (((1,), (1,)), ((), ())), preferred_element_type=F32)


def dot_tn(a, b):
    return lax.dot_general(a, b, (((0,), (0,)), ((), ())), preferred_element_type=F32)


def row_grads(left, right, by_head):
    head, core = lax.axis_index("head"), lax.axis_index("seq") % 2
    tokens = left.shape[0]
    chips = lax.axis_size("seq") // 2
    heads = 2 if by_head else 1
    rows = left.shape[1] // (heads * chips * 2)
    split = left.reshape(tokens, heads, chips, 2, rows)
    out = []
    for rel in range(heads):
        plane = pick(split, head ^ rel, 1) if by_head else split[:, 0]
        out.append([pick(plane, core ^ r, 2).reshape(tokens, chips * rows) for r in range(2)])
    if by_head:
        return [[dot_tn(part, right).astype(BF) for part in parts] for parts in out]
    return [[dot_tn(part, r).astype(BF) for part in out[0]] for r in right]


def plain_forward(
    inputs, segment_ids, norm1_gain, w_query, w_key, w_value, w_out, norm2_gain, w_gate, w_up,
    w_down, row_ids, col_ids, first, last, table,
):
    head, seq = lax.axis_index("head"), lax.axis_index("seq")
    n_seq = lax.axis_size("seq")
    rows, width = inputs.shape
    qk = HEADS * QD
    slot = head * n_seq + seq
    small = norm1_gain.shape[0]
    gains = jnp.zeros((2, width // small, small), F32)
    gains = lax.dynamic_update_slice(
        gains, jnp.stack([norm1_gain, norm2_gain]).astype(F32)[:, None, :], (0, slot, 0)
    ).reshape(2, width)
    gains = sum_everywhere(gains)
    gain_first, gain_second = gains[0], gains[1]

    qkv_full = gather_rows(jnp.concatenate([w_query, w_key, w_value], axis=1))
    out_full = gather_rows(w_out)
    gate_w = gather_halves(w_gate, False)
    up_w = gather_halves(w_up, False)
    down_w = gather_halves(w_down.T, True)

    normed_one = rms_scale(inputs, gain_first).astype(BF)
    qkv = dot_nn(normed_one, qkv_full).astype(BF)
    query, keys, values = qkv[:, :qk], qkv[:, qk : 2 * qk], qkv[:, 2 * qk :]
    vcols = HEADS * VD
    t_spec, q_spec = full_spec((8, FEATS)), full_spec((rows, qk))
    one_spec, row_spec = full_spec((rows, 1)), full_spec((1, rows))
    p_spec = pair_spec(rows)
    f32_like = jax.ShapeDtypeStruct((rows, vcols), F32)
    bf_like = jax.ShapeDtypeStruct((rows, vcols), BF)
    state = run(
        state_kernel,
        [t_spec, q_spec, p_spec, one_spec],
        state_specs(),
        STATE_SHAPES,
        (table, keys, values, last),
        flops=8 * rows * qk * FEATS * HEADS,
    )
    num, den = run(
        local_kernel,
        [q_spec, q_spec, p_spec, one_spec, row_spec],
        [p_spec, p_spec],
        [f32_like, f32_like],
        (query, keys, values, row_ids, col_ids),
        [pltpu.VMEM((rows, rows), F32)],
        flops=8 * rows * rows * qk * HEADS,
    )
    before = exchange(*state, segment_ids, rows, True)
    attended, rden = run(
        finish_kernel,
        [t_spec, q_spec, p_spec, p_spec, one_spec] + state_specs(),
        [p_spec, p_spec],
        [bf_like, f32_like],
        (table, query, num, den, first, *before),
        flops=8 * rows * qk * FEATS * HEADS,
    )
    residual = inputs + dot_nn(attended, out_full)
    normed_two = rms_scale(residual, gain_second).astype(BF)

    return (
        gate_w, up_w, down_w, qkv_full, out_full, gain_first, gain_second, normed_one,
        query, keys, values, attended, rden, residual, normed_two, before,
    )


def body(
    layer_input,
    segment_ids,
    norm1_gain,
    w_query,
    w_key,
    w_value,
    w_out,
    norm2_gain,
    w_gate,
    w_up,
    w_down,
    output_grad,
):
    rows = layer_input.shape[1]
    head, seq = lax.axis_index("head"), lax.axis_index("seq")
    n_seq = lax.axis_size("seq")
    qk = HEADS * QD
    inputs = layer_input[0].astype(F32)
    width = inputs.shape[1]

    table = jnp.asarray(feature_table())
    vcols = HEADS * VD
    t_spec, q_spec = full_spec((8, FEATS)), full_spec((rows, qk))
    one_spec, row_spec = full_spec((rows, 1)), full_spec((1, rows))
    p_spec = pair_spec(rows)
    f32_like = jax.ShapeDtypeStruct((rows, vcols), F32)
    bf_like = jax.ShapeDtypeStruct((rows, vcols), BF)
    slot = head * n_seq + seq
    small = norm1_gain.shape[0]

    if n_seq == 16:
        gain_cols = jnp.stack([norm1_gain, norm2_gain], axis=1)
        gain_cols = jnp.pad(gain_cols, ((0, 0), (0, GAIN_COLS - 2)))
        ids = segment_ids.reshape(2 * n_seq, rows)
        ends = jnp.concatenate([ids[:, 0], ids[:, rows - 1]])
        (
            g_own, u_own, d_own, dy_other, wq, wo, qkv, attended, rden, residual,
            normed_two, wide, thin, gains,
        ) = forward(
            layer_input[0],
            [w_query, w_key, w_value, gain_cols],
            w_out,
            [w_gate, w_up, w_down.T],
            output_grad[0],
            ids, table, ends,
        )
        d_gate, d_up, d_down, d_out, grad_attended, grad_middle, y, y_other, grad_gain = (
            feed_forward(
                normed_two, output_grad[0], dy_other, residual, [g_own, u_own, d_own],
                attended, wo, gains,
            )
        )
        d_gate, d_up, d_down, d_out, d_q, d_k, d_v, d_gains, grad_layer, outcome = backward(
            [d_gate, d_up, d_down], d_out, grad_attended, attended, rden, qkv, (wide, thin), wq,
            layer_input[0], grad_middle, y, y_other, gains, grad_gain, ids, table, ends,
        )
        (
            d_gate, d_up, d_down, d_q, d_out, outcome, grad_layer, d_v, d_k, gain_one, gain_two,
        ) = deliver(
            [d_gate, d_up, d_down, d_q, d_out, outcome, grad_layer, d_v, d_k], d_gains
        )
        return (
            outcome[None], grad_layer[None], gain_one[0], d_q, d_k, d_v, d_out, gain_two[0],
            d_gate, d_up, d_down.T,
        )

    segment = 2 * seq + head
    ids = lax.dynamic_slice_in_dim(segment_ids, segment * rows, rows)
    row_ids, col_ids = ids[:, None], ids[None, :]
    first = (row_ids == ids[0]).astype(F32)
    last = (row_ids == ids[rows - 1]).astype(F32)
    (
        gate_w, up_w, down_w, qkv_full, out_full, gain_first, gain_second, normed_one,
        query, keys, values, attended, rden, residual, normed_two, before,
    ) = plain_forward(
        inputs, segment_ids, norm1_gain, w_query, w_key, w_value, w_out, norm2_gain, w_gate,
        w_up, w_down, row_ids, col_ids, first, last, table,
    )

    grad_output = output_grad[0]
    outcome = residual
    grad_normed_two = None
    hiddens, grad_gates, grad_ups = [], [], []
    for w_g, w_u, w_d in zip(gate_w, up_w, down_w):
        gate = dot_nn(normed_two, w_g)
        up_proj = dot_nn(normed_two, w_u)
        grad_hidden = dot_nn(grad_output, w_d)
        hidden, mix_pull = jax.vjp(swish_mix, gate, up_proj)
        grad_gate, grad_up = mix_pull(grad_hidden)
        hiddens.append(hidden.astype(BF))
        grad_gates.append(grad_gate.astype(BF))
        grad_ups.append(grad_up.astype(BF))
        outcome = outcome + dot_nt(hiddens[-1], w_d)
        more = dot_nt(grad_gates[-1], w_g) + dot_nt(grad_ups[-1], w_u)
        grad_normed_two = more if grad_normed_two is None else grad_normed_two + more
    outcome = outcome.astype(BF)
    _, norm_pull = jax.vjp(rms_scale, residual, gain_second)
    grad_resid_two, grad_gain_two = norm_pull(grad_normed_two)
    grad_middle = grad_output.astype(F32) + grad_resid_two
    grad_middle_low = grad_middle.astype(BF)
    grad_attended = dot_nt(grad_middle_low, out_full).astype(BF)

    d_gate = scatter(row_grads(normed_two, grad_gates, False), True)
    d_up = scatter(row_grads(normed_two, grad_ups, False), True)
    d_down = scatter(row_grads(grad_output, hiddens, False), False).T

    d_out = scatter(row_grads(attended, grad_middle_low, True), True)

    grad_state = run(
        grad_state_kernel,
        [t_spec, q_spec, p_spec, p_spec, p_spec, one_spec],
        state_specs(),
        STATE_SHAPES,
        (table, query, grad_attended, attended, rden, first),
        flops=8 * rows * qk * FEATS * HEADS,
    )
    qk_f32 = jax.ShapeDtypeStruct((rows, qk), F32)
    qk_bf = jax.ShapeDtypeStruct((rows, qk), BF)
    grad_query, grad_key, grad_value = run(
        local_grad_kernel,
        [t_spec, q_spec, q_spec, p_spec, p_spec, p_spec, p_spec, one_spec, row_spec, one_spec]
        + state_specs(),
        [q_spec, q_spec, p_spec],
        [qk_bf, qk_f32, f32_like],
        (table, query, keys, values, grad_attended, attended, rden, row_ids, col_ids, first)
        + tuple(before),
        [pltpu.VMEM((rows, rows), F32), pltpu.VMEM((rows, qk), F32), pltpu.VMEM((rows, qk), F32)],
        flops=20 * rows * rows * qk * HEADS,
    )
    after = exchange(*grad_state, segment_ids, rows, False)
    grad_key, grad_value = run(
        finish_grad_kernel,
        [t_spec, q_spec, p_spec, q_spec, p_spec, one_spec] + state_specs(),
        [q_spec, p_spec],
        [qk_bf, bf_like],
        (table, keys, values, grad_key, grad_value, last, *after),
        [pltpu.VMEM((rows, qk), F32)],
        flops=16 * rows * qk * FEATS * HEADS,
    )
    grad_qkv = jnp.concatenate([grad_query, grad_key, grad_value], axis=1)
    d_qkv = scatter(row_grads(normed_one, grad_qkv, True), True)
    grad_normed_one = dot_nt(grad_qkv, qkv_full)
    _, first_pull = jax.vjp(rms_scale, inputs, gain_first)
    grad_inputs, grad_gain_one = first_pull(grad_normed_one)
    grad_layer = grad_middle + grad_inputs
    grad_gains = sum_everywhere(jnp.stack([grad_gain_one, grad_gain_two]))
    grad_gains = lax.dynamic_slice_in_dim(
        grad_gains.reshape(2, width // small, small), slot, 1, 1
    )[:, 0]
    return (
        outcome[None],
        grad_layer[None],
        grad_gains[0],
        d_qkv[:, :qk],
        d_qkv[:, qk : 2 * qk],
        d_qkv[:, 2 * qk :],
        d_out,
        grad_gains[1],
        d_gate,
        d_up,
        d_down,
    )


def solution(mesh):
    split = P(("head", "seq"))
    rows = P(("head", "seq"), None)
    block = P("seq", "head", None)
    wide, tall = P("seq", "head"), P("head", "seq")
    in_specs = (block, P(), split, rows, rows, rows, rows, split, wide, wide, tall, block)
    out_specs = (block, block, split, rows, rows, rows, rows, split, wide, wide, tall)
    return jax.shard_map(body, mesh=mesh, in_specs=in_specs, out_specs=out_specs, check_vma=False)
```

```python
import functools

import jax
import jax.numpy as jnp
import numpy as np
from jax import lax
from jax.experimental import pallas as pl
from jax.experimental.pallas import tpu as pltpu
from jax.sharding import PartitionSpec as P

HEADS = 16
QD = 16
VD = 64
DOC_MAX = 4096
EPSILON = 1e-05
PAIRS = HEADS // 2
WIDE = 2 * VD
FEATS = 160
TILE = 256
LANES = 128

BF = jnp.bfloat16
F32 = jnp.float32


def flip_seq(value, code):
    n = lax.axis_size("seq")
    return lax.ppermute(value, "seq", [(i, i ^ code) for i in range(n)])


def flip_head(value):
    n = lax.axis_size("head")
    return lax.ppermute(value, "head", [(i, i ^ 1) for i in range(n)])


def shift_seq(value, distance):
    n = lax.axis_size("seq")
    return lax.ppermute(
        value, "seq", [(i, i + distance) for i in range(n) if 0 <= i + distance < n]
    )


def layout():
    chips = lax.axis_size("seq") // 2
    near = 2 if chips <= 8 else 8
    far = chips // near
    return far, near


def place_kernel(groups, count, *refs):
    pieces, out, sem = refs[:count], refs[count], refs[count + 1]
    me = lax.axis_index("seq")
    head = lax.axis_index("head")
    n = lax.axis_size("seq")
    copies = []
    for piece, blocks in zip(pieces, groups):
        for index, (rel_head, rel_seq) in blocks:
            place = me ^ rel_seq
            if rel_head is not None:
                place = place + (head ^ rel_head) * n
            copies.append(
                pltpu.make_async_copy(piece.at[index], out.at[place], sem.at[len(copies)])
            )
    for copy in copies:
        copy.start()
    for copy in copies:
        copy.wait()


def place(pieces, groups, blocks):
    rows, cols = pieces[0].shape[-2:]
    total = sum(len(g) for g in groups)
    out = pl.pallas_call(
        functools.partial(place_kernel, groups, len(pieces)),
        out_shape=jax.ShapeDtypeStruct((blocks, rows, cols), pieces[0].dtype),
        in_specs=[pl.BlockSpec(memory_space=pl.ANY)] * len(pieces),
        out_specs=pl.BlockSpec(memory_space=pltpu.VMEM),
        scratch_shapes=[pltpu.SemaphoreType.DMA((total,))],
        compiler_params=pltpu.CompilerParams(vmem_limit_bytes=16 << 20),
        cost_estimate=pl.CostEstimate(
            flops=0, bytes_accessed=4 * blocks * rows * cols, transcendentals=0
        ),
        name="place",
    )(*pieces)
    return out.reshape(blocks * rows, cols)


def gather(shard, head_first):
    far, near = layout()
    far_codes = [2 * near * r for r in range(far)]
    near_codes = [2 * r for r in range(near)]
    if head_first:
        shard = jnp.stack([shard, flip_head(shard)])
    column = jnp.stack([shard] + [flip_seq(shard, code) for code in far_codes[1:]])
    held = [(column, 0, 0)]
    held += [(flip_seq(column, code), 0, code) for code in near_codes[1:]]
    if not head_first:
        held += [(flip_head(buf), 1, code) for buf, _, code in held]
    held += [(flip_seq(buf, 1), rel, code + 1) for buf, rel, code in held]
    result = []
    for buf, rel, code in held:
        if head_first:
            blocks = [((r, g), (g, code + far_codes[r])) for r in range(far) for g in range(2)]
        else:
            blocks = [((r,), (rel, code + far_codes[r])) for r in range(far)]
        result.append((buf, blocks))
    return result


def gather_rows(shard):
    got = gather(shard, False)
    return place([b for b, _ in got], [g for _, g in got], 2 * lax.axis_size("seq"))


def gather_halves(shard, head_first):
    got = gather(shard, head_first)
    halves = []
    for rel in range(2):
        pieces, groups = [], []
        for buf, blocks in got:
            mine = [(i, (None, code)) for i, (r, code) in blocks if r == rel]
            if mine:
                pieces.append(buf)
                groups.append(mine)
        halves.append(place(pieces, groups, lax.axis_size("seq")))
    return halves


def add_low(*terms):
    total = terms[0].astype(F32)
    for term in terms[1:]:
        total = total + term.astype(F32)
    return total.astype(BF)


def pick(value, index, axis):
    return lax.dynamic_index_in_dim(value, index, axis, keepdims=False)


def scatter(grads, head_first):
    far, near = layout()
    seq = lax.axis_index("seq")
    far_at, near_at = seq // (2 * near), (seq // 2) % near
    both = [
        add_low(grads[rel][0], flip_seq(grads[rel][1], 1)) for rel in range(2)
    ]
    rows = both[0].shape[0] // (far * near)
    cols = both[0].shape[1]
    if head_first:
        whole = add_low(both[0], flip_head(both[1])).reshape(far, near, rows, cols)
    else:
        whole = jnp.stack(both).reshape(2, far, near, rows, cols).transpose(1, 2, 0, 3, 4)
    parts = [pick(whole, near_at, 1)]
    parts += [flip_seq(pick(whole, near_at ^ r, 1), 2 * r) for r in range(1, near)]
    column = add_low(*parts)
    parts = [pick(column, far_at, 0)]
    parts += [flip_seq(pick(column, far_at ^ r, 0), 2 * near * r) for r in range(1, far)]
    if head_first:
        return sum(part.astype(F32) for part in parts)
    both = add_low(*parts)
    return both[0].astype(F32) + flip_head(both[1]).astype(F32)


def sum_everywhere(value):
    value = value + flip_head(value)
    code = 1
    while code < lax.axis_size("seq"):
        value = value + flip_seq(value, code)
        code *= 2
    return value


def feature_table():
    first, second, one, two, scale = [], [], [], [], []
    for a in range(QD):
        for b in range(a, QD):
            first.append(a)
            second.append(b)
            one.append(0.0)
            two.append(0.0)
            scale.append((1.0 if a == b else 2.0) / (2.0 * QD))
    for a in range(QD):
        first.append(a)
        second.append(-1000)
        one.append(0.0)
        two.append(1.0)
        scale.append(QD**-0.5)
    first.append(-1000)
    second.append(-1000)
    one.append(1.0)
    two.append(1.0)
    scale.append(1.0)
    pad = FEATS - len(first)
    table = np.zeros((8, FEATS), np.float32)
    table[0] = np.array(first + [-1000] * pad)
    table[1] = np.array(second + [-1000] * pad)
    table[2] = np.array(one + [0.0] * pad)
    table[3] = np.array(two + [0.0] * pad)
    table[4] = np.array(scale + [0.0] * pad)
    return table


def mm(a, b, dims):
    return lax.dot_general(a, b, ((dims[0], dims[1]), ((), ())), preferred_element_type=F32)


NN = ((1,), (0,))
NT = ((1,), (1,))
TN = ((0,), (0,))


def selectors(table, head, lanes=HEADS * QD):
    row = (lax.broadcasted_iota(jnp.int32, (lanes, FEATS), 0) - head * QD).astype(F32)
    one = (row == table[0:1, :]).astype(F32).astype(BF)
    two = (row == table[1:2, :]).astype(F32).astype(BF)
    return one, two


def factors(values, table, sel):
    return (
        mm(values, sel[0], NN) + table[2:3, :],
        mm(values, sel[1], NN) + table[3:4, :],
    )


def half_mask(rows, part):
    lane = lax.broadcasted_iota(jnp.int32, (rows, WIDE), 1)
    return (lane >= VD) if part else (lane < VD)


def head_mask(rows, head, lanes=HEADS * QD):
    lane = lax.broadcasted_iota(jnp.int32, (rows, lanes), 1)
    return (lane >= head * QD) & (lane < (head + 1) * QD)


def keep(mask, value):
    return jnp.where(mask, value.astype(F32), 0.0).astype(BF)


def state_kernel(table_ref, keys_ref, values_ref, last_ref, wide_ref, thin_ref):
    pair = pl.program_id(0)
    table = table_ref[...]
    keys = keys_ref[...]
    rows = keys.shape[0]
    last = last_ref[...]
    total = None
    for part in range(2):
        sel = selectors(table, 2 * pair + part)
        one, two = factors(keys, table, sel)
        phi = one * two * last
        value = keep(half_mask(rows, part), values_ref[...])
        new = mm(phi.astype(BF), value, TN)
        total = new if total is None else total + new
        thin_ref[0, part : part + 1, :] = jnp.sum(phi, axis=0, keepdims=True)
    thin_ref[0, 2:, :] = jnp.zeros((6, FEATS), F32)
    wide_ref[0] = total.astype(BF)


def visible_tile(mask_ref, row_ids_ref, col_ids_ref, rows):
    for i in range(rows // TILE):
        for j in range(i + 1):
            same = (
                row_ids_ref[i * TILE : (i + 1) * TILE, :]
                == col_ids_ref[:, j * TILE : (j + 1) * TILE]
            )
            if i == j:
                same = same & (
                    lax.broadcasted_iota(jnp.int32, (TILE, TILE), 1)
                    <= lax.broadcasted_iota(jnp.int32, (TILE, TILE), 0)
                )
            mask_ref[i * TILE : (i + 1) * TILE, j * TILE : (j + 1) * TILE] = same.astype(F32)


def local_kernel(
    query_ref, keys_ref, values_ref, row_ids_ref, col_ids_ref, num_ref, den_ref, mask_ref
):
    pair = pl.program_id(0)
    rows = query_ref.shape[0]

    @pl.when(pair == 0)
    def _():
        visible_tile(mask_ref, row_ids_ref, col_ids_ref, rows)

    for i in range(rows // TILE):
        here = slice(i * TILE, (i + 1) * TILE)
        num = jnp.zeros((TILE, WIDE), F32)
        dens = []
        for part in range(2):
            head = 2 * pair + part
            query = keep(head_mask(TILE, head), query_ref[here, :] * (QD**-0.5))
            den = jnp.zeros((TILE, 1), F32)
            for j in range(i + 1):
                there = slice(j * TILE, (j + 1) * TILE)
                s = mm(query, keys_ref[there, :], NT)
                w = (1.0 + s + 0.5 * s * s) * mask_ref[here, there]
                den = den + jnp.sum(w, axis=1, keepdims=True)
                num = num + mm(
                    w.astype(BF), keep(half_mask(TILE, part), values_ref[there, :]), NN
                )
            dens.append(den)
        num_ref[here, :] = num
        den_ref[here, :] = jnp.where(half_mask(TILE, 0), dens[0], dens[1])


def finish_kernel(
    table_ref, query_ref, num_ref, den_ref, first_ref, wide_ref, thin_ref, out_ref, rden_ref
):
    pair = pl.program_id(0)
    table = table_ref[...]
    query = query_ref[...]
    rows = query.shape[0]
    first = first_ref[...]
    num, den = num_ref[...], den_ref[...]
    for part in range(2):
        sel = selectors(table, 2 * pair + part)
        one, two = factors(query, table, sel)
        phi = one * two * (table[4:5, :] * first)
        mask = half_mask(rows, part)
        extra = mm(phi.astype(BF), wide_ref[0], NN)
        num = num + jnp.where(mask, extra, 0.0)
        more = jnp.sum(phi * thin_ref[0, part : part + 1, :], axis=1, keepdims=True)
        den = den + jnp.where(mask, more, 0.0)
    rden = 1.0 / den
    rden_ref[...] = rden
    out_ref[...] = (num * rden).astype(BF)


def prepare(grad_ref, out_ref, rden_ref):
    rows = grad_ref.shape[0]
    grad = grad_ref[...].astype(F32)
    rden = rden_ref[...]
    dnum = (grad * rden).astype(BF)
    prod = grad * out_ref[...].astype(F32) * rden
    deltas = [
        jnp.sum(jnp.where(half_mask(rows, part), prod, 0.0), axis=1, keepdims=True)
        for part in range(2)
    ]
    return dnum, deltas


def grad_state_kernel(
    table_ref, query_ref, grad_ref, out_ref, rden_ref, first_ref, wide_ref, thin_ref
):
    pair = pl.program_id(0)
    table = table_ref[...]
    query = query_ref[...]
    rows = query.shape[0]
    dnum, deltas = prepare(grad_ref, out_ref, rden_ref)
    total = None
    for part in range(2):
        sel = selectors(table, 2 * pair + part)
        one, two = factors(query, table, sel)
        phi = one * two * (table[4:5, :] * first_ref[...])
        new = mm(phi.astype(BF), keep(half_mask(rows, part), dnum), TN)
        total = new if total is None else total + new
        thin_ref[0, part : part + 1, :] = -jnp.sum(phi * deltas[part], axis=0, keepdims=True)
    thin_ref[0, 2:, :] = jnp.zeros((6, FEATS), F32)
    wide_ref[0] = total.astype(BF)


def local_grad_kernel(
    table_ref,
    query_ref,
    keys_ref,
    values_ref,
    grad_ref,
    out_ref,
    rden_ref,
    row_ids_ref,
    col_ids_ref,
    first_ref,
    wide_ref,
    thin_ref,
    dq_ref,
    dk_ref,
    dv_ref,
    mask_ref,
    dq_acc,
    dk_acc,
):
    pair = pl.program_id(0)
    table = table_ref[...]
    query = query_ref[...]
    keys = keys_ref[...]
    rows = query.shape[0]
    tiles = rows // TILE
    scale = QD**-0.5

    @pl.when(pair == 0)
    def _():
        visible_tile(mask_ref, row_ids_ref, col_ids_ref, rows)
        dq_acc[...] = jnp.zeros_like(dq_acc)
        dk_acc[...] = jnp.zeros_like(dk_acc)

    dnum, deltas = prepare(grad_ref, out_ref, rden_ref)
    dv = [jnp.zeros((TILE, WIDE), F32) for _ in range(tiles)]
    for part in range(2):
        head = 2 * pair + part
        at_head = head_mask(rows, head)
        q_head = keep(at_head, query * scale)
        k_head = keep(at_head, keys * scale)
        d_head = keep(half_mask(rows, part), dnum)
        for i in range(tiles):
            here = slice(i * TILE, (i + 1) * TILE)
            dq = dq_acc[here, :]
            for j in range(i + 1):
                there = slice(j * TILE, (j + 1) * TILE)
                s = mm(q_head[here], keys[there], NT)
                mask = mask_ref[here, there]
                w = ((1.0 + s + 0.5 * s * s) * mask).astype(BF)
                dp = mm(d_head[here], values_ref[there, :], NT)
                ds = ((dp - deltas[part][here]) * ((1.0 + s) * mask)).astype(BF)
                dq = dq + mm(ds, k_head[there], NN)
                dk_acc[there, :] += mm(ds, q_head[here], TN)
                dv[j] = dv[j] + mm(w, d_head[here], TN)
            dq_acc[here, :] = dq
        sel = selectors(table, head)
        one, two = factors(query, table, sel)
        dphi = mm(d_head, wide_ref[0], NT) - deltas[part] * thin_ref[0, part : part + 1, :]
        dphi = dphi * (table[4:5, :] * first_ref[...])
        dq_acc[...] += mm((dphi * two).astype(BF), sel[0], NT) + mm(
            (dphi * one).astype(BF), sel[1], NT
        )
    for j in range(tiles):
        dv_ref[j * TILE : (j + 1) * TILE, :] = dv[j]

    @pl.when(pair == PAIRS - 1)
    def _():
        dq_ref[...] = dq_acc[...].astype(BF)
        dk_ref[...] = dk_acc[...]


def finish_grad_kernel(
    table_ref, keys_ref, values_ref, dk_in_ref, dv_in_ref, last_ref, wide_ref, thin_ref,
    dk_ref, dv_ref, dk_acc,
):
    pair = pl.program_id(0)
    table = table_ref[...]
    keys = keys_ref[...]
    rows = keys.shape[0]
    last = last_ref[...]

    @pl.when(pair == 0)
    def _():
        dk_acc[...] = dk_in_ref[...]

    dv = dv_in_ref[...]
    for part in range(2):
        sel = selectors(table, 2 * pair + part)
        one, two = factors(keys, table, sel)
        mask = half_mask(rows, part)
        phi = one * two * last
        dv = dv + jnp.where(mask, mm(phi.astype(BF), wide_ref[0], NN), 0.0)
        dphi = mm(keep(mask, values_ref[...]), wide_ref[0], NT) + thin_ref[0, part : part + 1, :]
        dphi = dphi * last
        dk_acc[...] += mm((dphi * two).astype(BF), sel[0], NT) + mm(
            (dphi * one).astype(BF), sel[1], NT
        )
    dv_ref[...] = dv.astype(BF)

    @pl.when(pair == PAIRS - 1)
    def _():
        dk_ref[...] = dk_acc[...].astype(BF)


def full_spec(shape):
    return pl.BlockSpec(shape, lambda p: (0,) * len(shape))


def pair_spec(rows):
    return pl.BlockSpec((rows, WIDE), lambda p: (0, p))


def state_specs():
    return [
        pl.BlockSpec((1, FEATS, WIDE), lambda p: (p, 0, 0)),
        pl.BlockSpec((1, 8, FEATS), lambda p: (p, 0, 0)),
    ]


STATE_SHAPES = (
    jax.ShapeDtypeStruct((PAIRS, FEATS, WIDE), BF),
    jax.ShapeDtypeStruct((PAIRS, 8, FEATS), F32),
)


def run(kernel, in_specs, out_specs, out_shape, args, scratch=(), flops=0):
    moved = sum(a.size * a.dtype.itemsize for a in args)
    return pl.pallas_call(
        kernel,
        grid=(PAIRS,),
        in_specs=in_specs,
        out_specs=out_specs,
        out_shape=out_shape,
        scratch_shapes=scratch,
        compiler_params=pltpu.CompilerParams(vmem_limit_bytes=48 << 20),
        cost_estimate=pl.CostEstimate(flops=flops, bytes_accessed=moved, transcendentals=0),
        name=kernel.__name__,
    )(*args)


def exchange(wide, thin, ids, rows, forward):
    head, seq = lax.axis_index("head"), lax.axis_index("seq")
    n = lax.axis_size("seq")
    segments = 2 * n
    firsts = ids.reshape(segments, rows)[:, 0]
    lasts = ids.reshape(segments, rows)[:, rows - 1]
    step = 1 if forward else -1
    near_end, far_end = (lasts, firsts) if forward else (firsts, lasts)

    def end_of(which, segment):
        return which[jnp.clip(segment, 0, segments - 1)]

    seg = 2 * seq + head
    takes = end_of(far_end, seg)
    core = seq % 2
    late_head = head if forward else 1 - head
    late_core = core if forward else 1 - core

    def gate(flag):
        return jnp.where(flag, 1.0, 0.0).astype(F32)

    def wider(state):
        return [part.astype(F32) for part in state]

    def narrow(state):
        return [state[0].astype(BF), state[1]]

    def merge(own, other, late, other_takes, joined):
        gained = [part * (gate(other_takes) * late) for part in other]
        own_factor = jnp.where(late == 1, 1.0, gate(joined))
        other_factor = jnp.where(late == 1, gate(joined), 1.0)
        joint = [a * own_factor + b * other_factor for a, b in zip(own, other)]
        return gained, joint

    own = [wide, thin]
    other = [flip_head(part) for part in own]
    first_of, second_of = 2 * seq, 2 * seq + 1
    if not forward:
        first_of, second_of = second_of, first_of
    total, joint = merge(
        wider(own),
        wider(other),
        late_head,
        end_of(near_end, seg - step) == takes,
        end_of(near_end, first_of) == end_of(near_end, second_of),
    )
    joint = narrow(joint)
    other = [flip_seq(part, 1) for part in joint]
    base = 4 * (seq // 2)
    early_end, late_end = (base + 1, base + 3) if forward else (base + 2, base)
    gained, joint = merge(
        wider(joint),
        wider(other),
        late_core,
        end_of(near_end, early_end) == takes,
        end_of(near_end, early_end) == end_of(near_end, late_end),
    )
    total = [a + b for a, b in zip(total, gained)]
    joint = narrow(joint)
    half = PAIRS // 2
    mine = [lax.dynamic_slice_in_dim(part, core * half, half, 0) for part in joint]
    hops = -(-DOC_MAX // (4 * rows))
    far = None
    for hop in range(1, hops + 1):
        got = wider([shift_seq(part, 2 * hop * step) for part in mine])
        nearer, farther = late_end - 4 * step, late_end - 4 * step * hop
        joined = gate(end_of(near_end, nearer) == end_of(near_end, farther))
        got = [part * joined for part in got]
        far = got if far is None else [a + b for a, b in zip(far, got)]
    far = narrow(far)
    other = [flip_seq(part, 1) for part in far]
    comes = (seq // 2 >= 1) if forward else (seq // 2 < n // 2 - 1)
    use = gate(comes & (end_of(near_end, late_end - 4 * step) == takes))
    result = []
    for a, b, so_far in zip(far, other, total):
        low = jnp.where(core == 0, a, b).astype(F32)
        high = jnp.where(core == 0, b, a).astype(F32)
        result.append(so_far + use * jnp.concatenate([low, high], axis=0))
    return narrow(result)


MESH = pl.DeviceIdType.MESH
GAIN_COLS = 128


class Links:
    def __init__(self):
        self.head, self.seq = lax.axis_index("head"), lax.axis_index("seq")
        self.n = lax.axis_size("seq")
        self.z, self.y, self.c = self.seq // 4, (self.seq // 2) % 2, self.seq % 2
        self.core = self.at(self.head, self.seq ^ 1)
        self.x = self.at(1 - self.head, self.seq)
        self.near = self.at(self.head, self.seq ^ 2)
        self.far = [self.at(self.head, self.seq ^ (4 * r)) for r in range(4)]

    def at(self, head, seq):
        return {"head": head, "seq": seq}

    def shifted(self, distance):
        return self.at(self.head, lax.rem(self.seq + distance + self.n, self.n))

    def greet(self):
        barrier = pltpu.get_barrier_semaphore()
        partners = [self.core, self.x, self.near] + self.far[1:]
        partners += [self.shifted(d) for d in (2, 4, -2, -4)]
        for partner in partners:
            pl.semaphore_signal(barrier, inc=1, device_id=partner, device_id_type=MESH)
        pl.semaphore_wait(barrier, len(partners))


class Copies:
    def __init__(self, send, recv, local):
        self.send, self.recv, self.local = send, recv, local
        self.used, self.used_local = 0, 0
        self.started, self.started_local = [], []

    def remote(self, src, dst, partner):
        i = self.used
        self.used += 1
        return pltpu.make_async_remote_copy(
            src_ref=src,
            dst_ref=dst,
            send_sem=self.send.at[i],
            recv_sem=self.recv.at[i],
            device_id=partner,
            device_id_type=MESH,
        )

    def go(self, *copies):
        for copy in copies:
            copy.start()
            self.started.append(copy)

    def keep(self, src, dst):
        copy = pltpu.make_async_copy(src, dst, self.local.at[self.used_local])
        self.used_local += 1
        copy.start()
        self.started_local.append(copy)
        return copy

    def finish(self, copy):
        copy.wait()
        self.started_local = [other for other in self.started_local if other is not copy]

    def drain(self):
        for copy in self.started:
            copy.wait_send()
        for copy in self.started_local:
            copy.wait()


def arrived(*copies):
    for copy in copies:
        copy.wait_recv()


class WideGather:
    def __init__(self, copies, links, shard, own, other, other_there, near_last=False):
        n, y, c = links, links.y, links.c
        self.copies, self.near_last = copies, near_last
        self.place = own.at[n.z, y, c]
        self.shard = shard
        self.far = [copies.remote(shard, self.place, n.far[r]) for r in range(1, 4)]
        mine, theirs = own.at[:, y, c], own.at[:, 1 - y, c]
        self.near = copies.remote(mine, mine, n.near)
        across = other.at[:, y, c]
        self.cross = copies.remote(mine, other_there.at[:, y, c], n.x)
        if near_last:
            self.last = copies.remote(across, across, n.near)
        else:
            self.last = copies.remote(theirs, other_there.at[:, 1 - y, c], n.x)
        self.core = [
            copies.remote(part, part, n.core)
            for part in (mine, theirs, other.at[:, y, c], other.at[:, 1 - y, c])
        ]

    def begin(self):
        self.copies.go(*self.far)
        self.own = self.copies.keep(self.shard, self.place)

    def far_here(self):
        arrived(*self.far)
        self.copies.finish(self.own)

    def one(self):
        self.copies.go(self.near, self.cross, self.core[0])

    def two(self):
        arrived(self.near)
        if not self.near_last:
            self.copies.go(self.last)
        self.copies.go(self.core[1])

    def three(self):
        arrived(self.cross)
        if self.near_last:
            self.copies.go(self.last)
        self.copies.go(self.core[2])

    def four(self):
        arrived(self.last)
        self.copies.go(self.core[3])

    def end(self):
        arrived(*self.core)


class PlaneGather:
    COPIES = 6

    def __init__(self, copies, links, shard, own):
        n, y, c = links, links.y, links.c
        self.copies, self.shard, self.place = copies, shard, own.at[n.z, y, c]
        self.far = [copies.remote(shard, self.place, n.far[r]) for r in range(1, 4)]
        mine, theirs = own.at[:, y, c], own.at[:, 1 - y, c]
        self.near = copies.remote(mine, mine, n.near)
        self.core = [copies.remote(part, part, n.core) for part in (mine, theirs)]

    def begin(self):
        self.copies.go(*self.far)
        self.own = self.copies.keep(self.shard, self.place)

    def far_here(self):
        arrived(*self.far)
        self.copies.finish(self.own)

    def one(self):
        self.copies.go(self.near, self.core[0])

    def two(self):
        arrived(self.near)
        self.copies.go(self.core[1])

    def end(self):
        arrived(*self.core)


class Exchange:
    def __init__(self, copies, links, gates, first, bufs, forward):
        n = links
        self.copies, self.gates, self.first, self.bufs = copies, gates, first, bufs
        half = PAIRS // 2
        step = 2 if forward else -2
        own, a, j, b, j2, r1, r2, far = bufs

        def both(src, dst, partner, groups=4):
            size = src[0].shape[0] // groups
            cuts = [pl.ds(i * size, size) for i in range(groups)]
            made = [copies.remote(src[0].at[cut], dst[0].at[cut], partner) for cut in cuts]
            return made + [copies.remote(src[1], dst[1], partner)]

        def halves(state):
            return [
                state[0].at[pl.ds(n.c * half, half)],
                state[1].at[pl.ds(n.c * half, half)],
            ]

        self.rounds = [
            both(own, a, n.x),
            both(j, b, n.core, 1),
            both(halves(j2), r1, n.shifted(step)) + both(halves(j2), r2, n.shifted(2 * step)),
            both(halves(far), halves(far), n.core, 1),
        ]
        self.halves = halves
        self.total = None

    def gate(self, i):
        return self.gates[self.first + i]

    def begin(self):
        self.copies.go(*self.rounds[0])

    def one(self):
        own, a, j, b, j2, r1, r2, far = self.bufs
        arrived(*self.rounds[0])
        for s, d, t in zip(own, a, j):
            t[...] = (
                s[...].astype(F32) * self.gate(1) + d[...].astype(F32) * self.gate(2)
            ).astype(t.dtype)
        self.copies.go(*self.rounds[1])

    def two(self):
        own, a, j, b, j2, r1, r2, far = self.bufs
        arrived(*self.rounds[1])
        for s, d, t in zip(j, b, j2):
            t[...] = (
                s[...].astype(F32) * self.gate(4) + d[...].astype(F32) * self.gate(5)
            ).astype(t.dtype)
        self.copies.go(*self.rounds[2])

    def three(self):
        own, a, j, b, j2, r1, r2, far = self.bufs
        arrived(*self.rounds[2])
        for s, d, t in zip(r1, r2, self.halves(far)):
            t[...] = (s[...].astype(F32) + d[...].astype(F32) * self.gate(6)).astype(t.dtype)
        self.copies.go(*self.rounds[3])

    def four(self, out):
        own, a, j, b, j2, r1, r2, far = self.bufs
        arrived(*self.rounds[3])
        for s, d, f, t in zip(a, b, far, out):
            t[...] = (
                s[...].astype(F32) * self.gate(0)
                + d[...].astype(F32) * self.gate(3)
                + f[...].astype(F32) * self.gate(7)
            ).astype(t.dtype)


def exchange_shapes():
    shapes = []
    for name in range(8):
        pairs = PAIRS // 2 if name in (5, 6) else PAIRS
        shapes += [pltpu.VMEM((pairs, FEATS, WIDE), BF), pltpu.VMEM((pairs, 8, FEATS), F32)]
    return shapes


def documents(ids_ref, ends_ref, links, mask, first, last):
    rows = ids_ref.shape[1]
    segment = 2 * links.seq + links.head
    row = ids_ref[pl.ds(segment, 1), :].astype(F32)
    column = jnp.transpose(jnp.broadcast_to(row, (128, rows)))[:, :1]
    visible_tile(mask, column, row, rows)
    first[...] = (column == ends_ref[segment].astype(F32)).astype(F32)
    last[...] = (column == ends_ref[2 * links.n + segment].astype(F32)).astype(F32)


def exchange_gates(ends_ref, links, forward):
    head, seq, core, n = links.head, links.seq, links.c, links.n
    segments = 2 * n
    step = 1 if forward else -1
    near_at, far_at = (segments, 0) if forward else (0, segments)
    seg = 2 * seq + head
    chip = seq // 2
    base = 4 * chip
    late_head = (head == 1) if forward else (head == 0)
    late_core = (core == 1) if forward else (core == 0)
    pair_early, pair_late = (2 * seq, 2 * seq + 1) if forward else (2 * seq + 1, 2 * seq)
    early_end, late_end = (base + 1, base + 3) if forward else (base + 2, base)
    near_ok = (chip >= 1) if forward else (chip < n // 2 - 1)
    far_ok = (chip >= 2) if forward else (chip < n // 2 - 2)

    def doc(segment):
        return ends_ref[near_at + jnp.minimum(jnp.maximum(segment, 0), segments - 1)]

    def factor(flag):
        return jnp.where(flag, 1.0, 0.0).astype(F32)

    takes = ends_ref[far_at + seg]
    joined = doc(pair_early) == doc(pair_late)
    joined2 = doc(early_end) == doc(late_end)
    nearer, farther = doc(late_end - 4 * step), doc(late_end - 8 * step)
    flags = [
        late_head & (doc(seg - step) == takes),
        late_head | joined,
        jnp.logical_not(late_head) | joined,
        late_core & (doc(early_end) == takes),
        late_core | joined2,
        jnp.logical_not(late_core) | joined2,
        far_ok & (nearer == farther),
        near_ok & (nearer == takes),
    ]
    return [factor(flag) for flag in flags]


def pair_lanes(pair, start=0):
    return pl.ds(pl.multiple_of(start + pair * WIDE, WIDE), WIDE)


def head_tile(pair, part):
    tile = pair // (LANES // (2 * QD))
    return tile, 2 * pair + part - tile * (LANES // QD)


def tile_lanes(pair, start=0):
    return pl.ds(pl.multiple_of(start + head_tile(pair, 0)[0] * LANES, LANES), LANES)


def state_pair(pair, table, qkv, last, wide_ref, thin_ref):
    rows = qkv.shape[0]
    qk = HEADS * QD
    keys, value = qkv[:, tile_lanes(pair, qk)], qkv[:, pair_lanes(pair, 2 * qk)]
    total = None
    for part in range(2):
        sel = selectors(table, head_tile(pair, part)[1], LANES)
        one, two = factors(keys, table, sel)
        phi = one * two * last
        new = mm(phi.astype(BF), keep(half_mask(rows, part), value), TN)
        total = new if total is None else total + new
        thin_ref[pair, part : part + 1, :] = jnp.sum(phi, axis=0, keepdims=True)
    thin_ref[pair, 2:, :] = jnp.zeros((6, FEATS), F32)
    wide_ref[pair] = total.astype(BF)


def local_pair(pair, qkv, num_ref, den_ref, mask_ref):
    rows = qkv.shape[0]
    qk = HEADS * QD
    for i in range(rows // TILE):
        here = slice(i * TILE, (i + 1) * TILE)
        num = jnp.zeros((TILE, WIDE), F32)
        dens = []
        for part in range(2):
            head = head_tile(pair, part)[1]
            query = keep(
                head_mask(TILE, head, LANES), qkv[here, tile_lanes(pair)] * (QD**-0.5)
            )
            den = jnp.zeros((TILE, 1), F32)
            for j in range(i + 1):
                there = slice(j * TILE, (j + 1) * TILE)
                s = mm(query, qkv[there, tile_lanes(pair, qk)], NT)
                mask = mask_ref[here, there]
                t = (1.0 + s) * mask
                w = t * t + mask
                den = den + jnp.sum(w, axis=1, keepdims=True)
                value = qkv[there, pair_lanes(pair, 2 * qk)]
                num = num + mm(w.astype(BF), keep(half_mask(TILE, part), value), NN)
            dens.append(den)
        num_ref[here, pair_lanes(pair)] = 0.5 * num
        den_ref[here, pair_lanes(pair)] = 0.5 * jnp.where(half_mask(TILE, 0), dens[0], dens[1])


def finish_pair(pair, table, qkv, first, num_ref, den_ref, wide_ref, thin_ref, out_ref):
    rows = qkv.shape[0]
    query = qkv[:, tile_lanes(pair)]
    lanes = pair_lanes(pair)
    num, den = num_ref[:, lanes], den_ref[:, lanes]
    for part in range(2):
        sel = selectors(table, head_tile(pair, part)[1], LANES)
        one, two = factors(query, table, sel)
        phi = one * two * (table[4:5, :] * first)
        mask = half_mask(rows, part)
        num = num + jnp.where(mask, mm(phi.astype(BF), wide_ref[pair], NN), 0.0)
        more = jnp.sum(phi * thin_ref[pair, part : part + 1, :], axis=1, keepdims=True)
        den = den + jnp.where(mask, more, 0.0)
    rden = 1.0 / den
    den_ref[:, lanes] = rden
    out_ref[:, lanes] = (num * rden).astype(BF)


def each_pair(low, high, step):
    def one(pair, carry):
        step(pair)
        return carry

    lax.fori_loop(low, high, one, 0)


WIDE_COPIES, EXCHANGE_COPIES = 10, 19
FWD_COPIES = 3 * WIDE_COPIES + 6 * PlaneGather.COPIES + EXCHANGE_COPIES + 1
FWD_LOCALS = 20


def forward_kernel(
    x_ref, wq_ref, wk_ref, wv_ref, gs_in, os_ref, gs_ref, us_ref, ds_ref, ids_ref, table_ref,
    dy_ref, ends_ref,
    g_own, u_own, d_own, dy_out, wq_out, wo_out, qkv_out, att_out, rden_out,
    res_out, n2_out, wide_out, thin_out, gain_out,
    wq, wo, normed, qkv, num, den, mask, first_ref, last_ref, att, res, n2, wide, thin, gain,
    qs_ref, *rest,
):
    bufs, (send, recv, local) = rest[:16], rest[16:]
    states = [(bufs[2 * i], bufs[2 * i + 1]) for i in range(8)]
    n = Links()
    copies = Copies(send, recv, local)
    rows, width = x_ref.shape
    qk, hv = HEADS * QD, HEADS * VD
    cut = 7 * 128
    full = wq.shape[-1]

    def side(ref, head, lo=None, hi=None):
        return ref.at[head] if lo is None else ref.at[head, :, :, :, :, pl.ds(lo, hi - lo)]

    q_parts = []
    for lo, hi in ((0, cut), (cut, full)):
        shard = qs_ref.at[:, pl.ds(lo, hi - lo)]
        own, other = side(wq, n.head, lo, hi), side(wq, 1 - n.head, lo, hi)
        q_parts.append(WideGather(copies, n, shard, own, other, own, near_last=lo > 0))
    own, other = side(wo, n.head), side(wo, 1 - n.head)
    outs = WideGather(copies, n, os_ref, own, other, own)
    ffn = []
    for shard, own in ((gs_ref, g_own), (us_ref, u_own), (ds_ref, d_own)):
        for lo, hi in half_columns(ds_ref.shape[-1]):
            part = own.at[:, :, :, :, pl.ds(lo, hi - lo)]
            ffn.append(PlaneGather(copies, n, shard.at[:, pl.ds(lo, hi - lo)], part))

    def pass_on(i):
        ffn[i].far_here()
        ffn[i].one()
        if i + 2 < len(ffn):
            ffn[i + 2].begin()
        if i >= 2:
            ffn[i - 2].two()

    other_dy = copies.remote(dy_ref, dy_out, n.x)
    swap = Exchange(copies, n, exchange_gates(ends_ref, n, True), 0, states, True)

    qs_ref[:, :qk] = wq_ref[...]
    qs_ref[:, qk : 2 * qk] = wk_ref[...]
    qs_ref[:, 2 * qk : 2 * qk + hv] = wv_ref[...]
    qs_ref[:, 2 * qk + hv :] = gs_in[...]
    n.greet()
    for part in q_parts:
        part.begin()

    table = table_ref[...]
    x = x_ref[...].astype(F32)
    scaled = x * lax.rsqrt(jnp.mean(x * x, axis=-1, keepdims=True) + EPSILON)
    documents(ids_ref, ends_ref, n, mask, first_ref, last_ref)
    for part in q_parts:
        part.far_here()
        part.one()
    outs.begin()
    ffn[0].begin()
    q_parts[0].two()
    q_parts[1].three()
    q_parts[1].two()
    q_parts[0].three()
    outs.far_here()
    ffn[1].begin()
    for part in q_parts:
        part.four()
    outs.one()
    for part in q_parts:
        part.end()
    pass_on(0)

    pick_gain = (
        lax.broadcasted_iota(jnp.int32, (8, GAIN_COLS), 0)
        == lax.broadcasted_iota(jnp.int32, (8, GAIN_COLS), 1)
    ).astype(F32).astype(BF)
    gain[...] = mm(pick_gain, wq[..., full - GAIN_COLS :].reshape(width, GAIN_COLS), NT)
    normed[...] = (scaled * gain[0:1, :]).astype(BF)

    def project(i):
        at = pl.ds(pl.multiple_of(i * 512, 512), 512)
        weight = wq[:, :, :, :, :, at].reshape(width, 512)
        qkv[:, at] = mm(normed[...], weight, NN).astype(BF)

    each_pair(0, (2 * qk + hv) // 512, project)
    copies.keep(qkv, qkv_out)
    copies.keep(wq, wq_out)
    copies.keep(gain, gain_out)

    def do_state(pair):
        state_pair(
            pair, table, qkv, last_ref[...], states[0][0], states[0][1]
        )

    def do_local(pair):
        local_pair(pair, qkv, num, den, mask)

    def do_finish(pair):
        finish_pair(
            pair, table, qkv, first_ref[...], num, den, wide, thin, att
        )

    each_pair(0, PAIRS // 2, do_state)
    pass_on(1)
    each_pair(PAIRS // 2, PAIRS, do_state)
    swap.begin()
    each_pair(0, 4, do_local)
    swap.one()
    outs.two()
    outs.three()
    pass_on(2)
    each_pair(4, 5, do_local)
    swap.two()
    outs.four()
    copies.go(other_dy)
    each_pair(5, PAIRS, do_local)
    pass_on(3)
    swap.three()
    swap.four((wide, thin))
    copies.keep(wide, wide_out)
    copies.keep(thin, thin_out)
    each_pair(0, 4, do_finish)
    pass_on(4)
    each_pair(4, PAIRS, do_finish)
    outs.end()
    copies.keep(wo, wo_out)
    copies.keep(att, att_out)
    copies.keep(den, rden_out)

    def leave(i):
        at = pl.ds(pl.multiple_of(i * 512, 512), 512)
        weight = wo[:, :, :, :, :, at].reshape(hv, 512)
        res[:, at] = x_ref[:, at].astype(F32) + mm(att[...], weight, NN)

    each_pair(0, width // 512, leave)
    copies.keep(res, res_out)
    y1 = res[...]
    n2[...] = (
        y1 * lax.rsqrt(jnp.mean(y1 * y1, axis=-1, keepdims=True) + EPSILON) * gain[1:2, :]
    ).astype(BF)
    copies.keep(n2, n2_out)
    pass_on(5)
    ffn[4].two()
    ffn[5].two()
    for part in ffn:
        part.end()
    arrived(other_dy)
    copies.drain()


def forward(x, projections, o_shard, ffn, dy, ids, table, ends):
    rows, width = x.shape
    qk, hv = HEADS * QD, HEADS * VD
    full = sum(part.shape[1] for part in projections)
    small, fine, ff = o_shard.shape[0], ffn[0].shape[0], ffn[0].shape[1]
    half = jax.ShapeDtypeStruct((4, 2, 2, fine, ff), BF)
    wq_shape, wo_shape = (2, 4, 2, 2, small, full), (2, 4, 2, 2, small, width)

    def like(shape, dtype):
        return jax.ShapeDtypeStruct(shape, dtype)

    out_shape = [half] * 3 + [
        like(dy.shape, BF), like(wq_shape, BF), like(wo_shape, BF), like((rows, 2 * qk + hv), BF),
        like((rows, hv), BF), like((rows, hv), F32), like((rows, width), F32),
        like((rows, width), BF), STATE_SHAPES[0], STATE_SHAPES[1], like((8, width), F32),
    ]
    scratch = [
        pltpu.VMEM(wq_shape, BF), pltpu.VMEM(wo_shape, BF), pltpu.VMEM((rows, width), BF),
        pltpu.VMEM((rows, 2 * qk + hv), BF), pltpu.VMEM((rows, hv), F32),
        pltpu.VMEM((rows, hv), F32), pltpu.VMEM((rows, rows), F32), pltpu.VMEM((rows, 1), F32),
        pltpu.VMEM((rows, 1), F32), pltpu.VMEM((rows, hv), BF),
        pltpu.VMEM((rows, width), F32), pltpu.VMEM((rows, width), BF),
        pltpu.VMEM((PAIRS, FEATS, WIDE), BF), pltpu.VMEM((PAIRS, 8, FEATS), F32),
        pltpu.VMEM((8, width), F32), pltpu.VMEM((small, full), BF),
    ] + exchange_shapes() + [
        pltpu.SemaphoreType.DMA((FWD_COPIES,)), pltpu.SemaphoreType.DMA((FWD_COPIES,)),
        pltpu.SemaphoreType.DMA((FWD_LOCALS,)),
    ]
    vmem = pl.BlockSpec(memory_space=pltpu.VMEM)
    return pl.pallas_call(
        forward_kernel,
        out_shape=out_shape,
        in_specs=[vmem] * 11
        + [pl.BlockSpec(memory_space=pl.ANY)]
        + [pl.BlockSpec(memory_space=pltpu.SMEM)],
        out_specs=[pl.BlockSpec(memory_space=pl.ANY)] * len(out_shape),
        scratch_shapes=scratch,
        compiler_params=pltpu.CompilerParams(
            collective_id=1, has_side_effects=True, vmem_limit_bytes=56 << 20
        ),
        cost_estimate=pl.CostEstimate(flops=8 << 30, bytes_accessed=64 << 20, transcendentals=0),
        name="forward",
    )(x, *projections, o_shard, *ffn, ids, table, dy, ends)


def as_f32(ref, index):
    return ref[index].astype(F32)


class WideScatter:
    REMOTE, LOCAL = 7, 3

    def __init__(self, copies, links, own, other, bufs, out):
        n, y, c = links, links.y, links.c
        self.n, self.copies, self.out = n, copies, out
        a_own, a_oth, c_own, c_oth, xx, yy, zz, done = bufs
        self.bufs = bufs
        self.own_part, self.oth_part = own.at[:, :, c], other.at[:, :, c]
        self.core = [
            copies.remote(other.at[:, :, 1 - c], c_oth, n.core),
            copies.remote(own.at[:, :, 1 - c], c_own, n.core),
        ]
        self.cross = copies.remote(a_oth, xx, n.x)
        self.near = copies.remote(a_own.at[:, 1 - y], yy, n.near)
        self.far = [
            copies.remote(a_own.at[n.z ^ r, y], zz.at[r - 1], n.far[r]) for r in range(1, 4)
        ]

    def begin(self):
        a_own, a_oth = self.bufs[:2]
        self.copies.go(*self.core)
        self.loads = [
            self.copies.keep(self.oth_part, a_oth), self.copies.keep(self.own_part, a_own)
        ]

    def loaded(self, i):
        self.copies.finish(self.loads[i])

    def one(self):
        a_own, a_oth, c_own, c_oth, xx, yy, zz, done = self.bufs
        self.loaded(0)
        arrived(self.core[0])

        def add(i, carry):
            for at in ((i, 0), (i, 1)):
                a_oth[at] = (as_f32(a_oth, at) + as_f32(c_oth, at)).astype(BF)
            return carry

        lax.fori_loop(0, 4, add, 0)
        self.copies.go(self.cross)

    def two(self):
        a_own, a_oth, c_own, c_oth, xx, yy, zz, done = self.bufs
        self.loaded(1)
        arrived(self.core[1], self.cross)

        def add(i, carry):
            for at in ((i, 0), (i, 1)):
                total = as_f32(a_own, at) + as_f32(c_own, at) + as_f32(xx, at)
                a_own[at] = total.astype(BF)
            return carry

        lax.fori_loop(0, 4, add, 0)
        self.copies.go(self.near)

    def three(self):
        a_own, a_oth, c_own, c_oth, xx, yy, zz, done = self.bufs
        arrived(self.near)

        def add(i, carry):
            at = (i, self.n.y)
            a_own[at] = (as_f32(a_own, at) + as_f32(yy, i)).astype(BF)
            return carry

        lax.fori_loop(0, 4, add, 0)
        self.copies.go(*self.far)

    def four(self):
        a_own, a_oth, c_own, c_oth, xx, yy, zz, done = self.bufs
        arrived(*self.far)
        total = as_f32(a_own, (self.n.z, self.n.y))
        for r in range(3):
            total = total + as_f32(zz, r)
        done[...] = total
        if self.out is not None:
            self.copies.keep(done, self.out)

    @staticmethod
    def shapes(rows, cols):
        part = [pltpu.VMEM((4, 2, rows, cols), BF)]
        return part * 5 + [
            pltpu.VMEM((4, rows, cols), BF), pltpu.VMEM((3, rows, cols), BF),
            pltpu.VMEM((rows, cols), F32),
        ]


class PlaneScatter:
    REMOTE = 5

    def __init__(self, copies, links, own, bufs, out):
        n, y, c = links, links.y, links.c
        self.n, self.copies, self.out, self.bufs = n, copies, out, bufs
        a, cc, yy, zz, done = bufs
        self.part = own.at[:, :, c]
        self.core = copies.remote(own.at[:, :, 1 - c], cc, n.core)
        self.near = copies.remote(a.at[:, 1 - y], yy, n.near)
        self.far = [copies.remote(a.at[n.z ^ r, y], zz.at[r - 1], n.far[r]) for r in range(1, 4)]

    def begin(self):
        self.copies.go(self.core)
        self.load = self.copies.keep(self.part, self.bufs[0])

    def one(self):
        a, cc, yy, zz, done = self.bufs
        self.copies.finish(self.load)
        arrived(self.core)

        def add(i, carry):
            for at in ((i, 0), (i, 1)):
                a[at] = (as_f32(a, at) + as_f32(cc, at)).astype(BF)
            return carry

        lax.fori_loop(0, 4, add, 0)
        self.copies.go(self.near)

    def two(self):
        a, cc, yy, zz, done = self.bufs
        arrived(self.near)

        def add(i, carry):
            at = (i, self.n.y)
            a[at] = (as_f32(a, at) + as_f32(yy, i)).astype(BF)
            return carry

        lax.fori_loop(0, 4, add, 0)
        self.copies.go(*self.far)

    def three(self):
        a, cc, yy, zz, done = self.bufs
        arrived(*self.far)
        total = as_f32(a, (self.n.z, self.n.y))
        for r in range(3):
            total = total + as_f32(zz, r)
        done[...] = total
        self.copies.keep(done, self.out)

    @staticmethod
    def shapes(rows, cols):
        return [pltpu.VMEM((4, 2, rows, cols), BF)] * 2 + [
            pltpu.VMEM((4, rows, cols), BF), pltpu.VMEM((3, rows, cols), BF),
            pltpu.VMEM((rows, cols), F32),
        ]


def prepare_pair(pair, grad, out, rden):
    rows = grad.shape[0]
    lanes = pair_lanes(pair)
    g = grad[:, lanes].astype(F32)
    r = rden[:, lanes]
    prod = g * out[:, lanes].astype(F32) * r
    low = half_mask(rows, 0)
    first = jnp.sum(jnp.where(low, prod, 0.0), axis=1, keepdims=True)
    second = jnp.sum(jnp.where(low, 0.0, prod), axis=1, keepdims=True)
    grad[:, lanes] = (g * r).astype(BF)
    rden[:, lanes] = jnp.where(low, first, second)


def delta_of(pair, part, deltas, where=slice(None)):
    return deltas[where, pair_lanes(pair)][:, part * VD : part * VD + 1]


def grad_state_pair(pair, table, qkv, first, dnum_ref, delta_ref, wide_ref, thin_ref):
    rows = qkv.shape[0]
    query = qkv[:, tile_lanes(pair)]
    dnum = dnum_ref[:, pair_lanes(pair)]
    total = None
    for part in range(2):
        sel = selectors(table, head_tile(pair, part)[1], LANES)
        one, two = factors(query, table, sel)
        phi = one * two * (table[4:5, :] * first)
        new = mm(phi.astype(BF), keep(half_mask(rows, part), dnum), TN)
        total = new if total is None else total + new
        delta = delta_of(pair, part, delta_ref)
        thin_ref[pair, part : part + 1, :] = -jnp.sum(phi * delta, axis=0, keepdims=True)
    thin_ref[pair, 2:, :] = jnp.zeros((6, FEATS), F32)
    wide_ref[pair] = total.astype(BF)


def local_grad_pair(
    pair, table, qkv, first, dnum_ref, delta_ref, wide_ref, thin_ref, dq_acc, dk_acc, dv_ref,
    mask_ref,
):
    qk = HEADS * QD
    at_tile = tile_lanes(pair)
    query, keys = qkv[:, at_tile], qkv[:, tile_lanes(pair, qk)]
    rows = query.shape[0]
    tiles = rows // TILE
    scale = QD**-0.5
    lanes = pair_lanes(pair)
    values = qkv[:, pair_lanes(pair, 2 * qk)]
    dnum = dnum_ref[:, lanes]
    dv = [jnp.zeros((TILE, WIDE), F32) for _ in range(tiles)]
    for part in range(2):
        head = head_tile(pair, part)[1]
        at_head = head_mask(rows, head, LANES)
        q_head = keep(at_head, query * scale)
        k_head = keep(at_head, keys * scale)
        d_head = keep(half_mask(rows, part), dnum)
        delta = delta_of(pair, part, delta_ref)
        for i in range(tiles):
            here = slice(i * TILE, (i + 1) * TILE)
            dq = dq_acc[here, at_tile]
            for j in range(i + 1):
                there = slice(j * TILE, (j + 1) * TILE)
                s = mm(q_head[here], keys[there], NT)
                mask = mask_ref[here, there]
                t = (1.0 + s) * mask
                w = (t * t + mask).astype(BF)
                dp = mm(d_head[here], values[there], NT)
                ds = ((dp - delta[here]) * t).astype(BF)
                dq = dq + mm(ds, k_head[there], NN)
                dk_acc[there, at_tile] += mm(ds, q_head[here], TN)
                dv[j] = dv[j] + mm(w, d_head[here], TN)
            dq_acc[here, at_tile] = dq
        sel = selectors(table, head, LANES)
        one, two = factors(query, table, sel)
        dphi = mm(d_head, wide_ref[pair], NT) - delta * thin_ref[pair, part : part + 1, :]
        dphi = dphi * (table[4:5, :] * first)
        dq_acc[:, at_tile] += mm((dphi * two).astype(BF), sel[0], NT) + mm(
            (dphi * one).astype(BF), sel[1], NT
        )
    for j in range(tiles):
        dv_ref[j * TILE : (j + 1) * TILE, lanes] = 0.5 * dv[j]


def finish_grad_pair(pair, table, qkv, last, wide_ref, thin_ref, dk_acc, dv_ref, grads):
    qk = HEADS * QD
    at_tile = tile_lanes(pair)
    keys = qkv[:, tile_lanes(pair, qk)]
    rows = keys.shape[0]
    lanes = pair_lanes(pair)
    values = qkv[:, pair_lanes(pair, 2 * qk)]
    dv = dv_ref[:, lanes]
    for part in range(2):
        sel = selectors(table, head_tile(pair, part)[1], LANES)
        one, two = factors(keys, table, sel)
        mask = half_mask(rows, part)
        phi = one * two * last
        dv = dv + jnp.where(mask, mm(phi.astype(BF), wide_ref[pair], NN), 0.0)
        dphi = mm(keep(mask, values), wide_ref[pair], NT) + thin_ref[pair, part : part + 1, :]
        dphi = dphi * last
        dk_acc[:, at_tile] += mm((dphi * two).astype(BF), sel[0], NT) + mm(
            (dphi * one).astype(BF), sel[1], NT
        )
    grads[:, pair_lanes(pair, 2 * qk)] = dv.astype(BF)


def half_columns(ff):
    middle = -(-ff // 256) * 128
    return ((0, middle), (middle, ff))


def projection_chunks(qk, hv, full):
    middle = (3 * qk + hv // 2) // 2
    return (
        (0, qk), (2 * qk + hv // 2, 2 * qk + hv), (qk, middle), (middle, 2 * qk + hv // 2),
        (2 * qk + hv, full),
    )


BWD_COPIES = 6 * WideScatter.REMOTE + 6 * PlaneScatter.REMOTE + EXCHANGE_COPIES + 4
BWD_LOCALS = 12 * 3 + 16


def backward_kernel(
    gg_own, gu_own, gd_own, go_ref, grad_in, att_in, rden_in, qkv_in,
    wide_in, thin_in, wq_in, x_in, middle_in, y_in, y_other_in, gain_ref, dgain_ref, ids_ref,
    table_ref, ends_ref,
    dg_out, du_out, dd_out, do_out, dq_out, dk_out, dv_out, dgains_out, din_out, outcome_out,
    *rest,
):
    rest = list(rest)

    def take(count):
        got = rest[:count]
        del rest[:count]
        return got

    f_bufs = [take(5) for _ in range(6)]
    o_bufs = take(8)
    q_bufs = [take(8) for _ in range(5)]
    bufs = take(16)
    states = [(bufs[2 * i], bufs[2 * i + 1]) for i in range(8)]
    (
        y_got, outcome, wq, first_ref, last_ref, grad, out, rden, mask, dq_acc, dk_acc, dv, before_wide, before_thin, wqg, qkv, grads,
        wide, thin, dgain, turned, send, recv, local,
    ) = rest
    n = Links()
    copies = Copies(send, recv, local)
    rows, width = out.shape
    qk, hv = HEADS * QD, HEADS * VD
    table = table_ref[...]
    full = wqg.shape[-1]

    ffn = []
    for grad_ref, result in ((gg_own, dg_out), (gu_own, du_out), (gd_own, dd_out)):
        for lo, hi in half_columns(result.shape[-1]):
            cols = pl.ds(lo, hi - lo)
            part = grad_ref.at[:, :, :, :, cols]
            ffn.append(PlaneScatter(copies, n, part, f_bufs[len(ffn)], result.at[:, cols]))

    def pass_on(i):
        ffn[i].two()
        if i + 2 < len(ffn):
            ffn[i + 2].one()
        if i >= 2:
            ffn[i - 2].three()

    outs = WideScatter(copies, n, go_ref.at[n.head], go_ref.at[1 - n.head], o_bufs, do_out)
    qs = []
    for bufs_of, (lo, hi) in zip(q_bufs, projection_chunks(qk, hv, full)):
        cols = pl.ds(lo, hi - lo)
        own = wqg.at[n.head, :, :, :, :, cols]
        oth = wqg.at[1 - n.head, :, :, :, :, cols]
        qs.append(WideScatter(copies, n, own, oth, bufs_of, None))
    q_grad, v_late, kv_low, kv_high, gain_grad = qs
    middle_at = projection_chunks(qk, hv, full)[2][1]
    swap = Exchange(copies, n, exchange_gates(ends_ref, n, False), 0, states, False)
    piece = rows // 4
    y_back = [
        copies.remote(y_other_in.at[pl.ds(i * piece, piece)], y_got.at[pl.ds(i * piece, piece)], n.x)
        for i in range(4)
    ]

    def fetch(*pairs):
        loads = [copies.keep(src, dst) for src, dst in pairs]

        def ready():
            for load in loads:
                copies.finish(load)

        return ready

    n.greet()

    ready = fetch(
        (grad_in, grad), (att_in, out), (rden_in, rden), (qkv_in, qkv),
        (wide_in, before_wide), (thin_in, before_thin),
    )
    for part in ffn:
        part.begin()
    outs.begin()
    documents(ids_ref, ends_ref, n, mask, first_ref, last_ref)
    dq_acc[...] = jnp.zeros_like(dq_acc)
    dk_acc[...] = jnp.zeros_like(dk_acc)
    ready()
    each_pair(0, PAIRS, lambda pair: prepare_pair(pair, grad, out, rden))
    ready_x = fetch((x_in, out), (wq_in, wq))
    ffn[0].one()
    ffn[1].one()

    def do_state(pair):
        grad_state_pair(
            pair, table, qkv, first_ref[...], grad, rden, states[0][0], states[0][1]
        )

    def do_local(pair):
        local_grad_pair(
            pair, table, qkv, first_ref[...], grad, rden, before_wide, before_thin, dq_acc,
            dk_acc, dv, mask,
        )

    def do_finish(pair):
        finish_grad_pair(pair, table, qkv, last_ref[...], wide, thin, dk_acc, dv, grads)

    each_pair(0, PAIRS, do_state)
    swap.begin()
    each_pair(0, 2, do_local)
    swap.one()
    pass_on(0)
    each_pair(2, 3, do_local)
    swap.two()
    copies.go(*y_back[0:1])
    outs.one()
    pass_on(1)
    each_pair(3, 5, do_local)
    swap.three()
    pass_on(2)
    copies.go(*y_back[1:2])
    each_pair(5, 6, do_local)
    outs.two()
    pass_on(3)
    copies.go(*y_back[2:3])
    each_pair(6, PAIRS, do_local)
    ready_middle = fetch((middle_in, rden))
    swap.four((wide, thin))
    outs.three()
    copies.go(*y_back[3:4])

    ready_x()
    x_buf, middle = out, rden
    x = x_buf[...].astype(F32)
    scale = lax.rsqrt(jnp.mean(x * x, axis=-1, keepdims=True) + EPSILON)
    normed = (x * scale * gain_ref[0:1, :]).astype(BF)
    turned[...] = jnp.transpose(normed)
    grads[:, :qk] = dq_acc[...].astype(BF)

    def project(lo, hi):
        def rows_step(half):
            left = turned[pl.ds(pl.multiple_of(half * 512, 512), 512), :]
            part = mm(left, grads[:, lo:hi], NN).astype(BF)
            wqg[half, :, :, :, :, lo:hi] = part.reshape(wqg.shape[1:-1] + (hi - lo,))

        each_pair(0, 2, rows_step)

    project(0, qk)
    q_grad.begin()
    each_pair(PAIRS // 2, PAIRS, do_finish)
    q_grad.one()
    project(2 * qk + hv // 2, 2 * qk + hv)
    v_late.begin()
    pass_on(4)
    each_pair(0, PAIRS // 2, do_finish)
    v_late.one()
    grads[:, qk : 2 * qk] = dk_acc[...].astype(BF)
    project(qk, middle_at)
    kv_low.begin()
    q_grad.two()
    project(middle_at, 2 * qk + hv // 2)
    kv_high.begin()
    kv_low.one()
    pass_on(5)
    kv_high.one()

    ready_middle()
    dv[...] = jnp.zeros_like(dv)

    def back_step(i):
        at = pl.ds(pl.multiple_of(i * 512, 512), 512)
        weight = wq[:, :, :, :, :, at].reshape(width, 512)
        dv[...] += mm(grads[:, at], weight, NT)

    each_pair(0, (2 * qk + hv) // 512, back_step)
    v_late.two()
    q_grad.three()
    dh = dv[...]
    hat = x_buf[...].astype(F32) * scale
    dgain[...] = jnp.zeros_like(dgain)
    dgain[0:1, :] = jnp.sum(dh * hat, axis=0, keepdims=True)
    dgain[1:2, :] = dgain_ref[...]
    spread = (
        lax.broadcasted_iota(jnp.int32, (8, GAIN_COLS), 0)
        == lax.broadcasted_iota(jnp.int32, (8, GAIN_COLS), 1)
    ).astype(F32).astype(BF)
    gain_part = mm(dgain[...].astype(BF), spread, TN).astype(BF)
    wqg[:, :, :, :, :, full - GAIN_COLS :] = gain_part.reshape(wqg.shape[:-1] + (GAIN_COLS,))
    gain_grad.begin()
    dhat = dh * gain_ref[0:1, :]
    inner = jnp.mean(dhat * hat, axis=-1, keepdims=True)
    middle[...] = middle[...] + (dhat - hat * inner) * scale
    copies.keep(middle, din_out)
    ready_y = fetch((y_in, dv))
    gain_grad.one()
    kv_low.two()
    v_late.three()
    kv_high.two()
    outs.four()
    ready_y()
    arrived(*y_back)
    outcome[...] = (dv[...] + y_got[...].astype(F32)).astype(BF)
    copies.keep(outcome, outcome_out)
    ffn[4].three()
    ffn[5].three()
    q_grad.four()
    copies.keep(q_bufs[0][7], dq_out)
    gain_grad.two()
    kv_low.three()
    kv_high.three()
    gain_grad.three()
    v_late.four()
    copies.keep(q_bufs[1][7], dv_out.at[:, pl.ds(hv // 2, hv // 2)])
    kv_low.four()
    low, high = q_bufs[2][7], q_bufs[3][7]
    early = middle_at - 2 * qk
    copies.keep(low.at[:, pl.ds(0, qk)], dk_out)
    copies.keep(low.at[:, pl.ds(qk, early)], dv_out.at[:, pl.ds(0, early)])
    kv_high.four()
    copies.keep(high, dv_out.at[:, pl.ds(early, hv // 2 - early)])
    gain_grad.four()
    copies.keep(q_bufs[4][7], dgains_out)
    copies.drain()


def swish_grads(gate, up, grad_hidden):
    sig = 1.0 / (1.0 + jnp.exp(-gate))
    silu = gate * sig
    grad_up = grad_hidden * silu
    grad_gate = grad_hidden * up * (sig * (1.0 + gate * (1.0 - sig)))
    return (silu * up).astype(BF), grad_gate.astype(BF), grad_up.astype(BF)


FFN_COPIES, FFN_LOCALS = 4, 32


def ffn_kernel(
    n2_in, dy_in, dy_other_in, res_in, g_in, u_in, d_in, att_in, wo_in, gain_ref,
    dwg_out, dwu_out, dwd_out, dwo_out, do_out, middle_out, y_out, y_other_out, dgain_out,
    weights, n2, dy, flipped, inner_grads, y_acc, h_acc, h_sent,
    h_got, res, att, wo, dwo, low, dgain, send, recv, local,
):
    n = Links()
    copies = Copies(send, recv, local)
    rows, width = res.shape
    ff = weights.shape[-1]
    wg, wu, wd = weights.at[0], weights.at[1], weights.at[2]
    grad_gates, grad_ups, acts = inner_grads.at[0], inner_grads.at[1], inner_grads.at[2]

    def cols(ref, lo, hi):
        return ref[..., lo:hi].reshape(width, hi - lo)

    def fetch(*pairs):
        loads = [copies.keep(src, dst) for src, dst in pairs]

        def ready():
            for load in loads:
                copies.finish(load)

        return ready

    barrier = pltpu.get_barrier_semaphore()
    pl.semaphore_signal(barrier, inc=1, device_id=n.x, device_id_type=MESH)
    pl.semaphore_wait(barrier, 1)
    part = rows // 2
    halves = [pl.ds(0, part), pl.ds(part, part)]
    tokens = [copies.remote(n2_in.at[half], n2.at[1, half], n.x) for half in halves]
    back = [copies.remote(h_sent.at[half], h_got.at[half], n.x) for half in halves]
    tokens[0].start()
    steps = [(lo, min(lo + 512, ff)) for lo in range(0, ff, 512)]
    first = fetch((n2_in, n2.at[0]), (dy_in, dy.at[0]))
    weight_loads = []
    for lo, hi in steps:
        at = pl.ds(lo, hi - lo)
        loads = []
        for src, dst in ((g_in, wg), (u_in, wu), (d_in, wd)):
            i = copies.used_local
            copies.used_local += 1
            loads.append(
                pltpu.make_async_copy(
                    src.at[:, :, :, :, at], dst.at[:, :, :, :, at], local.at[i]
                )
            )
            loads[-1].start()
        weight_loads.append(loads)
    later_loads = []
    for src, dst in ((dy_other_in, dy.at[1]), (res_in, res), (att_in, att), (wo_in, wo)):
        i = copies.used_local
        copies.used_local += 1
        later_loads.append(pltpu.make_async_copy(src, dst, local.at[i]))
        later_loads[-1].start()
    first()

    def tokens_step(unit, carry):
        side, row = unit // 2, unit - 2 * (unit // 2)
        here = pl.ds(pl.multiple_of(row * part, part), part)
        there = pl.ds(pl.multiple_of(unit * part, part), part)

        @pl.when(unit == 2)
        def _():
            tokens[0].wait_recv()
            for load in later_loads:
                load.wait()

        @pl.when(unit == 3)
        def _():
            tokens[1].wait()

        n2_here, dy_here = n2[side, here, :], dy[side, here, :]
        for step, (lo, hi) in enumerate(steps):
            @pl.when(unit == 0)
            def _(step=step):
                for load in weight_loads[step]:
                    load.wait()

            w_g, w_u, w_d = cols(wg, lo, hi), cols(wu, lo, hi), cols(wd, lo, hi)
            gate = mm(n2_here, w_g, NN)
            up = mm(n2_here, w_u, NN)
            a, dg, du = swish_grads(gate, up, mm(dy_here, w_d, NN))
            acts[there, lo:hi] = a
            grad_gates[there, lo:hi] = dg
            grad_ups[there, lo:hi] = du
            more_h = mm(dg, w_g, NT) + mm(du, w_u, NT)
            more_y = mm(a, w_d, NT)
            if lo == 0:
                h_acc[side, here, :] = more_h
                y_acc[side, here, :] = more_y

                @pl.when(unit == 1)
                def _():
                    tokens[0].wait_send()
                    tokens[1].start()
            else:
                h_acc[side, here, :] += more_h
                y_acc[side, here, :] += more_y

        @pl.when(unit == 2)
        def _():
            h_sent[halves[0], :] = h_acc[1, halves[0], :].astype(BF)
            back[0].start()

        @pl.when(unit == 3)
        def _():
            h_sent[halves[1], :] = h_acc[1, halves[1], :].astype(BF)
            back[1].start()

        return carry

    lax.fori_loop(0, 4, tokens_step, 0)
    low[...] = y_acc[1].astype(BF)
    y_kept = copies.keep(low, y_other_out)
    y_acc[0] += res[...]
    copies.keep(y_acc.at[0], y_out)

    for side, source in enumerate((n2, dy)):
        for t in range(2):
            def flip(i, side=side, source=source, t=t):
                at = pl.ds(pl.multiple_of(i * 256, 256), 256)
                flipped[side, at, t * rows : (t + 1) * rows] = jnp.transpose(source[t, :, at])

            each_pair(0, width // 256, flip)

    def weight_grad(m):
        def rows_step(z):
            left = flipped[m // 2, pl.ds(pl.multiple_of(z * 256, 256), 256), :]
            for lo, hi in steps:
                total = mm(left, inner_grads[m, :, lo:hi], NN).astype(BF)
                weights[m, z, :, :, :, lo:hi] = total.reshape(weights.shape[2:-1] + (hi - lo,))

        each_pair(0, 4, rows_step)

    each_pair(0, 3, weight_grad)
    for m, out in enumerate((dwg_out, dwu_out, dwd_out)):
        copies.keep(weights.at[m], out)

    copies.finish(y_kept)
    for copy in back:
        copy.wait()
    gain = gain_ref[1:2, :]
    y1 = res[...]
    scale = lax.rsqrt(jnp.mean(y1 * y1, axis=-1, keepdims=True) + EPSILON)
    hat = y1 * scale
    dh = h_acc[0] + h_got[...].astype(F32)
    dgain[...] = jnp.sum(dh * hat, axis=0, keepdims=True)
    dhat = dh * gain
    inner = jnp.mean(dhat * hat, axis=-1, keepdims=True)
    middle = dy[0].astype(F32) + (dhat - hat * inner) * scale
    h_acc[0] = middle
    low[...] = middle.astype(BF)
    copies.keep(h_acc.at[0], middle_out)
    copies.keep(dgain, dgain_out)
    weight = wo[...].reshape(-1, width)

    def out_step(i):
        at = pl.ds(pl.multiple_of(i * 256, 256), 256)
        total = mm(att[...], low[:, at], TN).astype(BF)
        dwo[:, :, :, :, :, at] = total.reshape(dwo.shape[:-1] + (256,))

    each_pair(0, width // 256, out_step)
    copies.keep(dwo, dwo_out)
    n2[0] = mm(low[...], weight, NT).astype(BF)
    copies.keep(n2.at[0], do_out)
    copies.drain()


def feed_forward(n2, dy, dy_other, res, weights, att, wo, gain):
    rows, width = n2.shape
    full, ff = weights[0].shape, weights[0].shape[-1]

    def like(shape, dtype):
        return jax.ShapeDtypeStruct(shape, dtype)

    def scratch(shape, dtype):
        return pltpu.VMEM(shape, dtype)

    out_shape = [like(full, BF)] * 3 + [
        like(wo.shape, BF), like((rows, width), BF), like((rows, width), F32),
        like((rows, width), F32), like((rows, width), BF), like((1, width), F32),
    ]
    token = (rows, width)
    anywhere = pl.BlockSpec(memory_space=pl.ANY)
    return pl.pallas_call(
        ffn_kernel,
        out_shape=out_shape,
        in_specs=[anywhere] * 9 + [pl.BlockSpec(memory_space=pltpu.VMEM)],
        out_specs=[anywhere] * len(out_shape),
        scratch_shapes=[scratch((3,) + full, BF)]
        + [scratch((2,) + token, BF)] * 2
        + [scratch((2, width, 2 * rows), BF)]
        + [scratch((3, 2 * rows, ff), BF)]
        + [scratch((2,) + token, F32)] * 2
        + [scratch(token, BF)] * 2
        + [scratch(token, F32), scratch(token, BF), scratch(wo.shape, BF), scratch(wo.shape, BF)]
        + [scratch(token, BF), scratch((1, width), F32)]
        + [
            pltpu.SemaphoreType.DMA((FFN_COPIES,)), pltpu.SemaphoreType.DMA((FFN_COPIES,)),
            pltpu.SemaphoreType.DMA((FFN_LOCALS,)),
        ],
        compiler_params=pltpu.CompilerParams(
            collective_id=3, has_side_effects=True, vmem_limit_bytes=62 << 20
        ),
        cost_estimate=pl.CostEstimate(flops=26 << 30, bytes_accessed=64 << 20, transcendentals=0),
        name="feed_forward",
    )(n2, dy, dy_other, res, *weights, att, wo, gain)


def backward(
    ffn_grads, out_grad, grad, att, rden, qkv, before, wq, x, middle, y, y_other, gain, dgain, ids,
    table, ends,
):
    rows, width = x.shape
    qk, hv = HEADS * QD, HEADS * VD
    fine, ff = ffn_grads[0].shape[-2:]
    small, full = wq.shape[-2:]

    def like(shape, dtype):
        return jax.ShapeDtypeStruct(shape, dtype)

    out_shape = [like((fine, ff), F32)] * 3 + [
        like((small, width), F32), like((small, qk), F32), like((small, qk), F32),
        like((small, hv), F32), like((small, GAIN_COLS), F32), like((rows, width), F32),
        like((rows, width), BF),
    ]
    scratch = []
    for _ in range(3):
        for lo, hi in half_columns(ff):
            scratch += PlaneScatter.shapes(fine, hi - lo)
    scratch += WideScatter.shapes(small, width)
    for lo, hi in projection_chunks(qk, hv, full):
        scratch += WideScatter.shapes(small, hi - lo)
    scratch += exchange_shapes()
    scratch += [
        pltpu.VMEM((rows, width), BF), pltpu.VMEM((rows, width), BF),
        pltpu.VMEM((2, 4, 2, 2, small, full), BF), pltpu.VMEM((rows, 1), F32),
        pltpu.VMEM((rows, 1), F32),
        pltpu.VMEM((rows, hv), BF), pltpu.VMEM((rows, width), BF), pltpu.VMEM((rows, hv), F32),
        pltpu.VMEM((rows, rows), F32), pltpu.VMEM((rows, qk), F32), pltpu.VMEM((rows, qk), F32),
        pltpu.VMEM((rows, hv), F32), pltpu.VMEM((PAIRS, FEATS, WIDE), BF),
        pltpu.VMEM((PAIRS, 8, FEATS), F32),
        pltpu.VMEM((2, 4, 2, 2, small, full), BF), pltpu.VMEM((rows, 2 * qk + hv), BF),
        pltpu.VMEM((rows, 2 * qk + hv), BF),
        pltpu.VMEM((PAIRS, FEATS, WIDE), BF), pltpu.VMEM((PAIRS, 8, FEATS), F32),
        pltpu.VMEM((8, width), F32), pltpu.VMEM((width, rows), BF),
        pltpu.SemaphoreType.DMA((BWD_COPIES,)), pltpu.SemaphoreType.DMA((BWD_COPIES,)),
        pltpu.SemaphoreType.DMA((BWD_LOCALS,)),
    ]
    vmem = pl.BlockSpec(memory_space=pltpu.VMEM)
    anywhere = pl.BlockSpec(memory_space=pl.ANY)
    return pl.pallas_call(
        backward_kernel,
        out_shape=out_shape,
        in_specs=[anywhere] * 15 + [vmem] * 4 + [pl.BlockSpec(memory_space=pltpu.SMEM)],
        out_specs=[anywhere] * len(out_shape),
        scratch_shapes=scratch,
        compiler_params=pltpu.CompilerParams(
            collective_id=2, has_side_effects=True, vmem_limit_bytes=62 << 20
        ),
        cost_estimate=pl.CostEstimate(flops=16 << 30, bytes_accessed=64 << 20, transcendentals=0),
        name="backward",
    )(
        *ffn_grads, out_grad, grad, att, rden, qkv, *before, wq, x, middle, y, y_other, gain,
        dgain, ids, table, ends,
    )


def result_pieces(shape):
    parts = 4 if shape[0] % 64 == 0 and shape[0] >= 512 else 1
    size = shape[0] // parts
    return [pl.ds(i * size, size) for i in range(parts)]


def deliver_kernel(count, *refs):
    ins, gains_in, rest = refs[:count], refs[count], refs[count + 1 :]
    outs, one_out, two_out, rest = rest[:count], rest[count], rest[count + 1], rest[count + 2 :]
    bufs, (sem_in, sem_out) = rest[:count], rest[count:]
    loads, stores = [], []
    for i in range(count):
        pieces = result_pieces(ins[i].shape)
        for at in pieces:
            k = len(loads)
            loads.append(pltpu.make_async_copy(ins[i].at[at], bufs[i].at[at], sem_in.at[k]))
            stores.append(pltpu.make_async_copy(bufs[i].at[at], outs[i].at[at], sem_out.at[k]))
            loads[-1].start()
    turned = jnp.transpose(gains_in[...])
    one_out[...] = turned[0:1, :]
    two_out[...] = turned[1:2, :]
    for load, store in zip(loads, stores):
        load.wait()
        store.start()
    for store in stores:
        store.wait()


def deliver(plain, gains):
    count = len(plain)
    far, vmem = pl.BlockSpec(memory_space=pltpu.HBM), pl.BlockSpec(memory_space=pltpu.VMEM)
    small = gains.shape[0]
    return pl.pallas_call(
        functools.partial(deliver_kernel, count),
        out_shape=[jax.ShapeDtypeStruct(a.shape, a.dtype) for a in plain]
        + [jax.ShapeDtypeStruct((1, small), F32)] * 2,
        in_specs=[far] * count + [vmem],
        out_specs=[far] * count + [vmem] * 2,
        scratch_shapes=[pltpu.VMEM(a.shape, a.dtype) for a in plain]
        + [pltpu.SemaphoreType.DMA((sum(len(result_pieces(a.shape)) for a in plain),))] * 2,
        compiler_params=pltpu.CompilerParams(vmem_limit_bytes=62 << 20),
        name="deliver",
    )(*plain, gains)


def rms_scale(values, gain):
    return values * lax.rsqrt(jnp.mean(values * values, axis=-1, keepdims=True) + EPSILON) * gain


def swish_mix(gate, up_proj):
    return jax.nn.silu(gate) * up_proj


def dot_nn(a, b):
    return jnp.dot(a, b, preferred_element_type=F32)


def dot_nt(a, b):
    return lax.dot_general(a, b, (((1,), (1,)), ((), ())), preferred_element_type=F32)


def dot_tn(a, b):
    return lax.dot_general(a, b, (((0,), (0,)), ((), ())), preferred_element_type=F32)


def row_grads(left, right, by_head):
    head, core = lax.axis_index("head"), lax.axis_index("seq") % 2
    tokens = left.shape[0]
    chips = lax.axis_size("seq") // 2
    heads = 2 if by_head else 1
    rows = left.shape[1] // (heads * chips * 2)
    split = left.reshape(tokens, heads, chips, 2, rows)
    out = []
    for rel in range(heads):
        plane = pick(split, head ^ rel, 1) if by_head else split[:, 0]
        out.append([pick(plane, core ^ r, 2).reshape(tokens, chips * rows) for r in range(2)])
    if by_head:
        return [[dot_tn(part, right).astype(BF) for part in parts] for parts in out]
    return [[dot_tn(part, r).astype(BF) for part in out[0]] for r in right]


def plain_forward(
    inputs, segment_ids, norm1_gain, w_query, w_key, w_value, w_out, norm2_gain, w_gate, w_up,
    w_down, row_ids, col_ids, first, last, table,
):
    head, seq = lax.axis_index("head"), lax.axis_index("seq")
    n_seq = lax.axis_size("seq")
    rows, width = inputs.shape
    qk = HEADS * QD
    slot = head * n_seq + seq
    small = norm1_gain.shape[0]
    gains = jnp.zeros((2, width // small, small), F32)
    gains = lax.dynamic_update_slice(
        gains, jnp.stack([norm1_gain, norm2_gain]).astype(F32)[:, None, :], (0, slot, 0)
    ).reshape(2, width)
    gains = sum_everywhere(gains)
    gain_first, gain_second = gains[0], gains[1]

    qkv_full = gather_rows(jnp.concatenate([w_query, w_key, w_value], axis=1))
    out_full = gather_rows(w_out)
    gate_w = gather_halves(w_gate, False)
    up_w = gather_halves(w_up, False)
    down_w = gather_halves(w_down.T, True)

    normed_one = rms_scale(inputs, gain_first).astype(BF)
    qkv = dot_nn(normed_one, qkv_full).astype(BF)
    query, keys, values = qkv[:, :qk], qkv[:, qk : 2 * qk], qkv[:, 2 * qk :]
    vcols = HEADS * VD
    t_spec, q_spec = full_spec((8, FEATS)), full_spec((rows, qk))
    one_spec, row_spec = full_spec((rows, 1)), full_spec((1, rows))
    p_spec = pair_spec(rows)
    f32_like = jax.ShapeDtypeStruct((rows, vcols), F32)
    bf_like = jax.ShapeDtypeStruct((rows, vcols), BF)
    state = run(
        state_kernel,
        [t_spec, q_spec, p_spec, one_spec],
        state_specs(),
        STATE_SHAPES,
        (table, keys, values, last),
        flops=8 * rows * qk * FEATS * HEADS,
    )
    num, den = run(
        local_kernel,
        [q_spec, q_spec, p_spec, one_spec, row_spec],
        [p_spec, p_spec],
        [f32_like, f32_like],
        (query, keys, values, row_ids, col_ids),
        [pltpu.VMEM((rows, rows), F32)],
        flops=8 * rows * rows * qk * HEADS,
    )
    before = exchange(*state, segment_ids, rows, True)
    attended, rden = run(
        finish_kernel,
        [t_spec, q_spec, p_spec, p_spec, one_spec] + state_specs(),
        [p_spec, p_spec],
        [bf_like, f32_like],
        (table, query, num, den, first, *before),
        flops=8 * rows * qk * FEATS * HEADS,
    )
    residual = inputs + dot_nn(attended, out_full)
    normed_two = rms_scale(residual, gain_second).astype(BF)

    return (
        gate_w, up_w, down_w, qkv_full, out_full, gain_first, gain_second, normed_one,
        query, keys, values, attended, rden, residual, normed_two, before,
    )


def body(
    layer_input,
    segment_ids,
    norm1_gain,
    w_query,
    w_key,
    w_value,
    w_out,
    norm2_gain,
    w_gate,
    w_up,
    w_down,
    output_grad,
):
    rows = layer_input.shape[1]
    head, seq = lax.axis_index("head"), lax.axis_index("seq")
    n_seq = lax.axis_size("seq")
    qk = HEADS * QD
    inputs = layer_input[0].astype(F32)
    width = inputs.shape[1]

    table = jnp.asarray(feature_table())
    vcols = HEADS * VD
    t_spec, q_spec = full_spec((8, FEATS)), full_spec((rows, qk))
    one_spec, row_spec = full_spec((rows, 1)), full_spec((1, rows))
    p_spec = pair_spec(rows)
    f32_like = jax.ShapeDtypeStruct((rows, vcols), F32)
    bf_like = jax.ShapeDtypeStruct((rows, vcols), BF)
    slot = head * n_seq + seq
    small = norm1_gain.shape[0]

    if n_seq == 16:
        gain_cols = jnp.stack([norm1_gain, norm2_gain], axis=1)
        gain_cols = jnp.pad(gain_cols, ((0, 0), (0, GAIN_COLS - 2)))
        ids = segment_ids.reshape(2 * n_seq, rows)
        ends = jnp.concatenate([ids[:, 0], ids[:, rows - 1]])
        (
            g_own, u_own, d_own, dy_other, wq, wo, qkv, attended, rden, residual,
            normed_two, wide, thin, gains,
        ) = forward(
            layer_input[0],
            [w_query, w_key, w_value, gain_cols],
            w_out,
            [w_gate, w_up, w_down.T],
            output_grad[0],
            ids, table, ends,
        )
        d_gate, d_up, d_down, d_out, grad_attended, grad_middle, y, y_other, grad_gain = (
            feed_forward(
                normed_two, output_grad[0], dy_other, residual, [g_own, u_own, d_own],
                attended, wo, gains,
            )
        )
        d_gate, d_up, d_down, d_out, d_q, d_k, d_v, d_gains, grad_layer, outcome = backward(
            [d_gate, d_up, d_down], d_out, grad_attended, attended, rden, qkv, (wide, thin), wq,
            layer_input[0], grad_middle, y, y_other, gains, grad_gain, ids, table, ends,
        )
        (
            d_gate, d_up, d_down, d_q, d_out, outcome, grad_layer, d_v, d_k, gain_one, gain_two,
        ) = deliver(
            [d_gate, d_up, d_down, d_q, d_out, outcome, grad_layer, d_v, d_k], d_gains
        )
        return (
            outcome[None], grad_layer[None], gain_one[0], d_q, d_k, d_v, d_out, gain_two[0],
            d_gate, d_up, d_down.T,
        )

    segment = 2 * seq + head
    ids = lax.dynamic_slice_in_dim(segment_ids, segment * rows, rows)
    row_ids, col_ids = ids[:, None], ids[None, :]
    first = (row_ids == ids[0]).astype(F32)
    last = (row_ids == ids[rows - 1]).astype(F32)
    (
        gate_w, up_w, down_w, qkv_full, out_full, gain_first, gain_second, normed_one,
        query, keys, values, attended, rden, residual, normed_two, before,
    ) = plain_forward(
        inputs, segment_ids, norm1_gain, w_query, w_key, w_value, w_out, norm2_gain, w_gate,
        w_up, w_down, row_ids, col_ids, first, last, table,
    )

    grad_output = output_grad[0]
    outcome = residual
    grad_normed_two = None
    hiddens, grad_gates, grad_ups = [], [], []
    for w_g, w_u, w_d in zip(gate_w, up_w, down_w):
        gate = dot_nn(normed_two, w_g)
        up_proj = dot_nn(normed_two, w_u)
        grad_hidden = dot_nn(grad_output, w_d)
        hidden, mix_pull = jax.vjp(swish_mix, gate, up_proj)
        grad_gate, grad_up = mix_pull(grad_hidden)
        hiddens.append(hidden.astype(BF))
        grad_gates.append(grad_gate.astype(BF))
        grad_ups.append(grad_up.astype(BF))
        outcome = outcome + dot_nt(hiddens[-1], w_d)
        more = dot_nt(grad_gates[-1], w_g) + dot_nt(grad_ups[-1], w_u)
        grad_normed_two = more if grad_normed_two is None else grad_normed_two + more
    outcome = outcome.astype(BF)
    _, norm_pull = jax.vjp(rms_scale, residual, gain_second)
    grad_resid_two, grad_gain_two = norm_pull(grad_normed_two)
    grad_middle = grad_output.astype(F32) + grad_resid_two
    grad_middle_low = grad_middle.astype(BF)
    grad_attended = dot_nt(grad_middle_low, out_full).astype(BF)

    d_gate = scatter(row_grads(normed_two, grad_gates, False), True)
    d_up = scatter(row_grads(normed_two, grad_ups, False), True)
    d_down = scatter(row_grads(grad_output, hiddens, False), False).T

    d_out = scatter(row_grads(attended, grad_middle_low, True), True)

    grad_state = run(
        grad_state_kernel,
        [t_spec, q_spec, p_spec, p_spec, p_spec, one_spec],
        state_specs(),
        STATE_SHAPES,
        (table, query, grad_attended, attended, rden, first),
        flops=8 * rows * qk * FEATS * HEADS,
    )
    qk_f32 = jax.ShapeDtypeStruct((rows, qk), F32)
    qk_bf = jax.ShapeDtypeStruct((rows, qk), BF)
    grad_query, grad_key, grad_value = run(
        local_grad_kernel,
        [t_spec, q_spec, q_spec, p_spec, p_spec, p_spec, p_spec, one_spec, row_spec, one_spec]
        + state_specs(),
        [q_spec, q_spec, p_spec],
        [qk_bf, qk_f32, f32_like],
        (table, query, keys, values, grad_attended, attended, rden, row_ids, col_ids, first)
        + tuple(before),
        [pltpu.VMEM((rows, rows), F32), pltpu.VMEM((rows, qk), F32), pltpu.VMEM((rows, qk), F32)],
        flops=20 * rows * rows * qk * HEADS,
    )
    after = exchange(*grad_state, segment_ids, rows, False)
    grad_key, grad_value = run(
        finish_grad_kernel,
        [t_spec, q_spec, p_spec, q_spec, p_spec, one_spec] + state_specs(),
        [q_spec, p_spec],
        [qk_bf, bf_like],
        (table, keys, values, grad_key, grad_value, last, *after),
        [pltpu.VMEM((rows, qk), F32)],
        flops=16 * rows * qk * FEATS * HEADS,
    )
    grad_qkv = jnp.concatenate([grad_query, grad_key, grad_value], axis=1)
    d_qkv = scatter(row_grads(normed_one, grad_qkv, True), True)
    grad_normed_one = dot_nt(grad_qkv, qkv_full)
    _, first_pull = jax.vjp(rms_scale, inputs, gain_first)
    grad_inputs, grad_gain_one = first_pull(grad_normed_one)
    grad_layer = grad_middle + grad_inputs
    grad_gains = sum_everywhere(jnp.stack([grad_gain_one, grad_gain_two]))
    grad_gains = lax.dynamic_slice_in_dim(
        grad_gains.reshape(2, width // small, small), slot, 1, 1
    )[:, 0]
    return (
        outcome[None],
        grad_layer[None],
        grad_gains[0],
        d_qkv[:, :qk],
        d_qkv[:, qk : 2 * qk],
        d_qkv[:, 2 * qk :],
        d_out,
        grad_gains[1],
        d_gate,
        d_up,
        d_down,
    )


def solution(mesh):
    split = P(("head", "seq"))
    rows = P(("head", "seq"), None)
    block = P("seq", "head", None)
    wide, tall = P("seq", "head"), P("head", "seq")
    in_specs = (block, P(), split, rows, rows, rows, rows, split, wide, wide, tall, block)
    out_specs = (block, block, split, rows, rows, rows, rows, split, wide, wide, tall)
    return jax.shard_map(body, mesh=mesh, in_specs=in_specs, out_specs=out_specs, check_vma=False)
```
